32 devices in a mesh: grp: 4 (over y, x), sec: 8 (over z, core).
Axes of the slice: x: 2, y: 2, z: 4, core: 2. Of those that a mesh axis runs over, the one named last changes fastest.
Arguments:
- fields: bfloat16 [8, 32, 32, 192], P('grp', None, 'sec'), may hold values from -6 to 6
- valid_rows: int32 [8], P('grp'), may hold values from 8 to 32, as said below
- w_embed: bfloat16 [3, 192, 1024], replicated, may hold values from -0.25 to 0.25
- ln1_gain: bfloat16 [1024], replicated, may hold values from 0.25 to 1.75
- w_qkv: bfloat16 [1024, 3072], replicated, may hold values from -0.1875 to 0.1875
- w_out: bfloat16 [1024, 1024], replicated, may hold values from -6 to 6
- ln2_gain: bfloat16 [1024], replicated, may hold values from 0.25 to 1.75
- w_up: bfloat16 [1024, 4096], replicated, may hold values from -0.1875 to 0.1875
- b_up: bfloat16 [4096], replicated, may hold values from -3 to 3
- w_down: bfloat16 [4096, 1024], replicated, may hold values from -0.09375 to 0.09375
- w_head: bfloat16 [3, 1024, 192], replicated, may hold values from -0.109375 to 0.109375
- cotangent: bfloat16 [8, 32, 32, 192], P('grp', None, 'sec'), may hold values from -6 to 6
Outputs:
- head_output: float32 [8, 32, 32, 192], P('grp', None, 'sec')
- input_grad: float32 [8, 32, 32, 192], P('grp', None, 'sec')
- embed_grad: float32 [3, 192, 1024], P(None, None, 'sec')
- gain_one_grad: float32 [1024], P('sec')
- qkv_grad: float32 [1024, 3072], P('sec')
- out_grad: float32 [1024, 1024], P('sec')
- gain_two_grad: float32 [1024], P('sec')
- up_grad: float32 [1024, 4096], P('sec')
- bias_grad: float32 [4096], P('sec')
- down_grad: float32 [4096, 1024], P('sec')
- head_grad: float32 [3, 1024, 192], P(None, 'sec')
The draws below stay inside these ranges and needn't reach their ends.
Inputs may be any that keep to these rules, and one draw needn't show every extreme that they name: Rows 0 to valid_rows - 1 of a sample are data, the rest padding; at least 8 rows (one at least) are data, and some sample has all 32 rows.
All inputs are finite; a program needn't handle non-finite values.
Results may differ from the reference program's by a relative error of at most 0.022.
Values may be sent and summed in bfloat16 or wider, within the bound.
No kernel may reach another device: no remote copies, remote signals or barrier semaphores. Data moves between devices by JAX's collectives and lax.ppermute only.
A program may use at most 192 MiB of HBM per device.

```python
from functools import partial
import jax
import jax.numpy as jnp
from jax import lax

D = 1024
HEADS = 16
HEAD_DIM = 64
FF = 4096
LAT = 32
COL_DEV = 4
CHAN = 192
LON = 32
SAMPLES = 8
N_SEC = 8


def draw_valid_rows(key, part):
    least_rows = max(1, LAT // 4)
    drawn_rows = jax.random.randint(key, (SAMPLES,), least_rows, LAT + 1)
    full_index = jax.random.randint(jax.random.fold_in(key, 7), (), 0, SAMPLES)
    return jnp.where(jnp.arange(SAMPLES) == full_index, LAT, drawn_rows).astype(jnp.int32)


def shard_levels(rng, dims, pieces, smallest, largest):
    factor_of = 1.0
    for axis_at, parts in pieces:
        steps = jax.random.uniform(jax.random.fold_in(jax.random.fold_in(rng, 6), axis_at), (parts,), jnp.float32, smallest / len(pieces), largest / len(pieces))
        factor_of = factor_of * jnp.repeat(jnp.exp(steps), dims[axis_at] // parts).reshape((-1,) + (1,) * (len(dims) - 1 - axis_at))
    return factor_of


def noise(rng, dims, deviation, bound, split=(), kind=jnp.bfloat16):
    drawn = jax.random.normal(rng, dims, jnp.float32) * deviation
    if len(split) > 0:
        drawn = shard_levels(rng, dims, split, -0.22, 0.18) * drawn
    return jnp.clip(drawn, min=-bound, max=bound).astype(kind)


def setup_inputs(seed: int = 0) -> dict:
    arg_keys = jax.random.split(jax.random.key(seed), 13)
    fields = noise(arg_keys[0], (SAMPLES, LAT, LON, CHAN), 1.0, 6.0, ((0, 4), (2, 8)))
    valid_rows = draw_valid_rows(jax.random.fold_in(arg_keys[12], 71), 0)
    w_embed = noise(arg_keys[2], (3, CHAN, D), (3 * CHAN) ** -0.5, 0.25)
    ln1_gain = jnp.clip(1.0 + 0.15 * jax.random.normal(arg_keys[3], (D,), jnp.float32), 0.25, 1.75).astype(jnp.bfloat16)
    w_qkv = noise(arg_keys[4], (D, 3 * D), D ** -0.5, 0.1875)
    w_out = noise(arg_keys[5], (D, D), (max(1, (LAT * COL_DEV * N_SEC // D) ** 0.5)), 6.0)
    ln2_gain = jnp.clip(1.0 + 0.15 * jax.random.normal(arg_keys[6], (D,), jnp.float32), 0.25, 1.75).astype(jnp.bfloat16)
    w_up = noise(arg_keys[7], (D, FF), D ** -0.5, 0.1875)
    b_up = noise(arg_keys[8], (FF,), 0.5, 3.0)
    w_down = noise(arg_keys[9], (FF, D), FF ** -0.5, 0.09375)
    w_head = noise(arg_keys[10], (3, D, CHAN), (3 * D) ** -0.5, 0.109375)
    cotangent = noise(arg_keys[11], (SAMPLES, LAT, LON, CHAN), 1.0, 6.0, ((0, 4), (2, 8)))
    return dict(fields=fields, valid_rows=valid_rows, w_embed=w_embed, ln1_gain=ln1_gain, w_qkv=w_qkv, w_out=w_out, ln2_gain=ln2_gain, w_up=w_up, b_up=b_up, w_down=w_down, w_head=w_head, cotangent=cotangent)


highest = lax.Precision.HIGHEST

@jax.custom_vjp
def low(v):
    return lax.optimization_barrier(v.astype(jnp.bfloat16)).astype(jnp.float32)

@jax.custom_vjp
def low_back(v):
    return v

def low_keep(v):
    return (low(v), None)

def low_pass(kept, grad):
    return (grad,)

def back_keep(v):
    return (v, None)

def back_low(kept, grad):
    return (low(grad),)
low.defvjp(low_keep, low_pass)
low_back.defvjp(back_keep, back_low)

def widen(field):
    return jnp.concatenate([jnp.roll(field, 1, axis=2), field, jnp.roll(field, -1, axis=2)], axis=-1)

def layer_norm(hidden, gains):
    center = hidden - lax.optimization_barrier(jnp.mean(hidden, axis=-1, keepdims=True))
    spread = lax.optimization_barrier(jnp.mean(center * center, axis=-1, keepdims=True))
    return center * lax.rsqrt(spread + 1e-05) * gains

def project(values, matrix):
    return jnp.einsum('...i,ij->...j', values, matrix, precision=highest)

def attend_sample(packed):
    queries, keys, values, valid = packed
    key_heads = keys.reshape(LAT * LON, HEADS, HEAD_DIM)
    value_heads = values.reshape(LAT * LON, HEADS, HEAD_DIM)
    allowed = jnp.broadcast_to(jnp.arange(LAT)[:, None] < valid, (LAT, LON)).reshape(LAT * LON)
    sectors = queries.reshape(LAT, N_SEC, COL_DEV, HEADS, HEAD_DIM).transpose(1, 0, 2, 3, 4)
    sectors = sectors.reshape(N_SEC, LAT * COL_DEV, HEADS, HEAD_DIM)

    def attend_block(block_queries):
        key_low = low_back(key_heads)
        value_low = low_back(value_heads)
        raw_scores = jnp.einsum('qhd,khd->hqk', block_queries, key_low, precision=highest)
        scores = low_back(raw_scores * 0.125)
        scores = jnp.where(allowed[None, None, :], scores, -1e+30)
        row_max = lax.optimization_barrier(jnp.max(scores, axis=-1, keepdims=True))
        log_total = row_max + jnp.log(lax.optimization_barrier(jnp.sum(jnp.exp(scores - row_max), axis=-1, keepdims=True)))
        probs = low(jnp.exp(scores - log_total))
        return jnp.einsum('hqk,khd->qhd', probs, value_low, precision=highest)
    outputs = lax.map(jax.checkpoint(attend_block), sectors)
    outputs = outputs.reshape(N_SEC, LAT, COL_DEV, D).transpose(1, 0, 2, 3)
    return outputs.reshape(LAT, LON, D)

def forward(valid_rows, input_f, embed_w, gain_one, qkv_w, out_w, gain_two, up_w, up_bias, down_w, head_w):
    embedded = low_back(project(widen(input_f), embed_w.reshape(3 * CHAN, D)))
    normed_one = low(layer_norm(embedded, gain_one))
    qkv_all = low(low_back(project(normed_one, qkv_w)))
    attended_raw = lax.map(attend_sample, (qkv_all[..., :D], qkv_all[..., D:2 * D], qkv_all[..., 2 * D:], valid_rows))
    attended = low(low_back(attended_raw))
    hidden1 = embedded + low_back(project(attended, out_w))
    normed_two = low(layer_norm(hidden1, gain_two))
    preact = low_back(project(normed_two, up_w) + up_bias)
    activ = low(jax.nn.gelu(preact, approximate=False))
    hidden2 = hidden1 + low_back(project(activ, down_w))
    return project(widen(low(hidden2)), head_w.reshape(3 * D, CHAN))

def reference(fields, valid_rows, w_embed, ln1_gain, w_qkv, w_out, ln2_gain, w_up, b_up, w_down, w_head, cotangent):
    inputs = (fields, w_embed, ln1_gain, w_qkv, w_out, ln2_gain, w_up, b_up, w_down, w_head)
    floats = tuple((item.astype(jnp.float32) for item in inputs))
    head_out, vjp_fn = jax.vjp(partial(forward, valid_rows), *floats)
    grads = vjp_fn(cotangent.astype(jnp.float32))
    return (head_out, grads[0], grads[1], grads[2], grads[3], grads[4], grads[5], grads[6], grads[7], grads[8], grads[9])
```

```python
import jax
import jax.numpy as jnp
import numpy as np
from jax import lax
from jax.experimental import pallas as pl
from jax.experimental.pallas import tpu as pltpu
from jax.sharding import PartitionSpec as P

HEAD_DIM = 64
HEADS = 16
LANES = 128
BF = jnp.bfloat16
F32 = jnp.float32

NN = ((1,), (0,))
NT = ((1,), (1,))
TN = ((0,), (0,))

TEAM, ME, GRP, VALID = range(4)


def dot(a, b, dims):
    return lax.dot_general(a, b, (dims, ((), ())), preferred_element_type=F32)


def swap(x, axis, bit):
    n = lax.axis_size(axis)
    return lax.ppermute(x, axis, [(i, i ^ bit) for i in range(n)])


def kernel(body, name, scalars, grid, ins, outs, scratch=(), aliases=None):
    def spec(block, index):
        if block is None:
            return pl.BlockSpec(memory_space=pl.ANY)
        return pl.BlockSpec(block, index)

    return pl.pallas_call(
        body,
        grid_spec=pltpu.PrefetchScalarGridSpec(
            num_scalar_prefetch=1,
            grid=grid,
            in_specs=[spec(block, index) for _, block, index in ins],
            out_specs=[spec(block, index) for _, _, block, index in outs],
            scratch_shapes=list(scratch),
        ),
        out_shape=[jax.ShapeDtypeStruct(shape, kind) for shape, kind, _, _ in outs],
        input_output_aliases=aliases or {},
        compiler_params=pltpu.CompilerParams(vmem_limit_bytes=56 * 1024 * 1024),
        name=name,
    )(scalars, *[array for array, _, _ in ins])


def whole(array):
    rank = len(array.shape)
    return (array, array.shape, lambda *_: (0,) * rank)


def whole_out(shape, kind):
    rank = len(shape)
    return (shape, kind, shape, lambda *_: (0,) * rank)


class Sizes:
    def __init__(self, fields, w_qkv, w_up):
        self.teams, self.lat, self.cols, self.chan = fields.shape
        self.sectors = lax.axis_size("sec")
        self.members = self.sectors // self.teams
        self.group = lax.axis_size("grp")
        self.d = w_qkv.shape[0]
        self.ff = w_up.shape[1]
        self.sec_tokens = self.lat * self.cols
        self.tokens = self.sectors * self.sec_tokens
        self.heads = HEADS // self.members
        self.width = self.heads * HEAD_DIM
        self.db = self.d // self.sectors
        self.fb = self.ff // self.sectors
        self.dn = self.teams * self.db
        self.fn = self.teams * self.fb
        self.own = self.tokens // self.members
        self.half = self.tokens // 2


def line_up(s, scalars, pieces, canon):
    for j, piece in enumerate(pieces):
        for k in range(s.teams):
            at = (scalars[TEAM] ^ k) * s.members + (scalars[ME] ^ j)
            canon[at] = piece[k]


def beside(s, canon, sector):
    mid = canon[sector].astype(F32)
    before = canon[lax.rem(sector + s.sectors - 1, s.sectors)].astype(F32)
    after = canon[lax.rem(sector + 1, s.sectors)].astype(F32)
    col = lax.rem(lax.broadcasted_iota(jnp.int32, mid.shape, 0), s.cols)
    rows = s.sec_tokens
    west = jnp.where(col == 0, pltpu.roll(before, rows - (s.cols - 1), 0), pltpu.roll(mid, 1, 0))
    east = jnp.where(col == s.cols - 1, pltpu.roll(after, s.cols - 1, 0), pltpu.roll(mid, rows - 1, 0))
    return west, mid, east


def normed_rows(rows):
    center = rows - jnp.mean(rows, axis=-1, keepdims=True)
    rstd = lax.rsqrt(jnp.mean(center * center, axis=-1, keepdims=True) + 1e-05)
    return center * rstd, rstd


def embed_qkv(s, scalars, pieces, w_embed, gain, w_qkv):
    rows = s.half
    per = rows // s.sec_tokens
    chunk = s.sec_tokens

    def body(sc, *refs):
        parts = refs[: s.members]
        we, g, wq, wk, wv = refs[s.members : s.members + 5]
        cat_ref, hid_ref, norm_ref, qkv_ref, canon = refs[s.members + 5 :]
        i = pl.program_id(0)

        @pl.when(i == 0)
        def _():
            line_up(s, sc, parts, canon)

        for p in range(per):
            at = slice(p * chunk, (p + 1) * chunk)
            west, mid, east = beside(s, canon, i * per + p)
            cat_ref[at, :] = jnp.concatenate([west, mid, east], axis=1).astype(BF)
        hid_ref[...] = dot(cat_ref[...], we[...], NN)
        for p in range(per):
            at = slice(p * chunk, (p + 1) * chunk)
            xhat, _ = normed_rows(hid_ref[at, :])
            norm_ref[at, :] = (xhat * g[...]).astype(BF)
        for k, w in enumerate((wq, wk, wv)):
            qkv_ref[:, k * s.width : (k + 1) * s.width] = dot(norm_ref[...], w[...], NN).astype(BF)

    def third(k):
        return (w_qkv, (s.d, s.width), lambda i, sc: (0, k * s.members + sc[ME]))

    row = lambda i, sc: (i, 0)
    return kernel(
        body,
        "embed_qkv",
        scalars,
        (s.tokens // rows,),
        [whole(p) for p in pieces] + [whole(w_embed), whole(gain), third(0), third(1), third(2)],
        [
            ((s.tokens, 3 * s.chan), BF, (rows, 3 * s.chan), row),
            ((s.tokens, s.d), F32, (rows, s.d), row),
            ((s.tokens, s.d), BF, (rows, s.d), row),
            ((s.tokens, 3 * s.width), BF, (rows, 3 * s.width), row),
        ],
        [pltpu.VMEM((s.sectors, s.sec_tokens, s.chan), BF)],
    )


def cotangent_grad(s, scalars, pieces, w_head):
    rows = s.half
    per = rows // s.sec_tokens

    def body(sc, *refs):
        parts = refs[: s.members]
        wh, cat_ref, grad_ref, canon = refs[s.members :]
        i = pl.program_id(0)

        @pl.when(i == 0)
        def _():
            line_up(s, sc, parts, canon)

        for p in range(per):
            at = slice(p * s.sec_tokens, (p + 1) * s.sec_tokens)
            west, mid, east = beside(s, canon, i * per + p)
            cat_ref[at, :] = jnp.concatenate([east, mid, west], axis=1).astype(BF)
        total = dot(cat_ref[:, : s.chan], wh[0], NT)
        total += dot(cat_ref[:, s.chan : 2 * s.chan], wh[1], NT)
        total += dot(cat_ref[:, 2 * s.chan :], wh[2], NT)
        grad_ref[...] = total.astype(BF)

    row = lambda i, sc: (i, 0)
    return kernel(
        body,
        "cotangent_grad",
        scalars,
        (s.tokens // rows,),
        [whole(p) for p in pieces] + [whole(w_head)],
        [
            ((s.tokens, 3 * s.chan), BF, (rows, 3 * s.chan), row),
            ((s.tokens, s.d), BF, (rows, s.d), row),
        ],
        [pltpu.VMEM((s.sectors, s.sec_tokens, s.chan), BF)],
    )


def side_of(s, sc, far):
    own = sc[ME] // (s.members // 2)
    return own ^ 1 if far else own


def attention_fwd(s, scalars, qkv, far):
    rows = min(256, s.half)
    steps = s.half // rows

    def body(sc, q_ref, kv_ref, att_ref, prob_ref):
        key = lax.broadcasted_iota(jnp.int32, (1, s.tokens), 1)
        allowed = lax.rem(key, s.sec_tokens) // s.cols < sc[VALID]
        for h in range(s.heads):
            cols = slice(h * HEAD_DIM, (h + 1) * HEAD_DIM)
            kcols = slice(s.width + h * HEAD_DIM, s.width + (h + 1) * HEAD_DIM)
            vcols = slice(2 * s.width + h * HEAD_DIM, 2 * s.width + (h + 1) * HEAD_DIM)
            scores = dot(q_ref[:, cols] * jnp.asarray(0.125, BF), kv_ref[:, kcols], NT)
            scores = jnp.where(allowed, scores, -1e30)
            weights = jnp.exp(scores - jnp.max(scores, axis=-1, keepdims=True))
            probs = (weights * (1.0 / jnp.sum(weights, axis=-1, keepdims=True))).astype(BF)
            prob_ref[h] = probs
            att_ref[:, cols] = dot(probs, kv_ref[:, vcols], NN).astype(BF)

    return kernel(
        body,
        "attention_fwd",
        scalars,
        (steps,),
        [
            (qkv, (rows, 3 * s.width), lambda i, sc: (side_of(s, sc, far) * steps + i, 0)),
            whole(qkv),
        ],
        [
            ((s.half, s.width), BF, (rows, s.width), lambda i, sc: (i, 0)),
            ((s.heads, s.half, s.tokens), BF, (s.heads, rows, s.tokens), lambda i, sc: (0, i, 0)),
        ],
    )


def mlp(s, scalars, att, hidden0, grad_mlp, w_out, gain, w_up, b_up, w_down, far):
    extra = 16
    chunk = 64
    rows = s.half
    count = len(att)

    def body(sc, *refs):
        parts = refs[:count]
        h0, gm, g, bias, wo_hbm, wu_hbm, wd_hbm = refs[count : count + 7]
        outs = refs[count + 7 :]
        att_ref, n2_ref, act_ref, gpre_ref, gkeep, gsend, pkeep, psend, hown, bsum = outs[:10]
        h1_ref = outs[10]
        wo, wu, wd, pre, gact, sem = outs[11:]
        me = sc[ME]

        copies = [pltpu.make_async_copy(wo_hbm, wo, sem.at[0])]
        for k in range(s.teams):
            at = pl.multiple_of((k * s.members + me) * s.fb, s.fb)
            copies.append(
                pltpu.make_async_copy(
                    wu_hbm.at[:, pl.ds(at, s.fb)], wu.at[:, pl.ds(k * s.fb, s.fb)], sem.at[1 + k]
                )
            )
        for k in range(s.teams):
            at = pl.multiple_of((k * s.members + me) * s.fb, s.fb)
            copies.append(
                pltpu.make_async_copy(
                    wd_hbm.at[pl.ds(at, s.fb), :],
                    wd.at[pl.ds(k * s.fb, s.fb), :],
                    sem.at[1 + s.teams + k],
                )
            )
        for copy in copies:
            copy.start()
        for j in range(count):
            at = pl.multiple_of((me ^ j) * s.width, s.width)
            att_ref[:, pl.ds(at, s.width)] = parts[j][...]
        copies[0].wait()
        h1_ref[...] = h0[...] + dot(att_ref[...], wo[...], NN)

        def norm_chunk(c, carry):
            at = pl.ds(pl.multiple_of(c * chunk, chunk), chunk)
            xhat, _ = normed_rows(h1_ref[at, :])
            n2_ref[at, :] = (xhat * g[...]).astype(BF)
            return carry

        lax.fori_loop(0, rows // chunk, norm_chunk, 0)
        for k in range(s.teams):
            at = pl.multiple_of((k * s.members + me) * s.db, s.db)
            hown[:, k * s.db : (k + 1) * s.db] = h1_ref[:, pl.ds(at, s.db)]
        for copy in copies[1 : 1 + s.teams]:
            copy.wait()
        pre[...] = dot(n2_ref[...], wu[...], NN)
        for copy in copies[1 + s.teams :]:
            copy.wait()
        gact[...] = dot(gm[...], wd[...], NT)

        def gelu_chunk(c, total):
            at = pl.ds(pl.multiple_of(c * chunk, chunk), chunk)
            u = pre[at, :] + bias[...]
            cdf = 0.5 * (1.0 + lax.erf(u * np.float32(2**-0.5)))
            act_ref[at, :] = (u * cdf).astype(BF)
            slope = cdf + u * jnp.exp(-0.5 * u * u) * np.float32((2 * np.pi) ** -0.5)
            low = (gact[at, :] * slope).astype(BF)
            gpre_ref[at, :] = low
            return total + jnp.sum(low.astype(F32), axis=0, keepdims=True)

        bsum[...] = lax.fori_loop(0, rows // chunk, gelu_chunk, jnp.zeros((1, s.fn), F32))
        pre[...] = dot(gpre_ref[...], wu[...], NT)

        def gain_chunk(c, total):
            at = pl.ds(pl.multiple_of(c * chunk, chunk), chunk)
            xhat, _ = normed_rows(h1_ref[at, :])
            return total + jnp.sum(pre[at, :] * xhat, axis=0, keepdims=True)

        gsum = lax.fori_loop(0, rows // chunk, gain_chunk, jnp.zeros((1, s.d), F32))
        mine = lax.rem(me, 2)
        keep_at = pl.ds(pl.multiple_of(mine * s.own, s.own), s.own)
        send_at = pl.ds(pl.multiple_of((1 - mine) * s.own, s.own), s.own)
        gkeep[...] = pre[keep_at, :].astype(BF)
        gsend[...] = pre[send_at, :].astype(BF)
        gact[...] = dot(act_ref[...], wd[...], NN)
        zeros = jnp.zeros((extra - 1, s.db), F32)
        for m in range(s.members):
            j = me ^ m
            for keep, ref in ((0, pkeep), (1, psend)):

                @pl.when(lax.rem(j, 2) == keep)
                def _():
                    for k in range(s.teams):
                        cols = slice((k * s.members + m) * s.db, (k * s.members + m + 1) * s.db)
                        to = slice(k * s.db, (k + 1) * s.db)
                        ref[j // 2, :rows, to] = gact[:, cols].astype(BF)
                        tail = jnp.concatenate([gsum[:, cols], zeros], axis=0)
                        ref[j // 2, rows:, to] = tail.astype(BF)

    index = lambda i, sc: (side_of(s, sc, far), 0)
    fb_at = lambda k: (lambda i, sc: (0, k * s.members + sc[ME]))
    bias_own = jnp.concatenate(
        [
            lax.dynamic_slice_in_dim(b_up, (k * s.members + scalars[ME]) * s.fb, s.fb, 0)
            for k in range(s.teams)
        ]
    ).astype(F32)[None]
    return kernel(
        body,
        "mlp",
        scalars,
        (1,),
        [whole(a) for a in att]
        + [
            (hidden0, (rows, s.d), index),
            (grad_mlp, (rows, s.d), index),
            whole(gain),
            whole(bias_own),
            (w_out, None, None),
            (w_up, None, None),
            (w_down, None, None),
        ],
        [
            whole_out((rows, s.d), BF),
            whole_out((rows, s.d), BF),
            whole_out((rows, s.fn), BF),
            whole_out((rows, s.fn), BF),
            whole_out((s.own, s.d), BF),
            whole_out((s.own, s.d), BF),
            whole_out((s.members // 2, rows + extra, s.dn), BF),
            whole_out((s.members // 2, rows + extra, s.dn), BF),
            whole_out((rows, s.dn), F32),
            whole_out((1, s.fn), F32),
            whole_out((rows, s.d), F32),
        ],
        [
            pltpu.VMEM((s.d, s.d), BF),
            pltpu.VMEM((s.d, s.fn), BF),
            pltpu.VMEM((s.fn, s.d), BF),
            pltpu.VMEM((rows, s.fn), F32),
            pltpu.VMEM((rows, s.fn), F32),
            pltpu.SemaphoreType.DMA((1 + 2 * s.teams,)),
        ],
    )


def norm_two_back(s, scalars, parts, hidden1, grad_mlp, gain):
    chunk = 64
    count = len(parts)

    def body(sc, *refs):
        h1, gm, g, out_ref = refs[count:]

        def rows_chunk(c, carry):
            at = pl.ds(pl.multiple_of(c * chunk, chunk), chunk)
            xhat, rstd = normed_rows(h1[at, :])
            grad = refs[0][at, :].astype(F32)
            for ref in refs[1:count]:
                grad += ref[at, :].astype(F32)
            grad *= g[...]
            back = grad - jnp.mean(grad, axis=-1, keepdims=True)
            back -= xhat * jnp.mean(grad * xhat, axis=-1, keepdims=True)
            out_ref[at, :] = (gm[at, :].astype(F32) + rstd * back).astype(BF)
            return carry

        lax.fori_loop(0, s.own // chunk, rows_chunk, 0)

    return kernel(
        body,
        "norm_two_back",
        scalars,
        (1,),
        [whole(p) for p in parts]
        + [
            (hidden1, (s.own, s.d), lambda i, sc: (lax.rem(sc[ME], 2), 0)),
            (grad_mlp, (s.own, s.d), lambda i, sc: (sc[ME], 0)),
            whole(gain),
        ],
        [whole_out((s.own, s.d), BF)],
    )[0]


def attention_bwd(s, scalars, qkv, probs, grads, w_out, far, before=None):
    base = s.members // 2 if far else 0
    rows = s.own
    last = before is not None

    def body(sc, *refs):
        q_ref, kv_ref, prob_ref, first, second, wo = refs[:6]
        if last:
            old_ref = refs[8]
            dq_ref, own_ref, out_ref, gh, dk_acc, dv_acc = refs[9:]
        else:
            dq_ref, own_ref, out_ref, gh, dk_acc, dv_acc = refs[6:]
        i = pl.program_id(0)

        @pl.when(i == 0)
        def _():
            if last:
                dk_acc[...] = old_ref[:, : s.width]
                dv_acc[...] = old_ref[:, s.width :]
            else:
                dk_acc[...] = jnp.zeros_like(dk_acc)
                dv_acc[...] = jnp.zeros_like(dv_acc)

        for step, piece in enumerate((first, second)):

            @pl.when(i == step)
            def _():
                gh[...] = dot(piece[...], wo[...], NT).astype(BF)
                for k in range(s.teams):
                    at = pl.multiple_of((k * s.members + sc[ME]) * s.db, s.db)
                    own_ref[:, k * s.db : (k + 1) * s.db] = piece[:, pl.ds(at, s.db)]

        for h in range(s.heads):
            cols = slice(h * HEAD_DIM, (h + 1) * HEAD_DIM)
            kcols = slice(s.width + h * HEAD_DIM, s.width + (h + 1) * HEAD_DIM)
            vcols = slice(2 * s.width + h * HEAD_DIM, 2 * s.width + (h + 1) * HEAD_DIM)
            out = gh[:, cols]
            low = prob_ref[h]
            prob = low.astype(F32)
            gprob = dot(out, kv_ref[:, vcols], NT)
            mean = jnp.sum(prob * gprob, axis=-1, keepdims=True)
            gscore = (prob * (gprob - mean)).astype(BF)
            dq_ref[:, cols] = (dot(gscore, kv_ref[:, kcols], NN) * 0.125).astype(BF)
            dk_acc[:, cols] += dot(gscore, q_ref[:, cols], TN)
            dv_acc[:, cols] += dot(low, out, TN)

        @pl.when(i == pl.num_programs(0) - 1)
        def _():
            if last:
                out_ref[:, : s.width] = (dk_acc[...] * 0.125).astype(BF)
                out_ref[:, s.width :] = dv_acc[...].astype(BF)
            else:
                out_ref[:, : s.width] = dk_acc[...]
                out_ref[:, s.width :] = dv_acc[...]

    member = lambda i, sc: (sc[ME] ^ (base + i), 0)
    ins = [
        (qkv, (rows, 3 * s.width), member),
        whole(qkv),
        (probs, (s.heads, rows, s.tokens), lambda i, sc: (0, lax.rem(sc[ME] ^ i, s.members // 2), 0)),
        whole(grads[0]),
        whole(grads[1]),
        (w_out, (s.width, s.d), lambda i, sc: (sc[ME], 0)),
    ]
    aliases = None
    if last:
        ins += [(before[0], None, None), (before[1], None, None), whole(before[2])]
        aliases = {7: 0, 8: 1}
    return kernel(
        body,
        "attention_bwd",
        scalars,
        (2,),
        ins,
        [
            ((s.tokens, s.width), BF, (rows, s.width), member),
            ((s.tokens, s.dn), BF, (rows, s.dn), member),
            whole_out((s.tokens, 2 * s.width), BF if last else F32),
        ],
        [
            pltpu.VMEM((rows, s.width), BF),
            pltpu.VMEM((s.tokens, s.width), F32),
            pltpu.VMEM((s.tokens, s.width), F32),
        ],
        aliases,
    )


def norm_one_grad(s, scalars, dq, dkv, w_qkv, hidden0, gain):
    rows = s.half
    chunk = 64

    def body(sc, dq_ref, dkv_ref, wq, wk, wv, h0, g, keep, send, sums, xown, grad, stat):
        me = sc[ME]
        total = dot(dq_ref[...], wq[...], NT)
        total += dot(dkv_ref[:, : s.width], wk[...], NT)
        grad[...] = total + dot(dkv_ref[:, s.width :], wv[...], NT)
        for m in range(s.members):
            j = me ^ m
            for odd, ref in ((0, keep), (1, send)):

                @pl.when(lax.rem(j, 2) == odd)
                def _():
                    for k in range(s.teams):
                        cols = slice((k * s.members + m) * s.db, (k * s.members + m + 1) * s.db)
                        ref[j // 2, :, k * s.db : (k + 1) * s.db] = grad[:, cols].astype(BF)

        lane = lax.broadcasted_iota(jnp.int32, (chunk, LANES), 1)

        def stat_chunk(c, carry):
            at = pl.ds(pl.multiple_of(c * chunk, chunk), chunk)
            xhat, rstd = normed_rows(h0[at, :])
            scaled = grad[at, :] * g[...]
            one = jnp.sum(scaled, axis=-1, keepdims=True)
            two = jnp.sum(scaled * xhat, axis=-1, keepdims=True)
            stat[at, :] = jnp.where(lane == 0, one, jnp.where(lane == 1, two, rstd))
            grad[at, :] = xhat
            return carry

        lax.fori_loop(0, rows // chunk, stat_chunk, 0)
        for k in range(s.teams):
            at = pl.multiple_of((k * s.members + me) * s.db, s.db)
            xown[:, k * s.db : (k + 1) * s.db] = grad[:, pl.ds(at, s.db)]
        sums[...] = jnp.transpose(stat[...])[:8, :]

    def third(k):
        return (w_qkv, (s.d, s.width), lambda i, sc: (0, k * s.members + sc[ME]))

    row = lambda i, sc: (i, 0)
    deep = lambda i, sc: (0, i, 0)
    pair = (s.members // 2, s.tokens, s.dn)
    return kernel(
        body,
        "norm_one_grad",
        scalars,
        (s.tokens // rows,),
        [
            (dq, (rows, s.width), row),
            (dkv, (rows, 2 * s.width), row),
            third(0),
            third(1),
            third(2),
            (hidden0, (rows, s.d), row),
            whole(gain),
        ],
        [
            (pair, BF, (s.members // 2, rows, s.dn), deep),
            (pair, BF, (s.members // 2, rows, s.dn), deep),
            ((8, s.tokens), F32, (8, rows), lambda i, sc: (0, i)),
            ((s.tokens, s.dn), F32, (rows, s.dn), row),
        ],
        [pltpu.VMEM((rows, s.d), F32), pltpu.VMEM((rows, LANES), F32)],
    )


def shifted_sum(s, parts, out_of):
    west_ref, mid_ref, east_ref = parts
    rows = s.sec_tokens
    col = lax.rem(lax.broadcasted_iota(jnp.int32, (rows, s.chan), 0), s.cols)
    for sector in range(s.sectors):
        before = west_ref[(sector - 1) % s.sectors]
        after = east_ref[(sector + 1) % s.sectors]
        west = jnp.where(
            col == 0, pltpu.roll(before, rows - (s.cols - 1), 0), pltpu.roll(west_ref[sector], 1, 0)
        )
        east = jnp.where(
            col == s.cols - 1,
            pltpu.roll(after, s.cols - 1, 0),
            pltpu.roll(east_ref[sector], rows - 1, 0),
        )
        out_of(sector, west + mid_ref[sector] + east)


def put_home(s, sc, sector, value, keep, send):
    team, member = sector // s.members, sector % s.members
    j = sc[ME] ^ member
    for odd, ref in ((0, keep), (1, send)):

        @pl.when(lax.rem(j, 2) == odd)
        def _():
            ref[j // 2, team] = value.astype(BF)


def put_rows(s, sc, value, lanes, refs):
    size = s.db // s.group
    for k in range(s.teams):
        for q in range(s.group):
            j = sc[GRP] ^ q
            rows = value[k * s.db + q * size : k * s.db + (q + 1) * size, :].astype(BF)
            to_group(s, k, j, rows, lanes, refs)


def to_group(s, k, j, value, lanes, refs):
    keep, send = refs[2 * (k % 2)], refs[2 * (k % 2) + 1]
    half = s.group // 2
    if k % 2 == 0:
        odd, rest = lax.rem(j, 2), j // 2
    else:
        odd, rest = j // half, lax.rem(j, half)
    for side, ref in ((0, keep), (1, send)):

        @pl.when(odd == side)
        def _():
            ref[(rest,) + lanes] = value


def trunk_head(s, scalars, mine, w_head, cot_cat):
    rows = s.half
    extra = 16

    def body(sc, *refs):
        near, far = refs[:4], refs[4:8]
        wh0, wh1, cat, keep, send, grad_ref, gain_ref, h2, y0, y1, y2 = refs[8:]
        own = sc[ME] // (s.members // 2)
        gains = []
        for side, (h1, a, b, c) in ((own, near), (own ^ 1, far)):
            total = a[0, :rows, :].astype(F32) + b[0, :rows, :].astype(F32)
            total += c[0, :rows, :].astype(F32)
            h2[pl.ds(pl.multiple_of(side * rows, rows), rows), :] = (h1[...] + total).astype(BF)
            tail = a[0, rows:, :].astype(F32) + b[0, rows:, :].astype(F32)
            gains.append(tail + c[0, rows:, :].astype(F32))
        gain_ref[...] = (gains[0] + gains[1])[:8, :]
        grad_ref[...] = dot(h2[...], cat[...], TN)
        for j, ref in enumerate((y0, y1, y2)):
            value = dot(h2[:, : s.db], wh0[j], NN) + dot(h2[:, s.db :], wh1[j], NN)
            ref[...] = value.reshape(s.sectors, s.sec_tokens, s.chan)
        shifted_sum(s, (y0, y1, y2), lambda sector, v: put_home(s, sc, sector, v, keep, send))

    def part(k):
        return (w_head, (3, s.db, s.chan), lambda i, sc: (0, k * s.members + sc[ME], 0))

    home = (s.members // 2, s.teams, s.sec_tokens, s.chan)
    flat = [item for half in mine for item in half]
    return kernel(
        body,
        "trunk_head",
        scalars,
        (1,),
        [first(x) if len(x.shape) == 3 else whole(x) for x in flat] + [part(0), part(1), whole(cot_cat)],
        [
            whole_out(home, BF),
            whole_out(home, BF),
            whole_out((s.dn, 3 * s.chan), F32),
            whole_out((8, s.dn), F32),
        ],
        [pltpu.VMEM((s.tokens, s.dn), BF)]
        + [pltpu.VMEM((s.sectors, s.sec_tokens, s.chan), F32) for _ in range(3)],
    )


def embed_back(s, scalars, g1, sums, own, xown, gain, w_embed, in_cat, head_part, gain2, bias):
    wide = 3 * s.chan
    count = len(sums)

    def body(sc, *refs):
        a, b, c = refs[:3]
        stats = refs[3 : 3 + count]
        own_ref, xr, g, we0, we1, cat, head, gain2_ref, bias_ref = refs[3 + count : 12 + count]
        keep, send, ka, sa, kb, sb, grad, stat, y0, y1, y2, part = refs[12 + count :]
        total = stats[0][...]
        for other in stats[1:]:
            total += other[...]
        rows8 = lax.broadcasted_iota(jnp.int32, (8, s.tokens), 0)
        total = jnp.where(rows8 < 2, total * np.float32(1.0 / s.d), 0.5 * stats[0][...])
        stat[...] = jnp.transpose(jnp.concatenate([total] * (LANES // 8), axis=0))
        gain_own = jnp.concatenate(
            [
                g[:, pl.ds(pl.multiple_of((k * s.members + sc[ME]) * s.db, s.db), s.db)]
                for k in range(s.teams)
            ],
            axis=1,
        )
        chunk = s.sec_tokens

        def rows_chunk(i, acc):
            at = pl.ds(pl.multiple_of(i * chunk, chunk), chunk)
            g1 = a[0, at, :].astype(F32) + b[0, at, :].astype(F32) + c[0, at, :].astype(F32)
            x = xr[at, :]
            st = stat[at, :]
            back = g1 * gain_own - st[:, 0:1] - x * st[:, 1:2]
            grad[at, :] = (own_ref[at, :].astype(F32) + st[:, 2:3] * back).astype(BF)
            return acc + jnp.sum(g1 * x, axis=0, keepdims=True)

        gain1 = lax.fori_loop(0, s.tokens // chunk, rows_chunk, jnp.zeros((1, s.dn), F32))
        for j, ref in enumerate((y0, y1, y2)):
            value = dot(grad[:, : s.db], we0[j], NT) + dot(grad[:, s.db :], we1[j], NT)
            ref[...] = value.reshape(s.sectors, s.sec_tokens, s.chan)
        shifted_sum(s, (y2, y1, y0), lambda sector, v: put_home(s, sc, sector, v, keep, send))
        out = (ka, sa, kb, sb)
        part[...] = dot(grad[...], cat[...], TN)
        size = s.db // s.group
        for k in range(s.teams):
            smalls = jnp.concatenate(
                [bias_ref[:, (k * s.fb + n * LANES) : (k * s.fb + (n + 1) * LANES)] for n in range(s.fb // LANES)]
                + [gain1[:, k * s.db : (k + 1) * s.db], gain2_ref[0:1, k * s.db : (k + 1) * s.db]],
                axis=0,
            )
            smalls = jnp.concatenate([smalls, jnp.zeros((size - smalls.shape[0], LANES), F32)], axis=0)
            for q in range(s.group):
                at = slice(k * s.db + q * size, k * s.db + (q + 1) * size)
                value = jnp.concatenate([head[at, :], part[at, :], smalls], axis=1).astype(BF)
                to_group(s, k, sc[GRP] ^ q, value, (), out)

    def part_of(k):
        return (w_embed, (3, s.chan, s.db), lambda i, sc: (0, 0, k * s.members + sc[ME]))

    home = (s.members // 2, s.teams, s.sec_tokens, s.chan)
    block = (s.group // 2, s.db // s.group, 2 * wide + LANES)
    return kernel(
        body,
        "embed_back",
        scalars,
        (1,),
        [first(x) for x in g1]
        + [whole(x) for x in sums]
        + [whole(own), whole(xown), whole(gain), part_of(0), part_of(1), whole(in_cat)]
        + [whole(head_part), whole(gain2), whole(bias)],
        [whole_out(home, BF), whole_out(home, BF)] + [whole_out(block, BF)] * 4,
        [pltpu.VMEM((s.tokens, s.dn), BF), pltpu.VMEM((s.tokens, LANES), F32)]
        + [pltpu.VMEM((s.sectors, s.sec_tokens, s.chan), F32) for _ in range(3)]
        + [pltpu.VMEM((s.dn, wide), F32)],
    )


def mlp_weight_grads(s, scalars, near, far, grad_mlp):
    sub = s.fb // s.group

    def body(sc, an, pn, nn_ref, af, pf, nf, gn, gf, *outs):
        refs, scr = outs[:4], outs[4]
        k = pl.program_id(0)
        kind = pl.program_id(1)

        @pl.when(kind == 0)
        def _():
            scr[...] = (dot(an[...], gn[...], TN) + dot(af[...], gf[...], TN)).astype(BF)

        for color in range(s.teams):
            for q in range(s.group):

                @pl.when((kind == 0) & (k == color))
                def _():
                    value = jnp.concatenate(
                        [
                            scr[q * sub : (q + 1) * sub, c * LANES : (c + 1) * LANES]
                            for c in range(s.d // LANES)
                        ],
                        axis=0,
                    )
                    to_group(s, color, sc[GRP] ^ q, value, (0,), refs)

        @pl.when(kind == 1)
        def _():
            up = dot(nn_ref[...], pn[...], TN) + dot(nf[...], pf[...], TN)
            for q in range(s.group):
                value = up[:, q * sub : (q + 1) * sub].astype(BF)
                for color in range(s.teams):

                    @pl.when(k == color)
                    def _():
                        to_group(s, color, sc[GRP] ^ q, value, (0,), refs)

    def out(color):
        shape = (s.group // 2, 2, s.d, LANES)
        block = (s.group // 2, 1, s.d, LANES)
        if color == 0:
            index = lambda k, kind, sc: (0, jnp.where(k == 0, kind, 1), 0, 0)
        else:
            index = lambda k, kind, sc: (0, jnp.where(k == 0, 0, kind), 0, 0)
        return (shape, BF, block, index)

    cols = lambda k, kind, sc: (0, k)
    ins = []
    for activ, grad_pre, normed in (near, far):
        ins += [
            (activ, (s.half, s.fb), cols),
            (grad_pre, (s.half, s.fb), cols),
            whole(normed),
        ]
    ins += [
        (grad_mlp, (s.half, s.d), lambda k, kind, sc: (side_of(s, sc, False), 0)),
        (grad_mlp, (s.half, s.d), lambda k, kind, sc: (side_of(s, sc, True), 0)),
    ]
    return kernel(
        body,
        "mlp_weight_grads",
        scalars,
        (s.teams, 2),
        ins,
        [out(0), out(0), out(1), out(1)],
        [pltpu.VMEM((s.fb, s.d), BF)],
    )


def attention_weight_grads(s, scalars, normed1, dq, dkv, att_near, att_far, own):
    blocks = 2 * s.group

    def body(sc, n1, dq_ref, dkv_ref, an, af, own_near, own_far, *refs):
        def place(first, value):
            for b in range(value.shape[1] // LANES):
                n = first + b
                to_group(
                    s,
                    n // s.group,
                    sc[GRP] ^ (n % s.group),
                    value[:, b * LANES : (b + 1) * LANES].astype(BF),
                    (),
                    refs,
                )

        place(0, dot(n1[...], dq_ref[...], TN))
        place(s.width // LANES, dot(n1[...], dkv_ref[...], TN))
        place(3 * s.width // LANES, dot(an[...], own_near[...], TN) + dot(af[...], own_far[...], TN))

    shape = (s.group // 2, s.d, LANES)
    return kernel(
        body,
        "attention_weight_grads",
        scalars,
        (1,),
        [
            whole(normed1),
            whole(dq),
            whole(dkv),
            whole(att_near),
            whole(att_far),
            (own, (s.half, s.dn), lambda i, sc: (side_of(s, sc, False), 0)),
            (own, (s.half, s.dn), lambda i, sc: (side_of(s, sc, True), 0)),
        ],
        [whole_out(shape, BF)] * 4,
    )


def add_low(a, b):
    return (a.astype(F32) + b.astype(F32)).astype(BF)


def first(x):
    rank = len(x.shape)
    return (x, (1,) + tuple(x.shape[1:]), lambda *_: (0,) * rank)


def three_terms(keep, got, more):
    return keep.astype(F32) + got.astype(F32) + more.astype(F32)


def group_sums(keep_a, send_a, keep_b, send_b):
    got_a = swap(send_a, "grp", 1)
    got_b = swap(send_b, "grp", 2)
    more_a = swap(add_low(keep_a[1], got_a[1]), "grp", 2)
    more_b = swap(add_low(keep_b[1], got_b[1]), "grp", 1)
    return (keep_a, got_a, more_a[None]), (keep_b, got_b, more_b[None])


def pick_team(s, scalars, terms_a, terms_b, kinds):
    half = s.d // 2

    def body(sc, *refs):
        a, b = refs[:3], refs[3:6]
        keep, send = refs[6:]
        team = sc[TEAM]

        def total(terms, k, rows):
            at = (0, k, rows) if kinds == 2 else (0, rows)
            return three_terms(*[ref[at] for ref in terms]).astype(BF)

        if kinds == 2:
            for side in range(2):

                @pl.when(team == side)
                def _():
                    same, other = (a, b) if side == 0 else (b, a)
                    keep[0] = total(same, 0, slice(None))
                    send[0] = total(other, 0, slice(None))

        mine = pl.ds(pl.multiple_of(team * half, half), half)
        theirs = pl.ds(pl.multiple_of((1 - team) * half, half), half)
        for color, terms in enumerate((a, b)):
            at = slice(color * half, (color + 1) * half)
            keep[kinds - 1, at] = total(terms, 1, mine)
            send[kinds - 1, at] = total(terms, 1, theirs)

    return kernel(
        body,
        "pick_team",
        scalars,
        (1,),
        [first(x) for x in terms_a + terms_b],
        [whole_out((kinds, s.d, LANES), BF)] * 2,
    )


def pick_member(s, scalars, keep, got):
    kinds = keep.shape[0]
    half = s.d // 2

    def body(sc, k_ref, g_ref, *refs):
        for j in range(s.members):
            m = sc[ME] ^ j
            for color in range(2):
                at = pl.ds(pl.multiple_of(color * half + m * s.db, s.db), s.db)
                value = k_ref[kinds - 1, at].astype(F32) + g_ref[kinds - 1, at].astype(F32)
                refs[j][color] = value.astype(BF)
        if kinds == 2:
            refs[s.members][...] = (k_ref[0].astype(F32) + g_ref[0].astype(F32)).astype(BF)

    outs = [whole_out((2, s.db, LANES), BF)] * s.members
    if kinds == 2:
        outs = outs + [whole_out((s.d, LANES), BF)]
    return kernel(body, "pick_member", scalars, (1,), [whole(keep), whole(got)], outs)


def all_of_group(x, x_first):
    near, far = (1, 2) if x_first else (2, 1)
    one = swap(x, "grp", near)
    two = swap(x, "grp", far)
    both = swap(one, "grp", far)
    return [x, one, two, both] if x_first else [x, two, one, both]


def cross(s, pieces):
    got = [pieces[0]] + [swap(pieces[j], "sec", j) for j in range(1, s.members)]
    return jnp.stack(got)


def mlp_grads_out(s, scalars, downs, ups):
    sub = s.fb // s.group

    def body(sc, *refs):
        d_refs, u_refs = refs[: s.group], refs[s.group : 2 * s.group]
        down, up = refs[2 * s.group :]
        for j in range(s.group):
            q = sc[GRP] ^ j
            rows = pl.ds(pl.multiple_of(q * sub, sub), sub)
            for c in range(s.d // LANES):
                down[rows, c * LANES : (c + 1) * LANES] = d_refs[j][c * sub : (c + 1) * sub, :].astype(F32)
            for jm in range(s.members):
                m = sc[ME] ^ jm
                for color in range(s.teams):
                    at = ((color * s.members + m) * s.group + q) * LANES
                    up[:, pl.ds(pl.multiple_of(at, LANES), LANES)] = u_refs[j][jm, color].astype(F32)

    return kernel(
        body,
        "mlp_grads_out",
        scalars,
        (1,),
        [whole(x) for x in downs + ups],
        [whole_out((s.fb, s.d), F32), whole_out((s.db, s.ff), F32)],
    )


def attention_grads_out(s, scalars, parts):
    def body(sc, *refs):
        u_refs = refs[: s.group]
        qkv, out = refs[s.group :]
        for j in range(s.group):
            q = sc[GRP] ^ j
            for jm in range(s.members):
                m = sc[ME] ^ jm
                at = (q // 2) * s.d + m * s.width + lax.rem(q, 2) * LANES
                qkv[:, pl.ds(pl.multiple_of(at, LANES), LANES)] = u_refs[j][jm, 0].astype(F32)

                @pl.when(q < 2)
                def _():
                    at = 2 * s.d + m * s.width + q * LANES
                    qkv[:, pl.ds(pl.multiple_of(at, LANES), LANES)] = u_refs[j][jm, 1].astype(F32)

                @pl.when(q >= 2)
                def _():
                    at = ((q - 2) * s.members + m) * s.db
                    out[:, pl.ds(pl.multiple_of(at, LANES), LANES)] = u_refs[j][jm, 1].astype(F32)

    return kernel(
        body,
        "attention_grads_out",
        scalars,
        (1,),
        [whole(x) for x in parts],
        [whole_out((s.db, 3 * s.d), F32), whole_out((s.db, s.d), F32)],
    )


def edge_grads_out(s, scalars, parts):
    wide = 3 * s.chan
    size = s.db // s.group

    def body(sc, *refs):
        ins = refs[: s.group]
        embed, head, small, scr = refs[s.group :]
        for j in range(s.group):
            at = pl.ds(pl.multiple_of((sc[GRP] ^ j) * size, size), size)
            scr[at, :] = ins[j][...].astype(F32)
        for n in range(3):
            head[n] = scr[:, n * s.chan : (n + 1) * s.chan]
        embed[...] = jnp.transpose(scr[:, wide : 2 * wide])
        small[...] = ins[0][:16, 2 * wide :].astype(F32)

    return kernel(
        body,
        "edge_grads_out",
        scalars,
        (1,),
        [whole(x) for x in parts],
        [
            whole_out((wide, s.db), F32),
            whole_out((3, s.db, s.chan), F32),
            whole_out((16, LANES), F32),
        ],
        [pltpu.VMEM((s.db, 2 * wide + LANES), F32)],
    )


def on_team(
    fields,
    valid_rows,
    w_embed,
    ln1_gain,
    w_qkv,
    w_out,
    ln2_gain,
    w_up,
    b_up,
    w_down,
    w_head,
    cotangent,
):
    s = Sizes(fields, w_qkv, w_up)
    place = lax.axis_index("sec")
    team, me = place // s.members, place % s.members
    core, chip = 1, 2
    first_team = team == 0
    valid = jnp.where(first_team, valid_rows[0], valid_rows[1])
    scalars = jnp.stack([team, me, lax.axis_index("grp"), valid]).astype(jnp.int32)
    gain1 = ln1_gain.astype(F32)[None]
    gain2 = ln2_gain.astype(F32)[None]

    def gather_sample(x):
        flat = x.reshape(s.teams, s.sec_tokens, s.chan)
        mine = jnp.where(first_team, flat[0], flat[1])
        other = swap(jnp.where(first_team, flat[1], flat[0]), "sec", s.members)
        pair = jnp.stack([mine, other])
        across = swap(pair, "sec", chip)
        return [pair, swap(pair, "sec", core), across, swap(across, "sec", core)]

    def go_home(keep, send):
        got = swap(send, "sec", core)
        far = swap(add_low(keep[1], got[1]), "sec", chip)
        mine = three_terms(keep[0], got[0], far)
        own = jnp.where(first_team, mine[0], mine[1])
        other = jnp.where(first_team, mine[1], mine[0]).astype(BF)
        other = swap(other, "sec", s.members).astype(F32)
        both = jnp.stack([jnp.where(first_team, own, other), jnp.where(first_team, other, own)])
        return both.reshape(fields.shape)

    def scatter_features(keep, send):
        got = swap(send, "sec", core)
        return keep, got, swap(add_low(keep[1:2], got[1:2]), "sec", chip)

    in_cat, hidden0, normed1, qkv = embed_qkv(
        s, scalars, gather_sample(fields), w_embed.reshape(3 * s.chan, s.d), gain1, w_qkv
    )
    att_near, probs_near = attention_fwd(s, scalars, qkv, False)
    from_chip_far = swap(att_near, "sec", chip)
    att_far, probs_far = attention_fwd(s, scalars, qkv, True)
    cot_cat, grad_mlp = cotangent_grad(s, scalars, gather_sample(cotangent), w_head)
    from_chip_near = swap(att_far, "sec", chip)
    att_pieces_far = [att_far, swap(att_far, "sec", core), from_chip_far, swap(from_chip_far, "sec", core)]
    att_pieces_near = [att_near, swap(att_near, "sec", core), from_chip_near, swap(from_chip_near, "sec", core)]

    def run_mlp(pieces, far):
        return mlp(s, scalars, pieces, hidden0, grad_mlp, w_out, gain2, w_up, b_up, w_down, far)

    attended_far, normed2_far, activ_far, pre_far, gkeep, gsend, pkeep_far, psend_far, hown_far, bias_far, _ = run_mlp(
        att_pieces_far, True
    )
    g2_chip = swap(add_low(gkeep, swap(gsend, "sec", core)), "sec", chip)
    attended_near, normed2_near, activ_near, pre_near, gkeep, gsend, pkeep_near, psend_near, hown_near, bias_near, hidden1 = run_mlp(
        att_pieces_near, False
    )
    bias_grad = bias_far + bias_near
    b0 = norm_two_back(s, scalars, [gkeep, swap(gsend, "sec", core), g2_chip], hidden1, grad_mlp, gain2)
    b1 = swap(b0, "sec", core)
    b2 = swap(b0, "sec", chip)
    b3 = swap(b2, "sec", core)

    mlp_blocks = mlp_weight_grads(
        s, scalars, (activ_near, pre_near, normed2_near), (activ_far, pre_far, normed2_far), grad_mlp
    )
    mlp_terms = group_sums(*mlp_blocks)
    keep_f, got_f, for_near = scatter_features(pkeep_far, psend_far)
    keep_n, got_n, for_far = scatter_features(pkeep_near, psend_near)
    trunk_far = (hown_far, keep_f, got_f, for_far)
    trunk_near = (hown_near, keep_n, got_n, for_near)
    keep, send, head_part, gain2_grad = trunk_head(s, scalars, (trunk_near, trunk_far), w_head, cot_cat)
    head_output = go_home(keep, send)

    before = attention_bwd(s, scalars, qkv, probs_near, (b0, b1), w_out, False)
    dq, own, dkv = attention_bwd(s, scalars, qkv, probs_far, (b2, b3), w_out, True, before)
    att_blocks = attention_weight_grads(s, scalars, normed1, dq, dkv, attended_near, attended_far, own)
    att_terms = group_sums(*att_blocks)
    keep, send, sums, xown = norm_one_grad(s, scalars, dq, dkv, w_qkv, hidden0, gain1)
    sums = sums + swap(sums, "sec", core)
    sums = [sums, swap(sums, "sec", chip)]
    g1 = scatter_features(keep, send)
    keep, send, *edge_blocks = embed_back(
        s, scalars, g1, sums, own, xown, gain1, w_embed, in_cat, head_part, gain2_grad, bias_grad
    )
    input_grad = go_home(keep, send)

    keep, send = pick_team(s, scalars, *mlp_terms, 2)
    *crossed, downs = pick_member(s, scalars, keep, swap(send, "sec", s.members))
    down_grad, up_grad = mlp_grads_out(
        s, scalars, all_of_group(downs, False), all_of_group(cross(s, crossed), True)
    )

    keep, send = pick_team(s, scalars, *att_terms, 1)
    crossed = pick_member(s, scalars, keep, swap(send, "sec", s.members))
    qkv_grad, out_grad = attention_grads_out(s, scalars, all_of_group(cross(s, crossed), True))

    terms_a, terms_b = group_sums(*edge_blocks)
    rows_a = three_terms(*[x[0] for x in terms_a])
    rows_b = three_terms(*[x[0] for x in terms_b])
    kept = jnp.where(first_team, rows_a, rows_b)
    given = jnp.where(first_team, rows_b, rows_a).astype(BF)
    edges = (kept + swap(given, "sec", s.members).astype(F32)).astype(BF)
    embed_t, head_grad, small = edge_grads_out(s, scalars, all_of_group(edges, True))
    embed_grad = embed_t.reshape(3, s.chan, s.db)
    nb = s.fb // LANES
    return (
        head_output,
        input_grad,
        embed_grad,
        small[nb],
        qkv_grad,
        out_grad,
        small[nb + 1],
        up_grad,
        small[:nb].reshape(s.fb),
        down_grad,
        head_grad,
    )

LAT = 32
KCOLS = 8


def extended(cells, sides, width):
    for axis, dim in sides:
        count = lax.axis_size(axis)
        head = lax.slice_in_dim(cells, 0, width, axis=dim)
        tail = lax.slice_in_dim(cells, cells.shape[dim] - width, cells.shape[dim], axis=dim)
        cells = jnp.concatenate(
            [
                lax.ppermute(tail, axis, [(i, (i + 1) % count) for i in range(count)]),
                cells,
                lax.ppermute(head, axis, [((i + 1) % count, i) for i in range(count)]),
            ],
            axis=dim,
        )
    return cells


def normed(hidden, gains):
    center = hidden - jnp.mean(hidden, axis=-1, keepdims=True)
    spread = jnp.mean(center * center, axis=-1, keepdims=True)
    return center * lax.rsqrt(spread + 1e-05) * gains


def gelu_exact(values):
    return jax.nn.gelu(values, approximate=False)


def three_cols(padded, col_count, west_first):
    west_cols = padded[:, :, 0:col_count]
    middle_cols = padded[:, :, 1 : col_count + 1]
    east_cols = padded[:, :, 2 : col_count + 2]
    if west_first:
        return jnp.stack([west_cols, middle_cols, east_cols], axis=3)
    return jnp.stack([east_cols, middle_cols, west_cols], axis=3)


def split_heads(values):
    return values.reshape(values.shape[0], -1, HEADS, HEAD_DIM)


def key_mask(valid_rows, count_cols):
    rows_ok = jnp.arange(LAT)[None, :] < valid_rows[:, None]
    spread_ok = jnp.broadcast_to(rows_ok[:, :, None], (rows_ok.shape[0], LAT, count_cols))
    return spread_ok.reshape(rows_ok.shape[0], LAT * count_cols)


def key_scores(queries, kv_piece, valid_rows):
    d_model = HEADS * HEAD_DIM
    key_part = split_heads(kv_piece[..., :d_model])
    value_part = split_heads(kv_piece[..., d_model:])
    scores = (
        jnp.einsum("sqhd,skhd->shqk", queries, key_part, preferred_element_type=jnp.float32) * 0.125
    )
    allowed = key_mask(valid_rows, kv_piece.shape[2])
    scores = jnp.where(allowed[:, None, None, :], scores, -1e30)
    return (scores, key_part, value_part)


def softmax_fold(queries, valid_rows):

    def fold_piece(run_state, kv_piece, first_col):
        run_max, run_sum, run_acc = run_state
        scores, key_part, value_part = key_scores(queries, kv_piece, valid_rows)
        new_max = jnp.maximum(run_max, jnp.max(scores, axis=-1))
        factor = jnp.exp(run_max - new_max)
        weights = jnp.exp(scores - new_max[..., None])
        new_sum = run_sum * factor + jnp.sum(weights, axis=-1)
        added = jnp.einsum(
            "shqk,skhd->sqhd",
            weights.astype(jnp.bfloat16),
            value_part,
            preferred_element_type=jnp.float32,
        )
        new_acc = run_acc * jnp.transpose(factor, (0, 2, 1))[..., None] + added
        return (new_max, new_sum, new_acc)

    return fold_piece


def on_sectors(
    fields,
    valid_rows,
    w_embed,
    ln1_gain,
    w_qkv,
    w_out,
    ln2_gain,
    w_up,
    b_up,
    w_down,
    w_head,
    cotangent,
):
    samples, lat_rows, col_count, channels = fields.shape
    d_model = w_qkv.shape[0]
    token_count = lat_rows * col_count
    padded_in = extended(fields, (("sec", 2),), 1)
    input_cat = three_cols(padded_in, col_count, True)
    hidden0 = jnp.einsum("slcoi,oid->slcd", input_cat, w_embed, preferred_element_type=jnp.float32)
    normed_one, norm_one_back = jax.vjp(normed, hidden0, ln1_gain.astype(jnp.float32))
    normed_one_low = normed_one.astype(jnp.bfloat16)
    qkv_full = jnp.einsum(
        "slcd,de->slce", normed_one_low, w_qkv, preferred_element_type=jnp.float32
    ).astype(jnp.bfloat16)
    queries = split_heads(qkv_full[..., :d_model])
    key_vals = qkv_full[..., d_model:]
    init_state = (
        jnp.full((samples, HEADS, token_count), -1e30, jnp.float32),
        jnp.zeros((samples, HEADS, token_count), jnp.float32),
        jnp.zeros((samples, token_count, HEADS, HEAD_DIM), jnp.float32),
    )
    fold_piece = softmax_fold(queries, valid_rows)
    all_kv = lax.all_gather(key_vals, "sec", axis=2, tiled=True)

    def forward_block(block_index, run_state):
        kv_block = lax.dynamic_slice_in_dim(all_kv, block_index * KCOLS, KCOLS, 2)
        return fold_piece(run_state, kv_block, block_index * KCOLS)

    run_max, run_sum, run_acc = lax.fori_loop(
        0, all_kv.shape[2] // KCOLS, forward_block, init_state
    )
    attended = run_acc / jnp.transpose(run_sum, (0, 2, 1))[..., None]
    log_total = run_max + jnp.log(run_sum)
    attended_low = attended.reshape(samples, lat_rows, col_count, d_model).astype(jnp.bfloat16)
    hidden1 = hidden0 + jnp.einsum(
        "slcd,de->slce", attended_low, w_out, preferred_element_type=jnp.float32
    )
    normed_two, norm_two_back = jax.vjp(normed, hidden1, ln2_gain.astype(jnp.float32))
    normed_two_low = normed_two.astype(jnp.bfloat16)
    preact = jnp.einsum(
        "slcd,df->slcf", normed_two_low, w_up, preferred_element_type=jnp.float32
    ) + b_up.astype(jnp.float32)
    activ, gelu_back = jax.vjp(gelu_exact, preact)
    activ_low = activ.astype(jnp.bfloat16)
    hidden2 = hidden1 + jnp.einsum(
        "slcf,fd->slcd", activ_low, w_down, preferred_element_type=jnp.float32
    )
    hidden2_low = hidden2.astype(jnp.bfloat16)
    padded_hidden = extended(hidden2_low, (("sec", 2),), 1)
    hidden_cat = three_cols(padded_hidden, col_count, True)
    head_output = jnp.einsum(
        "slcod,odi->slci", hidden_cat, w_head, preferred_element_type=jnp.float32
    )
    padded_cot = extended(cotangent, (("sec", 2),), 1)
    cot_cat = three_cols(padded_cot, col_count, False)
    head_grad = jnp.einsum(
        "slcod,slci->odi", hidden_cat, cotangent, preferred_element_type=jnp.float32
    )
    grad_two = jnp.einsum("slcoi,odi->slcd", cot_cat, w_head, preferred_element_type=jnp.float32)
    grad_mlp = grad_two.astype(jnp.bfloat16)
    down_grad = jnp.einsum("slcf,slcd->fd", activ_low, grad_mlp, preferred_element_type=jnp.float32)
    grad_act = jnp.einsum("slcd,fd->slcf", grad_mlp, w_down, preferred_element_type=jnp.float32)
    grad_pre = gelu_back(grad_act)[0].astype(jnp.bfloat16)
    bias_grad = jnp.sum(grad_pre.astype(jnp.float32), axis=(0, 1, 2))
    up_grad = jnp.einsum(
        "slcd,slcf->df", normed_two_low, grad_pre, preferred_element_type=jnp.float32
    )
    grad_normed_two = jnp.einsum(
        "slcf,df->slcd", grad_pre, w_up, preferred_element_type=jnp.float32
    )
    grad_from_norm, gain_two_grad = norm_two_back(grad_normed_two)
    grad_one = grad_two + grad_from_norm
    grad_att = grad_one.astype(jnp.bfloat16)
    out_grad = jnp.einsum(
        "slcd,slce->de", attended_low, grad_att, preferred_element_type=jnp.float32
    )
    grad_heads = split_heads(
        jnp.einsum("slce,de->slcd", grad_att, w_out, preferred_element_type=jnp.float32).astype(
            jnp.bfloat16
        )
    )
    row_delta = jnp.transpose(
        jnp.sum(grad_heads.astype(jnp.float32) * attended, axis=-1), (0, 2, 1)
    )

    def sample_backward(unused_carry, sample_in):
        one_query, one_grad, one_lse, one_delta, one_valid, one_kv = sample_in
        term_zero = jnp.zeros((1, lat_rows, one_kv.shape[2], 2 * d_model), jnp.bfloat16)
        grad_zero = jnp.zeros(one_query.shape, jnp.float32)

        def backward_block(block_index, run_state):
            grad_query, term = run_state
            kv_block = lax.dynamic_slice_in_dim(one_kv, block_index * KCOLS, KCOLS, 2)
            scores, key_part, value_part = key_scores(one_query, kv_block, one_valid)
            probs = jnp.exp(scores - one_lse[..., None])
            grad_probs = jnp.einsum(
                "sqhd,skhd->shqk", one_grad, value_part, preferred_element_type=jnp.float32
            )
            grad_scores = (probs * (grad_probs - one_delta[..., None])).astype(jnp.bfloat16)
            grad_query = (
                grad_query
                + jnp.einsum(
                    "shqk,skhd->sqhd", grad_scores, key_part, preferred_element_type=jnp.float32
                )
                * 0.125
            )
            grad_keys = (
                jnp.einsum(
                    "shqk,sqhd->skhd", grad_scores, one_query, preferred_element_type=jnp.float32
                )
                * 0.125
            )
            grad_values = jnp.einsum(
                "shqk,sqhd->skhd",
                probs.astype(jnp.bfloat16),
                one_grad,
                preferred_element_type=jnp.float32,
            )
            joined = jnp.concatenate(
                [
                    grad_keys.reshape(1, lat_rows, KCOLS, d_model),
                    grad_values.reshape(1, lat_rows, KCOLS, d_model),
                ],
                axis=-1,
            ).astype(jnp.bfloat16)
            term = lax.dynamic_update_slice_in_dim(term, joined, block_index * KCOLS, 2)
            return (grad_query, term)

        grad_query, term = lax.fori_loop(
            0, one_kv.shape[2] // KCOLS, backward_block, (grad_zero, term_zero)
        )
        summed = lax.psum_scatter(
            term.astype(jnp.float32).astype(jnp.bfloat16), "sec", scatter_dimension=2, tiled=True
        ).astype(jnp.float32)
        return (unused_carry, (grad_query, summed))

    scan_inputs = (
        queries.reshape(samples, 1, token_count, HEADS, HEAD_DIM),
        grad_heads.reshape(samples, 1, token_count, HEADS, HEAD_DIM),
        log_total.reshape(samples, 1, HEADS, token_count),
        row_delta.reshape(samples, 1, HEADS, token_count),
        valid_rows.reshape(samples, 1),
        all_kv.reshape(samples, 1, lat_rows, all_kv.shape[2], 2 * d_model),
    )
    scan_end, (grad_queries, grad_kv) = lax.scan(sample_backward, 0, scan_inputs)
    grad_qkv = jnp.concatenate(
        [
            grad_queries.reshape(samples, lat_rows, col_count, d_model),
            grad_kv.reshape(samples, lat_rows, col_count, 2 * d_model),
        ],
        axis=-1,
    ).astype(jnp.bfloat16)
    qkv_grad = jnp.einsum(
        "slcd,slce->de", normed_one_low, grad_qkv, preferred_element_type=jnp.float32
    )
    grad_normed_one = jnp.einsum(
        "slce,de->slcd", grad_qkv, w_qkv, preferred_element_type=jnp.float32
    )
    grad_from_first, gain_one_grad = norm_one_back(grad_normed_one)
    grad_zero_low = (grad_one + grad_from_first).astype(jnp.bfloat16)
    embed_grad = jnp.einsum(
        "slcoi,slcd->oid", input_cat, grad_zero_low, preferred_element_type=jnp.float32
    )
    padded_grad = extended(grad_zero_low, (("sec", 2),), 1)
    grad_cat = three_cols(padded_grad, col_count, False)
    input_grad = jnp.einsum(
        "slcod,oid->slci", grad_cat, w_embed, preferred_element_type=jnp.float32
    )
    shard_grads = (
        lax.psum_scatter(
            embed_grad.astype(jnp.bfloat16), "sec", scatter_dimension=2, tiled=True
        ).astype(jnp.float32),
        lax.psum_scatter(
            gain_one_grad.astype(jnp.bfloat16), "sec", scatter_dimension=0, tiled=True
        ).astype(jnp.float32),
        lax.psum_scatter(
            qkv_grad.astype(jnp.bfloat16), "sec", scatter_dimension=0, tiled=True
        ).astype(jnp.float32),
        lax.psum_scatter(
            out_grad.astype(jnp.bfloat16), "sec", scatter_dimension=0, tiled=True
        ).astype(jnp.float32),
        lax.psum_scatter(
            gain_two_grad.astype(jnp.bfloat16), "sec", scatter_dimension=0, tiled=True
        ).astype(jnp.float32),
        lax.psum_scatter(
            up_grad.astype(jnp.bfloat16), "sec", scatter_dimension=0, tiled=True
        ).astype(jnp.float32),
        lax.psum_scatter(
            bias_grad.astype(jnp.bfloat16), "sec", scatter_dimension=0, tiled=True
        ).astype(jnp.float32),
        lax.psum_scatter(
            down_grad.astype(jnp.bfloat16), "sec", scatter_dimension=0, tiled=True
        ).astype(jnp.float32),
        lax.psum_scatter(
            head_grad.astype(jnp.bfloat16), "sec", scatter_dimension=1, tiled=True
        ).astype(jnp.float32),
    )
    total_grads = (
        lax.psum(shard_grads[0].astype(jnp.bfloat16), "grp").astype(jnp.float32),
        lax.psum(shard_grads[1].astype(jnp.bfloat16), "grp").astype(jnp.float32),
        lax.psum(shard_grads[2].astype(jnp.bfloat16), "grp").astype(jnp.float32),
        lax.psum(shard_grads[3].astype(jnp.bfloat16), "grp").astype(jnp.float32),
        lax.psum(shard_grads[4].astype(jnp.bfloat16), "grp").astype(jnp.float32),
        lax.psum(shard_grads[5].astype(jnp.bfloat16), "grp").astype(jnp.float32),
        lax.psum(shard_grads[6].astype(jnp.bfloat16), "grp").astype(jnp.float32),
        lax.psum(shard_grads[7].astype(jnp.bfloat16), "grp").astype(jnp.float32),
        lax.psum(shard_grads[8].astype(jnp.bfloat16), "grp").astype(jnp.float32),
    )
    return (
        head_output,
        input_grad,
        total_grads[0],
        total_grads[1],
        total_grads[2],
        total_grads[3],
        total_grads[4],
        total_grads[5],
        total_grads[6],
        total_grads[7],
        total_grads[8],
    )


def on_device(*args):
    fields, w_qkv = args[0], args[4]
    sectors = lax.axis_size("sec")
    fits = (
        fields.shape[0] == 2
        and sectors == 8
        and lax.axis_size("grp") == 4
        and w_qkv.shape[0] == sectors * LANES
    )
    return on_team(*args) if fits else on_sectors(*args)


def solution(mesh):
    tokens_in = P("grp", None, "sec", None)
    return jax.shard_map(
        on_device,
        mesh=mesh,
        in_specs=(tokens_in, P("grp")) + (P(),) * 9 + (tokens_in,),
        out_specs=(
            tokens_in,
            tokens_in,
            P(None, None, "sec"),
            P("sec"),
            P("sec", None),
            P("sec", None),
            P("sec"),
            P("sec", None),
            P("sec"),
            P("sec", None),
            P(None, "sec", None),
        ),
        check_vma=False,
    )
```

```python
import jax
import jax.numpy as jnp
import numpy as np
from jax import lax
from jax.experimental import pallas as pl
from jax.experimental.pallas import tpu as pltpu
from jax.sharding import PartitionSpec as P

HEAD_DIM = 64
HEADS = 16
LANES = 128
KEY_CHUNK = 512
VMEM_LIMIT = 127 * 512 * 1024
BF = jnp.bfloat16
F32 = jnp.float32

NN = ((1,), (0,))
NT = ((1,), (1,))
TN = ((0,), (0,))

MICROS = {
    "embed_qkv": 9.6,
    "cotangent_grad": 6.1,
    "attention_fwd": 9.2,
    "mlp": 17.0,
    "trunk_part": 4.0,
    "norm_two_back": 4.9,
    "attention_bwd": 13.3,
    "norm_one_grad": 11.7,
    "trunk_head": 7.0,
    "embed_back": 9.0,
    "mlp_weight_grads": 11.5,
    "attention_weight_grads": 9.0,
    "pick_team": 3.4,
    "pick_member": 2.5,
    "mlp_grads_out": 4.7,
    "attention_grads_out": 3.5,
    "edge_grads_out": 2.8,
}

TEAM, ME, GRP, VALID = range(4)


def dot(a, b, dims):
    return lax.dot_general(a, b, (dims, ((), ())), preferred_element_type=F32)


def swap(x, axis, bit):
    n = lax.axis_size(axis)
    return lax.ppermute(x, axis, [(i, i ^ bit) for i in range(n)])


def kernel(body, name, scalars, grid, ins, outs, scratch=(), aliases=None):
    micros = MICROS[name]
    scalars, chain = scalars
    values = lax.optimization_barrier((scalars, *chain))[0] if chain else scalars
    def spec(block, index):
        if block is None:
            return pl.BlockSpec(memory_space=pl.ANY)
        return pl.BlockSpec(block, index)

    results = pl.pallas_call(
        body,
        grid_spec=pltpu.PrefetchScalarGridSpec(
            num_scalar_prefetch=1,
            grid=grid,
            in_specs=[spec(block, index) for _, block, index in ins],
            out_specs=[spec(block, index) for _, _, block, index in outs],
            scratch_shapes=list(scratch),
        ),
        out_shape=[jax.ShapeDtypeStruct(shape, kind) for shape, kind, _, _ in outs],
        input_output_aliases=aliases or {},
        compiler_params=pltpu.CompilerParams(vmem_limit_bytes=VMEM_LIMIT),
        cost_estimate=pl.CostEstimate(
            flops=int(micros * 1.15e9), transcendentals=0, bytes_accessed=int(micros * 3.6e6)
        ),
        name=name,
    )(values, *[array for array, _, _ in ins])
    chain[:] = [results[-1]]
    return results


def hold(scalars, *values):
    scalars[1].extend(values)


def whole(array):
    rank = len(array.shape)
    return (array, array.shape, lambda *_: (0,) * rank)


def whole_out(shape, kind):
    rank = len(shape)
    return (shape, kind, shape, lambda *_: (0,) * rank)


class Sizes:
    def __init__(self, fields, w_qkv, w_up):
        self.teams, self.lat, self.cols, self.chan = fields.shape
        self.sectors = lax.axis_size("sec")
        self.members = self.sectors // self.teams
        self.group = lax.axis_size("grp")
        self.d = w_qkv.shape[0]
        self.ff = w_up.shape[1]
        self.sec_tokens = self.lat * self.cols
        self.tokens = self.sectors * self.sec_tokens
        self.heads = HEADS // self.members
        self.width = self.heads * HEAD_DIM
        self.db = self.d // self.sectors
        self.fb = self.ff // self.sectors
        self.dn = self.teams * self.db
        self.fn = self.teams * self.fb
        self.own = self.tokens // self.members
        self.half = self.tokens // 2


def line_up(s, scalars, pieces, canon):
    for j, piece in enumerate(pieces):
        for k in range(s.teams):
            at = (scalars[TEAM] ^ k) * s.members + (scalars[ME] ^ j)
            canon[at] = piece[k]


def beside(s, canon, sector):
    mid = canon[sector].astype(F32)
    before = canon[lax.rem(sector + s.sectors - 1, s.sectors)].astype(F32)
    after = canon[lax.rem(sector + 1, s.sectors)].astype(F32)
    col = lax.rem(lax.broadcasted_iota(jnp.int32, mid.shape, 0), s.cols)
    rows = s.sec_tokens
    west = jnp.where(col == 0, pltpu.roll(before, rows - (s.cols - 1), 0), pltpu.roll(mid, 1, 0))
    east = jnp.where(col == s.cols - 1, pltpu.roll(after, s.cols - 1, 0), pltpu.roll(mid, rows - 1, 0))
    return west, mid, east


def row_stats(rows):
    mean = jnp.mean(rows, axis=-1, keepdims=True)
    center = rows - mean
    return mean, lax.rsqrt(jnp.mean(center * center, axis=-1, keepdims=True) + 1e-05)


def normed_rows(rows):
    mean, rstd = row_stats(rows)
    return (rows - mean) * rstd, rstd


def embed_qkv(s, scalars, pieces, w_embed, gain, w_qkv):
    rows = s.half
    per = rows // s.sec_tokens
    chunk = s.sec_tokens

    def body(sc, *refs):
        parts = refs[: s.members]
        we, g, wq, wk, wv = refs[s.members : s.members + 5]
        cat_ref, hid_ref, norm_ref, qkv_ref, stat_ref, canon = refs[s.members + 5 :]
        i = pl.program_id(0)

        @pl.when(i == 0)
        def _():
            line_up(s, sc, parts, canon)

        for p in range(per):
            at = slice(p * chunk, (p + 1) * chunk)
            west, mid, east = beside(s, canon, i * per + p)
            cat_ref[at, :] = jnp.concatenate([west, mid, east], axis=1).astype(BF)
        hid_ref[...] = dot(cat_ref[...], we[...], NN)
        lane = lax.broadcasted_iota(jnp.int32, (chunk, LANES), 1)
        for p in range(per):
            at = slice(p * chunk, (p + 1) * chunk)
            value = hid_ref[at, :]
            mean, rstd = row_stats(value)
            norm_ref[at, :] = ((value - mean) * rstd * g[...]).astype(BF)
            stat_ref[at, :] = jnp.where(lane == 0, mean, rstd)
        for k, w in enumerate((wq, wk, wv)):
            qkv_ref[:, k * s.width : (k + 1) * s.width] = dot(norm_ref[...], w[...], NN).astype(BF)

    def third(k):
        return (w_qkv, (s.d, s.width), lambda i, sc: (0, k * s.members + sc[ME]))

    row = lambda i, sc: (i, 0)
    return kernel(
        body,
        "embed_qkv",
        scalars,
        (s.tokens // rows,),
        [whole(p) for p in pieces] + [whole(w_embed), whole(gain), third(0), third(1), third(2)],
        [
            ((s.tokens, 3 * s.chan), BF, (rows, 3 * s.chan), row),
            ((s.tokens, s.d), F32, (rows, s.d), row),
            ((s.tokens, s.d), BF, (rows, s.d), row),
            ((s.tokens, 3 * s.width), BF, (rows, 3 * s.width), row),
            ((s.tokens, LANES), F32, (rows, LANES), row),
        ],
        [pltpu.VMEM((s.sectors, s.sec_tokens, s.chan), BF)],
    )


def cotangent_grad(s, scalars, pieces, w_head):
    rows = s.half
    per = rows // s.sec_tokens

    def body(sc, *refs):
        parts = refs[: s.members]
        wh, cat_ref, grad_ref, canon = refs[s.members :]
        i = pl.program_id(0)

        @pl.when(i == 0)
        def _():
            line_up(s, sc, parts, canon)

        for p in range(per):
            at = slice(p * s.sec_tokens, (p + 1) * s.sec_tokens)
            west, mid, east = beside(s, canon, i * per + p)
            cat_ref[at, :] = jnp.concatenate([east, mid, west], axis=1).astype(BF)
        grad_ref[...] = dot(cat_ref[...], wh[...], NN).astype(BF)

    row = lambda i, sc: (i, 0)
    return kernel(
        body,
        "cotangent_grad",
        scalars,
        (s.tokens // rows,),
        [whole(p) for p in pieces] + [whole(w_head)],
        [
            ((s.tokens, 3 * s.chan), BF, (rows, 3 * s.chan), row),
            ((s.tokens, s.d), BF, (rows, s.d), row),
        ],
        [pltpu.VMEM((s.sectors, s.sec_tokens, s.chan), BF)],
    )


def side_of(s, sc, far):
    own = sc[ME] // (s.members // 2)
    return own ^ 1 if far else own


def lanes_of(value, side):
    lane = lax.broadcasted_iota(jnp.int32, value.shape, 1)
    return jnp.where(lane // HEAD_DIM == side, value, jnp.zeros_like(value))


def attention_fwd(s, scalars, qkv, far):
    rows = s.own
    steps = s.half // rows
    chunk = KEY_CHUNK

    def body(sc, q_ref, kv_ref, att_ref, weight_ref, inv_ref, bias, values, buf):
        @pl.when(pl.program_id(0) == 0)
        def _():
            key = lax.broadcasted_iota(jnp.int32, (s.tokens, LANES), 0)
            bias[...] = jnp.where(lax.rem(key, s.sec_tokens) // s.cols < sc[VALID], 0.0, -1e30)
            values[...] = jnp.transpose(kv_ref[:, 2 * s.width :].astype(F32)).astype(BF)

        outs = []
        invs = []
        for h in range(s.heads):
            pair = slice(h // 2 * LANES, (h // 2 + 1) * LANES)
            kcols = slice(s.width + h // 2 * LANES, s.width + (h // 2 + 1) * LANES)
            query = lanes_of(q_ref[:, pair] * jnp.asarray(0.125, BF), h % 2)
            top = None
            for c in range(0, s.tokens, chunk):
                at = slice(c, c + chunk)
                wide = jnp.concatenate([bias[at, :]] * (rows // LANES), axis=1)
                scores = dot(kv_ref[at, kcols], query, NT) + wide
                buf[h % 2, at, :] = scores
                peak = jnp.max(scores, axis=0, keepdims=True)
                top = peak if top is None else jnp.maximum(top, peak)
            total = None
            out = None
            for c in range(0, s.tokens, chunk):
                at = slice(c, c + chunk)
                weights = jnp.exp(buf[h % 2, at, :] - top)
                part = jnp.sum(weights, axis=0, keepdims=True)
                low = weights.astype(BF)
                weight_ref[h, 0, at, :] = low
                more = dot(values[h * HEAD_DIM : (h + 1) * HEAD_DIM, at], low, NN)
                total = part if total is None else total + part
                out = more if out is None else out + more
            inv = 1.0 / total
            invs.append(inv)
            outs.append(out * inv)
        att_ref[...] = jnp.transpose(jnp.concatenate(outs, axis=0)).astype(BF)
        spare = jnp.zeros((LANES - s.heads, rows), F32)
        inv_ref[...] = jnp.transpose(jnp.concatenate(invs + [spare], axis=0))

    row = lambda i, sc: (i, 0)
    return kernel(
        body,
        "attention_fwd",
        scalars,
        (steps,),
        [
            (qkv, (rows, 3 * s.width), lambda i, sc: (side_of(s, sc, far) * steps + i, 0)),
            whole(qkv),
        ],
        [
            ((s.half, s.width), BF, (rows, s.width), row),
            ((s.heads, steps, s.tokens, rows), BF, (s.heads, 1, s.tokens, rows), lambda i, sc: (0, i, 0, 0)),
            ((s.half, LANES), F32, (rows, LANES), row),
        ],
        [
            pltpu.VMEM((s.tokens, LANES), F32),
            pltpu.VMEM((s.width, s.tokens), BF),
            pltpu.VMEM((2, s.tokens, rows), F32),
        ],
    )


def mlp(s, scalars, att, hidden0, grad_mlp, w_out, gain, w_up, b_up, w_down, far):
    chunk = 64
    rows = s.half
    count = len(att)

    def body(sc, *refs):
        parts = refs[:count]
        h0, gm, g, bias, wo_hbm, wu_hbm, wd_hbm = refs[count : count + 7]
        outs = refs[count + 7 :]
        att_ref, n2_ref, act_ref, gpre_ref, gkeep, gsend, gsum_ref, hown, bsum, h1_ref = outs[:10]
        wo, wu, wd, pre, gact, means, rstds, sem = outs[10:]
        me = sc[ME]

        copies = [pltpu.make_async_copy(wo_hbm, wo, sem.at[0])]
        for k in range(s.teams):
            at = pl.multiple_of((k * s.members + me) * s.fb, s.fb)
            copies.append(
                pltpu.make_async_copy(
                    wu_hbm.at[:, pl.ds(at, s.fb)], wu.at[:, pl.ds(k * s.fb, s.fb)], sem.at[1 + k]
                )
            )
        for k in range(s.teams):
            at = pl.multiple_of((k * s.members + me) * s.fb, s.fb)
            copies.append(
                pltpu.make_async_copy(
                    wd_hbm.at[pl.ds(at, s.fb), :],
                    wd.at[pl.ds(k * s.fb, s.fb), :],
                    sem.at[1 + s.teams + k],
                )
            )
        for copy in copies:
            copy.start()
        for j in range(count):
            at = pl.multiple_of((me ^ j) * s.width, s.width)
            att_ref[:, pl.ds(at, s.width)] = parts[j][...]
        copies[0].wait()
        h1_ref[...] = h0[...] + dot(att_ref[...], wo[...], NN)

        def norm_chunk(c, carry):
            at = pl.ds(pl.multiple_of(c * chunk, chunk), chunk)
            value = h1_ref[at, :]
            mean, rstd = row_stats(value)
            n2_ref[at, :] = ((value - mean) * rstd * g[...]).astype(BF)
            means[at, :] = jnp.broadcast_to(mean, (chunk, LANES))
            rstds[at, :] = jnp.broadcast_to(rstd, (chunk, LANES))
            return carry

        lax.fori_loop(0, rows // chunk, norm_chunk, 0)
        for k in range(s.teams):
            at = pl.multiple_of((k * s.members + me) * s.db, s.db)
            hown[:, k * s.db : (k + 1) * s.db] = h1_ref[:, pl.ds(at, s.db)]
        for copy in copies[1 : 1 + s.teams]:
            copy.wait()
        pre[...] = dot(n2_ref[...], wu[...], NN)
        for copy in copies[1 + s.teams :]:
            copy.wait()
        gact[...] = dot(gm[...], wd[...], NT)

        def gelu_chunk(c, total):
            at = pl.ds(pl.multiple_of(c * chunk, chunk), chunk)
            u = pre[at, :] + bias[...]
            cdf = 0.5 * (1.0 + lax.erf(u * np.float32(2**-0.5)))
            act_ref[at, :] = (u * cdf).astype(BF)
            slope = cdf + u * jnp.exp(-0.5 * u * u) * np.float32((2 * np.pi) ** -0.5)
            low = (gact[at, :] * slope).astype(BF)
            gpre_ref[at, :] = low
            return total + jnp.sum(low.astype(F32), axis=0, keepdims=True)

        bsum[...] = lax.fori_loop(0, rows // chunk, gelu_chunk, jnp.zeros((1, s.fn), F32))
        pre[...] = dot(gpre_ref[...], wu[...], NT)

        def gain_chunk(c, total):
            at = pl.ds(pl.multiple_of(c * chunk, chunk), chunk)
            mean, rstd = means[at, :], rstds[at, :]
            sums = []
            for n in range(s.d // LANES):
                cols = slice(n * LANES, (n + 1) * LANES)
                xhat = (h1_ref[at, cols] - mean) * rstd
                sums.append(jnp.sum(pre[at, cols] * xhat, axis=0, keepdims=True))
            return total + jnp.concatenate(sums, axis=1)

        gsum = lax.fori_loop(0, rows // chunk, gain_chunk, jnp.zeros((1, s.d), F32))
        mine = lax.rem(me, 2)
        keep_at = pl.ds(pl.multiple_of(mine * s.own, s.own), s.own)
        send_at = pl.ds(pl.multiple_of((1 - mine) * s.own, s.own), s.own)
        gkeep[...] = pre[keep_at, :].astype(BF)
        gsend[...] = pre[send_at, :].astype(BF)
        gsum_ref[...] = gsum

    index = lambda i, sc: (side_of(s, sc, far), 0)
    bias_own = jnp.concatenate(
        [
            lax.dynamic_slice_in_dim(b_up, (k * s.members + scalars[0][ME]) * s.fb, s.fb, 0)
            for k in range(s.teams)
        ]
    ).astype(F32)[None]
    return kernel(
        body,
        "mlp",
        scalars,
        (1,),
        [whole(a) for a in att]
        + [
            (hidden0, (rows, s.d), index),
            (grad_mlp, (rows, s.d), index),
            whole(gain),
            whole(bias_own),
            (w_out, None, None),
            (w_up, None, None),
            (w_down, None, None),
        ],
        [
            whole_out((rows, s.d), BF),
            whole_out((rows, s.d), BF),
            whole_out((rows, s.fn), BF),
            whole_out((rows, s.fn), BF),
            whole_out((s.own, s.d), BF),
            whole_out((s.own, s.d), BF),
            whole_out((1, s.d), F32),
            whole_out((rows, s.dn), F32),
            whole_out((1, s.fn), F32),
            whole_out((rows, s.d), F32),
        ],
        [
            pltpu.VMEM((s.d, s.d), BF),
            pltpu.VMEM((s.d, s.fn), BF),
            pltpu.VMEM((s.fn, s.d), BF),
            pltpu.VMEM((rows, s.fn), F32),
            pltpu.VMEM((rows, s.fn), F32),
            pltpu.VMEM((rows, LANES), F32),
            pltpu.VMEM((rows, LANES), F32),
            pltpu.SemaphoreType.DMA((1 + 2 * s.teams,)),
        ],
    )


def trunk_part(s, scalars, parts, w_down):
    extra = 16
    rows = s.half

    def body(sc, act0, gs0, act1, gs1, *refs):
        downs, (keep, send, out) = refs[: s.teams], refs[s.teams :]
        for half, (act, gs) in enumerate(((act0, gs0), (act1, gs1))):
            total = dot(act[:, : s.fb], downs[0][...], NN)
            for k in range(1, s.teams):
                total += dot(act[:, k * s.fb : (k + 1) * s.fb], downs[k][...], NN)
            out[:rows] = total
            out[rows:] = jnp.broadcast_to(gs[...], (extra, s.d))
            for odd, ref in ((0, keep), (1, send)):
                for n in range(s.members // 2):
                    m = sc[ME] ^ (2 * n + odd)
                    for k in range(s.teams):
                        cols = pl.ds(pl.multiple_of((k * s.members + m) * s.db, s.db), s.db)
                        ref[n, half, :, k * s.db : (k + 1) * s.db] = out[:, cols].astype(BF)

    pair = (s.members // 2, 2, rows + extra, s.dn)
    return kernel(
        body,
        "trunk_part",
        scalars,
        (1,),
        [whole(x) for part in parts for x in part]
        + [
            (w_down, (s.fb, s.d), lambda i, sc, k=k: (k * s.members + sc[ME], 0))
            for k in range(s.teams)
        ],
        [whole_out(pair, BF), whole_out(pair, BF)],
        [pltpu.VMEM((rows + extra, s.d), F32)],
    )


def norm_two_back(s, scalars, parts, hidden1, grad_mlp, gain):
    chunk = 64
    count = len(parts)

    def body(sc, *refs):
        h1, gm, g, out_ref = refs[count:]

        def rows_chunk(c, carry):
            at = pl.ds(pl.multiple_of(c * chunk, chunk), chunk)
            xhat, rstd = normed_rows(h1[at, :])
            grad = refs[0][at, :].astype(F32)
            for ref in refs[1:count]:
                grad += ref[at, :].astype(F32)
            grad *= g[...]
            back = grad - jnp.mean(grad, axis=-1, keepdims=True)
            back -= xhat * jnp.mean(grad * xhat, axis=-1, keepdims=True)
            out_ref[at, :] = (gm[at, :].astype(F32) + rstd * back).astype(BF)
            return carry

        lax.fori_loop(0, s.own // chunk, rows_chunk, 0)

    return kernel(
        body,
        "norm_two_back",
        scalars,
        (1,),
        [whole(p) for p in parts]
        + [
            (hidden1, (s.own, s.d), lambda i, sc: (lax.rem(sc[ME], 2), 0)),
            (grad_mlp, (s.own, s.d), lambda i, sc: (sc[ME], 0)),
            whole(gain),
        ],
        [whole_out((s.own, s.d), BF)],
    )[0]


def attention_bwd(s, scalars, qkv, saved, grads, w_out, far, before=None):
    base = s.members // 2 if far else 0
    rows = s.own
    last = before is not None
    attended, weights, inverse = saved

    def body(sc, *refs):
        q_ref, kv_ref, att_ref, weight_ref, inv_ref, first, second, wo = refs[:8]
        if last:
            old_ref = refs[10]
            dq_ref, own_ref, out_ref, gh, acc, keys = refs[11:]
        else:
            dq_ref, own_ref, out_ref, gh, acc, keys = refs[8:]
        i = pl.program_id(0)

        @pl.when(i == 0)
        def _():
            if last:
                acc[...] = old_ref[...]
            else:
                acc[...] = jnp.zeros_like(acc)
            keys[...] = jnp.transpose(kv_ref[:, s.width : 2 * s.width].astype(F32)).astype(BF)

        for step, piece in enumerate((first, second)):

            @pl.when(i == step)
            def _():
                gh[...] = dot(piece[...], wo[...], NT)
                for k in range(s.teams):
                    at = pl.multiple_of((k * s.members + sc[ME]) * s.db, s.db)
                    own_ref[:, k * s.db : (k + 1) * s.db] = piece[:, pl.ds(at, s.db)]

        outs = []
        means = jnp.zeros((rows, LANES), F32)
        lane = lax.broadcasted_iota(jnp.int32, (rows, LANES), 1)
        for h in range(s.heads):
            pair = slice(h // 2 * LANES, (h // 2 + 1) * LANES)
            out = (lanes_of(gh[:, pair], h % 2) * inv_ref[:, h : h + 1]).astype(BF)
            mean = jnp.sum(out.astype(F32) * att_ref[:, pair].astype(F32), axis=-1, keepdims=True)
            means = jnp.where(lane == h, mean, means)
            outs.append(out)
        means = jnp.transpose(means)
        turned = [None] * s.heads
        for p in range(s.heads // 2):
            pair = slice(p * LANES, (p + 1) * LANES)
            vcols = slice(2 * s.width + p * LANES, 2 * s.width + (p + 1) * LANES)
            asks = [lanes_of(q_ref[:, pair], side) for side in range(2)]
            for c in range(0, s.tokens, KEY_CHUNK):
                at = slice(c, c + KEY_CHUNK)
                dk = None
                dv = None
                for side in range(2):
                    h = 2 * p + side
                    gprob = dot(kv_ref[at, vcols], outs[h], NT) - means[h : h + 1, :]
                    weight = weight_ref[h, 0, at, :]
                    gscore = (weight.astype(F32) * gprob).astype(BF)
                    dq = dot(keys[h * HEAD_DIM : (h + 1) * HEAD_DIM, at], gscore, NN)
                    turned[h] = dq if turned[h] is None else turned[h] + dq
                    one = dot(gscore, asks[side], NN)
                    two = dot(weight, outs[h], NN)
                    dk = one if dk is None else dk + one
                    dv = two if dv is None else dv + two
                acc[at, pair] += dk
                acc[at, s.width + p * LANES : s.width + (p + 1) * LANES] += dv
        dq_ref[...] = (jnp.transpose(jnp.concatenate(turned, axis=0)) * 0.125).astype(BF)

        @pl.when(i == pl.num_programs(0) - 1)
        def _():
            if last:
                out_ref[:, : s.width] = (acc[:, : s.width] * 0.125).astype(BF)
                out_ref[:, s.width :] = acc[:, s.width :].astype(BF)
            else:
                out_ref[...] = acc[...]

    member = lambda i, sc: (sc[ME] ^ (base + i), 0)
    side = lambda i, sc: lax.rem(sc[ME] ^ i, s.members // 2)
    ins = [
        (qkv, (rows, 3 * s.width), member),
        whole(qkv),
        (attended, (rows, s.width), lambda i, sc: (side(i, sc), 0)),
        (weights, (s.heads, 1, s.tokens, rows), lambda i, sc: (0, side(i, sc), 0, 0)),
        (inverse, (rows, LANES), lambda i, sc: (side(i, sc), 0)),
        whole(grads[0]),
        whole(grads[1]),
        (w_out, (s.width, s.d), lambda i, sc: (sc[ME], 0)),
    ]
    aliases = None
    if last:
        ins += [(before[0], None, None), (before[1], None, None), whole(before[2])]
        aliases = {9: 0, 10: 1}
    return kernel(
        body,
        "attention_bwd",
        scalars,
        (2,),
        ins,
        [
            ((s.tokens, s.width), BF, (rows, s.width), member),
            ((s.tokens, s.dn), BF, (rows, s.dn), member),
            whole_out((s.tokens, 2 * s.width), BF if last else F32),
        ],
        [
            pltpu.VMEM((rows, s.width), F32),
            pltpu.VMEM((s.tokens, 2 * s.width), F32),
            pltpu.VMEM((s.width, s.tokens), BF),
        ],
        aliases,
    )


def norm_one_grad(s, scalars, qkv, dq, dkv, w_qkv, gain):
    rows = s.half

    def body(sc, qkv_ref, dq_ref, dkv_ref, wq, wk, wv, g, keep, send, grad, stat, lines):
        me = sc[ME]
        total = dot(dq_ref[...], wq[...], NT)
        total += dot(dkv_ref[:, : s.width], wk[...], NT)
        grad[...] = total + dot(dkv_ref[:, s.width :], wv[...], NT)
        gain8 = jnp.broadcast_to(g[...], (8, s.d)).astype(BF)
        parts = ((dq_ref[...], wq), (dkv_ref[:, : s.width], wk), (dkv_ref[:, s.width :], wv))
        one = jnp.zeros((rows, s.width), F32)
        two = jnp.zeros((rows, s.width), F32)
        for k, (value, w) in enumerate(parts):
            value = value.astype(F32)
            one += value * dot(gain8, w[...], NN)[0:1, :]
            two += value * qkv_ref[:, k * s.width : (k + 1) * s.width].astype(F32)
        one = jnp.sum(one, axis=-1, keepdims=True)
        two = jnp.sum(two, axis=-1, keepdims=True)
        lane = lax.broadcasted_iota(jnp.int32, (rows, LANES), 1)
        stat[...] = jnp.where(lane == 0, one, two)
        turned = jnp.transpose(stat[...])
        count = s.tokens // s.dn
        for kind in range(2):
            for n in range(rows // s.dn):
                at = kind * count + n
                step = rows // s.dn
                line = turned[kind : kind + 1, n * s.dn : (n + 1) * s.dn].astype(BF).astype(F32)
                for i in range(s.tokens // rows):

                    @pl.when(pl.program_id(0) == i)
                    def _():
                        lines[at + i * step : at + i * step + 1, :] = line
        at = pl.ds(pl.multiple_of(pl.program_id(0) * rows, rows), rows)
        for odd, ref in ((0, keep), (1, send)):
            for n in range(s.members // 2):
                m = me ^ (2 * n + odd)
                for k in range(s.teams):
                    cols = pl.ds(pl.multiple_of((k * s.members + m) * s.db, s.db), s.db)
                    ref[n, at, k * s.db : (k + 1) * s.db] = grad[:, cols].astype(BF)
                ref[n, s.tokens :, :] = lines[...].astype(BF)

    def third(k):
        return (w_qkv, (s.d, s.width), lambda i, sc: (0, k * s.members + sc[ME]))

    row = lambda i, sc: (i, 0)
    pair = (s.members // 2, s.tokens + 16, s.dn)
    return kernel(
        body,
        "norm_one_grad",
        scalars,
        (s.tokens // rows,),
        [
            (qkv, (rows, 3 * s.width), row),
            (dq, (rows, s.width), row),
            (dkv, (rows, 2 * s.width), row),
            third(0),
            third(1),
            third(2),
            whole(gain),
        ],
        [
            whole_out(pair, BF),
            whole_out(pair, BF),
        ],
        [
            pltpu.VMEM((rows, s.d), F32),
            pltpu.VMEM((rows, LANES), F32),
            pltpu.VMEM((16, s.dn), F32),
        ],
    )


def shift_all(s, parts, out_ref):
    west_ref, mid_ref, east_ref = parts
    rows = s.sec_tokens
    col = lax.rem(lax.broadcasted_iota(jnp.int32, (rows, s.chan), 0), s.cols)

    def one(sector, carry):
        before = west_ref[lax.rem(sector + s.sectors - 1, s.sectors)]
        after = east_ref[lax.rem(sector + 1, s.sectors)]
        west = jnp.where(
            col == 0, pltpu.roll(before, rows - (s.cols - 1), 0), pltpu.roll(west_ref[sector], 1, 0)
        )
        east = jnp.where(
            col == s.cols - 1,
            pltpu.roll(after, s.cols - 1, 0),
            pltpu.roll(east_ref[sector], rows - 1, 0),
        )
        out_ref[sector] = (west + mid_ref[sector] + east).astype(BF)
        return carry

    lax.fori_loop(0, s.sectors, one, 0)


def group_blocks(s, sc, color):
    half = s.group // 2
    for side in range(2):
        for slot in range(half):
            j = 2 * slot + side if color == 0 else side * half + slot
            yield side, slot, sc[GRP] ^ j


def trunk_head(s, scalars, hown, terms, w_head, cot_cat):
    rows = s.half

    def body(sc, near, far, a, b, c, wh0, wh1, cat, home_ref, grad_ref, gain_ref, h2, y0, y1, y2):
        own = sc[ME] // (s.members // 2)
        gains = []
        for half, h1 in enumerate((near, far)):
            side = own ^ half
            total = three_terms(a[0, half, :rows, :], b[0, half, :rows, :], c[0, 1 - half, :rows, :])
            h2[pl.ds(pl.multiple_of(side * rows, rows), rows), :] = (h1[...] + total).astype(BF)
            at = slice(rows, rows + 8)
            gains.append(three_terms(a[0, half, at, :], b[0, half, at, :], c[0, 1 - half, at, :]))
        gain_ref[...] = gains[0] + gains[1]
        for j, ref in enumerate((y0, y1, y2)):
            weight = jnp.concatenate([wh0[j], wh1[j]], axis=1)
            ref[...] = dot(h2[...], weight, NT).reshape(s.sectors, s.sec_tokens, s.chan)
        shift_all(s, (y0, y1, y2), home_ref)
        grad_ref[...] = dot(h2[...], cat[...], TN)

    def part(k):
        return (w_head, (3, s.chan, s.db), lambda i, sc: (0, 0, k * s.members + sc[ME]))

    return kernel(
        body,
        "trunk_head",
        scalars,
        (1,),
        [whole(x) for x in hown]
        + [first(x) for x in terms]
        + [part(0), part(1), whole(cot_cat)],
        [
            whole_out((s.sectors, s.sec_tokens, s.chan), BF),
            whole_out((s.dn, 3 * s.chan), F32),
            whole_out((8, s.dn), F32),
        ],
        [pltpu.VMEM((s.tokens, s.dn), BF)]
        + [pltpu.VMEM((s.sectors, s.sec_tokens, s.chan), F32) for _ in range(3)],
    )


def embed_back(s, scalars, g1, own, stats, hidden0, gain, w_embed, in_cat, head_home, head_part, gain2, bias):
    wide = 3 * s.chan
    span = s.dn

    def body(sc, *refs):
        a, b, c, own_ref, st_ref, h0, h1, g, we0, we1, cat, home, head, gain2_ref, bias_ref = refs[:15]
        keep, send = refs[15:17]
        edges = refs[17 : 17 + s.group]
        grad, stat, y0, y1, y2, ours, part, smalls = refs[17 + s.group :]
        lines = slice(s.tokens, s.tokens + 16)
        total = three_terms(a[0, lines, :], b[0, lines, :], c[0, lines, :]) * np.float32(1.0 / s.d)
        for n in range(s.tokens // span):
            pair = [total[n : n + 1, :], total[s.tokens // span + n : s.tokens // span + n + 1, :]]
            pair = jnp.concatenate(pair + [jnp.zeros((LANES - 2, span), F32)], axis=0)
            stat[n * span : (n + 1) * span, :] = jnp.transpose(pair)
        gain_own = jnp.concatenate(
            [
                g[:, pl.ds(pl.multiple_of((k * s.members + sc[ME]) * s.db, s.db), s.db)]
                for k in range(s.teams)
            ],
            axis=1,
        )
        chunk = s.sec_tokens

        def rows_chunk(i, acc):
            at = pl.ds(pl.multiple_of(i * chunk, chunk), chunk)
            mean, rstd = st_ref[at, 0:1], st_ref[at, 1:2]
            one, two = stat[at, 0:1], stat[at, 1:2]
            g1 = three_terms(a[0, at, :], b[0, at, :], c[0, at, :])
            x = (jnp.concatenate([h0[at, :], h1[at, :]], axis=1) - mean) * rstd
            back = g1 * gain_own - one - x * two
            grad[at, :] = (own_ref[at, :].astype(F32) + rstd * back).astype(BF)
            return acc + jnp.sum(g1 * x, axis=0, keepdims=True)

        gain1 = lax.fori_loop(0, s.tokens // chunk, rows_chunk, jnp.zeros((1, s.dn), F32))
        for j, ref in enumerate((y0, y1, y2)):
            weight = jnp.concatenate([we0[j], we1[j]], axis=1)
            ref[...] = dot(grad[...], weight, NT).reshape(s.sectors, s.sec_tokens, s.chan)
        shift_all(s, (y2, y1, y0), ours)
        for odd, ref in ((0, keep), (1, send)):
            for n in range(s.members // 2):
                for team in range(s.teams):
                    sector = team * s.members + (sc[ME] ^ (2 * n + odd))
                    ref[n, team, 0] = home[sector]
                    ref[n, team, 1] = ours[sector]
        part[:, :wide] = head[...]
        part[:, wide : 2 * wide] = dot(grad[...], cat[...], TN)
        size = s.db // s.group
        for k in range(s.teams):
            lines = [
                bias_ref[:, k * s.fb + n * LANES : k * s.fb + (n + 1) * LANES] for n in range(s.fb // LANES)
            ]
            lines += [gain1[:, k * s.db : (k + 1) * s.db], gain2_ref[0:1, k * s.db : (k + 1) * s.db]]
            lines += [jnp.zeros((size - len(lines), LANES), F32)]
            smalls[...] = jnp.concatenate(lines, axis=0).astype(BF)
            for j, ref in enumerate(edges):
                at = pl.ds(pl.multiple_of(k * s.db + (sc[GRP] ^ j) * size, size), size)
                ref[k, :, : 2 * wide] = part[at, :].astype(BF)
                ref[k, :, 2 * wide :] = smalls[...]

    def part_of(k):
        return (w_embed, (3, s.chan, s.db), lambda i, sc: (0, 0, k * s.members + sc[ME]))

    def own_of(k):
        return (hidden0, (s.tokens, s.db), lambda i, sc: (0, k * s.members + sc[ME]))

    goes = (s.members // 2, s.teams, 2, s.sec_tokens, s.chan)
    size = s.db // s.group
    block = (s.teams, size, 2 * wide + LANES)
    return kernel(
        body,
        "embed_back",
        scalars,
        (1,),
        [first(x) for x in g1]
        + [whole(own), whole(stats), own_of(0), own_of(1), whole(gain), part_of(0), part_of(1)]
        + [whole(in_cat), whole(head_home), whole(head_part), whole(gain2), whole(bias)],
        [whole_out(goes, BF), whole_out(goes, BF)] + [whole_out(block, BF)] * s.group,
        [pltpu.VMEM((s.tokens, s.dn), BF), pltpu.VMEM((s.tokens, LANES), F32)]
        + [pltpu.VMEM((s.sectors, s.sec_tokens, s.chan), F32) for _ in range(3)]
        + [pltpu.VMEM((s.sectors, s.sec_tokens, s.chan), BF)]
        + [pltpu.VMEM((s.dn, 2 * wide), F32), pltpu.VMEM((size, LANES), BF)],
    )


def mlp_weight_grads(s, scalars, near, far, grad_mlp):
    sub = s.fb // s.group

    def body(sc, an, pn, nn_ref, af, pf, nf, gn, gf, ka, sa, kb, sb, scr):
        color = pl.program_id(0)
        kind = pl.program_id(1)

        @pl.when(kind == 0)
        def _():
            scr[...] = (dot(an[...], gn[...], TN) + dot(af[...], gf[...], TN)).astype(BF)

        @pl.when(kind == 1)
        def _():
            scr[...] = (dot(pn[...], nn_ref[...], TN) + dot(pf[...], nf[...], TN)).astype(BF)

        for k, refs in enumerate(((ka, sa), (kb, sb))):

            @pl.when(color == k)
            def _():
                for side, slot, q in group_blocks(s, sc, k):
                    rows = pl.ds(pl.multiple_of(q * sub, sub), sub)
                    for c in range(s.d // LANES):
                        refs[side][slot, 0, c * sub : (c + 1) * sub, :] = scr[rows, c * LANES : (c + 1) * LANES]

    def out(color):
        shape = (s.group // 2, 2, s.d, LANES)
        block = (s.group // 2, 1, s.d, LANES)
        if color == 0:
            index = lambda k, kind, sc: (0, jnp.where(k == 0, kind, 1), 0, 0)
        else:
            index = lambda k, kind, sc: (0, jnp.where(k == 0, 0, kind), 0, 0)
        return (shape, BF, block, index)

    cols = lambda k, kind, sc: (0, k)
    ins = []
    for activ, grad_pre, normed in (near, far):
        ins += [
            (activ, (s.half, s.fb), cols),
            (grad_pre, (s.half, s.fb), cols),
            whole(normed),
        ]
    ins += [
        (grad_mlp, (s.half, s.d), lambda k, kind, sc: (side_of(s, sc, False), 0)),
        (grad_mlp, (s.half, s.d), lambda k, kind, sc: (side_of(s, sc, True), 0)),
    ]
    return kernel(
        body,
        "mlp_weight_grads",
        scalars,
        (s.teams, 2),
        ins,
        [out(0), out(0), out(1), out(1)],
        [pltpu.VMEM((s.fb, s.d), BF)],
    )


def attention_weight_grads(s, scalars, normed1, dq, dkv, att_near, att_far, own):
    def body(sc, n1, dq_ref, dkv_ref, an, af, own_near, own_far, ka, sa, kb, sb, scr):
        scr[: s.width] = dot(dq_ref[...], n1[...], TN).astype(BF)
        scr[s.width : 3 * s.width] = dot(dkv_ref[...], n1[...], TN).astype(BF)
        scr[3 * s.width :] = (dot(own_near[...], an[...], TN) + dot(own_far[...], af[...], TN)).astype(BF)
        for k, refs in enumerate(((ka, sa), (kb, sb))):
            for side, slot, q in group_blocks(s, sc, k):
                rows = pl.ds(pl.multiple_of((k * s.group + q) * LANES, LANES), LANES)
                for c in range(s.d // LANES):
                    refs[side][slot, c * LANES : (c + 1) * LANES, :] = scr[rows, c * LANES : (c + 1) * LANES]

    shape = (s.group // 2, s.d, LANES)
    return kernel(
        body,
        "attention_weight_grads",
        scalars,
        (1,),
        [
            whole(normed1),
            whole(dq),
            whole(dkv),
            whole(att_near),
            whole(att_far),
            (own, (s.half, s.dn), lambda i, sc: (side_of(s, sc, False), 0)),
            (own, (s.half, s.dn), lambda i, sc: (side_of(s, sc, True), 0)),
        ],
        [whole_out(shape, BF)] * 4,
        [pltpu.VMEM((3 * s.width + s.dn, s.d), BF)],
    )


def add_low(a, b):
    return (a.astype(F32) + b.astype(F32)).astype(BF)


def first(x):
    rank = len(x.shape)
    return (x, (1,) + tuple(x.shape[1:]), lambda *_: (0,) * rank)


def three_terms(keep, got, more):
    return keep.astype(F32) + got.astype(F32) + more.astype(F32)


def group_first(keep_a, send_a, keep_b, send_b):
    got_a = swap(send_a, "grp", 1)
    got_b = swap(send_b, "grp", 2)
    return (keep_a, got_a), (keep_b, got_b), (add_low(keep_a[1], got_a[1]), add_low(keep_b[1], got_b[1]))


def group_second(terms_a, terms_b, sends):
    more_a = swap(sends[0], "grp", 2)
    more_b = swap(sends[1], "grp", 1)
    return terms_a + (more_a[None],), terms_b + (more_b[None],)


def pick_team(s, scalars, terms_a, terms_b, kinds):
    half = s.d // 2

    def body(sc, *refs):
        a, b = refs[:3], refs[3:6]
        keep, send = refs[6:]
        team = sc[TEAM]

        def total(terms, k, rows):
            at = (0, k, rows) if kinds == 2 else (0, rows)
            return three_terms(*[ref[at] for ref in terms]).astype(BF)

        if kinds == 2:
            for side in range(2):

                @pl.when(team == side)
                def _():
                    same, other = (a, b) if side == 0 else (b, a)
                    keep[0] = total(same, 0, slice(None))
                    send[0] = total(other, 0, slice(None))

        mine = pl.ds(pl.multiple_of(team * half, half), half)
        theirs = pl.ds(pl.multiple_of((1 - team) * half, half), half)
        for color, terms in enumerate((a, b)):
            at = slice(color * half, (color + 1) * half)
            keep[kinds - 1, at] = total(terms, 1, mine)
            send[kinds - 1, at] = total(terms, 1, theirs)

    return kernel(
        body,
        "pick_team",
        scalars,
        (1,),
        [first(x) for x in terms_a + terms_b],
        [whole_out((kinds, s.d, LANES), BF)] * 2,
    )


def pick_member(s, scalars, keep, got):
    kinds = keep.shape[0]
    half = s.d // 2

    def body(sc, k_ref, g_ref, *refs):
        for j in range(s.members):
            m = sc[ME] ^ j
            for color in range(2):
                at = pl.ds(pl.multiple_of(color * half + m * s.db, s.db), s.db)
                value = k_ref[kinds - 1, at].astype(F32) + g_ref[kinds - 1, at].astype(F32)
                refs[j][color] = value.astype(BF)
        if kinds == 2:
            refs[s.members][...] = (k_ref[0].astype(F32) + g_ref[0].astype(F32)).astype(BF)

    outs = [whole_out((2, s.db, LANES), BF)] * s.members
    if kinds == 2:
        outs = outs + [whole_out((s.d, LANES), BF)]
    return kernel(body, "pick_member", scalars, (1,), [whole(keep), whole(got)], outs)


def all_of_group(x, x_first):
    near, far = (1, 2) if x_first else (2, 1)
    one = swap(x, "grp", near)
    two = swap(x, "grp", far)
    both = swap(one, "grp", far)
    return [x, one, two, both] if x_first else [x, two, one, both]


def cross(s, pieces):
    got = [pieces[0]] + [swap(pieces[j], "sec", j) for j in range(1, s.members)]
    return jnp.stack(got)


def mlp_grads_out(s, scalars, downs, ups):
    sub = s.fb // s.group

    def body(sc, *refs):
        d_refs, u_refs = refs[: s.group], refs[s.group : 2 * s.group]
        down, up = refs[2 * s.group :]
        for j in range(s.group):
            q = sc[GRP] ^ j
            rows = pl.ds(pl.multiple_of(q * sub, sub), sub)
            for c in range(s.d // LANES):
                down[rows, c * LANES : (c + 1) * LANES] = d_refs[j][c * sub : (c + 1) * sub, :].astype(F32)
            for jm in range(s.members):
                m = sc[ME] ^ jm
                for color in range(s.teams):
                    at = ((color * s.members + m) * s.group + q) * LANES
                    up[:, pl.ds(pl.multiple_of(at, LANES), LANES)] = jnp.transpose(u_refs[j][jm, color].astype(F32))

    return kernel(
        body,
        "mlp_grads_out",
        scalars,
        (1,),
        [whole(x) for x in downs + ups],
        [whole_out((s.fb, s.d), F32), whole_out((s.db, s.ff), F32)],
    )


def attention_grads_out(s, scalars, parts):
    def body(sc, *refs):
        u_refs = refs[: s.group]
        qkv, out = refs[s.group :]
        for j in range(s.group):
            q = sc[GRP] ^ j
            for jm in range(s.members):
                m = sc[ME] ^ jm
                at = (q // 2) * s.d + m * s.width + lax.rem(q, 2) * LANES
                qkv[:, pl.ds(pl.multiple_of(at, LANES), LANES)] = jnp.transpose(u_refs[j][jm, 0].astype(F32))
                other = jnp.transpose(u_refs[j][jm, 1].astype(F32))

                @pl.when(q < 2)
                def _():
                    at = 2 * s.d + m * s.width + q * LANES
                    qkv[:, pl.ds(pl.multiple_of(at, LANES), LANES)] = other

                @pl.when(q >= 2)
                def _():
                    at = ((q - 2) * s.members + m) * s.db
                    out[:, pl.ds(pl.multiple_of(at, LANES), LANES)] = other

    return kernel(
        body,
        "attention_grads_out",
        scalars,
        (1,),
        [whole(x) for x in parts],
        [whole_out((s.db, 3 * s.d), F32), whole_out((s.db, s.d), F32)],
    )


def edge_grads_out(s, scalars, parts):
    wide = 3 * s.chan
    size = s.db // s.group

    def body(sc, *refs):
        ins = refs[: s.group]
        embed, head, small, scr = refs[s.group :]
        for j in range(s.group):
            at = pl.ds(pl.multiple_of((sc[GRP] ^ j) * size, size), size)
            scr[at, :] = ins[j][...].astype(F32)
        head[...] = jnp.transpose(scr[:, :wide])
        embed[...] = jnp.transpose(scr[:, wide : 2 * wide])
        small[...] = ins[0][:16, 2 * wide :].astype(F32)

    return kernel(
        body,
        "edge_grads_out",
        scalars,
        (1,),
        [whole(x) for x in parts],
        [
            whole_out((wide, s.db), F32),
            whole_out((wide, s.db), F32),
            whole_out((16, LANES), F32),
        ],
        [pltpu.VMEM((s.db, 2 * wide + LANES), F32)],
    )


def on_team(
    fields,
    valid_rows,
    w_embed,
    ln1_gain,
    w_qkv,
    w_out,
    ln2_gain,
    w_up,
    b_up,
    w_down,
    w_head,
    cotangent,
):
    s = Sizes(fields, w_qkv, w_up)
    place = lax.axis_index("sec")
    team, me = place // s.members, place % s.members
    core, chip = 1, 2
    first_team = team == 0
    valid = jnp.where(first_team, valid_rows[0], valid_rows[1])
    scalars = (jnp.stack([team, me, lax.axis_index("grp"), valid]).astype(jnp.int32), [])
    gain1 = ln1_gain.astype(F32)[None]
    gain2 = ln2_gain.astype(F32)[None]

    def gather_sample(x):
        flat = x.reshape(s.teams, s.sec_tokens, s.chan)
        mine = jnp.where(first_team, flat[0], flat[1])
        other = swap(jnp.where(first_team, flat[1], flat[0]), "sec", s.members)
        pair = jnp.stack([mine, other])
        across = swap(pair, "sec", chip)
        return [pair, swap(pair, "sec", core), across, swap(across, "sec", core)]

    def go_home(keep, send):
        got = swap(send, "sec", core)
        far = swap(add_low(keep[1], got[1]), "sec", chip)
        mine = three_terms(keep[0], got[0], far)
        own = jnp.where(first_team, mine[0], mine[1])
        other = jnp.where(first_team, mine[1], mine[0]).astype(BF)
        other = swap(other, "sec", s.members).astype(F32)
        both = [jnp.where(first_team, own, other), jnp.where(first_team, other, own)]
        return [jnp.stack([x[kind] for x in both]).reshape(fields.shape) for kind in range(2)]

    def scatter_features(keep, send):
        got = swap(send, "sec", core)
        return keep, got, swap(add_low(keep[1:2], got[1:2]), "sec", chip)

    w_head_t = jnp.transpose(w_head, (0, 2, 1))
    in_cat, hidden0, normed1, qkv, stats = embed_qkv(
        s, scalars, gather_sample(fields), w_embed.reshape(3 * s.chan, s.d), gain1, w_qkv
    )
    att_near, *rest = attention_fwd(s, scalars, qkv, False)
    saved_near = (att_near, *rest)
    from_chip_far = swap(att_near, "sec", chip)
    att_far, *rest = attention_fwd(s, scalars, qkv, True)
    saved_far = (att_far, *rest)
    from_chip_near = swap(att_far, "sec", chip)
    hold(scalars, from_chip_far)
    cot_cat, grad_mlp = cotangent_grad(
        s, scalars, gather_sample(cotangent), w_head_t.reshape(3 * s.chan, s.d)
    )
    att_pieces_far = [att_far, swap(att_far, "sec", core), from_chip_far, swap(from_chip_far, "sec", core)]
    att_pieces_near = [att_near, swap(att_near, "sec", core), from_chip_near, swap(from_chip_near, "sec", core)]

    def run_mlp(pieces, far):
        return mlp(s, scalars, pieces, hidden0, grad_mlp, w_out, gain2, w_up, b_up, w_down, far)

    attended_far, normed2_far, activ_far, pre_far, gkeep, gsend, gsum, hown_far, bias_far, _ = run_mlp(
        att_pieces_far, True
    )
    hold(scalars, from_chip_near)
    g2_chip = [swap(gkeep, "sec", chip), swap(gsend, "sec", chip + core)]
    attended_near, normed2_near, activ_near, pre_near, gkeep, gsend, gsum_near, hown_near, bias_near, hidden1 = run_mlp(
        att_pieces_near, False
    )
    bias_grad = bias_far + bias_near
    got = swap(gsend, "sec", core)
    pkeep, psend = trunk_part(s, scalars, ((activ_near, gsum_near), (activ_far, gsum)), w_down)
    b0 = norm_two_back(s, scalars, [gkeep, got, *g2_chip], hidden1, grad_mlp, gain2)
    b1 = swap(b0, "sec", core)
    b2 = swap(b0, "sec", chip)
    b3 = swap(b2, "sec", core)
    mlp_blocks = mlp_weight_grads(
        s, scalars, (activ_near, pre_near, normed2_near), (activ_far, pre_far, normed2_far), grad_mlp
    )
    hold(scalars, b2)
    mlp_a, mlp_b, mlp_sends = group_first(*mlp_blocks)
    before = attention_bwd(s, scalars, qkv, saved_near, (b0, b1), w_out, False)
    hold(scalars, b3, *mlp_sends)
    mlp_terms = group_second(mlp_a, mlp_b, mlp_sends)
    trunk_terms = scatter_features(pkeep, psend)
    dq, own, dkv = attention_bwd(s, scalars, qkv, saved_far, (b2, b3), w_out, True, before)
    hold(scalars, *[terms[2] for terms in mlp_terms])
    att_blocks = attention_weight_grads(s, scalars, normed1, dq, dkv, attended_near, attended_far, own)
    att_a, att_b, att_sends = group_first(*att_blocks)
    mlp_kept, send = pick_team(s, scalars, *mlp_terms, 2)
    mlp_swapped = swap(send, "sec", s.members)
    g1_keep, g1_send = norm_one_grad(s, scalars, qkv, dq, dkv, w_qkv, gain1)
    hold(scalars, *att_sends)
    att_terms = group_second(att_a, att_b, att_sends)
    hold(scalars, trunk_terms[2])
    head_home, head_part, gain2_grad = trunk_head(
        s, scalars, (hown_near, hown_far), trunk_terms, w_head_t, cot_cat
    )
    g1 = scatter_features(g1_keep, g1_send)
    hold(scalars, *[terms[2] for terms in att_terms])
    att_kept, send = pick_team(s, scalars, *att_terms, 1)
    att_swapped = swap(send, "sec", s.members)
    *crossed, downs = pick_member(s, scalars, mlp_kept, mlp_swapped)
    mlp_parts = (all_of_group(downs, False), all_of_group(cross(s, crossed), True))
    keep, send, *edges = embed_back(
        s, scalars, g1, own, stats, hidden0, gain1, w_embed, in_cat, head_home, head_part, gain2_grad, bias_grad
    )
    edges = edges[:1] + [swap(edges[j], "grp", j) for j in range(1, s.group)]
    hold(scalars, *mlp_parts[0], *mlp_parts[1])
    crossed = pick_member(s, scalars, att_kept, att_swapped)
    att_parts = all_of_group(cross(s, crossed), True)
    down_grad, up_grad = mlp_grads_out(s, scalars, *mlp_parts)
    head_output, input_grad = go_home(keep, send)

    total = edges[0].astype(F32) + edges[1].astype(F32) + edges[2].astype(F32) + edges[3].astype(F32)
    kept = jnp.where(first_team, total[0], total[1])
    given = jnp.where(first_team, total[1], total[0]).astype(BF)
    edges = (kept + swap(given, "sec", s.members).astype(F32)).astype(BF)
    edge_parts = all_of_group(edges, True)
    qkv_grad, out_grad = attention_grads_out(s, scalars, att_parts)
    embed_t, head_t, small = edge_grads_out(s, scalars, edge_parts)
    embed_grad = embed_t.reshape(3, s.chan, s.db)
    head_grad = jnp.transpose(head_t.reshape(3, s.chan, s.db), (0, 2, 1))
    nb = s.fb // LANES
    return (
        head_output,
        input_grad,
        embed_grad,
        small[nb],
        qkv_grad,
        out_grad,
        small[nb + 1],
        up_grad,
        small[:nb].reshape(s.fb),
        down_grad,
        head_grad,
    )

LAT = 32
KCOLS = 8


def extended(cells, sides, width):
    for axis, dim in sides:
        count = lax.axis_size(axis)
        head = lax.slice_in_dim(cells, 0, width, axis=dim)
        tail = lax.slice_in_dim(cells, cells.shape[dim] - width, cells.shape[dim], axis=dim)
        cells = jnp.concatenate(
            [
                lax.ppermute(tail, axis, [(i, (i + 1) % count) for i in range(count)]),
                cells,
                lax.ppermute(head, axis, [((i + 1) % count, i) for i in range(count)]),
            ],
            axis=dim,
        )
    return cells


def normed(hidden, gains):
    center = hidden - jnp.mean(hidden, axis=-1, keepdims=True)
    spread = jnp.mean(center * center, axis=-1, keepdims=True)
    return center * lax.rsqrt(spread + 1e-05) * gains


def gelu_exact(values):
    return jax.nn.gelu(values, approximate=False)


def three_cols(padded, col_count, west_first):
    west_cols = padded[:, :, 0:col_count]
    middle_cols = padded[:, :, 1 : col_count + 1]
    east_cols = padded[:, :, 2 : col_count + 2]
    if west_first:
        return jnp.stack([west_cols, middle_cols, east_cols], axis=3)
    return jnp.stack([east_cols, middle_cols, west_cols], axis=3)


def split_heads(values):
    return values.reshape(values.shape[0], -1, HEADS, HEAD_DIM)


def key_mask(valid_rows, count_cols):
    rows_ok = jnp.arange(LAT)[None, :] < valid_rows[:, None]
    spread_ok = jnp.broadcast_to(rows_ok[:, :, None], (rows_ok.shape[0], LAT, count_cols))
    return spread_ok.reshape(rows_ok.shape[0], LAT * count_cols)


def key_scores(queries, kv_piece, valid_rows):
    d_model = HEADS * HEAD_DIM
    key_part = split_heads(kv_piece[..., :d_model])
    value_part = split_heads(kv_piece[..., d_model:])
    scores = (
        jnp.einsum("sqhd,skhd->shqk", queries, key_part, preferred_element_type=jnp.float32) * 0.125
    )
    allowed = key_mask(valid_rows, kv_piece.shape[2])
    scores = jnp.where(allowed[:, None, None, :], scores, -1e30)
    return (scores, key_part, value_part)


def softmax_fold(queries, valid_rows):

    def fold_piece(run_state, kv_piece, first_col):
        run_max, run_sum, run_acc = run_state
        scores, key_part, value_part = key_scores(queries, kv_piece, valid_rows)
        new_max = jnp.maximum(run_max, jnp.max(scores, axis=-1))
        factor = jnp.exp(run_max - new_max)
        weights = jnp.exp(scores - new_max[..., None])
        new_sum = run_sum * factor + jnp.sum(weights, axis=-1)
        added = jnp.einsum(
            "shqk,skhd->sqhd",
            weights.astype(jnp.bfloat16),
            value_part,
            preferred_element_type=jnp.float32,
        )
        new_acc = run_acc * jnp.transpose(factor, (0, 2, 1))[..., None] + added
        return (new_max, new_sum, new_acc)

    return fold_piece


def on_sectors(
    fields,
    valid_rows,
    w_embed,
    ln1_gain,
    w_qkv,
    w_out,
    ln2_gain,
    w_up,
    b_up,
    w_down,
    w_head,
    cotangent,
):
    samples, lat_rows, col_count, channels = fields.shape
    d_model = w_qkv.shape[0]
    token_count = lat_rows * col_count
    padded_in = extended(fields, (("sec", 2),), 1)
    input_cat = three_cols(padded_in, col_count, True)
    hidden0 = jnp.einsum("slcoi,oid->slcd", input_cat, w_embed, preferred_element_type=jnp.float32)
    normed_one, norm_one_back = jax.vjp(normed, hidden0, ln1_gain.astype(jnp.float32))
    normed_one_low = normed_one.astype(jnp.bfloat16)
    qkv_full = jnp.einsum(
        "slcd,de->slce", normed_one_low, w_qkv, preferred_element_type=jnp.float32
    ).astype(jnp.bfloat16)
    queries = split_heads(qkv_full[..., :d_model])
    key_vals = qkv_full[..., d_model:]
    init_state = (
        jnp.full((samples, HEADS, token_count), -1e30, jnp.float32),
        jnp.zeros((samples, HEADS, token_count), jnp.float32),
        jnp.zeros((samples, token_count, HEADS, HEAD_DIM), jnp.float32),
    )
    fold_piece = softmax_fold(queries, valid_rows)
    all_kv = lax.all_gather(key_vals, "sec", axis=2, tiled=True)

    def forward_block(block_index, run_state):
        kv_block = lax.dynamic_slice_in_dim(all_kv, block_index * KCOLS, KCOLS, 2)
        return fold_piece(run_state, kv_block, block_index * KCOLS)

    run_max, run_sum, run_acc = lax.fori_loop(
        0, all_kv.shape[2] // KCOLS, forward_block, init_state
    )
    attended = run_acc / jnp.transpose(run_sum, (0, 2, 1))[..., None]
    log_total = run_max + jnp.log(run_sum)
    attended_low = attended.reshape(samples, lat_rows, col_count, d_model).astype(jnp.bfloat16)
    hidden1 = hidden0 + jnp.einsum(
        "slcd,de->slce", attended_low, w_out, preferred_element_type=jnp.float32
    )
    normed_two, norm_two_back = jax.vjp(normed, hidden1, ln2_gain.astype(jnp.float32))
    normed_two_low = normed_two.astype(jnp.bfloat16)
    preact = jnp.einsum(
        "slcd,df->slcf", normed_two_low, w_up, preferred_element_type=jnp.float32
    ) + b_up.astype(jnp.float32)
    activ, gelu_back = jax.vjp(gelu_exact, preact)
    activ_low = activ.astype(jnp.bfloat16)
    hidden2 = hidden1 + jnp.einsum(
        "slcf,fd->slcd", activ_low, w_down, preferred_element_type=jnp.float32
    )
    hidden2_low = hidden2.astype(jnp.bfloat16)
    padded_hidden = extended(hidden2_low, (("sec", 2),), 1)
    hidden_cat = three_cols(padded_hidden, col_count, True)
    head_output = jnp.einsum(
        "slcod,odi->slci", hidden_cat, w_head, preferred_element_type=jnp.float32
    )
    padded_cot = extended(cotangent, (("sec", 2),), 1)
    cot_cat = three_cols(padded_cot, col_count, False)
    head_grad = jnp.einsum(
        "slcod,slci->odi", hidden_cat, cotangent, preferred_element_type=jnp.float32
    )
    grad_two = jnp.einsum("slcoi,odi->slcd", cot_cat, w_head, preferred_element_type=jnp.float32)
    grad_mlp = grad_two.astype(jnp.bfloat16)
    down_grad = jnp.einsum("slcf,slcd->fd", activ_low, grad_mlp, preferred_element_type=jnp.float32)
    grad_act = jnp.einsum("slcd,fd->slcf", grad_mlp, w_down, preferred_element_type=jnp.float32)
    grad_pre = gelu_back(grad_act)[0].astype(jnp.bfloat16)
    bias_grad = jnp.sum(grad_pre.astype(jnp.float32), axis=(0, 1, 2))
    up_grad = jnp.einsum(
        "slcd,slcf->df", normed_two_low, grad_pre, preferred_element_type=jnp.float32
    )
    grad_normed_two = jnp.einsum(
        "slcf,df->slcd", grad_pre, w_up, preferred_element_type=jnp.float32
    )
    grad_from_norm, gain_two_grad = norm_two_back(grad_normed_two)
    grad_one = grad_two + grad_from_norm
    grad_att = grad_one.astype(jnp.bfloat16)
    out_grad = jnp.einsum(
        "slcd,slce->de", attended_low, grad_att, preferred_element_type=jnp.float32
    )
    grad_heads = split_heads(
        jnp.einsum("slce,de->slcd", grad_att, w_out, preferred_element_type=jnp.float32).astype(
            jnp.bfloat16
        )
    )
    row_delta = jnp.transpose(
        jnp.sum(grad_heads.astype(jnp.float32) * attended, axis=-1), (0, 2, 1)
    )

    def sample_backward(unused_carry, sample_in):
        one_query, one_grad, one_lse, one_delta, one_valid, one_kv = sample_in
        term_zero = jnp.zeros((1, lat_rows, one_kv.shape[2], 2 * d_model), jnp.bfloat16)
        grad_zero = jnp.zeros(one_query.shape, jnp.float32)

        def backward_block(block_index, run_state):
            grad_query, term = run_state
            kv_block = lax.dynamic_slice_in_dim(one_kv, block_index * KCOLS, KCOLS, 2)
            scores, key_part, value_part = key_scores(one_query, kv_block, one_valid)
            probs = jnp.exp(scores - one_lse[..., None])
            grad_probs = jnp.einsum(
                "sqhd,skhd->shqk", one_grad, value_part, preferred_element_type=jnp.float32
            )
            grad_scores = (probs * (grad_probs - one_delta[..., None])).astype(jnp.bfloat16)
            grad_query = (
                grad_query
                + jnp.einsum(
                    "shqk,skhd->sqhd", grad_scores, key_part, preferred_element_type=jnp.float32
                )
                * 0.125
            )
            grad_keys = (
                jnp.einsum(
                    "shqk,sqhd->skhd", grad_scores, one_query, preferred_element_type=jnp.float32
                )
                * 0.125
            )
            grad_values = jnp.einsum(
                "shqk,sqhd->skhd",
                probs.astype(jnp.bfloat16),
                one_grad,
                preferred_element_type=jnp.float32,
            )
            joined = jnp.concatenate(
                [
                    grad_keys.reshape(1, lat_rows, KCOLS, d_model),
                    grad_values.reshape(1, lat_rows, KCOLS, d_model),
                ],
                axis=-1,
            ).astype(jnp.bfloat16)
            term = lax.dynamic_update_slice_in_dim(term, joined, block_index * KCOLS, 2)
            return (grad_query, term)

        grad_query, term = lax.fori_loop(
            0, one_kv.shape[2] // KCOLS, backward_block, (grad_zero, term_zero)
        )
        summed = lax.psum_scatter(
            term.astype(jnp.float32).astype(jnp.bfloat16), "sec", scatter_dimension=2, tiled=True
        ).astype(jnp.float32)
        return (unused_carry, (grad_query, summed))

    scan_inputs = (
        queries.reshape(samples, 1, token_count, HEADS, HEAD_DIM),
        grad_heads.reshape(samples, 1, token_count, HEADS, HEAD_DIM),
        log_total.reshape(samples, 1, HEADS, token_count),
        row_delta.reshape(samples, 1, HEADS, token_count),
        valid_rows.reshape(samples, 1),
        all_kv.reshape(samples, 1, lat_rows, all_kv.shape[2], 2 * d_model),
    )
    scan_end, (grad_queries, grad_kv) = lax.scan(sample_backward, 0, scan_inputs)
    grad_qkv = jnp.concatenate(
        [
            grad_queries.reshape(samples, lat_rows, col_count, d_model),
            grad_kv.reshape(samples, lat_rows, col_count, 2 * d_model),
        ],
        axis=-1,
    ).astype(jnp.bfloat16)
    qkv_grad = jnp.einsum(
        "slcd,slce->de", normed_one_low, grad_qkv, preferred_element_type=jnp.float32
    )
    grad_normed_one = jnp.einsum(
        "slce,de->slcd", grad_qkv, w_qkv, preferred_element_type=jnp.float32
    )
    grad_from_first, gain_one_grad = norm_one_back(grad_normed_one)
    grad_zero_low = (grad_one + grad_from_first).astype(jnp.bfloat16)
    embed_grad = jnp.einsum(
        "slcoi,slcd->oid", input_cat, grad_zero_low, preferred_element_type=jnp.float32
    )
    padded_grad = extended(grad_zero_low, (("sec", 2),), 1)
    grad_cat = three_cols(padded_grad, col_count, False)
    input_grad = jnp.einsum(
        "slcod,oid->slci", grad_cat, w_embed, preferred_element_type=jnp.float32
    )
    shard_grads = (
        lax.psum_scatter(
            embed_grad.astype(jnp.bfloat16), "sec", scatter_dimension=2, tiled=True
        ).astype(jnp.float32),
        lax.psum_scatter(
            gain_one_grad.astype(jnp.bfloat16), "sec", scatter_dimension=0, tiled=True
        ).astype(jnp.float32),
        lax.psum_scatter(
            qkv_grad.astype(jnp.bfloat16), "sec", scatter_dimension=0, tiled=True
        ).astype(jnp.float32),
        lax.psum_scatter(
            out_grad.astype(jnp.bfloat16), "sec", scatter_dimension=0, tiled=True
        ).astype(jnp.float32),
        lax.psum_scatter(
            gain_two_grad.astype(jnp.bfloat16), "sec", scatter_dimension=0, tiled=True
        ).astype(jnp.float32),
        lax.psum_scatter(
            up_grad.astype(jnp.bfloat16), "sec", scatter_dimension=0, tiled=True
        ).astype(jnp.float32),
        lax.psum_scatter(
            bias_grad.astype(jnp.bfloat16), "sec", scatter_dimension=0, tiled=True
        ).astype(jnp.float32),
        lax.psum_scatter(
            down_grad.astype(jnp.bfloat16), "sec", scatter_dimension=0, tiled=True
        ).astype(jnp.float32),
        lax.psum_scatter(
            head_grad.astype(jnp.bfloat16), "sec", scatter_dimension=1, tiled=True
        ).astype(jnp.float32),
    )
    total_grads = (
        lax.psum(shard_grads[0].astype(jnp.bfloat16), "grp").astype(jnp.float32),
        lax.psum(shard_grads[1].astype(jnp.bfloat16), "grp").astype(jnp.float32),
        lax.psum(shard_grads[2].astype(jnp.bfloat16), "grp").astype(jnp.float32),
        lax.psum(shard_grads[3].astype(jnp.bfloat16), "grp").astype(jnp.float32),
        lax.psum(shard_grads[4].astype(jnp.bfloat16), "grp").astype(jnp.float32),
        lax.psum(shard_grads[5].astype(jnp.bfloat16), "grp").astype(jnp.float32),
        lax.psum(shard_grads[6].astype(jnp.bfloat16), "grp").astype(jnp.float32),
        lax.psum(shard_grads[7].astype(jnp.bfloat16), "grp").astype(jnp.float32),
        lax.psum(shard_grads[8].astype(jnp.bfloat16), "grp").astype(jnp.float32),
    )
    return (
        head_output,
        input_grad,
        total_grads[0],
        total_grads[1],
        total_grads[2],
        total_grads[3],
        total_grads[4],
        total_grads[5],
        total_grads[6],
        total_grads[7],
        total_grads[8],
    )


def on_device(*args):
    fields, w_qkv = args[0], args[4]
    sectors = lax.axis_size("sec")
    fits = (
        fields.shape[0] == 2
        and sectors == 8
        and lax.axis_size("grp") == 4
        and w_qkv.shape[0] == sectors * LANES
    )
    return on_team(*args) if fits else on_sectors(*args)


def solution(mesh):
    tokens_in = P("grp", None, "sec", None)
    return jax.shard_map(
        on_device,
        mesh=mesh,
        in_specs=(tokens_in, P("grp")) + (P(),) * 9 + (tokens_in,),
        out_specs=(
            tokens_in,
            tokens_in,
            P(None, None, "sec"),
            P("sec"),
            P("sec", None),
            P("sec", None),
            P("sec"),
            P("sec", None),
            P("sec"),
            P("sec", None),
            P(None, "sec", None),
        ),
        check_vma=False,
    )
```

```python
import jax
import jax.numpy as jnp
import numpy as np
from jax import lax
from jax.experimental import pallas as pl
from jax.experimental.pallas import tpu as pltpu
from jax.sharding import PartitionSpec as P

HEAD_DIM = 64
HEADS = 16
LANES = 128
KEY_CHUNK = 512
VMEM_LIMIT = 127 * 512 * 1024
BF = jnp.bfloat16
F32 = jnp.float32

NN = ((1,), (0,))
NT = ((1,), (1,))
TN = ((0,), (0,))

MICROS = {
    "embed_qkv": 9.6,
    "cotangent_grad": 6.1,
    "attention_fwd": 9.2,
    "mlp": 17.0,
    "trunk_part": 4.0,
    "norm_two_back": 4.9,
    "attention_bwd": 13.3,
    "norm_one_grad": 11.7,
    "trunk_head": 7.0,
    "embed_back": 9.0,
    "mlp_weight_grads": 11.5,
    "attention_weight_grads": 9.0,
    "pick_team": 3.4,
    "pick_member": 2.5,
    "mlp_grads_out": 4.7,
    "attention_grads_out": 3.5,
    "edge_grads_out": 2.8,
}

TEAM, ME, GRP, VALID = range(4)


def dot(a, b, dims):
    return lax.dot_general(a, b, (dims, ((), ())), preferred_element_type=F32)


def swap(x, axis, bit):
    n = lax.axis_size(axis)
    return lax.ppermute(x, axis, [(i, i ^ bit) for i in range(n)])


def kernel(body, name, scalars, grid, ins, outs, scratch=(), aliases=None):
    micros = MICROS[name]
    scalars, chain = scalars
    values = lax.optimization_barrier((scalars, *chain))[0] if chain else scalars
    def spec(block, index):
        if block is None:
            return pl.BlockSpec(memory_space=pl.ANY)
        return pl.BlockSpec(block, index)

    results = pl.pallas_call(
        body,
        grid_spec=pltpu.PrefetchScalarGridSpec(
            num_scalar_prefetch=1,
            grid=grid,
            in_specs=[spec(block, index) for _, block, index in ins],
            out_specs=[spec(block, index) for _, _, block, index in outs],
            scratch_shapes=list(scratch),
        ),
        out_shape=[jax.ShapeDtypeStruct(shape, kind) for shape, kind, _, _ in outs],
        input_output_aliases=aliases or {},
        compiler_params=pltpu.CompilerParams(vmem_limit_bytes=VMEM_LIMIT),
        cost_estimate=pl.CostEstimate(
            flops=int(micros * 1.15e9), transcendentals=0, bytes_accessed=int(micros * 3.6e6)
        ),
        name=name,
    )(values, *[array for array, _, _ in ins])
    chain[:] = [results[-1]]
    return results


def hold(scalars, *values):
    scalars[1].extend(values)


def whole(array):
    rank = len(array.shape)
    return (array, array.shape, lambda *_: (0,) * rank)


def whole_out(shape, kind):
    rank = len(shape)
    return (shape, kind, shape, lambda *_: (0,) * rank)


class Sizes:
    def __init__(self, fields, w_qkv, w_up):
        self.teams, self.lat, self.cols, self.chan = fields.shape
        self.sectors = lax.axis_size("sec")
        self.members = self.sectors // self.teams
        self.group = lax.axis_size("grp")
        self.d = w_qkv.shape[0]
        self.ff = w_up.shape[1]
        self.sec_tokens = self.lat * self.cols
        self.tokens = self.sectors * self.sec_tokens
        self.heads = HEADS // self.members
        self.width = self.heads * HEAD_DIM
        self.db = self.d // self.sectors
        self.fb = self.ff // self.sectors
        self.dn = self.teams * self.db
        self.fn = self.teams * self.fb
        self.own = self.tokens // self.members
        self.half = self.tokens // 2


def line_up(s, scalars, pieces, canon):
    for j, piece in enumerate(pieces):
        for k in range(s.teams):
            at = (scalars[TEAM] ^ k) * s.members + (scalars[ME] ^ j)
            canon[at] = piece[k]


def beside(s, canon, sector):
    mid = canon[sector].astype(F32)
    before = canon[lax.rem(sector + s.sectors - 1, s.sectors)].astype(F32)
    after = canon[lax.rem(sector + 1, s.sectors)].astype(F32)
    col = lax.rem(lax.broadcasted_iota(jnp.int32, mid.shape, 0), s.cols)
    rows = s.sec_tokens
    west = jnp.where(col == 0, pltpu.roll(before, rows - (s.cols - 1), 0), pltpu.roll(mid, 1, 0))
    east = jnp.where(col == s.cols - 1, pltpu.roll(after, s.cols - 1, 0), pltpu.roll(mid, rows - 1, 0))
    return west, mid, east


def row_stats(rows):
    mean = jnp.mean(rows, axis=-1, keepdims=True)
    center = rows - mean
    return mean, lax.rsqrt(jnp.mean(center * center, axis=-1, keepdims=True) + 1e-05)


def normed_rows(rows):
    mean, rstd = row_stats(rows)
    return (rows - mean) * rstd, rstd


def embed_qkv(s, scalars, pieces, w_embed, gain, w_qkv):
    rows = s.half
    per = rows // s.sec_tokens
    chunk = s.sec_tokens

    def body(sc, *refs):
        parts = refs[: s.members]
        we, g, wq, wk, wv = refs[s.members : s.members + 5]
        cat_ref, hid_ref, norm_ref, qkv_ref, stat_ref, canon = refs[s.members + 5 :]
        i = pl.program_id(0)

        @pl.when(i == 0)
        def _():
            line_up(s, sc, parts, canon)

        for p in range(per):
            at = slice(p * chunk, (p + 1) * chunk)
            west, mid, east = beside(s, canon, i * per + p)
            cat_ref[at, :] = jnp.concatenate([west, mid, east], axis=1).astype(BF)
        hid_ref[...] = dot(cat_ref[...], we[...], NN)
        lane = lax.broadcasted_iota(jnp.int32, (chunk, LANES), 1)
        for p in range(per):
            at = slice(p * chunk, (p + 1) * chunk)
            value = hid_ref[at, :]
            mean, rstd = row_stats(value)
            norm_ref[at, :] = ((value - mean) * rstd * g[...]).astype(BF)
            stat_ref[at, :] = jnp.where(lane == 0, mean, rstd)
        for k, w in enumerate((wq, wk, wv)):
            qkv_ref[:, k * s.width : (k + 1) * s.width] = dot(norm_ref[...], w[...], NN).astype(BF)

    def third(k):
        return (w_qkv, (s.d, s.width), lambda i, sc: (0, k * s.members + sc[ME]))

    row = lambda i, sc: (i, 0)
    return kernel(
        body,
        "embed_qkv",
        scalars,
        (s.tokens // rows,),
        [whole(p) for p in pieces] + [whole(w_embed), whole(gain), third(0), third(1), third(2)],
        [
            ((s.tokens, 3 * s.chan), BF, (rows, 3 * s.chan), row),
            ((s.tokens, s.d), F32, (rows, s.d), row),
            ((s.tokens, s.d), BF, (rows, s.d), row),
            ((s.tokens, 3 * s.width), BF, (rows, 3 * s.width), row),
            ((s.tokens, LANES), F32, (rows, LANES), row),
        ],
        [pltpu.VMEM((s.sectors, s.sec_tokens, s.chan), BF)],
    )


def cotangent_grad(s, scalars, pieces, w_head):
    rows = s.half
    per = rows // s.sec_tokens

    def body(sc, *refs):
        parts = refs[: s.members]
        wh, cat_ref, grad_ref, canon = refs[s.members :]
        i = pl.program_id(0)

        @pl.when(i == 0)
        def _():
            line_up(s, sc, parts, canon)

        for p in range(per):
            at = slice(p * s.sec_tokens, (p + 1) * s.sec_tokens)
            west, mid, east = beside(s, canon, i * per + p)
            cat_ref[at, :] = jnp.concatenate([east, mid, west], axis=1).astype(BF)
        grad_ref[...] = dot(cat_ref[...], wh[...], NN).astype(BF)

    row = lambda i, sc: (i, 0)
    return kernel(
        body,
        "cotangent_grad",
        scalars,
        (s.tokens // rows,),
        [whole(p) for p in pieces] + [whole(w_head)],
        [
            ((s.tokens, 3 * s.chan), BF, (rows, 3 * s.chan), row),
            ((s.tokens, s.d), BF, (rows, s.d), row),
        ],
        [pltpu.VMEM((s.sectors, s.sec_tokens, s.chan), BF)],
    )


def side_of(s, sc, far):
    own = sc[ME] // (s.members // 2)
    return own ^ 1 if far else own


def lanes_of(value, side):
    lane = lax.broadcasted_iota(jnp.int32, value.shape, 1)
    return jnp.where(lane // HEAD_DIM == side, value, jnp.zeros_like(value))


def attention_fwd(s, scalars, qkv, far):
    rows = s.own
    steps = s.half // rows
    chunk = KEY_CHUNK

    def body(sc, q_ref, kv_ref, att_ref, weight_ref, inv_ref, bias, values, buf_a, buf_b, top_a, top_b, outs, invs):
        @pl.when(pl.program_id(0) == 0)
        def _():
            key = lax.broadcasted_iota(jnp.int32, (s.tokens, LANES), 0)
            bias[...] = jnp.where(lax.rem(key, s.sec_tokens) // s.cols < sc[VALID], 0.0, -1e30)
            values[...] = jnp.transpose(kv_ref[:, 2 * s.width :].astype(F32)).astype(BF)
            invs[...] = jnp.zeros_like(invs)

        def score(p, side, buf, tops):
            at = pl.ds(pl.multiple_of(p * LANES, LANES), LANES)
            kat = pl.ds(pl.multiple_of(s.width + p * LANES, LANES), LANES)
            query = lanes_of(q_ref[:, at] * jnp.asarray(0.125, BF), side)
            top = None
            for c in range(0, s.tokens, chunk):
                rows_at = slice(c, c + chunk)
                wide = jnp.concatenate([bias[rows_at, :]] * (rows // LANES), axis=1)
                scores = dot(kv_ref[rows_at, kat], query, NT) + wide
                buf[rows_at, :] = scores
                peak = jnp.max(scores, axis=0, keepdims=True)
                top = peak if top is None else jnp.maximum(top, peak)
            tops[...] = jnp.broadcast_to(top, tops.shape)

        def weigh(p, side, buf, tops):
            h = 2 * p + side
            heads_at = pl.ds(pl.multiple_of(h * HEAD_DIM, HEAD_DIM), HEAD_DIM)
            top = tops[0:1, :]
            total = None
            out = None
            for c in range(0, s.tokens, chunk):
                at = slice(c, c + chunk)
                weights = jnp.exp(buf[at, :] - top)
                part = jnp.sum(weights, axis=0, keepdims=True)
                low = weights.astype(BF)
                weight_ref[h, 0, at, :] = low
                more = dot(values[heads_at, at], low, NN)
                total = part if total is None else total + part
                out = more if out is None else out + more
            inv = 1.0 / total
            invs[pl.ds(pl.multiple_of(h * 8, 8), 8), :] = jnp.broadcast_to(inv, (8, rows))
            outs[heads_at, :] = out * inv

        score(0, 0, buf_a, top_a)

        def pair_step(p, carry):
            weigh(p, 0, buf_a, top_a)
            score(p, 1, buf_b, top_b)

            @pl.when(p >= 0)
            def _():
                weigh(p, 1, buf_b, top_b)
                score(jnp.minimum(p + 1, s.heads // 2 - 1), 0, buf_a, top_a)

            return carry

        lax.fori_loop(0, s.heads // 2, pair_step, 0)
        att_ref[...] = jnp.transpose(outs[...]).astype(BF)
        inv_ref[...] = jnp.transpose(invs[...])

    row = lambda i, sc: (i, 0)
    return kernel(
        body,
        "attention_fwd",
        scalars,
        (steps,),
        [
            (qkv, (rows, 3 * s.width), lambda i, sc: (side_of(s, sc, far) * steps + i, 0)),
            whole(qkv),
        ],
        [
            ((s.half, s.width), BF, (rows, s.width), row),
            ((s.heads, steps, s.tokens, rows), BF, (s.heads, 1, s.tokens, rows), lambda i, sc: (0, i, 0, 0)),
            ((s.half, LANES), F32, (rows, LANES), row),
        ],
        [
            pltpu.VMEM((s.tokens, LANES), F32),
            pltpu.VMEM((s.width, s.tokens), BF),
            pltpu.VMEM((s.tokens, rows), F32),
            pltpu.VMEM((s.tokens, rows), F32),
            pltpu.VMEM((8, rows), F32),
            pltpu.VMEM((8, rows), F32),
            pltpu.VMEM((s.width, rows), F32),
            pltpu.VMEM((LANES, rows), F32),
        ],
    )


def mlp(s, scalars, att, hidden0, grad_mlp, w_out, gain, w_up, b_up, w_down, far):
    chunk = 64
    rows = s.half
    count = len(att)

    def body(sc, *refs):
        parts = refs[:count]
        h0, gm, g, bias, wo_hbm, wu_hbm, wd_hbm = refs[count : count + 7]
        outs = refs[count + 7 :]
        att_ref, n2_ref, act_ref, gpre_ref, gkeep, gsend, gsum_ref, hown, bsum, h1_ref = outs[:10]
        wo, wu, wd, pre, gact, means, rstds, sem = outs[10:]
        me = sc[ME]

        copies = [pltpu.make_async_copy(wo_hbm, wo, sem.at[0])]
        for k in range(s.teams):
            at = pl.multiple_of((k * s.members + me) * s.fb, s.fb)
            copies.append(
                pltpu.make_async_copy(
                    wu_hbm.at[:, pl.ds(at, s.fb)], wu.at[:, pl.ds(k * s.fb, s.fb)], sem.at[1 + k]
                )
            )
        for k in range(s.teams):
            at = pl.multiple_of((k * s.members + me) * s.fb, s.fb)
            copies.append(
                pltpu.make_async_copy(
                    wd_hbm.at[pl.ds(at, s.fb), :],
                    wd.at[pl.ds(k * s.fb, s.fb), :],
                    sem.at[1 + s.teams + k],
                )
            )
        for copy in copies:
            copy.start()
        for j in range(count):
            at = pl.multiple_of((me ^ j) * s.width, s.width)
            att_ref[:, pl.ds(at, s.width)] = parts[j][...]
        copies[0].wait()
        span = 512

        def by_columns(size, one):
            def step(n, carry):
                one(pl.ds(pl.multiple_of(n * span, span), span))
                return carry

            lax.fori_loop(0, size // span, step, 0)

        def attention_out(cols):
            h1_ref[:, cols] = h0[:, cols] + dot(att_ref[...], wo[:, cols], NN)

        by_columns(s.d, attention_out)

        def norm_chunk(c, carry):
            at = pl.ds(pl.multiple_of(c * chunk, chunk), chunk)
            value = h1_ref[at, :]
            mean, rstd = row_stats(value)
            n2_ref[at, :] = ((value - mean) * rstd * g[...]).astype(BF)
            means[at, :] = jnp.broadcast_to(mean, (chunk, LANES))
            rstds[at, :] = jnp.broadcast_to(rstd, (chunk, LANES))
            return carry

        lax.fori_loop(0, rows // chunk, norm_chunk, 0)
        for k in range(s.teams):
            at = pl.multiple_of((k * s.members + me) * s.db, s.db)
            hown[:, k * s.db : (k + 1) * s.db] = h1_ref[:, pl.ds(at, s.db)]
        for copy in copies[1 : 1 + s.teams]:
            copy.wait()

        def up_out(cols):
            pre[:, cols] = dot(n2_ref[...], wu[:, cols], NN)

        by_columns(s.fn, up_out)
        for copy in copies[1 + s.teams :]:
            copy.wait()

        def down_back(cols):
            gact[:, cols] = dot(gm[...], wd[cols, :], NT)

        by_columns(s.fn, down_back)

        def gelu_chunk(c, total):
            at = pl.ds(pl.multiple_of(c * chunk, chunk), chunk)
            u = pre[at, :] + bias[...]
            cdf = 0.5 * (1.0 + lax.erf(u * np.float32(2**-0.5)))
            act_ref[at, :] = (u * cdf).astype(BF)
            slope = cdf + u * jnp.exp(-0.5 * u * u) * np.float32((2 * np.pi) ** -0.5)
            low = (gact[at, :] * slope).astype(BF)
            gpre_ref[at, :] = low
            return total + jnp.sum(low.astype(F32), axis=0, keepdims=True)

        bsum[...] = lax.fori_loop(0, rows // chunk, gelu_chunk, jnp.zeros((1, s.fn), F32))

        def up_back(cols):
            pre[:, cols] = dot(gpre_ref[...], wu[cols, :], NT)

        by_columns(s.d, up_back)

        def gain_chunk(c, total):
            at = pl.ds(pl.multiple_of(c * chunk, chunk), chunk)
            mean, rstd = means[at, :], rstds[at, :]
            sums = []
            for n in range(s.d // LANES):
                cols = slice(n * LANES, (n + 1) * LANES)
                xhat = (h1_ref[at, cols] - mean) * rstd
                sums.append(jnp.sum(pre[at, cols] * xhat, axis=0, keepdims=True))
            return total + jnp.concatenate(sums, axis=1)

        gsum = lax.fori_loop(0, rows // chunk, gain_chunk, jnp.zeros((1, s.d), F32))
        mine = lax.rem(me, 2)
        keep_at = pl.ds(pl.multiple_of(mine * s.own, s.own), s.own)
        send_at = pl.ds(pl.multiple_of((1 - mine) * s.own, s.own), s.own)
        gkeep[...] = pre[keep_at, :].astype(BF)
        gsend[...] = pre[send_at, :].astype(BF)
        gsum_ref[...] = gsum

    index = lambda i, sc: (side_of(s, sc, far), 0)
    bias_own = jnp.concatenate(
        [
            lax.dynamic_slice_in_dim(b_up, (k * s.members + scalars[0][ME]) * s.fb, s.fb, 0)
            for k in range(s.teams)
        ]
    ).astype(F32)[None]
    return kernel(
        body,
        "mlp",
        scalars,
        (1,),
        [whole(a) for a in att]
        + [
            (hidden0, (rows, s.d), index),
            (grad_mlp, (rows, s.d), index),
            whole(gain),
            whole(bias_own),
            (w_out, None, None),
            (w_up, None, None),
            (w_down, None, None),
        ],
        [
            whole_out((rows, s.d), BF),
            whole_out((rows, s.d), BF),
            whole_out((rows, s.fn), BF),
            whole_out((rows, s.fn), BF),
            whole_out((s.own, s.d), BF),
            whole_out((s.own, s.d), BF),
            whole_out((1, s.d), F32),
            whole_out((rows, s.dn), F32),
            whole_out((1, s.fn), F32),
            whole_out((rows, s.d), F32),
        ],
        [
            pltpu.VMEM((s.d, s.d), BF),
            pltpu.VMEM((s.d, s.fn), BF),
            pltpu.VMEM((s.fn, s.d), BF),
            pltpu.VMEM((rows, s.fn), F32),
            pltpu.VMEM((rows, s.fn), F32),
            pltpu.VMEM((rows, LANES), F32),
            pltpu.VMEM((rows, LANES), F32),
            pltpu.SemaphoreType.DMA((1 + 2 * s.teams,)),
        ],
    )


def trunk_part(s, scalars, parts, w_down):
    extra = 16
    rows = s.half

    def body(sc, act0, gs0, act1, gs1, *refs):
        downs, (keep, send, out, both, sums) = refs[: s.teams], refs[s.teams :]
        both[0], both[1] = act0[...], act1[...]
        sums[0], sums[1] = gs0[...], gs1[...]

        def one_half(half, carry):
            total = dot(both[half, :, : s.fb], downs[0][...], NN)
            for k in range(1, s.teams):
                total += dot(both[half, :, k * s.fb : (k + 1) * s.fb], downs[k][...], NN)
            out[:rows] = total
            out[rows:] = jnp.broadcast_to(sums[half], (extra, s.d))
            for odd, ref in ((0, keep), (1, send)):
                for n in range(s.members // 2):
                    m = sc[ME] ^ (2 * n + odd)
                    for k in range(s.teams):
                        cols = pl.ds(pl.multiple_of((k * s.members + m) * s.db, s.db), s.db)
                        ref[n, half, :, k * s.db : (k + 1) * s.db] = out[:, cols].astype(BF)
            return carry

        lax.fori_loop(0, 2, one_half, 0)

    pair = (s.members // 2, 2, rows + extra, s.dn)
    return kernel(
        body,
        "trunk_part",
        scalars,
        (1,),
        [whole(x) for part in parts for x in part]
        + [
            (w_down, (s.fb, s.d), lambda i, sc, k=k: (k * s.members + sc[ME], 0))
            for k in range(s.teams)
        ],
        [whole_out(pair, BF), whole_out(pair, BF)],
        [
            pltpu.VMEM((rows + extra, s.d), F32),
            pltpu.VMEM((2, rows, s.fn), BF),
            pltpu.VMEM((2, 1, s.d), F32),
        ],
    )


def norm_two_back(s, scalars, parts, hidden1, grad_mlp, gain):
    chunk = 64
    count = len(parts)

    def body(sc, *refs):
        h1, gm, g, out_ref = refs[count:]

        def rows_chunk(c, carry):
            at = pl.ds(pl.multiple_of(c * chunk, chunk), chunk)
            xhat, rstd = normed_rows(h1[at, :])
            grad = refs[0][at, :].astype(F32)
            for ref in refs[1:count]:
                grad += ref[at, :].astype(F32)
            grad *= g[...]
            back = grad - jnp.mean(grad, axis=-1, keepdims=True)
            back -= xhat * jnp.mean(grad * xhat, axis=-1, keepdims=True)
            out_ref[at, :] = (gm[at, :].astype(F32) + rstd * back).astype(BF)
            return carry

        lax.fori_loop(0, s.own // chunk, rows_chunk, 0)

    return kernel(
        body,
        "norm_two_back",
        scalars,
        (1,),
        [whole(p) for p in parts]
        + [
            (hidden1, (s.own, s.d), lambda i, sc: (lax.rem(sc[ME], 2), 0)),
            (grad_mlp, (s.own, s.d), lambda i, sc: (sc[ME], 0)),
            whole(gain),
        ],
        [whole_out((s.own, s.d), BF)],
    )[0]


def attention_bwd(s, scalars, qkv, saved, grads, w_out, far, before=None):
    base = s.members // 2 if far else 0
    rows = s.own
    last = before is not None
    attended, weights, inverse = saved

    def body(sc, *refs):
        q_ref, kv_ref, att_ref, weight_ref, inv_ref, first, second, wo = refs[:8]
        if last:
            old_ref = refs[10]
            dq_ref, own_ref, out_ref, gh, acc, keys = refs[11:]
        else:
            dq_ref, own_ref, out_ref, gh, acc, keys = refs[8:]
        i = pl.program_id(0)

        @pl.when(i == 0)
        def _():
            if last:
                acc[...] = old_ref[...]
            else:
                acc[...] = jnp.zeros_like(acc)
            keys[...] = jnp.transpose(kv_ref[:, s.width : 2 * s.width].astype(F32)).astype(BF)

        for step, piece in enumerate((first, second)):

            @pl.when(i == step)
            def _():
                gh[...] = dot(piece[...], wo[...], NT)
                for k in range(s.teams):
                    at = pl.multiple_of((k * s.members + sc[ME]) * s.db, s.db)
                    own_ref[:, k * s.db : (k + 1) * s.db] = piece[:, pl.ds(at, s.db)]

        def pair_step(p, carry):
            pair = pl.ds(pl.multiple_of(p * LANES, LANES), LANES)
            value_at = pl.ds(pl.multiple_of(2 * s.width + p * LANES, LANES), LANES)
            dv_at = pl.ds(pl.multiple_of(s.width + p * LANES, LANES), LANES)
            inv = inv_ref[...]
            wide = lax.broadcasted_iota(jnp.int32, inv.shape, 1)
            outs = []
            means = jnp.zeros((rows, LANES), F32)
            for side in range(2):
                h = 2 * p + side
                one = jnp.sum(jnp.where(wide == 8 * h, inv, 0.0), axis=-1, keepdims=True)
                out = (lanes_of(gh[:, pair], side) * one).astype(BF)
                mean = jnp.sum(out.astype(F32) * att_ref[:, pair].astype(F32), axis=-1, keepdims=True)
                means = jnp.where(wide == side, mean, means)
                outs.append(out)
            means = jnp.transpose(means)
            turned = [None, None]
            units = [(c, side) for c in range(0, s.tokens, KEY_CHUNK) for side in range(2)]

            def first_dot(unit):
                c, side = unit
                return dot(kv_ref[c : c + KEY_CHUNK, value_at], outs[side], NT)

            ahead = first_dot(units[0])
            for n, (c, side) in enumerate(units):
                at = slice(c, c + KEY_CHUNK)
                h = 2 * p + side
                gprob = ahead - means[side : side + 1, :]
                if n + 1 < len(units):
                    ahead = first_dot(units[n + 1])
                weight = weight_ref[h, 0, at, :]
                gscore = (weight.astype(F32) * gprob).astype(BF)
                key_rows = pl.ds(pl.multiple_of(h * HEAD_DIM, HEAD_DIM), HEAD_DIM)
                dq = dot(keys[key_rows, at], gscore, NN)
                turned[side] = dq if turned[side] is None else turned[side] + dq
                one = dot(gscore, lanes_of(q_ref[:, pair], side), NN)
                two = dot(weight, outs[side], NN)
                if side == 0:
                    dk, dv = one, two
                else:
                    acc[at, pair] += dk + one
                    acc[at, dv_at] += dv + two
            dq_ref[:, pair] = (jnp.transpose(jnp.concatenate(turned, axis=0)) * 0.125).astype(BF)
            return carry

        lax.fori_loop(0, s.heads // 2, pair_step, 0)

        @pl.when(i == pl.num_programs(0) - 1)
        def _():
            if last:
                out_ref[:, : s.width] = (acc[:, : s.width] * 0.125).astype(BF)
                out_ref[:, s.width :] = acc[:, s.width :].astype(BF)
            else:
                out_ref[...] = acc[...]

    member = lambda i, sc: (sc[ME] ^ (base + i), 0)
    side = lambda i, sc: lax.rem(sc[ME] ^ i, s.members // 2)
    ins = [
        (qkv, (rows, 3 * s.width), member),
        whole(qkv),
        (attended, (rows, s.width), lambda i, sc: (side(i, sc), 0)),
        (weights, (s.heads, 1, s.tokens, rows), lambda i, sc: (0, side(i, sc), 0, 0)),
        (inverse, (rows, LANES), lambda i, sc: (side(i, sc), 0)),
        whole(grads[0]),
        whole(grads[1]),
        (w_out, (s.width, s.d), lambda i, sc: (sc[ME], 0)),
    ]
    aliases = None
    if last:
        ins += [(before[0], None, None), (before[1], None, None), whole(before[2])]
        aliases = {9: 0, 10: 1}
    return kernel(
        body,
        "attention_bwd",
        scalars,
        (2,),
        ins,
        [
            ((s.tokens, s.width), BF, (rows, s.width), member),
            ((s.tokens, s.dn), BF, (rows, s.dn), member),
            whole_out((s.tokens, 2 * s.width), BF if last else F32),
        ],
        [
            pltpu.VMEM((rows, s.width), F32),
            pltpu.VMEM((s.tokens, 2 * s.width), F32),
            pltpu.VMEM((s.width, s.tokens), BF),
        ],
        aliases,
    )


def norm_one_grad(s, scalars, qkv, dq, dkv, w_qkv, gain):
    rows = s.half

    def body(sc, qkv_ref, dq_ref, dkv_ref, wq, wk, wv, g, keep, send, grad, stat, lines):
        me = sc[ME]
        total = dot(dq_ref[...], wq[...], NT)
        total += dot(dkv_ref[:, : s.width], wk[...], NT)
        grad[...] = total + dot(dkv_ref[:, s.width :], wv[...], NT)
        gain8 = jnp.broadcast_to(g[...], (8, s.d)).astype(BF)
        parts = ((dq_ref[...], wq), (dkv_ref[:, : s.width], wk), (dkv_ref[:, s.width :], wv))
        one = jnp.zeros((rows, s.width), F32)
        two = jnp.zeros((rows, s.width), F32)
        for k, (value, w) in enumerate(parts):
            value = value.astype(F32)
            one += value * dot(gain8, w[...], NN)[0:1, :]
            two += value * qkv_ref[:, k * s.width : (k + 1) * s.width].astype(F32)
        one = jnp.sum(one, axis=-1, keepdims=True)
        two = jnp.sum(two, axis=-1, keepdims=True)
        lane = lax.broadcasted_iota(jnp.int32, (rows, LANES), 1)
        stat[...] = jnp.where(lane == 0, one, two)
        turned = jnp.transpose(stat[...])
        count = s.tokens // s.dn
        for kind in range(2):
            for n in range(rows // s.dn):
                at = kind * count + n
                step = rows // s.dn
                line = turned[kind : kind + 1, n * s.dn : (n + 1) * s.dn].astype(BF).astype(F32)
                for i in range(s.tokens // rows):

                    @pl.when(pl.program_id(0) == i)
                    def _():
                        lines[at + i * step : at + i * step + 1, :] = line
        at = pl.ds(pl.multiple_of(pl.program_id(0) * rows, rows), rows)
        for odd, ref in ((0, keep), (1, send)):
            for n in range(s.members // 2):
                m = me ^ (2 * n + odd)
                for k in range(s.teams):
                    cols = pl.ds(pl.multiple_of((k * s.members + m) * s.db, s.db), s.db)
                    ref[n, at, k * s.db : (k + 1) * s.db] = grad[:, cols].astype(BF)
                ref[n, s.tokens :, :] = lines[...].astype(BF)

    def third(k):
        return (w_qkv, (s.d, s.width), lambda i, sc: (0, k * s.members + sc[ME]))

    row = lambda i, sc: (i, 0)
    pair = (s.members // 2, s.tokens + 16, s.dn)
    return kernel(
        body,
        "norm_one_grad",
        scalars,
        (s.tokens // rows,),
        [
            (qkv, (rows, 3 * s.width), row),
            (dq, (rows, s.width), row),
            (dkv, (rows, 2 * s.width), row),
            third(0),
            third(1),
            third(2),
            whole(gain),
        ],
        [
            whole_out(pair, BF),
            whole_out(pair, BF),
        ],
        [
            pltpu.VMEM((rows, s.d), F32),
            pltpu.VMEM((rows, LANES), F32),
            pltpu.VMEM((16, s.dn), F32),
        ],
    )


def shift_all(s, parts, out_ref):
    west_ref, mid_ref, east_ref = parts
    rows = s.sec_tokens
    col = lax.rem(lax.broadcasted_iota(jnp.int32, (rows, s.chan), 0), s.cols)

    def one(sector, carry):
        before = west_ref[lax.rem(sector + s.sectors - 1, s.sectors)]
        after = east_ref[lax.rem(sector + 1, s.sectors)]
        west = jnp.where(
            col == 0, pltpu.roll(before, rows - (s.cols - 1), 0), pltpu.roll(west_ref[sector], 1, 0)
        )
        east = jnp.where(
            col == s.cols - 1,
            pltpu.roll(after, s.cols - 1, 0),
            pltpu.roll(east_ref[sector], rows - 1, 0),
        )
        out_ref[sector] = (west + mid_ref[sector] + east).astype(BF)
        return carry

    lax.fori_loop(0, s.sectors, one, 0)


def group_blocks(s, sc, color):
    half = s.group // 2
    for side in range(2):
        for slot in range(half):
            j = 2 * slot + side if color == 0 else side * half + slot
            yield side, slot, sc[GRP] ^ j


def trunk_head(s, scalars, hown, terms, w_head, cot_cat):
    rows = s.half

    def body(sc, near, far, a, b, c, wh0, wh1, cat, home_ref, grad_ref, gain_ref, h2, y0, y1, y2):
        own = sc[ME] // (s.members // 2)
        gains = []
        for half, h1 in enumerate((near, far)):
            side = own ^ half
            total = three_terms(a[0, half, :rows, :], b[0, half, :rows, :], c[0, 1 - half, :rows, :])
            h2[pl.ds(pl.multiple_of(side * rows, rows), rows), :] = (h1[...] + total).astype(BF)
            at = slice(rows, rows + 8)
            gains.append(three_terms(a[0, half, at, :], b[0, half, at, :], c[0, 1 - half, at, :]))
        gain_ref[...] = gains[0] + gains[1]
        for j, ref in enumerate((y0, y1, y2)):
            weight = jnp.concatenate([wh0[j], wh1[j]], axis=1)
            ref[...] = dot(h2[...], weight, NT).reshape(s.sectors, s.sec_tokens, s.chan)
        shift_all(s, (y0, y1, y2), home_ref)
        grad_ref[...] = dot(h2[...], cat[...], TN)

    def part(k):
        return (w_head, (3, s.chan, s.db), lambda i, sc: (0, 0, k * s.members + sc[ME]))

    return kernel(
        body,
        "trunk_head",
        scalars,
        (1,),
        [whole(x) for x in hown]
        + [first(x) for x in terms]
        + [part(0), part(1), whole(cot_cat)],
        [
            whole_out((s.sectors, s.sec_tokens, s.chan), BF),
            whole_out((s.dn, 3 * s.chan), F32),
            whole_out((8, s.dn), F32),
        ],
        [pltpu.VMEM((s.tokens, s.dn), BF)]
        + [pltpu.VMEM((s.sectors, s.sec_tokens, s.chan), F32) for _ in range(3)],
    )


def embed_back(s, scalars, g1, own, stats, hidden0, gain, w_embed, in_cat, head_home, head_part, gain2, bias):
    wide = 3 * s.chan
    span = s.dn

    def body(sc, *refs):
        a, b, c, own_ref, st_ref, h0, h1, g, we0, we1, cat, home, head, gain2_ref, bias_ref = refs[:15]
        keep, send = refs[15:17]
        edges = refs[17 : 17 + s.group]
        grad, stat, y0, y1, y2, ours, part, smalls = refs[17 + s.group :]
        lines = slice(s.tokens, s.tokens + 16)
        total = three_terms(a[0, lines, :], b[0, lines, :], c[0, lines, :]) * np.float32(1.0 / s.d)
        for n in range(s.tokens // span):
            pair = [total[n : n + 1, :], total[s.tokens // span + n : s.tokens // span + n + 1, :]]
            pair = jnp.concatenate(pair + [jnp.zeros((LANES - 2, span), F32)], axis=0)
            stat[n * span : (n + 1) * span, :] = jnp.transpose(pair)
        gain_own = jnp.concatenate(
            [
                g[:, pl.ds(pl.multiple_of((k * s.members + sc[ME]) * s.db, s.db), s.db)]
                for k in range(s.teams)
            ],
            axis=1,
        )
        chunk = s.sec_tokens

        def rows_chunk(i, acc):
            at = pl.ds(pl.multiple_of(i * chunk, chunk), chunk)
            mean, rstd = st_ref[at, 0:1], st_ref[at, 1:2]
            one, two = stat[at, 0:1], stat[at, 1:2]
            g1 = three_terms(a[0, at, :], b[0, at, :], c[0, at, :])
            x = (jnp.concatenate([h0[at, :], h1[at, :]], axis=1) - mean) * rstd
            back = g1 * gain_own - one - x * two
            grad[at, :] = (own_ref[at, :].astype(F32) + rstd * back).astype(BF)
            return acc + jnp.sum(g1 * x, axis=0, keepdims=True)

        gain1 = lax.fori_loop(0, s.tokens // chunk, rows_chunk, jnp.zeros((1, s.dn), F32))
        for j, ref in enumerate((y0, y1, y2)):
            weight = jnp.concatenate([we0[j], we1[j]], axis=1)
            ref[...] = dot(grad[...], weight, NT).reshape(s.sectors, s.sec_tokens, s.chan)
        shift_all(s, (y2, y1, y0), ours)
        for odd, ref in ((0, keep), (1, send)):
            for n in range(s.members // 2):
                for team in range(s.teams):
                    sector = team * s.members + (sc[ME] ^ (2 * n + odd))
                    ref[n, team, 0] = home[sector]
                    ref[n, team, 1] = ours[sector]
        part[:, :wide] = head[...]
        part[:, wide : 2 * wide] = dot(grad[...], cat[...], TN)
        size = s.db // s.group
        for k in range(s.teams):
            lines = [
                bias_ref[:, k * s.fb + n * LANES : k * s.fb + (n + 1) * LANES] for n in range(s.fb // LANES)
            ]
            lines += [gain1[:, k * s.db : (k + 1) * s.db], gain2_ref[0:1, k * s.db : (k + 1) * s.db]]
            lines += [jnp.zeros((size - len(lines), LANES), F32)]
            smalls[...] = jnp.concatenate(lines, axis=0).astype(BF)
            for j, ref in enumerate(edges):
                at = pl.ds(pl.multiple_of(k * s.db + (sc[GRP] ^ j) * size, size), size)
                ref[k, :, : 2 * wide] = part[at, :].astype(BF)
                ref[k, :, 2 * wide :] = smalls[...]

    def part_of(k):
        return (w_embed, (3, s.chan, s.db), lambda i, sc: (0, 0, k * s.members + sc[ME]))

    def own_of(k):
        return (hidden0, (s.tokens, s.db), lambda i, sc: (0, k * s.members + sc[ME]))

    goes = (s.members // 2, s.teams, 2, s.sec_tokens, s.chan)
    size = s.db // s.group
    block = (s.teams, size, 2 * wide + LANES)
    return kernel(
        body,
        "embed_back",
        scalars,
        (1,),
        [first(x) for x in g1]
        + [whole(own), whole(stats), own_of(0), own_of(1), whole(gain), part_of(0), part_of(1)]
        + [whole(in_cat), whole(head_home), whole(head_part), whole(gain2), whole(bias)],
        [whole_out(goes, BF), whole_out(goes, BF)] + [whole_out(block, BF)] * s.group,
        [pltpu.VMEM((s.tokens, s.dn), BF), pltpu.VMEM((s.tokens, LANES), F32)]
        + [pltpu.VMEM((s.sectors, s.sec_tokens, s.chan), F32) for _ in range(3)]
        + [pltpu.VMEM((s.sectors, s.sec_tokens, s.chan), BF)]
        + [pltpu.VMEM((s.dn, 2 * wide), F32), pltpu.VMEM((size, LANES), BF)],
    )


def mlp_weight_grads(s, scalars, near, far, grad_mlp):
    sub = s.fb // s.group

    def body(sc, an, pn, nn_ref, af, pf, nf, gn, gf, ka, sa, kb, sb, scr):
        color = pl.program_id(0)
        kind = pl.program_id(1)

        @pl.when(kind == 0)
        def _():
            scr[...] = (dot(an[...], gn[...], TN) + dot(af[...], gf[...], TN)).astype(BF)

        @pl.when(kind == 1)
        def _():
            scr[...] = (dot(pn[...], nn_ref[...], TN) + dot(pf[...], nf[...], TN)).astype(BF)

        for k, refs in enumerate(((ka, sa), (kb, sb))):

            @pl.when(color == k)
            def _():
                def lane_block(c, carry):
                    lanes = pl.ds(pl.multiple_of(c * LANES, LANES), LANES)
                    to = pl.ds(pl.multiple_of(c * sub, sub), sub)
                    for side, slot, q in group_blocks(s, sc, k):
                        rows = pl.ds(pl.multiple_of(q * sub, sub), sub)
                        refs[side][slot, 0, to, :] = scr[rows, lanes]
                    return carry

                lax.fori_loop(0, s.d // LANES, lane_block, 0)

    def out(color):
        shape = (s.group // 2, 2, s.d, LANES)
        block = (s.group // 2, 1, s.d, LANES)
        if color == 0:
            index = lambda k, kind, sc: (0, jnp.where(k == 0, kind, 1), 0, 0)
        else:
            index = lambda k, kind, sc: (0, jnp.where(k == 0, 0, kind), 0, 0)
        return (shape, BF, block, index)

    cols = lambda k, kind, sc: (0, k)
    ins = []
    for activ, grad_pre, normed in (near, far):
        ins += [
            (activ, (s.half, s.fb), cols),
            (grad_pre, (s.half, s.fb), cols),
            whole(normed),
        ]
    ins += [
        (grad_mlp, (s.half, s.d), lambda k, kind, sc: (side_of(s, sc, False), 0)),
        (grad_mlp, (s.half, s.d), lambda k, kind, sc: (side_of(s, sc, True), 0)),
    ]
    return kernel(
        body,
        "mlp_weight_grads",
        scalars,
        (s.teams, 2),
        ins,
        [out(0), out(0), out(1), out(1)],
        [pltpu.VMEM((s.fb, s.d), BF)],
    )


def attention_weight_grads(s, scalars, normed1, dq, dkv, att_near, att_far, own):
    def body(sc, n1, dq_ref, dkv_ref, an, af, own_near, own_far, ka, sa, kb, sb, scr):
        scr[: s.width] = dot(dq_ref[...], n1[...], TN).astype(BF)
        scr[s.width : 3 * s.width] = dot(dkv_ref[...], n1[...], TN).astype(BF)
        scr[3 * s.width :] = (dot(own_near[...], an[...], TN) + dot(own_far[...], af[...], TN)).astype(BF)

        def lane_block(c, carry):
            lanes = pl.ds(pl.multiple_of(c * LANES, LANES), LANES)
            for k, refs in enumerate(((ka, sa), (kb, sb))):
                for side, slot, q in group_blocks(s, sc, k):
                    rows = pl.ds(pl.multiple_of((k * s.group + q) * LANES, LANES), LANES)
                    refs[side][slot, lanes, :] = scr[rows, lanes]
            return carry

        lax.fori_loop(0, s.d // LANES, lane_block, 0)

    shape = (s.group // 2, s.d, LANES)
    return kernel(
        body,
        "attention_weight_grads",
        scalars,
        (1,),
        [
            whole(normed1),
            whole(dq),
            whole(dkv),
            whole(att_near),
            whole(att_far),
            (own, (s.half, s.dn), lambda i, sc: (side_of(s, sc, False), 0)),
            (own, (s.half, s.dn), lambda i, sc: (side_of(s, sc, True), 0)),
        ],
        [whole_out(shape, BF)] * 4,
        [pltpu.VMEM((3 * s.width + s.dn, s.d), BF)],
    )


def add_low(a, b):
    return (a.astype(F32) + b.astype(F32)).astype(BF)


def first(x):
    rank = len(x.shape)
    return (x, (1,) + tuple(x.shape[1:]), lambda *_: (0,) * rank)


def three_terms(keep, got, more):
    return keep.astype(F32) + got.astype(F32) + more.astype(F32)


def group_first(keep_a, send_a, keep_b, send_b):
    got_a = swap(send_a, "grp", 1)
    got_b = swap(send_b, "grp", 2)
    return (keep_a, got_a), (keep_b, got_b), (add_low(keep_a[1], got_a[1]), add_low(keep_b[1], got_b[1]))


def group_second(terms_a, terms_b, sends):
    more_a = swap(sends[0], "grp", 2)
    more_b = swap(sends[1], "grp", 1)
    return terms_a + (more_a[None],), terms_b + (more_b[None],)


def pick_team(s, scalars, terms_a, terms_b, kinds):
    half = s.d // 2

    def body(sc, *refs):
        a, b = refs[:3], refs[3:6]
        keep, send = refs[6:]
        team = sc[TEAM]

        def total(terms, k, rows):
            at = (0, k, rows) if kinds == 2 else (0, rows)
            return three_terms(*[ref[at] for ref in terms]).astype(BF)

        if kinds == 2:
            for side in range(2):

                @pl.when(team == side)
                def _():
                    same, other = (a, b) if side == 0 else (b, a)
                    keep[0] = total(same, 0, slice(None))
                    send[0] = total(other, 0, slice(None))

        mine = pl.ds(pl.multiple_of(team * half, half), half)
        theirs = pl.ds(pl.multiple_of((1 - team) * half, half), half)
        for color, terms in enumerate((a, b)):
            at = slice(color * half, (color + 1) * half)
            keep[kinds - 1, at] = total(terms, 1, mine)
            send[kinds - 1, at] = total(terms, 1, theirs)

    return kernel(
        body,
        "pick_team",
        scalars,
        (1,),
        [first(x) for x in terms_a + terms_b],
        [whole_out((kinds, s.d, LANES), BF)] * 2,
    )


def pick_member(s, scalars, keep, got):
    kinds = keep.shape[0]
    half = s.d // 2

    def body(sc, k_ref, g_ref, *refs):
        for j in range(s.members):
            m = sc[ME] ^ j
            for color in range(2):
                at = pl.ds(pl.multiple_of(color * half + m * s.db, s.db), s.db)
                value = k_ref[kinds - 1, at].astype(F32) + g_ref[kinds - 1, at].astype(F32)
                refs[j][color] = value.astype(BF)
        if kinds == 2:
            refs[s.members][...] = (k_ref[0].astype(F32) + g_ref[0].astype(F32)).astype(BF)

    outs = [whole_out((2, s.db, LANES), BF)] * s.members
    if kinds == 2:
        outs = outs + [whole_out((s.d, LANES), BF)]
    return kernel(body, "pick_member", scalars, (1,), [whole(keep), whole(got)], outs)


def all_of_group(x, x_first):
    near, far = (1, 2) if x_first else (2, 1)
    one = swap(x, "grp", near)
    two = swap(x, "grp", far)
    both = swap(one, "grp", far)
    return [x, one, two, both] if x_first else [x, two, one, both]


def cross(s, pieces):
    got = [pieces[0]] + [swap(pieces[j], "sec", j) for j in range(1, s.members)]
    return jnp.stack(got)


def mlp_grads_out(s, scalars, downs, ups):
    sub = s.fb // s.group

    def body(sc, *refs):
        d_refs, u_refs = refs[: s.group], refs[s.group : 2 * s.group]
        down, up = refs[2 * s.group :]
        for j in range(s.group):
            q = sc[GRP] ^ j
            rows = pl.ds(pl.multiple_of(q * sub, sub), sub)
            for c in range(s.d // LANES):
                down[rows, c * LANES : (c + 1) * LANES] = d_refs[j][c * sub : (c + 1) * sub, :].astype(F32)

            def member(jm, carry):
                m = sc[ME] ^ jm
                for color in range(s.teams):
                    at = ((color * s.members + m) * s.group + q) * LANES
                    up[:, pl.ds(pl.multiple_of(at, LANES), LANES)] = jnp.transpose(u_refs[j][jm, color].astype(F32))
                return carry

            lax.fori_loop(0, s.members, member, 0)

    return kernel(
        body,
        "mlp_grads_out",
        scalars,
        (1,),
        [whole(x) for x in downs + ups],
        [whole_out((s.fb, s.d), F32), whole_out((s.db, s.ff), F32)],
    )


def attention_grads_out(s, scalars, parts):
    def body(sc, *refs):
        u_refs = refs[: s.group]
        qkv, out = refs[s.group :]
        for j in range(s.group):
            q = sc[GRP] ^ j

            def member(jm, carry):
                m = sc[ME] ^ jm
                at = (q // 2) * s.d + m * s.width + lax.rem(q, 2) * LANES
                value = jnp.transpose(u_refs[j][jm, 0].astype(F32))
                qkv[:, pl.ds(pl.multiple_of(at, LANES), LANES)] = value
                other = jnp.transpose(u_refs[j][jm, 1].astype(F32))

                @pl.when(q < 2)
                def _():
                    at = 2 * s.d + m * s.width + q * LANES
                    qkv[:, pl.ds(pl.multiple_of(at, LANES), LANES)] = other

                @pl.when(q >= 2)
                def _():
                    at = ((q - 2) * s.members + m) * s.db
                    out[:, pl.ds(pl.multiple_of(at, LANES), LANES)] = other

                return carry

            lax.fori_loop(0, s.members, member, 0)

    return kernel(
        body,
        "attention_grads_out",
        scalars,
        (1,),
        [whole(x) for x in parts],
        [whole_out((s.db, 3 * s.d), F32), whole_out((s.db, s.d), F32)],
    )


def edge_grads_out(s, scalars, parts):
    wide = 3 * s.chan
    size = s.db // s.group

    def body(sc, *refs):
        ins = refs[: s.group]
        embed, head, small, scr = refs[s.group :]
        for j in range(s.group):
            at = pl.ds(pl.multiple_of((sc[GRP] ^ j) * size, size), size)
            scr[at, :] = ins[j][...].astype(F32)
        head[...] = jnp.transpose(scr[:, :wide])
        embed[...] = jnp.transpose(scr[:, wide : 2 * wide])
        small[...] = ins[0][:16, 2 * wide :].astype(F32)

    return kernel(
        body,
        "edge_grads_out",
        scalars,
        (1,),
        [whole(x) for x in parts],
        [
            whole_out((wide, s.db), F32),
            whole_out((wide, s.db), F32),
            whole_out((16, LANES), F32),
        ],
        [pltpu.VMEM((s.db, 2 * wide + LANES), F32)],
    )


def on_team(
    fields,
    valid_rows,
    w_embed,
    ln1_gain,
    w_qkv,
    w_out,
    ln2_gain,
    w_up,
    b_up,
    w_down,
    w_head,
    cotangent,
):
    s = Sizes(fields, w_qkv, w_up)
    place = lax.axis_index("sec")
    team, me = place // s.members, place % s.members
    core, chip = 1, 2
    first_team = team == 0
    valid = jnp.where(first_team, valid_rows[0], valid_rows[1])
    scalars = (jnp.stack([team, me, lax.axis_index("grp"), valid]).astype(jnp.int32), [])
    gain1 = ln1_gain.astype(F32)[None]
    gain2 = ln2_gain.astype(F32)[None]

    def gather_sample(x):
        flat = x.reshape(s.teams, s.sec_tokens, s.chan)
        mine = jnp.where(first_team, flat[0], flat[1])
        other = swap(jnp.where(first_team, flat[1], flat[0]), "sec", s.members)
        pair = jnp.stack([mine, other])
        across = swap(pair, "sec", chip)
        return [pair, swap(pair, "sec", core), across, swap(across, "sec", core)]

    def go_home(keep, got, far):
        mine = three_terms(keep[0], got[0], far)
        own = jnp.where(first_team, mine[0], mine[1])
        other = jnp.where(first_team, mine[1], mine[0]).astype(BF)
        other = swap(other, "sec", s.members).astype(F32)
        both = [jnp.where(first_team, own, other), jnp.where(first_team, other, own)]
        return [jnp.stack([x[kind] for x in both]).reshape(fields.shape) for kind in range(2)]

    def scatter_features(keep, send):
        got = swap(send, "sec", core)
        return keep, got, swap(add_low(keep[1:2], got[1:2]), "sec", chip)

    w_head_t = jnp.transpose(w_head, (0, 2, 1))
    in_cat, hidden0, normed1, qkv, stats = embed_qkv(
        s, scalars, gather_sample(fields), w_embed.reshape(3 * s.chan, s.d), gain1, w_qkv
    )
    att_near, *rest = attention_fwd(s, scalars, qkv, False)
    saved_near = (att_near, *rest)
    from_chip_far = swap(att_near, "sec", chip)
    att_far, *rest = attention_fwd(s, scalars, qkv, True)
    saved_far = (att_far, *rest)
    from_chip_near = swap(att_far, "sec", chip)
    hold(scalars, from_chip_far)
    cot_cat, grad_mlp = cotangent_grad(
        s, scalars, gather_sample(cotangent), w_head_t.reshape(3 * s.chan, s.d)
    )
    att_pieces_far = [att_far, swap(att_far, "sec", core), from_chip_far, swap(from_chip_far, "sec", core)]
    att_pieces_near = [att_near, swap(att_near, "sec", core), from_chip_near, swap(from_chip_near, "sec", core)]

    def run_mlp(pieces, far):
        return mlp(s, scalars, pieces, hidden0, grad_mlp, w_out, gain2, w_up, b_up, w_down, far)

    attended_far, normed2_far, activ_far, pre_far, gkeep, gsend, gsum, hown_far, bias_far, _ = run_mlp(
        att_pieces_far, True
    )
    hold(scalars, from_chip_near)
    g2_chip = [swap(gkeep, "sec", chip), swap(gsend, "sec", chip + core)]
    attended_near, normed2_near, activ_near, pre_near, gkeep, gsend, gsum_near, hown_near, bias_near, hidden1 = run_mlp(
        att_pieces_near, False
    )
    bias_grad = bias_far + bias_near
    got = swap(gsend, "sec", core)
    pkeep, psend = trunk_part(s, scalars, ((activ_near, gsum_near), (activ_far, gsum)), w_down)
    b0 = norm_two_back(s, scalars, [gkeep, got, *g2_chip], hidden1, grad_mlp, gain2)
    b1 = swap(b0, "sec", core)
    b2 = swap(b0, "sec", chip)
    b3 = swap(b2, "sec", core)
    mlp_blocks = mlp_weight_grads(
        s, scalars, (activ_near, pre_near, normed2_near), (activ_far, pre_far, normed2_far), grad_mlp
    )
    hold(scalars, b2)
    mlp_a, mlp_b, mlp_sends = group_first(*mlp_blocks)
    before = attention_bwd(s, scalars, qkv, saved_near, (b0, b1), w_out, False)
    hold(scalars, b3, *mlp_sends)
    mlp_terms = group_second(mlp_a, mlp_b, mlp_sends)
    trunk_terms = scatter_features(pkeep, psend)
    dq, own, dkv = attention_bwd(s, scalars, qkv, saved_far, (b2, b3), w_out, True, before)
    hold(scalars, *[terms[2] for terms in mlp_terms])
    att_blocks = attention_weight_grads(s, scalars, normed1, dq, dkv, attended_near, attended_far, own)
    att_a, att_b, att_sends = group_first(*att_blocks)
    mlp_kept, send = pick_team(s, scalars, *mlp_terms, 2)
    mlp_swapped = swap(send, "sec", s.members)
    g1_keep, g1_send = norm_one_grad(s, scalars, qkv, dq, dkv, w_qkv, gain1)
    hold(scalars, *att_sends)
    att_terms = group_second(att_a, att_b, att_sends)
    hold(scalars, trunk_terms[2])
    head_home, head_part, gain2_grad = trunk_head(
        s, scalars, (hown_near, hown_far), trunk_terms, w_head_t, cot_cat
    )
    g1 = scatter_features(g1_keep, g1_send)
    hold(scalars, *[terms[2] for terms in att_terms])
    att_kept, send = pick_team(s, scalars, *att_terms, 1)
    att_swapped = swap(send, "sec", s.members)
    *crossed, downs = pick_member(s, scalars, mlp_kept, mlp_swapped)
    mlp_parts = (all_of_group(downs, False), all_of_group(cross(s, crossed), True))
    keep, send, *edges = embed_back(
        s, scalars, g1, own, stats, hidden0, gain1, w_embed, in_cat, head_home, head_part, gain2_grad, bias_grad
    )
    edges = edges[:1] + [swap(edges[j], "grp", j) for j in range(1, s.group)]
    home_got = swap(send, "sec", core)
    hold(scalars, *mlp_parts[0], *mlp_parts[1])
    crossed = pick_member(s, scalars, att_kept, att_swapped)
    att_parts = all_of_group(cross(s, crossed), True)
    home_far = swap(add_low(keep[1], home_got[1]), "sec", chip)
    down_grad, up_grad = mlp_grads_out(s, scalars, *mlp_parts)
    hold(scalars, home_far)
    head_output, input_grad = go_home(keep, home_got, home_far)

    total = edges[0].astype(F32) + edges[1].astype(F32) + edges[2].astype(F32) + edges[3].astype(F32)
    kept = jnp.where(first_team, total[0], total[1])
    given = jnp.where(first_team, total[1], total[0]).astype(BF)
    edges = (kept + swap(given, "sec", s.members).astype(F32)).astype(BF)
    edge_parts = all_of_group(edges, True)
    qkv_grad, out_grad = attention_grads_out(s, scalars, att_parts)
    embed_t, head_t, small = edge_grads_out(s, scalars, edge_parts)
    embed_grad = embed_t.reshape(3, s.chan, s.db)
    head_grad = jnp.transpose(head_t.reshape(3, s.chan, s.db), (0, 2, 1))
    nb = s.fb // LANES
    return (
        head_output,
        input_grad,
        embed_grad,
        small[nb],
        qkv_grad,
        out_grad,
        small[nb + 1],
        up_grad,
        small[:nb].reshape(s.fb),
        down_grad,
        head_grad,
    )

LAT = 32
KCOLS = 8


def extended(cells, sides, width):
    for axis, dim in sides:
        count = lax.axis_size(axis)
        head = lax.slice_in_dim(cells, 0, width, axis=dim)
        tail = lax.slice_in_dim(cells, cells.shape[dim] - width, cells.shape[dim], axis=dim)
        cells = jnp.concatenate(
            [
                lax.ppermute(tail, axis, [(i, (i + 1) % count) for i in range(count)]),
                cells,
                lax.ppermute(head, axis, [((i + 1) % count, i) for i in range(count)]),
            ],
            axis=dim,
        )
    return cells


def normed(hidden, gains):
    center = hidden - jnp.mean(hidden, axis=-1, keepdims=True)
    spread = jnp.mean(center * center, axis=-1, keepdims=True)
    return center * lax.rsqrt(spread + 1e-05) * gains


def gelu_exact(values):
    return jax.nn.gelu(values, approximate=False)


def three_cols(padded, col_count, west_first):
    west_cols = padded[:, :, 0:col_count]
    middle_cols = padded[:, :, 1 : col_count + 1]
    east_cols = padded[:, :, 2 : col_count + 2]
    if west_first:
        return jnp.stack([west_cols, middle_cols, east_cols], axis=3)
    return jnp.stack([east_cols, middle_cols, west_cols], axis=3)


def split_heads(values):
    return values.reshape(values.shape[0], -1, HEADS, HEAD_DIM)


def key_mask(valid_rows, count_cols):
    rows_ok = jnp.arange(LAT)[None, :] < valid_rows[:, None]
    spread_ok = jnp.broadcast_to(rows_ok[:, :, None], (rows_ok.shape[0], LAT, count_cols))
    return spread_ok.reshape(rows_ok.shape[0], LAT * count_cols)


def key_scores(queries, kv_piece, valid_rows):
    d_model = HEADS * HEAD_DIM
    key_part = split_heads(kv_piece[..., :d_model])
    value_part = split_heads(kv_piece[..., d_model:])
    scores = (
        jnp.einsum("sqhd,skhd->shqk", queries, key_part, preferred_element_type=jnp.float32) * 0.125
    )
    allowed = key_mask(valid_rows, kv_piece.shape[2])
    scores = jnp.where(allowed[:, None, None, :], scores, -1e30)
    return (scores, key_part, value_part)


def softmax_fold(queries, valid_rows):

    def fold_piece(run_state, kv_piece, first_col):
        run_max, run_sum, run_acc = run_state
        scores, key_part, value_part = key_scores(queries, kv_piece, valid_rows)
        new_max = jnp.maximum(run_max, jnp.max(scores, axis=-1))
        factor = jnp.exp(run_max - new_max)
        weights = jnp.exp(scores - new_max[..., None])
        new_sum = run_sum * factor + jnp.sum(weights, axis=-1)
        added = jnp.einsum(
            "shqk,skhd->sqhd",
            weights.astype(jnp.bfloat16),
            value_part,
            preferred_element_type=jnp.float32,
        )
        new_acc = run_acc * jnp.transpose(factor, (0, 2, 1))[..., None] + added
        return (new_max, new_sum, new_acc)

    return fold_piece


def on_sectors(
    fields,
    valid_rows,
    w_embed,
    ln1_gain,
    w_qkv,
    w_out,
    ln2_gain,
    w_up,
    b_up,
    w_down,
    w_head,
    cotangent,
):
    samples, lat_rows, col_count, channels = fields.shape
    d_model = w_qkv.shape[0]
    token_count = lat_rows * col_count
    padded_in = extended(fields, (("sec", 2),), 1)
    input_cat = three_cols(padded_in, col_count, True)
    hidden0 = jnp.einsum("slcoi,oid->slcd", input_cat, w_embed, preferred_element_type=jnp.float32)
    normed_one, norm_one_back = jax.vjp(normed, hidden0, ln1_gain.astype(jnp.float32))
    normed_one_low = normed_one.astype(jnp.bfloat16)
    qkv_full = jnp.einsum(
        "slcd,de->slce", normed_one_low, w_qkv, preferred_element_type=jnp.float32
    ).astype(jnp.bfloat16)
    queries = split_heads(qkv_full[..., :d_model])
    key_vals = qkv_full[..., d_model:]
    init_state = (
        jnp.full((samples, HEADS, token_count), -1e30, jnp.float32),
        jnp.zeros((samples, HEADS, token_count), jnp.float32),
        jnp.zeros((samples, token_count, HEADS, HEAD_DIM), jnp.float32),
    )
    fold_piece = softmax_fold(queries, valid_rows)
    all_kv = lax.all_gather(key_vals, "sec", axis=2, tiled=True)

    def forward_block(block_index, run_state):
        kv_block = lax.dynamic_slice_in_dim(all_kv, block_index * KCOLS, KCOLS, 2)
        return fold_piece(run_state, kv_block, block_index * KCOLS)

    run_max, run_sum, run_acc = lax.fori_loop(
        0, all_kv.shape[2] // KCOLS, forward_block, init_state
    )
    attended = run_acc / jnp.transpose(run_sum, (0, 2, 1))[..., None]
    log_total = run_max + jnp.log(run_sum)
    attended_low = attended.reshape(samples, lat_rows, col_count, d_model).astype(jnp.bfloat16)
    hidden1 = hidden0 + jnp.einsum(
        "slcd,de->slce", attended_low, w_out, preferred_element_type=jnp.float32
    )
    normed_two, norm_two_back = jax.vjp(normed, hidden1, ln2_gain.astype(jnp.float32))
    normed_two_low = normed_two.astype(jnp.bfloat16)
    preact = jnp.einsum(
        "slcd,df->slcf", normed_two_low, w_up, preferred_element_type=jnp.float32
    ) + b_up.astype(jnp.float32)
    activ, gelu_back = jax.vjp(gelu_exact, preact)
    activ_low = activ.astype(jnp.bfloat16)
    hidden2 = hidden1 + jnp.einsum(
        "slcf,fd->slcd", activ_low, w_down, preferred_element_type=jnp.float32
    )
    hidden2_low = hidden2.astype(jnp.bfloat16)
    padded_hidden = extended(hidden2_low, (("sec", 2),), 1)
    hidden_cat = three_cols(padded_hidden, col_count, True)
    head_output = jnp.einsum(
        "slcod,odi->slci", hidden_cat, w_head, preferred_element_type=jnp.float32
    )
    padded_cot = extended(cotangent, (("sec", 2),), 1)
    cot_cat = three_cols(padded_cot, col_count, False)
    head_grad = jnp.einsum(
        "slcod,slci->odi", hidden_cat, cotangent, preferred_element_type=jnp.float32
    )
    grad_two = jnp.einsum("slcoi,odi->slcd", cot_cat, w_head, preferred_element_type=jnp.float32)
    grad_mlp = grad_two.astype(jnp.bfloat16)
    down_grad = jnp.einsum("slcf,slcd->fd", activ_low, grad_mlp, preferred_element_type=jnp.float32)
    grad_act = jnp.einsum("slcd,fd->slcf", grad_mlp, w_down, preferred_element_type=jnp.float32)
    grad_pre = gelu_back(grad_act)[0].astype(jnp.bfloat16)
    bias_grad = jnp.sum(grad_pre.astype(jnp.float32), axis=(0, 1, 2))
    up_grad = jnp.einsum(
        "slcd,slcf->df", normed_two_low, grad_pre, preferred_element_type=jnp.float32
    )
    grad_normed_two = jnp.einsum(
        "slcf,df->slcd", grad_pre, w_up, preferred_element_type=jnp.float32
    )
    grad_from_norm, gain_two_grad = norm_two_back(grad_normed_two)
    grad_one = grad_two + grad_from_norm
    grad_att = grad_one.astype(jnp.bfloat16)
    out_grad = jnp.einsum(
        "slcd,slce->de", attended_low, grad_att, preferred_element_type=jnp.float32
    )
    grad_heads = split_heads(
        jnp.einsum("slce,de->slcd", grad_att, w_out, preferred_element_type=jnp.float32).astype(
            jnp.bfloat16
        )
    )
    row_delta = jnp.transpose(
        jnp.sum(grad_heads.astype(jnp.float32) * attended, axis=-1), (0, 2, 1)
    )

    def sample_backward(unused_carry, sample_in):
        one_query, one_grad, one_lse, one_delta, one_valid, one_kv = sample_in
        term_zero = jnp.zeros((1, lat_rows, one_kv.shape[2], 2 * d_model), jnp.bfloat16)
        grad_zero = jnp.zeros(one_query.shape, jnp.float32)

        def backward_block(block_index, run_state):
            grad_query, term = run_state
            kv_block = lax.dynamic_slice_in_dim(one_kv, block_index * KCOLS, KCOLS, 2)
            scores, key_part, value_part = key_scores(one_query, kv_block, one_valid)
            probs = jnp.exp(scores - one_lse[..., None])
            grad_probs = jnp.einsum(
                "sqhd,skhd->shqk", one_grad, value_part, preferred_element_type=jnp.float32
            )
            grad_scores = (probs * (grad_probs - one_delta[..., None])).astype(jnp.bfloat16)
            grad_query = (
                grad_query
                + jnp.einsum(
                    "shqk,skhd->sqhd", grad_scores, key_part, preferred_element_type=jnp.float32
                )
                * 0.125
            )
            grad_keys = (
                jnp.einsum(
                    "shqk,sqhd->skhd", grad_scores, one_query, preferred_element_type=jnp.float32
                )
                * 0.125
            )
            grad_values = jnp.einsum(
                "shqk,sqhd->skhd",
                probs.astype(jnp.bfloat16),
                one_grad,
                preferred_element_type=jnp.float32,
            )
            joined = jnp.concatenate(
                [
                    grad_keys.reshape(1, lat_rows, KCOLS, d_model),
                    grad_values.reshape(1, lat_rows, KCOLS, d_model),
                ],
                axis=-1,
            ).astype(jnp.bfloat16)
            term = lax.dynamic_update_slice_in_dim(term, joined, block_index * KCOLS, 2)
            return (grad_query, term)

        grad_query, term = lax.fori_loop(
            0, one_kv.shape[2] // KCOLS, backward_block, (grad_zero, term_zero)
        )
        summed = lax.psum_scatter(
            term.astype(jnp.float32).astype(jnp.bfloat16), "sec", scatter_dimension=2, tiled=True
        ).astype(jnp.float32)
        return (unused_carry, (grad_query, summed))

    scan_inputs = (
        queries.reshape(samples, 1, token_count, HEADS, HEAD_DIM),
        grad_heads.reshape(samples, 1, token_count, HEADS, HEAD_DIM),
        log_total.reshape(samples, 1, HEADS, token_count),
        row_delta.reshape(samples, 1, HEADS, token_count),
        valid_rows.reshape(samples, 1),
        all_kv.reshape(samples, 1, lat_rows, all_kv.shape[2], 2 * d_model),
    )
    scan_end, (grad_queries, grad_kv) = lax.scan(sample_backward, 0, scan_inputs)
    grad_qkv = jnp.concatenate(
        [
            grad_queries.reshape(samples, lat_rows, col_count, d_model),
            grad_kv.reshape(samples, lat_rows, col_count, 2 * d_model),
        ],
        axis=-1,
    ).astype(jnp.bfloat16)
    qkv_grad = jnp.einsum(
        "slcd,slce->de", normed_one_low, grad_qkv, preferred_element_type=jnp.float32
    )
    grad_normed_one = jnp.einsum(
        "slce,de->slcd", grad_qkv, w_qkv, preferred_element_type=jnp.float32
    )
    grad_from_first, gain_one_grad = norm_one_back(grad_normed_one)
    grad_zero_low = (grad_one + grad_from_first).astype(jnp.bfloat16)
    embed_grad = jnp.einsum(
        "slcoi,slcd->oid", input_cat, grad_zero_low, preferred_element_type=jnp.float32
    )
    padded_grad = extended(grad_zero_low, (("sec", 2),), 1)
    grad_cat = three_cols(padded_grad, col_count, False)
    input_grad = jnp.einsum(
        "slcod,oid->slci", grad_cat, w_embed, preferred_element_type=jnp.float32
    )
    shard_grads = (
        lax.psum_scatter(
            embed_grad.astype(jnp.bfloat16), "sec", scatter_dimension=2, tiled=True
        ).astype(jnp.float32),
        lax.psum_scatter(
            gain_one_grad.astype(jnp.bfloat16), "sec", scatter_dimension=0, tiled=True
        ).astype(jnp.float32),
        lax.psum_scatter(
            qkv_grad.astype(jnp.bfloat16), "sec", scatter_dimension=0, tiled=True
        ).astype(jnp.float32),
        lax.psum_scatter(
            out_grad.astype(jnp.bfloat16), "sec", scatter_dimension=0, tiled=True
        ).astype(jnp.float32),
        lax.psum_scatter(
            gain_two_grad.astype(jnp.bfloat16), "sec", scatter_dimension=0, tiled=True
        ).astype(jnp.float32),
        lax.psum_scatter(
            up_grad.astype(jnp.bfloat16), "sec", scatter_dimension=0, tiled=True
        ).astype(jnp.float32),
        lax.psum_scatter(
            bias_grad.astype(jnp.bfloat16), "sec", scatter_dimension=0, tiled=True
        ).astype(jnp.float32),
        lax.psum_scatter(
            down_grad.astype(jnp.bfloat16), "sec", scatter_dimension=0, tiled=True
        ).astype(jnp.float32),
        lax.psum_scatter(
            head_grad.astype(jnp.bfloat16), "sec", scatter_dimension=1, tiled=True
        ).astype(jnp.float32),
    )
    total_grads = (
        lax.psum(shard_grads[0].astype(jnp.bfloat16), "grp").astype(jnp.float32),
        lax.psum(shard_grads[1].astype(jnp.bfloat16), "grp").astype(jnp.float32),
        lax.psum(shard_grads[2].astype(jnp.bfloat16), "grp").astype(jnp.float32),
        lax.psum(shard_grads[3].astype(jnp.bfloat16), "grp").astype(jnp.float32),
        lax.psum(shard_grads[4].astype(jnp.bfloat16), "grp").astype(jnp.float32),
        lax.psum(shard_grads[5].astype(jnp.bfloat16), "grp").astype(jnp.float32),
        lax.psum(shard_grads[6].astype(jnp.bfloat16), "grp").astype(jnp.float32),
        lax.psum(shard_grads[7].astype(jnp.bfloat16), "grp").astype(jnp.float32),
        lax.psum(shard_grads[8].astype(jnp.bfloat16), "grp").astype(jnp.float32),
    )
    return (
        head_output,
        input_grad,
        total_grads[0],
        total_grads[1],
        total_grads[2],
        total_grads[3],
        total_grads[4],
        total_grads[5],
        total_grads[6],
        total_grads[7],
        total_grads[8],
    )


def on_device(*args):
    fields, w_qkv = args[0], args[4]
    sectors = lax.axis_size("sec")
    fits = (
        fields.shape[0] == 2
        and sectors == 8
        and lax.axis_size("grp") == 4
        and w_qkv.shape[0] == sectors * LANES
    )
    return on_team(*args) if fits else on_sectors(*args)


def solution(mesh):
    tokens_in = P("grp", None, "sec", None)
    return jax.shard_map(
        on_device,
        mesh=mesh,
        in_specs=(tokens_in, P("grp")) + (P(),) * 9 + (tokens_in,),
        out_specs=(
            tokens_in,
            tokens_in,
            P(None, None, "sec"),
            P("sec"),
            P("sec", None),
            P("sec", None),
            P("sec"),
            P("sec", None),
            P("sec"),
            P("sec", None),
            P(None, "sec", None),
        ),
        check_vma=False,
    )
```

```python
import jax
import jax.numpy as jnp
import numpy as np
from jax import lax
from jax.experimental import pallas as pl
from jax.experimental.pallas import tpu as pltpu
from jax.sharding import PartitionSpec as P

HEAD_DIM = 64
HEADS = 16
LANES = 128
KEY_CHUNK = 512
VMEM_LIMIT = 48 * 1024 * 1024
BF = jnp.bfloat16
F32 = jnp.float32

NN = ((1,), (0,))
NT = ((1,), (1,))
TN = ((0,), (0,))

MICROS = {
    "embed_qkv": 9.6,
    "cotangent_grad": 6.1,
    "attention_fwd": 9.2,
    "mlp": 17.0,
    "trunk_part": 4.0,
    "norm_two_back": 4.9,
    "attention_bwd": 13.3,
    "norm_one_grad": 11.7,
    "trunk_head": 7.0,
    "embed_back": 9.0,
    "mlp_weight_grads": 11.5,
    "attention_weight_grads": 9.0,
    "pick_team": 3.4,
    "pick_member": 2.5,
    "mlp_grads_out": 4.7,
    "attention_grads_out": 3.5,
    "edge_grads_out": 2.8,
}

TEAM, ME, GRP, VALID = range(4)


def dot(a, b, dims):
    return lax.dot_general(a, b, (dims, ((), ())), preferred_element_type=F32)


def swap(x, axis, bit):
    n = lax.axis_size(axis)
    return lax.ppermute(x, axis, [(i, i ^ bit) for i in range(n)])


def kernel(body, name, scalars, grid, ins, outs, scratch=(), aliases=None):
    micros = MICROS[name]
    scalars, chain = scalars
    values = lax.optimization_barrier((scalars, *chain))[0] if chain else scalars
    def spec(block, index):
        if block is None:
            return pl.BlockSpec(memory_space=pl.ANY)
        return pl.BlockSpec(block, index)

    results = pl.pallas_call(
        body,
        grid_spec=pltpu.PrefetchScalarGridSpec(
            num_scalar_prefetch=1,
            grid=grid,
            in_specs=[spec(block, index) for _, block, index in ins],
            out_specs=[spec(block, index) for _, _, block, index in outs],
            scratch_shapes=list(scratch),
        ),
        out_shape=[jax.ShapeDtypeStruct(shape, kind) for shape, kind, _, _ in outs],
        input_output_aliases=aliases or {},
        compiler_params=pltpu.CompilerParams(vmem_limit_bytes=VMEM_LIMIT),
        cost_estimate=pl.CostEstimate(
            flops=int(micros * 1.15e9), transcendentals=0, bytes_accessed=int(micros * 3.6e6)
        ),
        name=name,
    )(values, *[array for array, _, _ in ins])
    chain[:] = [results[-1]]
    return results


def hold(scalars, *values):
    scalars[1].extend(values)


def after(values, *others):
    return list(lax.optimization_barrier((*values, *others))[: len(values)])


def whole(array):
    rank = len(array.shape)
    return (array, array.shape, lambda *_: (0,) * rank)


def whole_out(shape, kind):
    rank = len(shape)
    return (shape, kind, shape, lambda *_: (0,) * rank)


class Sizes:
    def __init__(self, fields, w_qkv, w_up):
        self.teams, self.lat, self.cols, self.chan = fields.shape
        self.sectors = lax.axis_size("sec")
        self.members = self.sectors // self.teams
        self.group = lax.axis_size("grp")
        self.d = w_qkv.shape[0]
        self.ff = w_up.shape[1]
        self.sec_tokens = self.lat * self.cols
        self.tokens = self.sectors * self.sec_tokens
        self.heads = HEADS // self.members
        self.width = self.heads * HEAD_DIM
        self.db = self.d // self.sectors
        self.fb = self.ff // self.sectors
        self.dn = self.teams * self.db
        self.fn = self.teams * self.fb
        self.own = self.tokens // self.members
        self.half = self.tokens // 2


def line_up(s, scalars, pieces, canon):
    for j, piece in enumerate(pieces):
        for k in range(s.teams):
            at = (scalars[TEAM] ^ k) * s.members + (scalars[ME] ^ j)
            canon[at] = piece[k]


def beside(s, canon, sector):
    mid = canon[sector].astype(F32)
    before = canon[lax.rem(sector + s.sectors - 1, s.sectors)].astype(F32)
    after = canon[lax.rem(sector + 1, s.sectors)].astype(F32)
    col = lax.rem(lax.broadcasted_iota(jnp.int32, mid.shape, 0), s.cols)
    rows = s.sec_tokens
    west = jnp.where(col == 0, pltpu.roll(before, rows - (s.cols - 1), 0), pltpu.roll(mid, 1, 0))
    east = jnp.where(col == s.cols - 1, pltpu.roll(after, s.cols - 1, 0), pltpu.roll(mid, rows - 1, 0))
    return west, mid, east


def row_stats(rows):
    mean = jnp.mean(rows, axis=-1, keepdims=True)
    center = rows - mean
    return mean, lax.rsqrt(jnp.mean(center * center, axis=-1, keepdims=True) + 1e-05)


def normed_rows(rows):
    mean, rstd = row_stats(rows)
    return (rows - mean) * rstd, rstd


def embed_qkv(s, scalars, pieces, w_embed, gain, w_qkv):
    rows = s.half
    per = rows // s.sec_tokens
    chunk = s.sec_tokens

    def body(sc, *refs):
        parts = refs[: s.members]
        we, g, wq, wk, wv = refs[s.members : s.members + 5]
        cat_ref, hid_ref, norm_ref, qkv_ref, stat_ref, canon = refs[s.members + 5 :]
        i = pl.program_id(0)

        @pl.when(i == 0)
        def _():
            line_up(s, sc, parts, canon)

        for p in range(per):
            at = slice(p * chunk, (p + 1) * chunk)
            west, mid, east = beside(s, canon, i * per + p)
            cat_ref[at, :] = jnp.concatenate([west, mid, east], axis=1).astype(BF)
        hid_ref[...] = dot(cat_ref[...], we[...], NN)
        lane = lax.broadcasted_iota(jnp.int32, (chunk, LANES), 1)
        for p in range(per):
            at = slice(p * chunk, (p + 1) * chunk)
            value = hid_ref[at, :]
            mean, rstd = row_stats(value)
            norm_ref[at, :] = ((value - mean) * rstd * g[...]).astype(BF)
            stat_ref[at, :] = jnp.where(lane == 0, mean, rstd)
        for k, w in enumerate((wq, wk, wv)):
            qkv_ref[:, k * s.width : (k + 1) * s.width] = dot(norm_ref[...], w[...], NN).astype(BF)

    def third(k):
        return (w_qkv, (s.d, s.width), lambda i, sc: (0, k * s.members + sc[ME]))

    row = lambda i, sc: (i, 0)
    return kernel(
        body,
        "embed_qkv",
        scalars,
        (s.tokens // rows,),
        [whole(p) for p in pieces] + [whole(w_embed), whole(gain), third(0), third(1), third(2)],
        [
            ((s.tokens, 3 * s.chan), BF, (rows, 3 * s.chan), row),
            ((s.tokens, s.d), F32, (rows, s.d), row),
            ((s.tokens, s.d), BF, (rows, s.d), row),
            ((s.tokens, 3 * s.width), BF, (rows, 3 * s.width), row),
            ((s.tokens, LANES), F32, (rows, LANES), row),
        ],
        [pltpu.VMEM((s.sectors, s.sec_tokens, s.chan), BF)],
    )


def cotangent_grad(s, scalars, pieces, w_head):
    rows = s.half
    per = rows // s.sec_tokens

    def body(sc, *refs):
        parts = refs[: s.members]
        wh, cat_ref, grad_ref, canon = refs[s.members :]
        i = pl.program_id(0)

        @pl.when(i == 0)
        def _():
            line_up(s, sc, parts, canon)

        for p in range(per):
            at = slice(p * s.sec_tokens, (p + 1) * s.sec_tokens)
            west, mid, east = beside(s, canon, i * per + p)
            cat_ref[at, :] = jnp.concatenate([east, mid, west], axis=1).astype(BF)
        grad_ref[...] = dot(cat_ref[...], wh[...], NN).astype(BF)

    row = lambda i, sc: (i, 0)
    return kernel(
        body,
        "cotangent_grad",
        scalars,
        (s.tokens // rows,),
        [whole(p) for p in pieces] + [whole(w_head)],
        [
            ((s.tokens, 3 * s.chan), BF, (rows, 3 * s.chan), row),
            ((s.tokens, s.d), BF, (rows, s.d), row),
        ],
        [pltpu.VMEM((s.sectors, s.sec_tokens, s.chan), BF)],
    )


def side_of(s, sc, far):
    own = sc[ME] // (s.members // 2)
    return own ^ 1 if far else own


def lanes_of(value, side):
    lane = lax.broadcasted_iota(jnp.int32, value.shape, 1)
    return jnp.where(lane // HEAD_DIM == side, value, jnp.zeros_like(value))


def attention_fwd(s, scalars, qkv, far):
    rows = s.own
    steps = s.half // rows
    chunk = KEY_CHUNK

    def body(sc, q_ref, kv_ref, att_ref, weight_ref, inv_ref, bias, values, buf_a, buf_b, top_a, top_b, outs, invs):
        @pl.when(pl.program_id(0) == 0)
        def _():
            key = lax.broadcasted_iota(jnp.int32, (s.tokens, LANES), 0)
            bias[...] = jnp.where(lax.rem(key, s.sec_tokens) // s.cols < sc[VALID], 0.0, -1e30)
            values[...] = jnp.transpose(kv_ref[:, 2 * s.width :].astype(F32)).astype(BF)
            invs[...] = jnp.zeros_like(invs)

        def score(p, side, buf, tops):
            at = pl.ds(pl.multiple_of(p * LANES, LANES), LANES)
            kat = pl.ds(pl.multiple_of(s.width + p * LANES, LANES), LANES)
            query = lanes_of(q_ref[:, at] * jnp.asarray(0.125, BF), side)
            top = None
            for c in range(0, s.tokens, chunk):
                rows_at = slice(c, c + chunk)
                wide = jnp.concatenate([bias[rows_at, :]] * (rows // LANES), axis=1)
                scores = dot(kv_ref[rows_at, kat], query, NT) + wide
                buf[rows_at, :] = scores
                peak = jnp.max(scores, axis=0, keepdims=True)
                top = peak if top is None else jnp.maximum(top, peak)
            tops[...] = jnp.broadcast_to(top, tops.shape)

        def weigh(p, side, buf, tops):
            h = 2 * p + side
            heads_at = pl.ds(pl.multiple_of(h * HEAD_DIM, HEAD_DIM), HEAD_DIM)
            top = tops[0:1, :]
            total = None
            out = None
            for c in range(0, s.tokens, chunk):
                at = slice(c, c + chunk)
                weights = jnp.exp(buf[at, :] - top)
                part = jnp.sum(weights, axis=0, keepdims=True)
                low = weights.astype(BF)
                weight_ref[h, 0, at, :] = low
                more = dot(values[heads_at, at], low, NN)
                total = part if total is None else total + part
                out = more if out is None else out + more
            inv = 1.0 / total
            invs[pl.ds(pl.multiple_of(h * 8, 8), 8), :] = jnp.broadcast_to(inv, (8, rows))
            outs[heads_at, :] = out * inv

        score(0, 0, buf_a, top_a)

        def pair_step(p, carry):
            weigh(p, 0, buf_a, top_a)
            score(p, 1, buf_b, top_b)

            @pl.when(p >= 0)
            def _():
                weigh(p, 1, buf_b, top_b)
                score(jnp.minimum(p + 1, s.heads // 2 - 1), 0, buf_a, top_a)

            return carry

        lax.fori_loop(0, s.heads // 2, pair_step, 0)
        att_ref[...] = jnp.transpose(outs[...]).astype(BF)
        inv_ref[...] = jnp.transpose(invs[...])

    row = lambda i, sc: (i, 0)
    return kernel(
        body,
        "attention_fwd",
        scalars,
        (steps,),
        [
            (qkv, (rows, 3 * s.width), lambda i, sc: (side_of(s, sc, far) * steps + i, 0)),
            whole(qkv),
        ],
        [
            ((s.half, s.width), BF, (rows, s.width), row),
            ((s.heads, steps, s.tokens, rows), BF, (s.heads, 1, s.tokens, rows), lambda i, sc: (0, i, 0, 0)),
            ((s.half, LANES), F32, (rows, LANES), row),
        ],
        [
            pltpu.VMEM((s.tokens, LANES), F32),
            pltpu.VMEM((s.width, s.tokens), BF),
            pltpu.VMEM((s.tokens, rows), F32),
            pltpu.VMEM((s.tokens, rows), F32),
            pltpu.VMEM((8, rows), F32),
            pltpu.VMEM((8, rows), F32),
            pltpu.VMEM((s.width, rows), F32),
            pltpu.VMEM((LANES, rows), F32),
        ],
    )


def mlp(s, scalars, att, hidden0, grad_mlp, w_out, gain, w_up, b_up, w_down, far):
    chunk = 64
    rows = s.half
    count = len(att)

    def body(sc, *refs):
        parts = refs[:count]
        h0, gm, g, bias, wo_hbm, wu_hbm, wd_hbm = refs[count : count + 7]
        outs = refs[count + 7 :]
        att_ref, n2_ref, act_ref, gpre_ref, gkeep, gsend, gsum_ref, hown, bsum, h1_ref = outs[:10]
        wo, wu, wd, pre, gact, means, rstds, sem = outs[10:]
        me = sc[ME]

        copies = [pltpu.make_async_copy(wo_hbm, wo, sem.at[0])]
        for k in range(s.teams):
            at = pl.multiple_of((k * s.members + me) * s.fb, s.fb)
            copies.append(
                pltpu.make_async_copy(
                    wu_hbm.at[:, pl.ds(at, s.fb)], wu.at[:, pl.ds(k * s.fb, s.fb)], sem.at[1 + k]
                )
            )
        for k in range(s.teams):
            at = pl.multiple_of((k * s.members + me) * s.fb, s.fb)
            copies.append(
                pltpu.make_async_copy(
                    wd_hbm.at[pl.ds(at, s.fb), :],
                    wd.at[pl.ds(k * s.fb, s.fb), :],
                    sem.at[1 + s.teams + k],
                )
            )
        for copy in copies:
            copy.start()
        for j in range(count):
            at = pl.multiple_of((me ^ j) * s.width, s.width)
            att_ref[:, pl.ds(at, s.width)] = parts[j][...]
        copies[0].wait()
        span = 512

        def by_columns(size, one):
            def step(n, carry):
                one(pl.ds(pl.multiple_of(n * span, span), span))
                return carry

            lax.fori_loop(0, size // span, step, 0)

        def attention_out(cols):
            h1_ref[:, cols] = h0[:, cols] + dot(att_ref[...], wo[:, cols], NN)

        by_columns(s.d, attention_out)

        def norm_chunk(c, carry):
            at = pl.ds(pl.multiple_of(c * chunk, chunk), chunk)
            value = h1_ref[at, :]
            mean, rstd = row_stats(value)
            n2_ref[at, :] = ((value - mean) * rstd * g[...]).astype(BF)
            means[at, :] = jnp.broadcast_to(mean, (chunk, LANES))
            rstds[at, :] = jnp.broadcast_to(rstd, (chunk, LANES))
            return carry

        lax.fori_loop(0, rows // chunk, norm_chunk, 0)
        for k in range(s.teams):
            at = pl.multiple_of((k * s.members + me) * s.db, s.db)
            hown[:, k * s.db : (k + 1) * s.db] = h1_ref[:, pl.ds(at, s.db)]
        for copy in copies[1 : 1 + s.teams]:
            copy.wait()

        def up_out(cols):
            pre[:, cols] = dot(n2_ref[...], wu[:, cols], NN)

        by_columns(s.fn, up_out)
        for copy in copies[1 + s.teams :]:
            copy.wait()

        def down_back(cols):
            gact[:, cols] = dot(gm[...], wd[cols, :], NT)

        by_columns(s.fn, down_back)

        def gelu_chunk(c, total):
            at = pl.ds(pl.multiple_of(c * chunk, chunk), chunk)
            u = pre[at, :] + bias[...]
            cdf = 0.5 * (1.0 + lax.erf(u * np.float32(2**-0.5)))
            act_ref[at, :] = (u * cdf).astype(BF)
            slope = cdf + u * jnp.exp(-0.5 * u * u) * np.float32((2 * np.pi) ** -0.5)
            low = (gact[at, :] * slope).astype(BF)
            gpre_ref[at, :] = low
            return total + jnp.sum(low.astype(F32), axis=0, keepdims=True)

        bsum[...] = lax.fori_loop(0, rows // chunk, gelu_chunk, jnp.zeros((1, s.fn), F32))

        def up_back(cols):
            pre[:, cols] = dot(gpre_ref[...], wu[cols, :], NT)

        by_columns(s.d, up_back)

        def gain_chunk(c, total):
            at = pl.ds(pl.multiple_of(c * chunk, chunk), chunk)
            mean, rstd = means[at, :], rstds[at, :]
            sums = []
            for n in range(s.d // LANES):
                cols = slice(n * LANES, (n + 1) * LANES)
                xhat = (h1_ref[at, cols] - mean) * rstd
                sums.append(jnp.sum(pre[at, cols] * xhat, axis=0, keepdims=True))
            return total + jnp.concatenate(sums, axis=1)

        gsum = lax.fori_loop(0, rows // chunk, gain_chunk, jnp.zeros((1, s.d), F32))
        mine = lax.rem(me, 2)
        keep_at = pl.ds(pl.multiple_of(mine * s.own, s.own), s.own)
        send_at = pl.ds(pl.multiple_of((1 - mine) * s.own, s.own), s.own)
        gkeep[...] = pre[keep_at, :].astype(BF)
        gsend[...] = pre[send_at, :].astype(BF)
        gsum_ref[...] = gsum

    index = lambda i, sc: (side_of(s, sc, far), 0)
    bias_own = jnp.concatenate(
        [
            lax.dynamic_slice_in_dim(b_up, (k * s.members + scalars[0][ME]) * s.fb, s.fb, 0)
            for k in range(s.teams)
        ]
    ).astype(F32)[None]
    return kernel(
        body,
        "mlp",
        scalars,
        (1,),
        [whole(a) for a in att]
        + [
            (hidden0, (rows, s.d), index),
            (grad_mlp, (rows, s.d), index),
            whole(gain),
            whole(bias_own),
            (w_out, None, None),
            (w_up, None, None),
            (w_down, None, None),
        ],
        [
            whole_out((rows, s.d), BF),
            whole_out((rows, s.d), BF),
            whole_out((rows, s.fn), BF),
            whole_out((rows, s.fn), BF),
            whole_out((s.own, s.d), BF),
            whole_out((s.own, s.d), BF),
            whole_out((1, s.d), F32),
            whole_out((rows, s.dn), F32),
            whole_out((1, s.fn), F32),
            whole_out((rows, s.d), F32),
        ],
        [
            pltpu.VMEM((s.d, s.d), BF),
            pltpu.VMEM((s.d, s.fn), BF),
            pltpu.VMEM((s.fn, s.d), BF),
            pltpu.VMEM((rows, s.fn), F32),
            pltpu.VMEM((rows, s.fn), F32),
            pltpu.VMEM((rows, LANES), F32),
            pltpu.VMEM((rows, LANES), F32),
            pltpu.SemaphoreType.DMA((1 + 2 * s.teams,)),
        ],
    )


def trunk_part(s, scalars, parts, w_down):
    extra = 16
    rows = s.half

    def body(sc, act0, gs0, act1, gs1, *refs):
        downs, (keep, send, out, both, sums) = refs[: s.teams], refs[s.teams :]
        both[0], both[1] = act0[...], act1[...]
        sums[0], sums[1] = gs0[...], gs1[...]

        def one_half(half, carry):
            total = dot(both[half, :, : s.fb], downs[0][...], NN)
            for k in range(1, s.teams):
                total += dot(both[half, :, k * s.fb : (k + 1) * s.fb], downs[k][...], NN)
            out[:rows] = total
            out[rows:] = jnp.broadcast_to(sums[half], (extra, s.d))
            for odd, ref in ((0, keep), (1, send)):
                for n in range(s.members // 2):
                    m = sc[ME] ^ (2 * n + odd)
                    for k in range(s.teams):
                        cols = pl.ds(pl.multiple_of((k * s.members + m) * s.db, s.db), s.db)
                        ref[n, half, :, k * s.db : (k + 1) * s.db] = out[:, cols].astype(BF)
            return carry

        lax.fori_loop(0, 2, one_half, 0)

    pair = (s.members // 2, 2, rows + extra, s.dn)
    return kernel(
        body,
        "trunk_part",
        scalars,
        (1,),
        [whole(x) for part in parts for x in part]
        + [
            (w_down, (s.fb, s.d), lambda i, sc, k=k: (k * s.members + sc[ME], 0))
            for k in range(s.teams)
        ],
        [whole_out(pair, BF), whole_out(pair, BF)],
        [
            pltpu.VMEM((rows + extra, s.d), F32),
            pltpu.VMEM((2, rows, s.fn), BF),
            pltpu.VMEM((2, 1, s.d), F32),
        ],
    )


def norm_two_back(s, scalars, parts, hidden1, grad_mlp, gain):
    chunk = 64
    count = len(parts)

    def body(sc, *refs):
        h1, gm, g, out_ref = refs[count:]

        def rows_chunk(c, carry):
            at = pl.ds(pl.multiple_of(c * chunk, chunk), chunk)
            xhat, rstd = normed_rows(h1[at, :])
            grad = refs[0][at, :].astype(F32)
            for ref in refs[1:count]:
                grad += ref[at, :].astype(F32)
            grad *= g[...]
            back = grad - jnp.mean(grad, axis=-1, keepdims=True)
            back -= xhat * jnp.mean(grad * xhat, axis=-1, keepdims=True)
            out_ref[at, :] = (gm[at, :].astype(F32) + rstd * back).astype(BF)
            return carry

        lax.fori_loop(0, s.own // chunk, rows_chunk, 0)

    return kernel(
        body,
        "norm_two_back",
        scalars,
        (1,),
        [whole(p) for p in parts]
        + [
            (hidden1, (s.own, s.d), lambda i, sc: (lax.rem(sc[ME], 2), 0)),
            (grad_mlp, (s.own, s.d), lambda i, sc: (sc[ME], 0)),
            whole(gain),
        ],
        [whole_out((s.own, s.d), BF)],
    )[0]


def attention_bwd(s, scalars, qkv, saved, grads, w_out, far, before=None):
    base = s.members // 2 if far else 0
    rows = s.own
    last = before is not None
    attended, weights, inverse = saved

    def body(sc, *refs):
        q_ref, kv_ref, att_ref, weight_ref, inv_ref, first, second, wo = refs[:8]
        if last:
            old_ref = refs[10]
            dq_ref, own_ref, out_ref, gh, acc, keys = refs[11:]
        else:
            dq_ref, own_ref, out_ref, gh, acc, keys = refs[8:]
        i = pl.program_id(0)

        @pl.when(i == 0)
        def _():
            if last:
                acc[...] = old_ref[...]
            else:
                acc[...] = jnp.zeros_like(acc)
            keys[...] = jnp.transpose(kv_ref[:, s.width : 2 * s.width].astype(F32)).astype(BF)

        for step, piece in enumerate((first, second)):

            @pl.when(i == step)
            def _():
                gh[...] = dot(piece[...], wo[...], NT)
                for k in range(s.teams):
                    at = pl.multiple_of((k * s.members + sc[ME]) * s.db, s.db)
                    own_ref[:, k * s.db : (k + 1) * s.db] = piece[:, pl.ds(at, s.db)]

        def pair_step(p, carry):
            pair = pl.ds(pl.multiple_of(p * LANES, LANES), LANES)
            value_at = pl.ds(pl.multiple_of(2 * s.width + p * LANES, LANES), LANES)
            dv_at = pl.ds(pl.multiple_of(s.width + p * LANES, LANES), LANES)
            inv = inv_ref[...]
            wide = lax.broadcasted_iota(jnp.int32, inv.shape, 1)
            outs = []
            means = jnp.zeros((rows, LANES), F32)
            for side in range(2):
                h = 2 * p + side
                one = jnp.sum(jnp.where(wide == 8 * h, inv, 0.0), axis=-1, keepdims=True)
                out = (lanes_of(gh[:, pair], side) * one).astype(BF)
                mean = jnp.sum(out.astype(F32) * att_ref[:, pair].astype(F32), axis=-1, keepdims=True)
                means = jnp.where(wide == side, mean, means)
                outs.append(out)
            means = jnp.transpose(means)
            turned = [None, None]
            units = [(c, side) for c in range(0, s.tokens, KEY_CHUNK) for side in range(2)]

            def first_dot(unit):
                c, side = unit
                return dot(kv_ref[c : c + KEY_CHUNK, value_at], outs[side], NT)

            ahead = first_dot(units[0])
            for n, (c, side) in enumerate(units):
                at = slice(c, c + KEY_CHUNK)
                h = 2 * p + side
                gprob = ahead - means[side : side + 1, :]
                if n + 1 < len(units):
                    ahead = first_dot(units[n + 1])
                weight = weight_ref[h, 0, at, :]
                gscore = (weight.astype(F32) * gprob).astype(BF)
                key_rows = pl.ds(pl.multiple_of(h * HEAD_DIM, HEAD_DIM), HEAD_DIM)
                dq = dot(keys[key_rows, at], gscore, NN)
                turned[side] = dq if turned[side] is None else turned[side] + dq
                one = dot(gscore, lanes_of(q_ref[:, pair], side), NN)
                two = dot(weight, outs[side], NN)
                if side == 0:
                    dk, dv = one, two
                else:
                    acc[at, pair] += dk + one
                    acc[at, dv_at] += dv + two
            dq_ref[:, pair] = (jnp.transpose(jnp.concatenate(turned, axis=0)) * 0.125).astype(BF)
            return carry

        lax.fori_loop(0, s.heads // 2, pair_step, 0)

        @pl.when(i == pl.num_programs(0) - 1)
        def _():
            if last:
                out_ref[:, : s.width] = (acc[:, : s.width] * 0.125).astype(BF)
                out_ref[:, s.width :] = acc[:, s.width :].astype(BF)
            else:
                out_ref[...] = acc[...]

    member = lambda i, sc: (sc[ME] ^ (base + i), 0)
    side = lambda i, sc: lax.rem(sc[ME] ^ i, s.members // 2)
    ins = [
        (qkv, (rows, 3 * s.width), member),
        whole(qkv),
        (attended, (rows, s.width), lambda i, sc: (side(i, sc), 0)),
        (weights, (s.heads, 1, s.tokens, rows), lambda i, sc: (0, side(i, sc), 0, 0)),
        (inverse, (rows, LANES), lambda i, sc: (side(i, sc), 0)),
        whole(grads[0]),
        whole(grads[1]),
        (w_out, (s.width, s.d), lambda i, sc: (sc[ME], 0)),
    ]
    aliases = None
    if last:
        ins += [(before[0], None, None), (before[1], None, None), whole(before[2])]
        aliases = {9: 0, 10: 1}
    return kernel(
        body,
        "attention_bwd",
        scalars,
        (2,),
        ins,
        [
            ((s.tokens, s.width), BF, (rows, s.width), member),
            ((s.tokens, s.dn), BF, (rows, s.dn), member),
            whole_out((s.tokens, 2 * s.width), BF if last else F32),
        ],
        [
            pltpu.VMEM((rows, s.width), F32),
            pltpu.VMEM((s.tokens, 2 * s.width), F32),
            pltpu.VMEM((s.width, s.tokens), BF),
        ],
        aliases,
    )


def norm_one_grad(s, scalars, qkv, dq, dkv, w_qkv, gain):
    rows = s.half

    def body(sc, qkv_ref, dq_ref, dkv_ref, wq, wk, wv, g, keep, send, grad, stat, lines):
        me = sc[ME]
        total = dot(dq_ref[...], wq[...], NT)
        total += dot(dkv_ref[:, : s.width], wk[...], NT)
        grad[...] = total + dot(dkv_ref[:, s.width :], wv[...], NT)
        gain8 = jnp.broadcast_to(g[...], (8, s.d)).astype(BF)
        parts = ((dq_ref[...], wq), (dkv_ref[:, : s.width], wk), (dkv_ref[:, s.width :], wv))
        one = jnp.zeros((rows, s.width), F32)
        two = jnp.zeros((rows, s.width), F32)
        for k, (value, w) in enumerate(parts):
            value = value.astype(F32)
            one += value * dot(gain8, w[...], NN)[0:1, :]
            two += value * qkv_ref[:, k * s.width : (k + 1) * s.width].astype(F32)
        one = jnp.sum(one, axis=-1, keepdims=True)
        two = jnp.sum(two, axis=-1, keepdims=True)
        lane = lax.broadcasted_iota(jnp.int32, (rows, LANES), 1)
        stat[...] = jnp.where(lane == 0, one, two)
        turned = jnp.transpose(stat[...])
        count = s.tokens // s.dn
        for kind in range(2):
            for n in range(rows // s.dn):
                at = kind * count + n
                step = rows // s.dn
                line = turned[kind : kind + 1, n * s.dn : (n + 1) * s.dn].astype(BF).astype(F32)
                for i in range(s.tokens // rows):

                    @pl.when(pl.program_id(0) == i)
                    def _():
                        lines[at + i * step : at + i * step + 1, :] = line
        at = pl.ds(pl.multiple_of(pl.program_id(0) * rows, rows), rows)
        for odd, ref in ((0, keep), (1, send)):
            for n in range(s.members // 2):
                m = me ^ (2 * n + odd)
                for k in range(s.teams):
                    cols = pl.ds(pl.multiple_of((k * s.members + m) * s.db, s.db), s.db)
                    ref[n, at, k * s.db : (k + 1) * s.db] = grad[:, cols].astype(BF)
                ref[n, s.tokens :, :] = lines[...].astype(BF)

    def third(k):
        return (w_qkv, (s.d, s.width), lambda i, sc: (0, k * s.members + sc[ME]))

    row = lambda i, sc: (i, 0)
    pair = (s.members // 2, s.tokens + 16, s.dn)
    return kernel(
        body,
        "norm_one_grad",
        scalars,
        (s.tokens // rows,),
        [
            (qkv, (rows, 3 * s.width), row),
            (dq, (rows, s.width), row),
            (dkv, (rows, 2 * s.width), row),
            third(0),
            third(1),
            third(2),
            whole(gain),
        ],
        [
            whole_out(pair, BF),
            whole_out(pair, BF),
        ],
        [
            pltpu.VMEM((rows, s.d), F32),
            pltpu.VMEM((rows, LANES), F32),
            pltpu.VMEM((16, s.dn), F32),
        ],
    )


def shift_all(s, parts, out_ref):
    west_ref, mid_ref, east_ref = parts
    rows = s.sec_tokens
    col = lax.rem(lax.broadcasted_iota(jnp.int32, (rows, s.chan), 0), s.cols)

    def one(sector, carry):
        before = west_ref[lax.rem(sector + s.sectors - 1, s.sectors)]
        after = east_ref[lax.rem(sector + 1, s.sectors)]
        west = jnp.where(
            col == 0, pltpu.roll(before, rows - (s.cols - 1), 0), pltpu.roll(west_ref[sector], 1, 0)
        )
        east = jnp.where(
            col == s.cols - 1,
            pltpu.roll(after, s.cols - 1, 0),
            pltpu.roll(east_ref[sector], rows - 1, 0),
        )
        out_ref[sector] = (west + mid_ref[sector] + east).astype(BF)
        return carry

    lax.fori_loop(0, s.sectors, one, 0)


def group_blocks(s, sc, color):
    half = s.group // 2
    for side in range(2):
        for slot in range(half):
            j = 2 * slot + side if color == 0 else side * half + slot
            yield side, slot, sc[GRP] ^ j


def trunk_head(s, scalars, hown, terms, w_head, cot_cat):
    rows = s.half

    def body(sc, near, far, a, b, c, wh0, wh1, cat, home_ref, grad_ref, gain_ref, h2, y0, y1, y2):
        own = sc[ME] // (s.members // 2)
        gains = []
        for half, h1 in enumerate((near, far)):
            side = own ^ half
            total = three_terms(a[0, half, :rows, :], b[0, half, :rows, :], c[0, 1 - half, :rows, :])
            h2[pl.ds(pl.multiple_of(side * rows, rows), rows), :] = (h1[...] + total).astype(BF)
            at = slice(rows, rows + 8)
            gains.append(three_terms(a[0, half, at, :], b[0, half, at, :], c[0, 1 - half, at, :]))
        gain_ref[...] = gains[0] + gains[1]
        for j, ref in enumerate((y0, y1, y2)):
            weight = jnp.concatenate([wh0[j], wh1[j]], axis=1)
            ref[...] = dot(h2[...], weight, NT).reshape(s.sectors, s.sec_tokens, s.chan)
        shift_all(s, (y0, y1, y2), home_ref)
        grad_ref[...] = dot(h2[...], cat[...], TN)

    def part(k):
        return (w_head, (3, s.chan, s.db), lambda i, sc: (0, 0, k * s.members + sc[ME]))

    return kernel(
        body,
        "trunk_head",
        scalars,
        (1,),
        [whole(x) for x in hown]
        + [first(x) for x in terms]
        + [part(0), part(1), whole(cot_cat)],
        [
            whole_out((s.sectors, s.sec_tokens, s.chan), BF),
            whole_out((s.dn, 3 * s.chan), F32),
            whole_out((8, s.dn), F32),
        ],
        [pltpu.VMEM((s.tokens, s.dn), BF)]
        + [pltpu.VMEM((s.sectors, s.sec_tokens, s.chan), F32) for _ in range(3)],
    )


def embed_back(s, scalars, g1, own, stats, hidden0, gain, w_embed, in_cat, head_home, head_part, gain2, bias):
    wide = 3 * s.chan
    span = s.dn

    def body(sc, *refs):
        a, b, c, own_ref, st_ref, h0, h1, g, we0, we1, cat, home, head, gain2_ref, bias_ref = refs[:15]
        keep, send = refs[15:17]
        edges = refs[17 : 17 + s.group]
        grad, stat, y0, y1, y2, ours, part, smalls = refs[17 + s.group :]
        lines = slice(s.tokens, s.tokens + 16)
        total = three_terms(a[0, lines, :], b[0, lines, :], c[0, lines, :]) * np.float32(1.0 / s.d)
        for n in range(s.tokens // span):
            pair = [total[n : n + 1, :], total[s.tokens // span + n : s.tokens // span + n + 1, :]]
            pair = jnp.concatenate(pair + [jnp.zeros((LANES - 2, span), F32)], axis=0)
            stat[n * span : (n + 1) * span, :] = jnp.transpose(pair)
        gain_own = jnp.concatenate(
            [
                g[:, pl.ds(pl.multiple_of((k * s.members + sc[ME]) * s.db, s.db), s.db)]
                for k in range(s.teams)
            ],
            axis=1,
        )
        chunk = s.sec_tokens

        def rows_chunk(i, acc):
            at = pl.ds(pl.multiple_of(i * chunk, chunk), chunk)
            mean, rstd = st_ref[at, 0:1], st_ref[at, 1:2]
            one, two = stat[at, 0:1], stat[at, 1:2]
            g1 = three_terms(a[0, at, :], b[0, at, :], c[0, at, :])
            x = (jnp.concatenate([h0[at, :], h1[at, :]], axis=1) - mean) * rstd
            back = g1 * gain_own - one - x * two
            grad[at, :] = (own_ref[at, :].astype(F32) + rstd * back).astype(BF)
            return acc + jnp.sum(g1 * x, axis=0, keepdims=True)

        gain1 = lax.fori_loop(0, s.tokens // chunk, rows_chunk, jnp.zeros((1, s.dn), F32))
        for j, ref in enumerate((y0, y1, y2)):
            weight = jnp.concatenate([we0[j], we1[j]], axis=1)
            ref[...] = dot(grad[...], weight, NT).reshape(s.sectors, s.sec_tokens, s.chan)
        shift_all(s, (y2, y1, y0), ours)
        for odd, ref in ((0, keep), (1, send)):
            for n in range(s.members // 2):
                for team in range(s.teams):
                    sector = team * s.members + (sc[ME] ^ (2 * n + odd))
                    ref[n, team, 0] = home[sector]
                    ref[n, team, 1] = ours[sector]
        part[:, :wide] = head[...]
        part[:, wide : 2 * wide] = dot(grad[...], cat[...], TN)
        size = s.db // s.group
        for k in range(s.teams):
            lines = [
                bias_ref[:, k * s.fb + n * LANES : k * s.fb + (n + 1) * LANES] for n in range(s.fb // LANES)
            ]
            lines += [gain1[:, k * s.db : (k + 1) * s.db], gain2_ref[0:1, k * s.db : (k + 1) * s.db]]
            lines += [jnp.zeros((size - len(lines), LANES), F32)]
            smalls[...] = jnp.concatenate(lines, axis=0).astype(BF)
            for j, ref in enumerate(edges):
                at = pl.ds(pl.multiple_of(k * s.db + (sc[GRP] ^ j) * size, size), size)
                ref[k, :, : 2 * wide] = part[at, :].astype(BF)
                ref[k, :, 2 * wide :] = smalls[...]

    def part_of(k):
        return (w_embed, (3, s.chan, s.db), lambda i, sc: (0, 0, k * s.members + sc[ME]))

    def own_of(k):
        return (hidden0, (s.tokens, s.db), lambda i, sc: (0, k * s.members + sc[ME]))

    goes = (s.members // 2, s.teams, 2, s.sec_tokens, s.chan)
    size = s.db // s.group
    block = (s.teams, size, 2 * wide + LANES)
    return kernel(
        body,
        "embed_back",
        scalars,
        (1,),
        [first(x) for x in g1]
        + [whole(own), whole(stats), own_of(0), own_of(1), whole(gain), part_of(0), part_of(1)]
        + [whole(in_cat), whole(head_home), whole(head_part), whole(gain2), whole(bias)],
        [whole_out(goes, BF), whole_out(goes, BF)] + [whole_out(block, BF)] * s.group,
        [pltpu.VMEM((s.tokens, s.dn), BF), pltpu.VMEM((s.tokens, LANES), F32)]
        + [pltpu.VMEM((s.sectors, s.sec_tokens, s.chan), F32) for _ in range(3)]
        + [pltpu.VMEM((s.sectors, s.sec_tokens, s.chan), BF)]
        + [pltpu.VMEM((s.dn, 2 * wide), F32), pltpu.VMEM((size, LANES), BF)],
    )


def mlp_weight_grads(s, scalars, near, far, grad_mlp):
    sub = s.fb // s.group

    def body(sc, an, pn, nn_ref, af, pf, nf, gn, gf, ka, sa, kb, sb, scr):
        color = pl.program_id(0)
        kind = pl.program_id(1)

        @pl.when(kind == 0)
        def _():
            scr[...] = (dot(an[...], gn[...], TN) + dot(af[...], gf[...], TN)).astype(BF)

        @pl.when(kind == 1)
        def _():
            scr[...] = (dot(pn[...], nn_ref[...], TN) + dot(pf[...], nf[...], TN)).astype(BF)

        for k, refs in enumerate(((ka, sa), (kb, sb))):

            @pl.when(color == k)
            def _():
                def lane_block(c, carry):
                    lanes = pl.ds(pl.multiple_of(c * LANES, LANES), LANES)
                    to = pl.ds(pl.multiple_of(c * sub, sub), sub)
                    for side, slot, q in group_blocks(s, sc, k):
                        rows = pl.ds(pl.multiple_of(q * sub, sub), sub)
                        refs[side][slot, 0, to, :] = scr[rows, lanes]
                    return carry

                lax.fori_loop(0, s.d // LANES, lane_block, 0)

    def out(color):
        shape = (s.group // 2, 2, s.d, LANES)
        block = (s.group // 2, 1, s.d, LANES)
        if color == 0:
            index = lambda k, kind, sc: (0, jnp.where(k == 0, kind, 1), 0, 0)
        else:
            index = lambda k, kind, sc: (0, jnp.where(k == 0, 0, kind), 0, 0)
        return (shape, BF, block, index)

    cols = lambda k, kind, sc: (0, k)
    ins = []
    for activ, grad_pre, normed in (near, far):
        ins += [
            (activ, (s.half, s.fb), cols),
            (grad_pre, (s.half, s.fb), cols),
            whole(normed),
        ]
    ins += [
        (grad_mlp, (s.half, s.d), lambda k, kind, sc: (side_of(s, sc, False), 0)),
        (grad_mlp, (s.half, s.d), lambda k, kind, sc: (side_of(s, sc, True), 0)),
    ]
    return kernel(
        body,
        "mlp_weight_grads",
        scalars,
        (s.teams, 2),
        ins,
        [out(0), out(0), out(1), out(1)],
        [pltpu.VMEM((s.fb, s.d), BF)],
    )


def attention_weight_grads(s, scalars, normed1, dq, dkv, att_near, att_far, own):
    def body(sc, n1, dq_ref, dkv_ref, an, af, own_near, own_far, ka, sa, kb, sb, scr):
        scr[: s.width] = dot(dq_ref[...], n1[...], TN).astype(BF)
        scr[s.width : 3 * s.width] = dot(dkv_ref[...], n1[...], TN).astype(BF)
        scr[3 * s.width :] = (dot(own_near[...], an[...], TN) + dot(own_far[...], af[...], TN)).astype(BF)

        def lane_block(c, carry):
            lanes = pl.ds(pl.multiple_of(c * LANES, LANES), LANES)
            for k, refs in enumerate(((ka, sa), (kb, sb))):
                for side, slot, q in group_blocks(s, sc, k):
                    rows = pl.ds(pl.multiple_of((k * s.group + q) * LANES, LANES), LANES)
                    refs[side][slot, lanes, :] = scr[rows, lanes]
            return carry

        lax.fori_loop(0, s.d // LANES, lane_block, 0)

    shape = (s.group // 2, s.d, LANES)
    return kernel(
        body,
        "attention_weight_grads",
        scalars,
        (1,),
        [
            whole(normed1),
            whole(dq),
            whole(dkv),
            whole(att_near),
            whole(att_far),
            (own, (s.half, s.dn), lambda i, sc: (side_of(s, sc, False), 0)),
            (own, (s.half, s.dn), lambda i, sc: (side_of(s, sc, True), 0)),
        ],
        [whole_out(shape, BF)] * 4,
        [pltpu.VMEM((3 * s.width + s.dn, s.d), BF)],
    )


def add_low(a, b):
    return (a.astype(F32) + b.astype(F32)).astype(BF)


def first(x):
    rank = len(x.shape)
    return (x, (1,) + tuple(x.shape[1:]), lambda *_: (0,) * rank)


def three_terms(keep, got, more):
    return keep.astype(F32) + got.astype(F32) + more.astype(F32)


def group_first(keep_a, send_a, keep_b, send_b):
    got_a = swap(send_a, "grp", 1)
    got_b = swap(send_b, "grp", 2)
    return (keep_a, got_a), (keep_b, got_b), (add_low(keep_a[1], got_a[1]), add_low(keep_b[1], got_b[1]))


def group_second(terms_a, terms_b, sends):
    more_a = swap(sends[0], "grp", 2)
    more_b = swap(sends[1], "grp", 1)
    return terms_a + (more_a[None],), terms_b + (more_b[None],)


def pick_team(s, scalars, terms_a, terms_b, kinds):
    half = s.d // 2

    def body(sc, *refs):
        a, b = refs[:3], refs[3:6]
        keep, send = refs[6:]
        team = sc[TEAM]

        def total(terms, k, rows):
            at = (0, k, rows) if kinds == 2 else (0, rows)
            return three_terms(*[ref[at] for ref in terms]).astype(BF)

        if kinds == 2:
            for side in range(2):

                @pl.when(team == side)
                def _():
                    same, other = (a, b) if side == 0 else (b, a)
                    keep[0] = total(same, 0, slice(None))
                    send[0] = total(other, 0, slice(None))

        mine = pl.ds(pl.multiple_of(team * half, half), half)
        theirs = pl.ds(pl.multiple_of((1 - team) * half, half), half)
        for color, terms in enumerate((a, b)):
            at = slice(color * half, (color + 1) * half)
            keep[kinds - 1, at] = total(terms, 1, mine)
            send[kinds - 1, at] = total(terms, 1, theirs)

    return kernel(
        body,
        "pick_team",
        scalars,
        (1,),
        [first(x) for x in terms_a + terms_b],
        [whole_out((kinds, s.d, LANES), BF)] * 2,
    )


def pick_member(s, scalars, keep, got):
    kinds = keep.shape[0]
    half = s.d // 2

    def body(sc, k_ref, g_ref, *refs):
        for j in range(s.members):
            m = sc[ME] ^ j
            for color in range(2):
                at = pl.ds(pl.multiple_of(color * half + m * s.db, s.db), s.db)
                value = k_ref[kinds - 1, at].astype(F32) + g_ref[kinds - 1, at].astype(F32)
                refs[j][color] = value.astype(BF)
        if kinds == 2:
            refs[s.members][...] = (k_ref[0].astype(F32) + g_ref[0].astype(F32)).astype(BF)

    outs = [whole_out((2, s.db, LANES), BF)] * s.members
    if kinds == 2:
        outs = outs + [whole_out((s.d, LANES), BF)]
    return kernel(body, "pick_member", scalars, (1,), [whole(keep), whole(got)], outs)


def all_of_group(x, x_first):
    near, far = (1, 2) if x_first else (2, 1)
    one = swap(x, "grp", near)
    two = swap(x, "grp", far)
    both = swap(one, "grp", far)
    return [x, one, two, both] if x_first else [x, two, one, both]


def cross(s, pieces):
    got = [pieces[0]] + [swap(pieces[j], "sec", j) for j in range(1, s.members)]
    return jnp.stack(got)


def mlp_grads_out(s, scalars, downs, ups):
    sub = s.fb // s.group

    def body(sc, *refs):
        d_refs, u_refs = refs[: s.group], refs[s.group : 2 * s.group]
        down, up = refs[2 * s.group :]
        for j in range(s.group):
            q = sc[GRP] ^ j
            rows = pl.ds(pl.multiple_of(q * sub, sub), sub)
            for c in range(s.d // LANES):
                down[rows, c * LANES : (c + 1) * LANES] = d_refs[j][c * sub : (c + 1) * sub, :].astype(F32)

            def member(jm, carry):
                m = sc[ME] ^ jm
                for color in range(s.teams):
                    at = ((color * s.members + m) * s.group + q) * LANES
                    up[:, pl.ds(pl.multiple_of(at, LANES), LANES)] = jnp.transpose(u_refs[j][jm, color].astype(F32))
                return carry

            lax.fori_loop(0, s.members, member, 0)

    return kernel(
        body,
        "mlp_grads_out",
        scalars,
        (1,),
        [whole(x) for x in downs + ups],
        [whole_out((s.fb, s.d), F32), whole_out((s.db, s.ff), F32)],
    )


def attention_grads_out(s, scalars, parts):
    def body(sc, *refs):
        u_refs = refs[: s.group]
        qkv, out = refs[s.group :]
        for j in range(s.group):
            q = sc[GRP] ^ j

            def member(jm, carry):
                m = sc[ME] ^ jm
                at = (q // 2) * s.d + m * s.width + lax.rem(q, 2) * LANES
                value = jnp.transpose(u_refs[j][jm, 0].astype(F32))
                qkv[:, pl.ds(pl.multiple_of(at, LANES), LANES)] = value
                other = jnp.transpose(u_refs[j][jm, 1].astype(F32))

                @pl.when(q < 2)
                def _():
                    at = 2 * s.d + m * s.width + q * LANES
                    qkv[:, pl.ds(pl.multiple_of(at, LANES), LANES)] = other

                @pl.when(q >= 2)
                def _():
                    at = ((q - 2) * s.members + m) * s.db
                    out[:, pl.ds(pl.multiple_of(at, LANES), LANES)] = other

                return carry

            lax.fori_loop(0, s.members, member, 0)

    return kernel(
        body,
        "attention_grads_out",
        scalars,
        (1,),
        [whole(x) for x in parts],
        [whole_out((s.db, 3 * s.d), F32), whole_out((s.db, s.d), F32)],
    )


def edge_grads_out(s, scalars, parts):
    wide = 3 * s.chan
    size = s.db // s.group

    def body(sc, *refs):
        ins = refs[: s.group]
        embed, head, small, scr = refs[s.group :]
        for j in range(s.group):
            at = pl.ds(pl.multiple_of((sc[GRP] ^ j) * size, size), size)
            scr[at, :] = ins[j][...].astype(F32)
        head[...] = jnp.transpose(scr[:, :wide])
        embed[...] = jnp.transpose(scr[:, wide : 2 * wide])
        small[...] = ins[0][:16, 2 * wide :].astype(F32)

    return kernel(
        body,
        "edge_grads_out",
        scalars,
        (1,),
        [whole(x) for x in parts],
        [
            whole_out((wide, s.db), F32),
            whole_out((wide, s.db), F32),
            whole_out((16, LANES), F32),
        ],
        [pltpu.VMEM((s.db, 2 * wide + LANES), F32)],
    )


def on_team(
    fields,
    valid_rows,
    w_embed,
    ln1_gain,
    w_qkv,
    w_out,
    ln2_gain,
    w_up,
    b_up,
    w_down,
    w_head,
    cotangent,
):
    s = Sizes(fields, w_qkv, w_up)
    place = lax.axis_index("sec")
    team, me = place // s.members, place % s.members
    core, chip = 1, 2
    first_team = team == 0
    valid = jnp.where(first_team, valid_rows[0], valid_rows[1])
    scalars = (jnp.stack([team, me, lax.axis_index("grp"), valid]).astype(jnp.int32), [])

    def gather_pair(x):
        flat = x.reshape(s.teams, s.sec_tokens, s.chan)
        mine = jnp.where(first_team, flat[0], flat[1])
        other = swap(jnp.where(first_team, flat[1], flat[0]), "sec", s.members)
        return jnp.stack([mine, other])

    def gather_sample(pair):
        across = swap(pair, "sec", chip)
        return [pair, swap(pair, "sec", core), across, swap(across, "sec", core)]

    def go_home(keep, got, far):
        mine = three_terms(keep[0], got[0], far)
        other = jnp.where(first_team, mine[1], mine[0]).astype(BF)
        return mine, swap(other, "sec", s.members)

    def at_home(mine, other):
        own = jnp.where(first_team, mine[0], mine[1])
        other = other.astype(F32)
        both = [jnp.where(first_team, own, other), jnp.where(first_team, other, own)]
        return [jnp.stack([x[kind] for x in both]).reshape(fields.shape) for kind in range(2)]

    def scatter_features(keep, send):
        got = swap(send, "sec", core)
        return keep, got, swap(add_low(keep[1:2], got[1:2]), "sec", chip)

    w_head_t = jnp.transpose(w_head, (0, 2, 1))
    fields_pair = gather_pair(fields)
    late1, late2, b_up = after([ln1_gain, ln2_gain, b_up], fields_pair)
    gain1 = late1.astype(F32)[None]
    gain2 = late2.astype(F32)[None]
    in_cat, hidden0, normed1, qkv, stats = embed_qkv(
        s, scalars, gather_sample(fields_pair), w_embed.reshape(3 * s.chan, s.d), gain1, w_qkv
    )
    att_near, *rest = attention_fwd(s, scalars, qkv, False)
    saved_near = (att_near, *rest)
    from_chip_far = swap(att_near, "sec", chip)
    att_far, *rest = attention_fwd(s, scalars, qkv, True)
    saved_far = (att_far, *rest)
    from_chip_near = swap(att_far, "sec", chip)
    hold(scalars, from_chip_far)
    cot_cat, grad_mlp = cotangent_grad(
        s, scalars, gather_sample(gather_pair(cotangent)), w_head_t.reshape(3 * s.chan, s.d)
    )
    att_pieces_far = [att_far, swap(att_far, "sec", core), from_chip_far, swap(from_chip_far, "sec", core)]
    att_pieces_near = [att_near, swap(att_near, "sec", core), from_chip_near, swap(from_chip_near, "sec", core)]

    def run_mlp(pieces, far):
        return mlp(s, scalars, pieces, hidden0, grad_mlp, w_out, gain2, w_up, b_up, w_down, far)

    attended_far, normed2_far, activ_far, pre_far, gkeep, gsend, gsum, hown_far, bias_far, _ = run_mlp(
        att_pieces_far, True
    )
    hold(scalars, from_chip_near)
    g2_chip = [swap(gkeep, "sec", chip), swap(gsend, "sec", chip + core)]
    attended_near, normed2_near, activ_near, pre_near, gkeep, gsend, gsum_near, hown_near, bias_near, hidden1 = run_mlp(
        att_pieces_near, False
    )
    bias_grad = bias_far + bias_near
    got = swap(gsend, "sec", core)
    pkeep, psend = trunk_part(s, scalars, ((activ_near, gsum_near), (activ_far, gsum)), w_down)
    b0 = norm_two_back(s, scalars, [gkeep, got, *g2_chip], hidden1, grad_mlp, gain2)
    b1 = swap(b0, "sec", core)
    b2 = swap(b0, "sec", chip)
    b3 = swap(b2, "sec", core)
    mlp_blocks = mlp_weight_grads(
        s, scalars, (activ_near, pre_near, normed2_near), (activ_far, pre_far, normed2_far), grad_mlp
    )
    hold(scalars, b2)
    mlp_a, mlp_b, mlp_sends = group_first(*mlp_blocks)
    before = attention_bwd(s, scalars, qkv, saved_near, (b0, b1), w_out, False)
    hold(scalars, b3, *mlp_sends)
    mlp_terms = group_second(mlp_a, mlp_b, mlp_sends)
    trunk_terms = scatter_features(pkeep, psend)
    dq, own, dkv = attention_bwd(s, scalars, qkv, saved_far, (b2, b3), w_out, True, before)
    hold(scalars, *[terms[2] for terms in mlp_terms])
    att_blocks = attention_weight_grads(s, scalars, normed1, dq, dkv, attended_near, attended_far, own)
    att_a, att_b, att_sends = group_first(*att_blocks)
    mlp_kept, send = pick_team(s, scalars, *mlp_terms, 2)
    mlp_swapped = swap(send, "sec", s.members)
    g1_keep, g1_send = norm_one_grad(s, scalars, qkv, dq, dkv, w_qkv, gain1)
    hold(scalars, *att_sends)
    att_terms = group_second(att_a, att_b, att_sends)
    hold(scalars, trunk_terms[2])
    head_home, head_part, gain2_grad = trunk_head(
        s, scalars, (hown_near, hown_far), trunk_terms, w_head_t, cot_cat
    )
    g1_got = swap(g1_send, "sec", core)
    g1_sum = add_low(g1_keep[1:2], g1_got[1:2])
    g1 = (g1_keep, g1_got, swap(g1_sum, "sec", chip))
    hold(scalars, g1_sum, *[terms[2] for terms in att_terms])
    att_kept, send = pick_team(s, scalars, *att_terms, 1)
    att_swapped = swap(send, "sec", s.members)
    *crossed, downs = pick_member(s, scalars, mlp_kept, mlp_swapped)
    ups = cross(s, crossed)
    downs = [downs, swap(downs, "grp", 1), swap(downs, "grp", 2)]
    ups = [ups, swap(ups, "grp", 1), swap(ups, "grp", 2)]
    keep, send, *edges = embed_back(
        s, scalars, g1, own, stats, hidden0, gain1, w_embed, in_cat, head_home, head_part, gain2_grad, bias_grad
    )
    edges = edges[:1] + [swap(edges[j], "grp", j) for j in range(1, s.group)]
    home_got = swap(send, "sec", core)
    mlp_parts = (
        downs + [swap(after(downs[2:], edges[0])[0], "grp", 1)],
        ups + [swap(after(ups[1:2], edges[0])[0], "grp", 2)],
    )
    crossed = pick_member(s, scalars, att_kept, att_swapped)
    att_parts = all_of_group(cross(s, crossed), True)
    home_far = swap(add_low(keep[1], home_got[1]), "sec", chip)
    down_grad, up_grad = mlp_grads_out(s, scalars, *mlp_parts)
    hold(scalars, home_far)
    home_mine, home_other = go_home(keep, home_got, home_far)

    total = edges[0].astype(F32) + edges[1].astype(F32) + edges[2].astype(F32) + edges[3].astype(F32)
    kept = jnp.where(first_team, total[0], total[1])
    given = jnp.where(first_team, total[1], total[0]).astype(BF)
    edges = (kept + swap(given, "sec", s.members).astype(F32)).astype(BF)
    edge_parts = all_of_group(edges, True)
    qkv_grad, out_grad = attention_grads_out(s, scalars, att_parts)
    hold(scalars, home_other)
    head_output, input_grad = at_home(home_mine, home_other)
    embed_t, head_t, small = edge_grads_out(s, scalars, edge_parts)
    embed_grad = embed_t.reshape(3, s.chan, s.db)
    head_grad = jnp.transpose(head_t.reshape(3, s.chan, s.db), (0, 2, 1))
    nb = s.fb // LANES
    return (
        head_output,
        input_grad,
        embed_grad,
        small[nb],
        qkv_grad,
        out_grad,
        small[nb + 1],
        up_grad,
        small[:nb].reshape(s.fb),
        down_grad,
        head_grad,
    )

LAT = 32
KCOLS = 8


def extended(cells, sides, width):
    for axis, dim in sides:
        count = lax.axis_size(axis)
        head = lax.slice_in_dim(cells, 0, width, axis=dim)
        tail = lax.slice_in_dim(cells, cells.shape[dim] - width, cells.shape[dim], axis=dim)
        cells = jnp.concatenate(
            [
                lax.ppermute(tail, axis, [(i, (i + 1) % count) for i in range(count)]),
                cells,
                lax.ppermute(head, axis, [((i + 1) % count, i) for i in range(count)]),
            ],
            axis=dim,
        )
    return cells


def normed(hidden, gains):
    center = hidden - jnp.mean(hidden, axis=-1, keepdims=True)
    spread = jnp.mean(center * center, axis=-1, keepdims=True)
    return center * lax.rsqrt(spread + 1e-05) * gains


def gelu_exact(values):
    return jax.nn.gelu(values, approximate=False)


def three_cols(padded, col_count, west_first):
    west_cols = padded[:, :, 0:col_count]
    middle_cols = padded[:, :, 1 : col_count + 1]
    east_cols = padded[:, :, 2 : col_count + 2]
    if west_first:
        return jnp.stack([west_cols, middle_cols, east_cols], axis=3)
    return jnp.stack([east_cols, middle_cols, west_cols], axis=3)


def split_heads(values):
    return values.reshape(values.shape[0], -1, HEADS, HEAD_DIM)


def key_mask(valid_rows, count_cols):
    rows_ok = jnp.arange(LAT)[None, :] < valid_rows[:, None]
    spread_ok = jnp.broadcast_to(rows_ok[:, :, None], (rows_ok.shape[0], LAT, count_cols))
    return spread_ok.reshape(rows_ok.shape[0], LAT * count_cols)


def key_scores(queries, kv_piece, valid_rows):
    d_model = HEADS * HEAD_DIM
    key_part = split_heads(kv_piece[..., :d_model])
    value_part = split_heads(kv_piece[..., d_model:])
    scores = (
        jnp.einsum("sqhd,skhd->shqk", queries, key_part, preferred_element_type=jnp.float32) * 0.125
    )
    allowed = key_mask(valid_rows, kv_piece.shape[2])
    scores = jnp.where(allowed[:, None, None, :], scores, -1e30)
    return (scores, key_part, value_part)


def softmax_fold(queries, valid_rows):

    def fold_piece(run_state, kv_piece, first_col):
        run_max, run_sum, run_acc = run_state
        scores, key_part, value_part = key_scores(queries, kv_piece, valid_rows)
        new_max = jnp.maximum(run_max, jnp.max(scores, axis=-1))
        factor = jnp.exp(run_max - new_max)
        weights = jnp.exp(scores - new_max[..., None])
        new_sum = run_sum * factor + jnp.sum(weights, axis=-1)
        added = jnp.einsum(
            "shqk,skhd->sqhd",
            weights.astype(jnp.bfloat16),
            value_part,
            preferred_element_type=jnp.float32,
        )
        new_acc = run_acc * jnp.transpose(factor, (0, 2, 1))[..., None] + added
        return (new_max, new_sum, new_acc)

    return fold_piece


def on_sectors(
    fields,
    valid_rows,
    w_embed,
    ln1_gain,
    w_qkv,
    w_out,
    ln2_gain,
    w_up,
    b_up,
    w_down,
    w_head,
    cotangent,
):
    samples, lat_rows, col_count, channels = fields.shape
    d_model = w_qkv.shape[0]
    token_count = lat_rows * col_count
    padded_in = extended(fields, (("sec", 2),), 1)
    input_cat = three_cols(padded_in, col_count, True)
    hidden0 = jnp.einsum("slcoi,oid->slcd", input_cat, w_embed, preferred_element_type=jnp.float32)
    normed_one, norm_one_back = jax.vjp(normed, hidden0, ln1_gain.astype(jnp.float32))
    normed_one_low = normed_one.astype(jnp.bfloat16)
    qkv_full = jnp.einsum(
        "slcd,de->slce", normed_one_low, w_qkv, preferred_element_type=jnp.float32
    ).astype(jnp.bfloat16)
    queries = split_heads(qkv_full[..., :d_model])
    key_vals = qkv_full[..., d_model:]
    init_state = (
        jnp.full((samples, HEADS, token_count), -1e30, jnp.float32),
        jnp.zeros((samples, HEADS, token_count), jnp.float32),
        jnp.zeros((samples, token_count, HEADS, HEAD_DIM), jnp.float32),
    )
    fold_piece = softmax_fold(queries, valid_rows)
    all_kv = lax.all_gather(key_vals, "sec", axis=2, tiled=True)

    def forward_block(block_index, run_state):
        kv_block = lax.dynamic_slice_in_dim(all_kv, block_index * KCOLS, KCOLS, 2)
        return fold_piece(run_state, kv_block, block_index * KCOLS)

    run_max, run_sum, run_acc = lax.fori_loop(
        0, all_kv.shape[2] // KCOLS, forward_block, init_state
    )
    attended = run_acc / jnp.transpose(run_sum, (0, 2, 1))[..., None]
    log_total = run_max + jnp.log(run_sum)
    attended_low = attended.reshape(samples, lat_rows, col_count, d_model).astype(jnp.bfloat16)
    hidden1 = hidden0 + jnp.einsum(
        "slcd,de->slce", attended_low, w_out, preferred_element_type=jnp.float32
    )
    normed_two, norm_two_back = jax.vjp(normed, hidden1, ln2_gain.astype(jnp.float32))
    normed_two_low = normed_two.astype(jnp.bfloat16)
    preact = jnp.einsum(
        "slcd,df->slcf", normed_two_low, w_up, preferred_element_type=jnp.float32
    ) + b_up.astype(jnp.float32)
    activ, gelu_back = jax.vjp(gelu_exact, preact)
    activ_low = activ.astype(jnp.bfloat16)
    hidden2 = hidden1 + jnp.einsum(
        "slcf,fd->slcd", activ_low, w_down, preferred_element_type=jnp.float32
    )
    hidden2_low = hidden2.astype(jnp.bfloat16)
    padded_hidden = extended(hidden2_low, (("sec", 2),), 1)
    hidden_cat = three_cols(padded_hidden, col_count, True)
    head_output = jnp.einsum(
        "slcod,odi->slci", hidden_cat, w_head, preferred_element_type=jnp.float32
    )
    padded_cot = extended(cotangent, (("sec", 2),), 1)
    cot_cat = three_cols(padded_cot, col_count, False)
    head_grad = jnp.einsum(
        "slcod,slci->odi", hidden_cat, cotangent, preferred_element_type=jnp.float32
    )
    grad_two = jnp.einsum("slcoi,odi->slcd", cot_cat, w_head, preferred_element_type=jnp.float32)
    grad_mlp = grad_two.astype(jnp.bfloat16)
    down_grad = jnp.einsum("slcf,slcd->fd", activ_low, grad_mlp, preferred_element_type=jnp.float32)
    grad_act = jnp.einsum("slcd,fd->slcf", grad_mlp, w_down, preferred_element_type=jnp.float32)
    grad_pre = gelu_back(grad_act)[0].astype(jnp.bfloat16)
    bias_grad = jnp.sum(grad_pre.astype(jnp.float32), axis=(0, 1, 2))
    up_grad = jnp.einsum(
        "slcd,slcf->df", normed_two_low, grad_pre, preferred_element_type=jnp.float32
    )
    grad_normed_two = jnp.einsum(
        "slcf,df->slcd", grad_pre, w_up, preferred_element_type=jnp.float32
    )
    grad_from_norm, gain_two_grad = norm_two_back(grad_normed_two)
    grad_one = grad_two + grad_from_norm
    grad_att = grad_one.astype(jnp.bfloat16)
    out_grad = jnp.einsum(
        "slcd,slce->de", attended_low, grad_att, preferred_element_type=jnp.float32
    )
    grad_heads = split_heads(
        jnp.einsum("slce,de->slcd", grad_att, w_out, preferred_element_type=jnp.float32).astype(
            jnp.bfloat16
        )
    )
    row_delta = jnp.transpose(
        jnp.sum(grad_heads.astype(jnp.float32) * attended, axis=-1), (0, 2, 1)
    )

    def sample_backward(unused_carry, sample_in):
        one_query, one_grad, one_lse, one_delta, one_valid, one_kv = sample_in
        term_zero = jnp.zeros((1, lat_rows, one_kv.shape[2], 2 * d_model), jnp.bfloat16)
        grad_zero = jnp.zeros(one_query.shape, jnp.float32)

        def backward_block(block_index, run_state):
            grad_query, term = run_state
            kv_block = lax.dynamic_slice_in_dim(one_kv, block_index * KCOLS, KCOLS, 2)
            scores, key_part, value_part = key_scores(one_query, kv_block, one_valid)
            probs = jnp.exp(scores - one_lse[..., None])
            grad_probs = jnp.einsum(
                "sqhd,skhd->shqk", one_grad, value_part, preferred_element_type=jnp.float32
            )
            grad_scores = (probs * (grad_probs - one_delta[..., None])).astype(jnp.bfloat16)
            grad_query = (
                grad_query
                + jnp.einsum(
                    "shqk,skhd->sqhd", grad_scores, key_part, preferred_element_type=jnp.float32
                )
                * 0.125
            )
            grad_keys = (
                jnp.einsum(
                    "shqk,sqhd->skhd", grad_scores, one_query, preferred_element_type=jnp.float32
                )
                * 0.125
            )
            grad_values = jnp.einsum(
                "shqk,sqhd->skhd",
                probs.astype(jnp.bfloat16),
                one_grad,
                preferred_element_type=jnp.float32,
            )
            joined = jnp.concatenate(
                [
                    grad_keys.reshape(1, lat_rows, KCOLS, d_model),
                    grad_values.reshape(1, lat_rows, KCOLS, d_model),
                ],
                axis=-1,
            ).astype(jnp.bfloat16)
            term = lax.dynamic_update_slice_in_dim(term, joined, block_index * KCOLS, 2)
            return (grad_query, term)

        grad_query, term = lax.fori_loop(
            0, one_kv.shape[2] // KCOLS, backward_block, (grad_zero, term_zero)
        )
        summed = lax.psum_scatter(
            term.astype(jnp.float32).astype(jnp.bfloat16), "sec", scatter_dimension=2, tiled=True
        ).astype(jnp.float32)
        return (unused_carry, (grad_query, summed))

    scan_inputs = (
        queries.reshape(samples, 1, token_count, HEADS, HEAD_DIM),
        grad_heads.reshape(samples, 1, token_count, HEADS, HEAD_DIM),
        log_total.reshape(samples, 1, HEADS, token_count),
        row_delta.reshape(samples, 1, HEADS, token_count),
        valid_rows.reshape(samples, 1),
        all_kv.reshape(samples, 1, lat_rows, all_kv.shape[2], 2 * d_model),
    )
    scan_end, (grad_queries, grad_kv) = lax.scan(sample_backward, 0, scan_inputs)
    grad_qkv = jnp.concatenate(
        [
            grad_queries.reshape(samples, lat_rows, col_count, d_model),
            grad_kv.reshape(samples, lat_rows, col_count, 2 * d_model),
        ],
        axis=-1,
    ).astype(jnp.bfloat16)
    qkv_grad = jnp.einsum(
        "slcd,slce->de", normed_one_low, grad_qkv, preferred_element_type=jnp.float32
    )
    grad_normed_one = jnp.einsum(
        "slce,de->slcd", grad_qkv, w_qkv, preferred_element_type=jnp.float32
    )
    grad_from_first, gain_one_grad = norm_one_back(grad_normed_one)
    grad_zero_low = (grad_one + grad_from_first).astype(jnp.bfloat16)
    embed_grad = jnp.einsum(
        "slcoi,slcd->oid", input_cat, grad_zero_low, preferred_element_type=jnp.float32
    )
    padded_grad = extended(grad_zero_low, (("sec", 2),), 1)
    grad_cat = three_cols(padded_grad, col_count, False)
    input_grad = jnp.einsum(
        "slcod,oid->slci", grad_cat, w_embed, preferred_element_type=jnp.float32
    )
    shard_grads = (
        lax.psum_scatter(
            embed_grad.astype(jnp.bfloat16), "sec", scatter_dimension=2, tiled=True
        ).astype(jnp.float32),
        lax.psum_scatter(
            gain_one_grad.astype(jnp.bfloat16), "sec", scatter_dimension=0, tiled=True
        ).astype(jnp.float32),
        lax.psum_scatter(
            qkv_grad.astype(jnp.bfloat16), "sec", scatter_dimension=0, tiled=True
        ).astype(jnp.float32),
        lax.psum_scatter(
            out_grad.astype(jnp.bfloat16), "sec", scatter_dimension=0, tiled=True
        ).astype(jnp.float32),
        lax.psum_scatter(
            gain_two_grad.astype(jnp.bfloat16), "sec", scatter_dimension=0, tiled=True
        ).astype(jnp.float32),
        lax.psum_scatter(
            up_grad.astype(jnp.bfloat16), "sec", scatter_dimension=0, tiled=True
        ).astype(jnp.float32),
        lax.psum_scatter(
            bias_grad.astype(jnp.bfloat16), "sec", scatter_dimension=0, tiled=True
        ).astype(jnp.float32),
        lax.psum_scatter(
            down_grad.astype(jnp.bfloat16), "sec", scatter_dimension=0, tiled=True
        ).astype(jnp.float32),
        lax.psum_scatter(
            head_grad.astype(jnp.bfloat16), "sec", scatter_dimension=1, tiled=True
        ).astype(jnp.float32),
    )
    total_grads = (
        lax.psum(shard_grads[0].astype(jnp.bfloat16), "grp").astype(jnp.float32),
        lax.psum(shard_grads[1].astype(jnp.bfloat16), "grp").astype(jnp.float32),
        lax.psum(shard_grads[2].astype(jnp.bfloat16), "grp").astype(jnp.float32),
        lax.psum(shard_grads[3].astype(jnp.bfloat16), "grp").astype(jnp.float32),
        lax.psum(shard_grads[4].astype(jnp.bfloat16), "grp").astype(jnp.float32),
        lax.psum(shard_grads[5].astype(jnp.bfloat16), "grp").astype(jnp.float32),
        lax.psum(shard_grads[6].astype(jnp.bfloat16), "grp").astype(jnp.float32),
        lax.psum(shard_grads[7].astype(jnp.bfloat16), "grp").astype(jnp.float32),
        lax.psum(shard_grads[8].astype(jnp.bfloat16), "grp").astype(jnp.float32),
    )
    return (
        head_output,
        input_grad,
        total_grads[0],
        total_grads[1],
        total_grads[2],
        total_grads[3],
        total_grads[4],
        total_grads[5],
        total_grads[6],
        total_grads[7],
        total_grads[8],
    )


def on_device(*args):
    fields, w_qkv = args[0], args[4]
    sectors = lax.axis_size("sec")
    fits = (
        fields.shape[0] == 2
        and sectors == 8
        and lax.axis_size("grp") == 4
        and w_qkv.shape[0] == sectors * LANES
    )
    return on_team(*args) if fits else on_sectors(*args)


def solution(mesh):
    tokens_in = P("grp", None, "sec", None)
    return jax.shard_map(
        on_device,
        mesh=mesh,
        in_specs=(tokens_in, P("grp")) + (P(),) * 9 + (tokens_in,),
        out_specs=(
            tokens_in,
            tokens_in,
            P(None, None, "sec"),
            P("sec"),
            P("sec", None),
            P("sec", None),
            P("sec"),
            P("sec", None),
            P("sec"),
            P("sec", None),
            P(None, "sec", None),
        ),
        check_vma=False,
    )
```

```python
import jax
import jax.numpy as jnp
import numpy as np
from jax import lax
from jax.experimental import pallas as pl
from jax.experimental.pallas import tpu as pltpu
from jax.sharding import PartitionSpec as P

HEAD_DIM = 64
HEADS = 16
LANES = 128
KEY_CHUNK = 512
VMEM_LIMIT = 48 * 1024 * 1024
BF = jnp.bfloat16
F32 = jnp.float32

NN = ((1,), (0,))
NT = ((1,), (1,))
TN = ((0,), (0,))

MICROS = {
    "embed_qkv": 9.6,
    "cotangent_grad": 6.1,
    "attention_fwd": 9.2,
    "mlp": 17.0,
    "trunk_part": 4.0,
    "norm_two_back": 4.9,
    "attention_bwd": 13.3,
    "norm_one_grad": 11.7,
    "trunk_head": 7.0,
    "embed_back": 9.0,
    "mlp_weight_grads": 11.5,
    "attention_weight_grads": 9.0,
    "pick_team": 3.4,
    "pick_member": 2.5,
    "mlp_grads_out": 4.7,
    "attention_grads_out": 3.5,
    "edge_grads_out": 2.8,
}

TEAM, ME, GRP, VALID = range(4)


def dot(a, b, dims):
    return lax.dot_general(a, b, (dims, ((), ())), preferred_element_type=F32)


def swap(x, axis, bit):
    n = lax.axis_size(axis)
    return lax.ppermute(x, axis, [(i, i ^ bit) for i in range(n)])


def kernel(body, name, scalars, grid, ins, outs, scratch=(), aliases=None):
    micros = MICROS[name]
    scalars, chain = scalars
    values = lax.optimization_barrier((scalars, *chain))[0] if chain else scalars
    def spec(block, index):
        if block is None:
            return pl.BlockSpec(memory_space=pl.ANY)
        return pl.BlockSpec(block, index)

    results = pl.pallas_call(
        body,
        grid_spec=pltpu.PrefetchScalarGridSpec(
            num_scalar_prefetch=1,
            grid=grid,
            in_specs=[spec(block, index) for _, block, index in ins],
            out_specs=[spec(block, index) for _, _, block, index in outs],
            scratch_shapes=list(scratch),
        ),
        out_shape=[jax.ShapeDtypeStruct(shape, kind) for shape, kind, _, _ in outs],
        input_output_aliases=aliases or {},
        compiler_params=pltpu.CompilerParams(vmem_limit_bytes=VMEM_LIMIT),
        cost_estimate=pl.CostEstimate(
            flops=int(micros * 1.15e9), transcendentals=0, bytes_accessed=int(micros * 3.6e6)
        ),
        name=name,
    )(values, *[array for array, _, _ in ins])
    chain[:] = [results[-1]]
    return results


def hold(scalars, *values):
    scalars[1].extend(values)


def after(values, *others):
    return list(lax.optimization_barrier((*values, *others))[: len(values)])


def whole(array):
    rank = len(array.shape)
    return (array, array.shape, lambda *_: (0,) * rank)


def whole_out(shape, kind):
    rank = len(shape)
    return (shape, kind, shape, lambda *_: (0,) * rank)


class Sizes:
    def __init__(self, fields, w_qkv, w_up):
        self.teams, self.lat, self.cols, self.chan = fields.shape
        self.sectors = lax.axis_size("sec")
        self.members = self.sectors // self.teams
        self.group = lax.axis_size("grp")
        self.d = w_qkv.shape[0]
        self.ff = w_up.shape[1]
        self.sec_tokens = self.lat * self.cols
        self.tokens = self.sectors * self.sec_tokens
        self.heads = HEADS // self.members
        self.width = self.heads * HEAD_DIM
        self.db = self.d // self.sectors
        self.fb = self.ff // self.sectors
        self.dn = self.teams * self.db
        self.fn = self.teams * self.fb
        self.own = self.tokens // self.members
        self.half = self.tokens // 2


def line_up(s, scalars, pieces, canon):
    for j, piece in enumerate(pieces):
        for k in range(s.teams):
            at = (scalars[TEAM] ^ k) * s.members + (scalars[ME] ^ j)
            canon[at] = piece[k]


def beside(s, canon, sector):
    mid = canon[sector].astype(F32)
    before = canon[lax.rem(sector + s.sectors - 1, s.sectors)].astype(F32)
    after = canon[lax.rem(sector + 1, s.sectors)].astype(F32)
    col = lax.rem(lax.broadcasted_iota(jnp.int32, mid.shape, 0), s.cols)
    rows = s.sec_tokens
    west = jnp.where(col == 0, pltpu.roll(before, rows - (s.cols - 1), 0), pltpu.roll(mid, 1, 0))
    east = jnp.where(col == s.cols - 1, pltpu.roll(after, s.cols - 1, 0), pltpu.roll(mid, rows - 1, 0))
    return west, mid, east


def row_stats(rows):
    mean = jnp.mean(rows, axis=-1, keepdims=True)
    center = rows - mean
    return mean, lax.rsqrt(jnp.mean(center * center, axis=-1, keepdims=True) + 1e-05)


def normed_rows(rows):
    mean, rstd = row_stats(rows)
    return (rows - mean) * rstd, rstd


def embed_qkv(s, scalars, pieces, w_embed, gain, w_qkv):
    rows = s.half
    per = rows // s.sec_tokens
    chunk = s.sec_tokens

    def body(sc, *refs):
        parts = refs[: s.members]
        we, g, wq, wk, wv = refs[s.members : s.members + 5]
        cat_ref, hid_ref, norm_ref, qkv_ref, stat_ref, canon = refs[s.members + 5 :]
        i = pl.program_id(0)

        @pl.when(i == 0)
        def _():
            line_up(s, sc, parts, canon)

        for p in range(per):
            at = slice(p * chunk, (p + 1) * chunk)
            west, mid, east = beside(s, canon, i * per + p)
            cat_ref[at, :] = jnp.concatenate([west, mid, east], axis=1).astype(BF)
        hid_ref[...] = dot(cat_ref[...], we[...], NN)
        lane = lax.broadcasted_iota(jnp.int32, (chunk, LANES), 1)
        for p in range(per):
            at = slice(p * chunk, (p + 1) * chunk)
            value = hid_ref[at, :]
            mean, rstd = row_stats(value)
            norm_ref[at, :] = ((value - mean) * rstd * g[...]).astype(BF)
            stat_ref[at, :] = jnp.where(lane == 0, mean, rstd)
        for k, w in enumerate((wq, wk, wv)):
            qkv_ref[:, k * s.width : (k + 1) * s.width] = dot(norm_ref[...], w[...], NN).astype(BF)

    def third(k):
        return (w_qkv, (s.d, s.width), lambda i, sc: (0, k * s.members + sc[ME]))

    row = lambda i, sc: (i, 0)
    return kernel(
        body,
        "embed_qkv",
        scalars,
        (s.tokens // rows,),
        [whole(p) for p in pieces] + [whole(w_embed), whole(gain), third(0), third(1), third(2)],
        [
            ((s.tokens, 3 * s.chan), BF, (rows, 3 * s.chan), row),
            ((s.tokens, s.d), F32, (rows, s.d), row),
            ((s.tokens, s.d), BF, (rows, s.d), row),
            ((s.tokens, 3 * s.width), BF, (rows, 3 * s.width), row),
            ((s.tokens, LANES), F32, (rows, LANES), row),
        ],
        [pltpu.VMEM((s.sectors, s.sec_tokens, s.chan), BF)],
    )


def cotangent_grad(s, scalars, pieces, w_head):
    rows = s.half
    per = rows // s.sec_tokens

    def body(sc, *refs):
        parts = refs[: s.members]
        wh, cat_ref, grad_ref, canon = refs[s.members :]
        i = pl.program_id(0)

        @pl.when(i == 0)
        def _():
            line_up(s, sc, parts, canon)

        for p in range(per):
            at = slice(p * s.sec_tokens, (p + 1) * s.sec_tokens)
            west, mid, east = beside(s, canon, i * per + p)
            cat_ref[at, :] = jnp.concatenate([east, mid, west], axis=1).astype(BF)
        grad_ref[...] = dot(cat_ref[...], wh[...], NN).astype(BF)

    row = lambda i, sc: (i, 0)
    return kernel(
        body,
        "cotangent_grad",
        scalars,
        (s.tokens // rows,),
        [whole(p) for p in pieces] + [whole(w_head)],
        [
            ((s.tokens, 3 * s.chan), BF, (rows, 3 * s.chan), row),
            ((s.tokens, s.d), BF, (rows, s.d), row),
        ],
        [pltpu.VMEM((s.sectors, s.sec_tokens, s.chan), BF)],
    )


def side_of(s, sc, far):
    own = sc[ME] // (s.members // 2)
    return own ^ 1 if far else own


def lanes_of(value, side):
    lane = lax.broadcasted_iota(jnp.int32, value.shape, 1)
    return jnp.where(lane // HEAD_DIM == side, value, jnp.zeros_like(value))


def attention_fwd(s, scalars, qkv, far):
    rows = s.own
    steps = s.half // rows
    chunk = KEY_CHUNK

    def body(sc, q_ref, kv_ref, att_ref, weight_ref, inv_ref, bias, values, buf_a, buf_b, top_a, top_b, outs, invs):
        @pl.when(pl.program_id(0) == 0)
        def _():
            key = lax.broadcasted_iota(jnp.int32, (s.tokens, LANES), 0)
            bias[...] = jnp.where(lax.rem(key, s.sec_tokens) // s.cols < sc[VALID], 0.0, -1e30)
            values[...] = jnp.transpose(kv_ref[:, 2 * s.width :].astype(F32)).astype(BF)
            invs[...] = jnp.zeros_like(invs)

        def score(p, side, buf, tops):
            at = pl.ds(pl.multiple_of(p * LANES, LANES), LANES)
            kat = pl.ds(pl.multiple_of(s.width + p * LANES, LANES), LANES)
            query = lanes_of(q_ref[:, at] * jnp.asarray(0.125, BF), side)
            top = None
            for c in range(0, s.tokens, chunk):
                rows_at = slice(c, c + chunk)
                wide = jnp.concatenate([bias[rows_at, :]] * (rows // LANES), axis=1)
                scores = dot(kv_ref[rows_at, kat], query, NT) + wide
                buf[rows_at, :] = scores
                peak = jnp.max(scores, axis=0, keepdims=True)
                top = peak if top is None else jnp.maximum(top, peak)
            tops[...] = jnp.broadcast_to(top, tops.shape)

        def weigh(p, side, buf, tops):
            h = 2 * p + side
            heads_at = pl.ds(pl.multiple_of(h * HEAD_DIM, HEAD_DIM), HEAD_DIM)
            top = tops[0:1, :]
            total = None
            out = None
            for c in range(0, s.tokens, chunk):
                at = slice(c, c + chunk)
                weights = jnp.exp(buf[at, :] - top)
                part = jnp.sum(weights, axis=0, keepdims=True)
                low = weights.astype(BF)
                weight_ref[h, 0, at, :] = low
                more = dot(values[heads_at, at], low, NN)
                total = part if total is None else total + part
                out = more if out is None else out + more
            inv = 1.0 / total
            invs[pl.ds(pl.multiple_of(h * 8, 8), 8), :] = jnp.broadcast_to(inv, (8, rows))
            outs[heads_at, :] = out * inv

        score(0, 0, buf_a, top_a)

        def pair_step(p, carry):
            weigh(p, 0, buf_a, top_a)
            score(p, 1, buf_b, top_b)

            @pl.when(p >= 0)
            def _():
                weigh(p, 1, buf_b, top_b)
                score(jnp.minimum(p + 1, s.heads // 2 - 1), 0, buf_a, top_a)

            return carry

        lax.fori_loop(0, s.heads // 2, pair_step, 0)
        att_ref[...] = jnp.transpose(outs[...]).astype(BF)
        inv_ref[...] = jnp.transpose(invs[...])

    row = lambda i, sc: (i, 0)
    return kernel(
        body,
        "attention_fwd",
        scalars,
        (steps,),
        [
            (qkv, (rows, 3 * s.width), lambda i, sc: (side_of(s, sc, far) * steps + i, 0)),
            whole(qkv),
        ],
        [
            ((s.half, s.width), BF, (rows, s.width), row),
            ((s.heads, steps, s.tokens, rows), BF, (s.heads, 1, s.tokens, rows), lambda i, sc: (0, i, 0, 0)),
            ((s.half, LANES), F32, (rows, LANES), row),
        ],
        [
            pltpu.VMEM((s.tokens, LANES), F32),
            pltpu.VMEM((s.width, s.tokens), BF),
            pltpu.VMEM((s.tokens, rows), F32),
            pltpu.VMEM((s.tokens, rows), F32),
            pltpu.VMEM((8, rows), F32),
            pltpu.VMEM((8, rows), F32),
            pltpu.VMEM((s.width, rows), F32),
            pltpu.VMEM((LANES, rows), F32),
        ],
    )


def mlp(s, scalars, att, hidden0, grad_mlp, w_out, gain, w_up, b_up, w_down, far):
    chunk = 64
    rows = s.half
    count = len(att)

    def body(sc, *refs):
        parts = refs[:count]
        h0, gm, g, bias, wo_hbm, wu_hbm, wd_hbm = refs[count : count + 7]
        outs = refs[count + 7 :]
        att_ref, n2_ref, act_ref, gpre_ref, gkeep, gsend, gsum_ref, hown, bsum, h1_ref = outs[:10]
        wo, wu, wd, pre, gact, means, rstds, sem = outs[10:]
        me = sc[ME]

        copies = [pltpu.make_async_copy(wo_hbm, wo, sem.at[0])]
        for k in range(s.teams):
            at = pl.multiple_of((k * s.members + me) * s.fb, s.fb)
            copies.append(
                pltpu.make_async_copy(
                    wu_hbm.at[:, pl.ds(at, s.fb)], wu.at[:, pl.ds(k * s.fb, s.fb)], sem.at[1 + k]
                )
            )
        for k in range(s.teams):
            at = pl.multiple_of((k * s.members + me) * s.fb, s.fb)
            copies.append(
                pltpu.make_async_copy(
                    wd_hbm.at[pl.ds(at, s.fb), :],
                    wd.at[pl.ds(k * s.fb, s.fb), :],
                    sem.at[1 + s.teams + k],
                )
            )
        for copy in copies:
            copy.start()
        for j in range(count):
            at = pl.multiple_of((me ^ j) * s.width, s.width)
            att_ref[:, pl.ds(at, s.width)] = parts[j][...]
        copies[0].wait()
        span = 512

        def by_columns(size, one):
            def step(n, carry):
                one(pl.ds(pl.multiple_of(n * span, span), span))
                return carry

            lax.fori_loop(0, size // span, step, 0)

        def attention_out(cols):
            h1_ref[:, cols] = h0[:, cols] + dot(att_ref[...], wo[:, cols], NN)

        by_columns(s.d, attention_out)

        def norm_chunk(c, carry):
            at = pl.ds(pl.multiple_of(c * chunk, chunk), chunk)
            value = h1_ref[at, :]
            mean, rstd = row_stats(value)
            n2_ref[at, :] = ((value - mean) * rstd * g[...]).astype(BF)
            means[at, :] = jnp.broadcast_to(mean, (chunk, LANES))
            rstds[at, :] = jnp.broadcast_to(rstd, (chunk, LANES))
            return carry

        lax.fori_loop(0, rows // chunk, norm_chunk, 0)
        for k in range(s.teams):
            at = pl.multiple_of((k * s.members + me) * s.db, s.db)
            hown[:, k * s.db : (k + 1) * s.db] = h1_ref[:, pl.ds(at, s.db)]
        for copy in copies[1 : 1 + s.teams]:
            copy.wait()

        def up_out(cols):
            pre[:, cols] = dot(n2_ref[...], wu[:, cols], NN)

        by_columns(s.fn, up_out)
        for copy in copies[1 + s.teams :]:
            copy.wait()

        def down_back(cols):
            gact[:, cols] = dot(gm[...], wd[cols, :], NT)

        by_columns(s.fn, down_back)

        def gelu_chunk(c, total):
            at = pl.ds(pl.multiple_of(c * chunk, chunk), chunk)
            u = pre[at, :] + bias[...]
            cdf = 0.5 * (1.0 + lax.erf(u * np.float32(2**-0.5)))
            act_ref[at, :] = (u * cdf).astype(BF)
            slope = cdf + u * jnp.exp(-0.5 * u * u) * np.float32((2 * np.pi) ** -0.5)
            low = (gact[at, :] * slope).astype(BF)
            gpre_ref[at, :] = low
            return total + jnp.sum(low.astype(F32), axis=0, keepdims=True)

        bsum[...] = lax.fori_loop(0, rows // chunk, gelu_chunk, jnp.zeros((1, s.fn), F32))

        def up_back(cols):
            pre[:, cols] = dot(gpre_ref[...], wu[cols, :], NT)

        by_columns(s.d, up_back)

        def gain_chunk(c, total):
            at = pl.ds(pl.multiple_of(c * chunk, chunk), chunk)
            mean, rstd = means[at, :], rstds[at, :]
            sums = []
            for n in range(s.d // LANES):
                cols = slice(n * LANES, (n + 1) * LANES)
                xhat = (h1_ref[at, cols] - mean) * rstd
                sums.append(jnp.sum(pre[at, cols] * xhat, axis=0, keepdims=True))
            return total + jnp.concatenate(sums, axis=1)

        gsum = lax.fori_loop(0, rows // chunk, gain_chunk, jnp.zeros((1, s.d), F32))
        mine = lax.rem(me, 2)
        keep_at = pl.ds(pl.multiple_of(mine * s.own, s.own), s.own)
        send_at = pl.ds(pl.multiple_of((1 - mine) * s.own, s.own), s.own)
        gkeep[...] = pre[keep_at, :].astype(BF)
        gsend[...] = pre[send_at, :].astype(BF)
        gsum_ref[...] = gsum

    index = lambda i, sc: (side_of(s, sc, far), 0)
    bias_own = jnp.concatenate(
        [
            lax.dynamic_slice_in_dim(b_up, (k * s.members + scalars[0][ME]) * s.fb, s.fb, 0)
            for k in range(s.teams)
        ]
    ).astype(F32)[None]
    return kernel(
        body,
        "mlp",
        scalars,
        (1,),
        [whole(a) for a in att]
        + [
            (hidden0, (rows, s.d), index),
            (grad_mlp, (rows, s.d), index),
            whole(gain),
            whole(bias_own),
            (w_out, None, None),
            (w_up, None, None),
            (w_down, None, None),
        ],
        [
            whole_out((rows, s.d), BF),
            whole_out((rows, s.d), BF),
            whole_out((rows, s.fn), BF),
            whole_out((rows, s.fn), BF),
            whole_out((s.own, s.d), BF),
            whole_out((s.own, s.d), BF),
            whole_out((1, s.d), F32),
            whole_out((rows, s.dn), F32),
            whole_out((1, s.fn), F32),
            whole_out((rows, s.d), F32),
        ],
        [
            pltpu.VMEM((s.d, s.d), BF),
            pltpu.VMEM((s.d, s.fn), BF),
            pltpu.VMEM((s.fn, s.d), BF),
            pltpu.VMEM((rows, s.fn), F32),
            pltpu.VMEM((rows, s.fn), F32),
            pltpu.VMEM((rows, LANES), F32),
            pltpu.VMEM((rows, LANES), F32),
            pltpu.SemaphoreType.DMA((1 + 2 * s.teams,)),
        ],
    )


def trunk_part(s, scalars, parts, w_down):
    extra = 16
    rows = s.half

    def body(sc, act0, gs0, act1, gs1, *refs):
        downs, (keep, send, out, both, sums) = refs[: s.teams], refs[s.teams :]
        both[0], both[1] = act0[...], act1[...]
        sums[0], sums[1] = gs0[...], gs1[...]

        def one_half(half, carry):
            total = dot(both[half, :, : s.fb], downs[0][...], NN)
            for k in range(1, s.teams):
                total += dot(both[half, :, k * s.fb : (k + 1) * s.fb], downs[k][...], NN)
            out[:rows] = total
            out[rows:] = jnp.broadcast_to(sums[half], (extra, s.d))
            for odd, ref in ((0, keep), (1, send)):
                for n in range(s.members // 2):
                    m = sc[ME] ^ (2 * n + odd)
                    for k in range(s.teams):
                        cols = pl.ds(pl.multiple_of((k * s.members + m) * s.db, s.db), s.db)
                        ref[n, half, :, k * s.db : (k + 1) * s.db] = out[:, cols].astype(BF)
            return carry

        lax.fori_loop(0, 2, one_half, 0)

    pair = (s.members // 2, 2, rows + extra, s.dn)
    return kernel(
        body,
        "trunk_part",
        scalars,
        (1,),
        [whole(x) for part in parts for x in part]
        + [
            (w_down, (s.fb, s.d), lambda i, sc, k=k: (k * s.members + sc[ME], 0))
            for k in range(s.teams)
        ],
        [whole_out(pair, BF), whole_out(pair, BF)],
        [
            pltpu.VMEM((rows + extra, s.d), F32),
            pltpu.VMEM((2, rows, s.fn), BF),
            pltpu.VMEM((2, 1, s.d), F32),
        ],
    )


def norm_two_back(s, scalars, parts, hidden1, grad_mlp, gain):
    chunk = 64
    count = len(parts)

    def body(sc, *refs):
        h1, gm, g, out_ref = refs[count:]

        def rows_chunk(c, carry):
            at = pl.ds(pl.multiple_of(c * chunk, chunk), chunk)
            xhat, rstd = normed_rows(h1[at, :])
            grad = refs[0][at, :].astype(F32)
            for ref in refs[1:count]:
                grad += ref[at, :].astype(F32)
            grad *= g[...]
            back = grad - jnp.mean(grad, axis=-1, keepdims=True)
            back -= xhat * jnp.mean(grad * xhat, axis=-1, keepdims=True)
            out_ref[at, :] = (gm[at, :].astype(F32) + rstd * back).astype(BF)
            return carry

        lax.fori_loop(0, s.own // chunk, rows_chunk, 0)

    return kernel(
        body,
        "norm_two_back",
        scalars,
        (1,),
        [whole(p) for p in parts]
        + [
            (hidden1, (s.own, s.d), lambda i, sc: (lax.rem(sc[ME], 2), 0)),
            (grad_mlp, (s.own, s.d), lambda i, sc: (sc[ME], 0)),
            whole(gain),
        ],
        [whole_out((s.own, s.d), BF)],
    )[0]


def attention_bwd(s, scalars, qkv, saved, grads, w_out, far, before=None):
    base = s.members // 2 if far else 0
    rows = s.own
    last = before is not None
    attended, weights, inverse = saved

    def body(sc, *refs):
        q_ref, kv_ref, att_ref, weight_ref, inv_ref, first, second, wo = refs[:8]
        if last:
            old_ref = refs[10]
            dq_ref, own_ref, out_ref, gh, acc, keys = refs[11:]
        else:
            dq_ref, own_ref, out_ref, gh, acc, keys = refs[8:]
        i = pl.program_id(0)

        @pl.when(i == 0)
        def _():
            if last:
                acc[...] = old_ref[...]
            else:
                acc[...] = jnp.zeros_like(acc)
            keys[...] = jnp.transpose(kv_ref[:, s.width : 2 * s.width].astype(F32)).astype(BF)

        for step, piece in enumerate((first, second)):

            @pl.when(i == step)
            def _():
                gh[...] = dot(piece[...], wo[...], NT)
                for k in range(s.teams):
                    at = pl.multiple_of((k * s.members + sc[ME]) * s.db, s.db)
                    own_ref[:, k * s.db : (k + 1) * s.db] = piece[:, pl.ds(at, s.db)]

        def pair_step(p, carry):
            pair = pl.ds(pl.multiple_of(p * LANES, LANES), LANES)
            value_at = pl.ds(pl.multiple_of(2 * s.width + p * LANES, LANES), LANES)
            dv_at = pl.ds(pl.multiple_of(s.width + p * LANES, LANES), LANES)
            inv = inv_ref[...]
            wide = lax.broadcasted_iota(jnp.int32, inv.shape, 1)
            outs = []
            means = jnp.zeros((rows, LANES), F32)
            for side in range(2):
                h = 2 * p + side
                one = jnp.sum(jnp.where(wide == 8 * h, inv, 0.0), axis=-1, keepdims=True)
                out = (lanes_of(gh[:, pair], side) * one).astype(BF)
                mean = jnp.sum(out.astype(F32) * att_ref[:, pair].astype(F32), axis=-1, keepdims=True)
                means = jnp.where(wide == side, mean, means)
                outs.append(out)
            means = jnp.transpose(means)
            turned = [None, None]
            units = [(c, side) for c in range(0, s.tokens, KEY_CHUNK) for side in range(2)]

            def first_dot(unit):
                c, side = unit
                return dot(kv_ref[c : c + KEY_CHUNK, value_at], outs[side], NT)

            ahead = first_dot(units[0])
            for n, (c, side) in enumerate(units):
                at = slice(c, c + KEY_CHUNK)
                h = 2 * p + side
                gprob = ahead - means[side : side + 1, :]
                if n + 1 < len(units):
                    ahead = first_dot(units[n + 1])
                weight = weight_ref[h, 0, at, :]
                gscore = (weight.astype(F32) * gprob).astype(BF)
                key_rows = pl.ds(pl.multiple_of(h * HEAD_DIM, HEAD_DIM), HEAD_DIM)
                dq = dot(keys[key_rows, at], gscore, NN)
                turned[side] = dq if turned[side] is None else turned[side] + dq
                one = dot(gscore, lanes_of(q_ref[:, pair], side), NN)
                two = dot(weight, outs[side], NN)
                if side == 0:
                    dk, dv = one, two
                else:
                    acc[at, pair] += dk + one
                    acc[at, dv_at] += dv + two
            dq_ref[:, pair] = (jnp.transpose(jnp.concatenate(turned, axis=0)) * 0.125).astype(BF)
            return carry

        lax.fori_loop(0, s.heads // 2, pair_step, 0)

        @pl.when(i == pl.num_programs(0) - 1)
        def _():
            if last:
                out_ref[:, : s.width] = (acc[:, : s.width] * 0.125).astype(BF)
                out_ref[:, s.width :] = acc[:, s.width :].astype(BF)
            else:
                out_ref[...] = acc[...]

    member = lambda i, sc: (sc[ME] ^ (base + i), 0)
    side = lambda i, sc: lax.rem(sc[ME] ^ i, s.members // 2)
    ins = [
        (qkv, (rows, 3 * s.width), member),
        whole(qkv),
        (attended, (rows, s.width), lambda i, sc: (side(i, sc), 0)),
        (weights, (s.heads, 1, s.tokens, rows), lambda i, sc: (0, side(i, sc), 0, 0)),
        (inverse, (rows, LANES), lambda i, sc: (side(i, sc), 0)),
        whole(grads[0]),
        whole(grads[1]),
        (w_out, (s.width, s.d), lambda i, sc: (sc[ME], 0)),
    ]
    aliases = None
    if last:
        ins += [(before[0], None, None), (before[1], None, None), whole(before[2])]
        aliases = {9: 0, 10: 1}
    return kernel(
        body,
        "attention_bwd",
        scalars,
        (2,),
        ins,
        [
            ((s.tokens, s.width), BF, (rows, s.width), member),
            ((s.tokens, s.dn), BF, (rows, s.dn), member),
            whole_out((s.tokens, 2 * s.width), BF if last else F32),
        ],
        [
            pltpu.VMEM((rows, s.width), F32),
            pltpu.VMEM((s.tokens, 2 * s.width), F32),
            pltpu.VMEM((s.width, s.tokens), BF),
        ],
        aliases,
    )


def norm_one_grad(s, scalars, qkv, dq, dkv, w_qkv, gain):
    rows = s.half

    def body(sc, qkv_ref, dq_ref, dkv_ref, wq, wk, wv, g, keep, send, grad, stat, lines):
        me = sc[ME]
        total = dot(dq_ref[...], wq[...], NT)
        total += dot(dkv_ref[:, : s.width], wk[...], NT)
        grad[...] = total + dot(dkv_ref[:, s.width :], wv[...], NT)
        gain8 = jnp.broadcast_to(g[...], (8, s.d)).astype(BF)
        parts = ((dq_ref[...], wq), (dkv_ref[:, : s.width], wk), (dkv_ref[:, s.width :], wv))
        one = jnp.zeros((rows, s.width), F32)
        two = jnp.zeros((rows, s.width), F32)
        for k, (value, w) in enumerate(parts):
            value = value.astype(F32)
            one += value * dot(gain8, w[...], NN)[0:1, :]
            two += value * qkv_ref[:, k * s.width : (k + 1) * s.width].astype(F32)
        one = jnp.sum(one, axis=-1, keepdims=True)
        two = jnp.sum(two, axis=-1, keepdims=True)
        lane = lax.broadcasted_iota(jnp.int32, (rows, LANES), 1)
        stat[...] = jnp.where(lane == 0, one, two)
        turned = jnp.transpose(stat[...])
        count = s.tokens // s.dn
        for kind in range(2):
            for n in range(rows // s.dn):
                at = kind * count + n
                step = rows // s.dn
                line = turned[kind : kind + 1, n * s.dn : (n + 1) * s.dn].astype(BF).astype(F32)
                for i in range(s.tokens // rows):

                    @pl.when(pl.program_id(0) == i)
                    def _():
                        lines[at + i * step : at + i * step + 1, :] = line
        at = pl.ds(pl.multiple_of(pl.program_id(0) * rows, rows), rows)
        for odd, ref in ((0, keep), (1, send)):
            for n in range(s.members // 2):
                m = me ^ (2 * n + odd)
                for k in range(s.teams):
                    cols = pl.ds(pl.multiple_of((k * s.members + m) * s.db, s.db), s.db)
                    ref[n, at, k * s.db : (k + 1) * s.db] = grad[:, cols].astype(BF)
                ref[n, s.tokens :, :] = lines[...].astype(BF)

    def third(k):
        return (w_qkv, (s.d, s.width), lambda i, sc: (0, k * s.members + sc[ME]))

    row = lambda i, sc: (i, 0)
    pair = (s.members // 2, s.tokens + 16, s.dn)
    return kernel(
        body,
        "norm_one_grad",
        scalars,
        (s.tokens // rows,),
        [
            (qkv, (rows, 3 * s.width), row),
            (dq, (rows, s.width), row),
            (dkv, (rows, 2 * s.width), row),
            third(0),
            third(1),
            third(2),
            whole(gain),
        ],
        [
            whole_out(pair, BF),
            whole_out(pair, BF),
        ],
        [
            pltpu.VMEM((rows, s.d), F32),
            pltpu.VMEM((rows, LANES), F32),
            pltpu.VMEM((16, s.dn), F32),
        ],
    )


def shift_all(s, parts, out_ref):
    west_ref, mid_ref, east_ref = parts
    rows = s.sec_tokens
    col = lax.rem(lax.broadcasted_iota(jnp.int32, (rows, s.chan), 0), s.cols)

    def one(sector, carry):
        before = west_ref[lax.rem(sector + s.sectors - 1, s.sectors)]
        after = east_ref[lax.rem(sector + 1, s.sectors)]
        west = jnp.where(
            col == 0, pltpu.roll(before, rows - (s.cols - 1), 0), pltpu.roll(west_ref[sector], 1, 0)
        )
        east = jnp.where(
            col == s.cols - 1,
            pltpu.roll(after, s.cols - 1, 0),
            pltpu.roll(east_ref[sector], rows - 1, 0),
        )
        out_ref[sector] = (west + mid_ref[sector] + east).astype(BF)
        return carry

    lax.fori_loop(0, s.sectors, one, 0)


def group_blocks(s, sc, color):
    half = s.group // 2
    for side in range(2):
        for slot in range(half):
            j = 2 * slot + side if color == 0 else side * half + slot
            yield side, slot, sc[GRP] ^ j


def trunk_head(s, scalars, hown, terms, w_head, cot_cat):
    rows = s.half

    def body(sc, near, far, a, b, c, wh0, wh1, cat, home_ref, grad_ref, gain_ref, h2, y0, y1, y2):
        own = sc[ME] // (s.members // 2)
        gains = []
        for half, h1 in enumerate((near, far)):
            side = own ^ half
            total = three_terms(a[0, half, :rows, :], b[0, half, :rows, :], c[0, 1 - half, :rows, :])
            h2[pl.ds(pl.multiple_of(side * rows, rows), rows), :] = (h1[...] + total).astype(BF)
            at = slice(rows, rows + 8)
            gains.append(three_terms(a[0, half, at, :], b[0, half, at, :], c[0, 1 - half, at, :]))
        gain_ref[...] = gains[0] + gains[1]
        for j, ref in enumerate((y0, y1, y2)):
            weight = jnp.concatenate([wh0[j], wh1[j]], axis=1)
            ref[...] = dot(h2[...], weight, NT).reshape(s.sectors, s.sec_tokens, s.chan)
        shift_all(s, (y0, y1, y2), home_ref)
        grad_ref[...] = dot(h2[...], cat[...], TN)

    def part(k):
        return (w_head, (3, s.chan, s.db), lambda i, sc: (0, 0, k * s.members + sc[ME]))

    return kernel(
        body,
        "trunk_head",
        scalars,
        (1,),
        [whole(x) for x in hown]
        + [first(x) for x in terms]
        + [part(0), part(1), whole(cot_cat)],
        [
            whole_out((s.sectors, s.sec_tokens, s.chan), BF),
            whole_out((s.dn, 3 * s.chan), F32),
            whole_out((8, s.dn), F32),
        ],
        [pltpu.VMEM((s.tokens, s.dn), BF)]
        + [pltpu.VMEM((s.sectors, s.sec_tokens, s.chan), F32) for _ in range(3)],
    )


def embed_back(s, scalars, g1, own, stats, hidden0, gain, w_embed, in_cat, head_home, head_part, gain2, bias):
    wide = 3 * s.chan
    span = s.dn

    def body(sc, *refs):
        a, b, c, own_ref, st_ref, h0, h1, g, we0, we1, cat, home, head, gain2_ref, bias_ref = refs[:15]
        keep, send = refs[15:17]
        edges = refs[17 : 17 + s.group]
        grad, stat, y0, y1, y2, ours, part, smalls = refs[17 + s.group :]
        lines = slice(s.tokens, s.tokens + 16)
        total = three_terms(a[0, lines, :], b[0, lines, :], c[0, lines, :]) * np.float32(1.0 / s.d)
        for n in range(s.tokens // span):
            pair = [total[n : n + 1, :], total[s.tokens // span + n : s.tokens // span + n + 1, :]]
            pair = jnp.concatenate(pair + [jnp.zeros((LANES - 2, span), F32)], axis=0)
            stat[n * span : (n + 1) * span, :] = jnp.transpose(pair)
        gain_own = jnp.concatenate(
            [
                g[:, pl.ds(pl.multiple_of((k * s.members + sc[ME]) * s.db, s.db), s.db)]
                for k in range(s.teams)
            ],
            axis=1,
        )
        chunk = s.sec_tokens

        def rows_chunk(i, acc):
            at = pl.ds(pl.multiple_of(i * chunk, chunk), chunk)
            mean, rstd = st_ref[at, 0:1], st_ref[at, 1:2]
            one, two = stat[at, 0:1], stat[at, 1:2]
            g1 = three_terms(a[0, at, :], b[0, at, :], c[0, at, :])
            x = (jnp.concatenate([h0[at, :], h1[at, :]], axis=1) - mean) * rstd
            back = g1 * gain_own - one - x * two
            grad[at, :] = (own_ref[at, :].astype(F32) + rstd * back).astype(BF)
            return acc + jnp.sum(g1 * x, axis=0, keepdims=True)

        gain1 = lax.fori_loop(0, s.tokens // chunk, rows_chunk, jnp.zeros((1, s.dn), F32))
        for j, ref in enumerate((y0, y1, y2)):
            weight = jnp.concatenate([we0[j], we1[j]], axis=1)
            ref[...] = dot(grad[...], weight, NT).reshape(s.sectors, s.sec_tokens, s.chan)
        shift_all(s, (y2, y1, y0), ours)
        for odd, ref in ((0, keep), (1, send)):
            for n in range(s.members // 2):
                for team in range(s.teams):
                    sector = team * s.members + (sc[ME] ^ (2 * n + odd))
                    ref[n, team, 0] = home[sector]
                    ref[n, team, 1] = ours[sector]
        part[:, :wide] = head[...]
        part[:, wide : 2 * wide] = dot(grad[...], cat[...], TN)
        size = s.db // s.group
        for k in range(s.teams):
            lines = [
                bias_ref[:, k * s.fb + n * LANES : k * s.fb + (n + 1) * LANES] for n in range(s.fb // LANES)
            ]
            lines += [gain1[:, k * s.db : (k + 1) * s.db], gain2_ref[0:1, k * s.db : (k + 1) * s.db]]
            lines += [jnp.zeros((size - len(lines), LANES), F32)]
            smalls[...] = jnp.concatenate(lines, axis=0).astype(BF)
            for j, ref in enumerate(edges):
                at = pl.ds(pl.multiple_of(k * s.db + (sc[GRP] ^ j) * size, size), size)
                ref[k, :, : 2 * wide] = part[at, :].astype(BF)
                ref[k, :, 2 * wide :] = smalls[...]

    def part_of(k):
        return (w_embed, (3, s.chan, s.db), lambda i, sc: (0, 0, k * s.members + sc[ME]))

    def own_of(k):
        return (hidden0, (s.tokens, s.db), lambda i, sc: (0, k * s.members + sc[ME]))

    goes = (s.members // 2, s.teams, 2, s.sec_tokens, s.chan)
    size = s.db // s.group
    block = (s.teams, size, 2 * wide + LANES)
    return kernel(
        body,
        "embed_back",
        scalars,
        (1,),
        [first(x) for x in g1]
        + [whole(own), whole(stats), own_of(0), own_of(1), whole(gain), part_of(0), part_of(1)]
        + [whole(in_cat), whole(head_home), whole(head_part), whole(gain2), whole(bias)],
        [whole_out(goes, BF), whole_out(goes, BF)] + [whole_out(block, BF)] * s.group,
        [pltpu.VMEM((s.tokens, s.dn), BF), pltpu.VMEM((s.tokens, LANES), F32)]
        + [pltpu.VMEM((s.sectors, s.sec_tokens, s.chan), F32) for _ in range(3)]
        + [pltpu.VMEM((s.sectors, s.sec_tokens, s.chan), BF)]
        + [pltpu.VMEM((s.dn, 2 * wide), F32), pltpu.VMEM((size, LANES), BF)],
    )


def mlp_weight_grads(s, scalars, near, far, grad_mlp):
    sub = s.fb // s.group

    def body(sc, an, pn, nn_ref, af, pf, nf, gn, gf, ka, sa, kb, sb, scr):
        color = pl.program_id(0)
        kind = pl.program_id(1)

        @pl.when(kind == 0)
        def _():
            scr[...] = (dot(an[...], gn[...], TN) + dot(af[...], gf[...], TN)).astype(BF)

        @pl.when(kind == 1)
        def _():
            scr[...] = (dot(pn[...], nn_ref[...], TN) + dot(pf[...], nf[...], TN)).astype(BF)

        for k, refs in enumerate(((ka, sa), (kb, sb))):

            @pl.when(color == k)
            def _():
                def lane_block(c, carry):
                    lanes = pl.ds(pl.multiple_of(c * LANES, LANES), LANES)
                    to = pl.ds(pl.multiple_of(c * sub, sub), sub)
                    for side, slot, q in group_blocks(s, sc, k):
                        rows = pl.ds(pl.multiple_of(q * sub, sub), sub)
                        refs[side][slot, 0, to, :] = scr[rows, lanes]
                    return carry

                lax.fori_loop(0, s.d // LANES, lane_block, 0)

    def out(color):
        shape = (s.group // 2, 2, s.d, LANES)
        block = (s.group // 2, 1, s.d, LANES)
        if color == 0:
            index = lambda k, kind, sc: (0, jnp.where(k == 0, kind, 1), 0, 0)
        else:
            index = lambda k, kind, sc: (0, jnp.where(k == 0, 0, kind), 0, 0)
        return (shape, BF, block, index)

    cols = lambda k, kind, sc: (0, k)
    ins = []
    for activ, grad_pre, normed in (near, far):
        ins += [
            (activ, (s.half, s.fb), cols),
            (grad_pre, (s.half, s.fb), cols),
            whole(normed),
        ]
    ins += [
        (grad_mlp, (s.half, s.d), lambda k, kind, sc: (side_of(s, sc, False), 0)),
        (grad_mlp, (s.half, s.d), lambda k, kind, sc: (side_of(s, sc, True), 0)),
    ]
    return kernel(
        body,
        "mlp_weight_grads",
        scalars,
        (s.teams, 2),
        ins,
        [out(0), out(0), out(1), out(1)],
        [pltpu.VMEM((s.fb, s.d), BF)],
    )


def attention_weight_grads(s, scalars, normed1, dq, dkv, att_near, att_far, own):
    def body(sc, n1, dq_ref, dkv_ref, an, af, own_near, own_far, ka, sa, kb, sb, scr):
        scr[: s.width] = dot(dq_ref[...], n1[...], TN).astype(BF)
        scr[s.width : 3 * s.width] = dot(dkv_ref[...], n1[...], TN).astype(BF)
        scr[3 * s.width :] = (dot(own_near[...], an[...], TN) + dot(own_far[...], af[...], TN)).astype(BF)

        def lane_block(c, carry):
            lanes = pl.ds(pl.multiple_of(c * LANES, LANES), LANES)
            for k, refs in enumerate(((ka, sa), (kb, sb))):
                for side, slot, q in group_blocks(s, sc, k):
                    rows = pl.ds(pl.multiple_of((k * s.group + q) * LANES, LANES), LANES)
                    refs[side][slot, lanes, :] = scr[rows, lanes]
            return carry

        lax.fori_loop(0, s.d // LANES, lane_block, 0)

    shape = (s.group // 2, s.d, LANES)
    return kernel(
        body,
        "attention_weight_grads",
        scalars,
        (1,),
        [
            whole(normed1),
            whole(dq),
            whole(dkv),
            whole(att_near),
            whole(att_far),
            (own, (s.half, s.dn), lambda i, sc: (side_of(s, sc, False), 0)),
            (own, (s.half, s.dn), lambda i, sc: (side_of(s, sc, True), 0)),
        ],
        [whole_out(shape, BF)] * 4,
        [pltpu.VMEM((3 * s.width + s.dn, s.d), BF)],
    )


def add_low(a, b):
    return (a.astype(F32) + b.astype(F32)).astype(BF)


def first(x):
    rank = len(x.shape)
    return (x, (1,) + tuple(x.shape[1:]), lambda *_: (0,) * rank)


def three_terms(keep, got, more):
    return keep.astype(F32) + got.astype(F32) + more.astype(F32)


def group_first(keep_a, send_a, keep_b, send_b):
    got_a = swap(send_a, "grp", 1)
    got_b = swap(send_b, "grp", 2)
    return (keep_a, got_a), (keep_b, got_b), (add_low(keep_a[1], got_a[1]), add_low(keep_b[1], got_b[1]))


def group_second(terms_a, terms_b, sends):
    more_a = swap(sends[0], "grp", 2)
    more_b = swap(sends[1], "grp", 1)
    return terms_a + (more_a[None],), terms_b + (more_b[None],)


def pick_team(s, scalars, terms_a, terms_b, kinds):
    half = s.d // 2

    def body(sc, *refs):
        a, b = refs[:3], refs[3:6]
        keep, send = refs[6:]
        team = sc[TEAM]

        def total(terms, k, rows):
            at = (0, k, rows) if kinds == 2 else (0, rows)
            return three_terms(*[ref[at] for ref in terms]).astype(BF)

        if kinds == 2:
            for side in range(2):

                @pl.when(team == side)
                def _():
                    same, other = (a, b) if side == 0 else (b, a)
                    keep[0] = total(same, 0, slice(None))
                    send[0] = total(other, 0, slice(None))

        mine = pl.ds(pl.multiple_of(team * half, half), half)
        theirs = pl.ds(pl.multiple_of((1 - team) * half, half), half)
        for color, terms in enumerate((a, b)):
            at = slice(color * half, (color + 1) * half)
            keep[kinds - 1, at] = total(terms, 1, mine)
            send[kinds - 1, at] = total(terms, 1, theirs)

    return kernel(
        body,
        "pick_team",
        scalars,
        (1,),
        [first(x) for x in terms_a + terms_b],
        [whole_out((kinds, s.d, LANES), BF)] * 2,
    )


def pick_member(s, scalars, keep, got):
    kinds = keep.shape[0]
    half = s.d // 2

    def body(sc, k_ref, g_ref, *refs):
        for j in range(s.members):
            m = sc[ME] ^ j
            for color in range(2):
                at = pl.ds(pl.multiple_of(color * half + m * s.db, s.db), s.db)
                value = k_ref[kinds - 1, at].astype(F32) + g_ref[kinds - 1, at].astype(F32)
                refs[j][color] = value.astype(BF)
        if kinds == 2:
            refs[s.members][...] = (k_ref[0].astype(F32) + g_ref[0].astype(F32)).astype(BF)

    outs = [whole_out((2, s.db, LANES), BF)] * s.members
    if kinds == 2:
        outs = outs + [whole_out((s.d, LANES), BF)]
    return kernel(body, "pick_member", scalars, (1,), [whole(keep), whole(got)], outs)


def all_of_group(x, x_first):
    near, far = (1, 2) if x_first else (2, 1)
    one = swap(x, "grp", near)
    two = swap(x, "grp", far)
    both = swap(one, "grp", far)
    return [x, one, two, both] if x_first else [x, two, one, both]


def cross(s, pieces):
    got = [pieces[0]] + [swap(pieces[j], "sec", j) for j in range(1, s.members)]
    return jnp.stack(got)


def mlp_grads_out(s, scalars, downs, ups):
    sub = s.fb // s.group

    def body(sc, *refs):
        d_refs, u_refs = refs[: s.group], refs[s.group : 2 * s.group]
        down, up = refs[2 * s.group :]
        for j in range(s.group):
            q = sc[GRP] ^ j
            rows = pl.ds(pl.multiple_of(q * sub, sub), sub)
            for c in range(s.d // LANES):
                down[rows, c * LANES : (c + 1) * LANES] = d_refs[j][c * sub : (c + 1) * sub, :].astype(F32)

            def member(jm, carry):
                m = sc[ME] ^ jm
                for color in range(s.teams):
                    at = ((color * s.members + m) * s.group + q) * LANES
                    up[:, pl.ds(pl.multiple_of(at, LANES), LANES)] = jnp.transpose(u_refs[j][jm, color].astype(F32))
                return carry

            lax.fori_loop(0, s.members, member, 0)

    return kernel(
        body,
        "mlp_grads_out",
        scalars,
        (1,),
        [whole(x) for x in downs + ups],
        [whole_out((s.fb, s.d), F32), whole_out((s.db, s.ff), F32)],
    )


def attention_grads_out(s, scalars, parts):
    def body(sc, *refs):
        u_refs = refs[: s.group]
        qkv, out = refs[s.group :]
        for j in range(s.group):
            q = sc[GRP] ^ j

            def member(jm, carry):
                m = sc[ME] ^ jm
                at = (q // 2) * s.d + m * s.width + lax.rem(q, 2) * LANES
                value = jnp.transpose(u_refs[j][jm, 0].astype(F32))
                qkv[:, pl.ds(pl.multiple_of(at, LANES), LANES)] = value
                other = jnp.transpose(u_refs[j][jm, 1].astype(F32))

                @pl.when(q < 2)
                def _():
                    at = 2 * s.d + m * s.width + q * LANES
                    qkv[:, pl.ds(pl.multiple_of(at, LANES), LANES)] = other

                @pl.when(q >= 2)
                def _():
                    at = ((q - 2) * s.members + m) * s.db
                    out[:, pl.ds(pl.multiple_of(at, LANES), LANES)] = other

                return carry

            lax.fori_loop(0, s.members, member, 0)

    return kernel(
        body,
        "attention_grads_out",
        scalars,
        (1,),
        [whole(x) for x in parts],
        [whole_out((s.db, 3 * s.d), F32), whole_out((s.db, s.d), F32)],
    )


def edge_grads_out(s, scalars, parts):
    wide = 3 * s.chan
    size = s.db // s.group

    def body(sc, *refs):
        ins = refs[: s.group]
        embed, head, small, scr = refs[s.group :]
        for j in range(s.group):
            at = pl.ds(pl.multiple_of((sc[GRP] ^ j) * size, size), size)
            scr[at, :] = ins[j][...].astype(F32)
        head[...] = jnp.transpose(scr[:, :wide])
        embed[...] = jnp.transpose(scr[:, wide : 2 * wide])
        small[...] = ins[0][:16, 2 * wide :].astype(F32)

    return kernel(
        body,
        "edge_grads_out",
        scalars,
        (1,),
        [whole(x) for x in parts],
        [
            whole_out((wide, s.db), F32),
            whole_out((wide, s.db), F32),
            whole_out((16, LANES), F32),
        ],
        [pltpu.VMEM((s.db, 2 * wide + LANES), F32)],
    )


def on_team(
    fields,
    valid_rows,
    w_embed,
    ln1_gain,
    w_qkv,
    w_out,
    ln2_gain,
    w_up,
    b_up,
    w_down,
    w_head,
    cotangent,
):
    s = Sizes(fields, w_qkv, w_up)
    place = lax.axis_index("sec")
    team, me = place // s.members, place % s.members
    core, chip = 1, 2
    first_team = team == 0
    valid = jnp.where(first_team, valid_rows[0], valid_rows[1])
    scalars = (jnp.stack([team, me, lax.axis_index("grp"), valid]).astype(jnp.int32), [])

    def gather_pair(x):
        flat = x.reshape(s.teams, s.sec_tokens, s.chan)
        mine = jnp.where(first_team, flat[0], flat[1])
        other = swap(jnp.where(first_team, flat[1], flat[0]), "sec", s.members)
        return jnp.stack([mine, other])

    def gather_sample(pair):
        across = swap(pair, "sec", chip)
        return [pair, swap(pair, "sec", core), across, swap(across, "sec", core)]

    def go_home(keep, got, far):
        mine = three_terms(keep[0], got[0], far)
        other = jnp.where(first_team, mine[1], mine[0]).astype(BF)
        return mine, swap(other, "sec", s.members)

    def at_home(mine, other):
        own = jnp.where(first_team, mine[0], mine[1])
        other = other.astype(F32)
        both = [jnp.where(first_team, own, other), jnp.where(first_team, other, own)]
        return [jnp.stack([x[kind] for x in both]).reshape(fields.shape) for kind in range(2)]

    def scatter_features(keep, send):
        got = swap(send, "sec", core)
        return keep, got, swap(add_low(keep[1:2], got[1:2]), "sec", chip)

    w_head_t = jnp.transpose(w_head, (0, 2, 1))
    fields_pair = gather_pair(fields)
    late1, late2, b_up = after([ln1_gain, ln2_gain, b_up], fields_pair)
    gain1 = late1.astype(F32)[None]
    gain2 = late2.astype(F32)[None]
    in_cat, hidden0, normed1, qkv, stats = embed_qkv(
        s, scalars, gather_sample(fields_pair), w_embed.reshape(3 * s.chan, s.d), gain1, w_qkv
    )
    att_near, *rest = attention_fwd(s, scalars, qkv, False)
    saved_near = (att_near, *rest)
    from_chip_far = swap(att_near, "sec", chip)
    att_far, *rest = attention_fwd(s, scalars, qkv, True)
    saved_far = (att_far, *rest)
    from_chip_near = swap(att_far, "sec", chip)
    hold(scalars, from_chip_far)
    cot_cat, grad_mlp = cotangent_grad(
        s, scalars, gather_sample(gather_pair(cotangent)), w_head_t.reshape(3 * s.chan, s.d)
    )
    att_pieces_far = [att_far, swap(att_far, "sec", core), from_chip_far, swap(from_chip_far, "sec", core)]
    att_pieces_near = [att_near, swap(att_near, "sec", core), from_chip_near, swap(from_chip_near, "sec", core)]

    def run_mlp(pieces, far):
        return mlp(s, scalars, pieces, hidden0, grad_mlp, w_out, gain2, w_up, b_up, w_down, far)

    attended_far, normed2_far, activ_far, pre_far, gkeep, gsend, gsum, hown_far, bias_far, _ = run_mlp(
        att_pieces_far, True
    )
    hold(scalars, from_chip_near)
    g2_chip = [swap(gkeep, "sec", chip), swap(gsend, "sec", chip + core)]
    attended_near, normed2_near, activ_near, pre_near, gkeep, gsend, gsum_near, hown_near, bias_near, hidden1 = run_mlp(
        att_pieces_near, False
    )
    bias_grad = bias_far + bias_near
    got = swap(gsend, "sec", core)
    pkeep, psend = trunk_part(s, scalars, ((activ_near, gsum_near), (activ_far, gsum)), w_down)
    b0 = norm_two_back(s, scalars, [gkeep, got, *g2_chip], hidden1, grad_mlp, gain2)
    b1 = swap(b0, "sec", core)
    b2 = swap(b0, "sec", chip)
    b3 = swap(b2, "sec", core)
    mlp_blocks = mlp_weight_grads(
        s, scalars, (activ_near, pre_near, normed2_near), (activ_far, pre_far, normed2_far), grad_mlp
    )
    hold(scalars, b2)
    mlp_a, mlp_b, mlp_sends = group_first(*mlp_blocks)
    before = attention_bwd(s, scalars, qkv, saved_near, (b0, b1), w_out, False)
    hold(scalars, b3, *mlp_sends)
    mlp_terms = group_second(mlp_a, mlp_b, mlp_sends)
    trunk_terms = scatter_features(pkeep, psend)
    dq, own, dkv = attention_bwd(s, scalars, qkv, saved_far, (b2, b3), w_out, True, before)
    hold(scalars, *[terms[2] for terms in mlp_terms])
    att_blocks = attention_weight_grads(s, scalars, normed1, dq, dkv, attended_near, attended_far, own)
    att_a, att_b, att_sends = group_first(*att_blocks)
    mlp_kept, send = pick_team(s, scalars, *mlp_terms, 2)
    mlp_swapped = swap(send, "sec", s.members)
    g1_keep, g1_send = norm_one_grad(s, scalars, qkv, dq, dkv, w_qkv, gain1)
    hold(scalars, *att_sends)
    att_terms = group_second(att_a, att_b, att_sends)
    hold(scalars, trunk_terms[2])
    head_home, head_part, gain2_grad = trunk_head(
        s, scalars, (hown_near, hown_far), trunk_terms, w_head_t, cot_cat
    )
    g1_got = swap(g1_send, "sec", core)
    g1_sum = add_low(g1_keep[1:2], g1_got[1:2])
    g1 = (g1_keep, g1_got, swap(g1_sum, "sec", chip))
    hold(scalars, g1_sum, *[terms[2] for terms in att_terms])
    att_kept, send = pick_team(s, scalars, *att_terms, 1)
    att_swapped = swap(after([send], g1[2])[0], "sec", s.members)
    *crossed, downs = pick_member(s, scalars, mlp_kept, mlp_swapped)
    crossed = [crossed[0]] + [swap(crossed[j], "sec", j) for j in range(1, s.members)]
    downs = [downs, swap(downs, "grp", 1), swap(downs, "grp", 2)]
    keep, send, *edges = embed_back(
        s, scalars, g1, own, stats, hidden0, gain1, w_embed, in_cat, head_home, head_part, gain2_grad, bias_grad
    )
    edges = edges[:1] + [swap(edges[j], "grp", j) for j in range(1, s.group)]
    home_got = swap(send, "sec", core)
    ups = jnp.stack(after(crossed, edges[0]))
    ups = [ups, swap(ups, "grp", 1), swap(ups, "grp", 2)]
    mlp_parts = (
        downs + [swap(after(downs[2:], edges[0])[0], "grp", 1)],
        ups + [swap(ups[1], "grp", 2)],
    )
    crossed = pick_member(s, scalars, att_kept, att_swapped)
    att_parts = all_of_group(cross(s, crossed), True)
    home_far = swap(add_low(keep[1], home_got[1]), "sec", chip)
    down_grad, up_grad = mlp_grads_out(s, scalars, *mlp_parts)
    hold(scalars, home_far)
    home_mine, home_other = go_home(keep, home_got, home_far)

    total = edges[0].astype(F32) + edges[1].astype(F32) + edges[2].astype(F32) + edges[3].astype(F32)
    kept = jnp.where(first_team, total[0], total[1])
    given = jnp.where(first_team, total[1], total[0]).astype(BF)
    edges = (kept + swap(given, "sec", s.members).astype(F32)).astype(BF)
    edge_parts = all_of_group(edges, True)
    qkv_grad, out_grad = attention_grads_out(s, scalars, att_parts)
    hold(scalars, home_other)
    head_output, input_grad = at_home(home_mine, home_other)
    embed_t, head_t, small = edge_grads_out(s, scalars, edge_parts)
    embed_grad = embed_t.reshape(3, s.chan, s.db)
    head_grad = jnp.transpose(head_t.reshape(3, s.chan, s.db), (0, 2, 1))
    nb = s.fb // LANES
    return (
        head_output,
        input_grad,
        embed_grad,
        small[nb],
        qkv_grad,
        out_grad,
        small[nb + 1],
        up_grad,
        small[:nb].reshape(s.fb),
        down_grad,
        head_grad,
    )

LAT = 32
KCOLS = 8


def extended(cells, sides, width):
    for axis, dim in sides:
        count = lax.axis_size(axis)
        head = lax.slice_in_dim(cells, 0, width, axis=dim)
        tail = lax.slice_in_dim(cells, cells.shape[dim] - width, cells.shape[dim], axis=dim)
        cells = jnp.concatenate(
            [
                lax.ppermute(tail, axis, [(i, (i + 1) % count) for i in range(count)]),
                cells,
                lax.ppermute(head, axis, [((i + 1) % count, i) for i in range(count)]),
            ],
            axis=dim,
        )
    return cells


def normed(hidden, gains):
    center = hidden - jnp.mean(hidden, axis=-1, keepdims=True)
    spread = jnp.mean(center * center, axis=-1, keepdims=True)
    return center * lax.rsqrt(spread + 1e-05) * gains


def gelu_exact(values):
    return jax.nn.gelu(values, approximate=False)


def three_cols(padded, col_count, west_first):
    west_cols = padded[:, :, 0:col_count]
    middle_cols = padded[:, :, 1 : col_count + 1]
    east_cols = padded[:, :, 2 : col_count + 2]
    if west_first:
        return jnp.stack([west_cols, middle_cols, east_cols], axis=3)
    return jnp.stack([east_cols, middle_cols, west_cols], axis=3)


def split_heads(values):
    return values.reshape(values.shape[0], -1, HEADS, HEAD_DIM)


def key_mask(valid_rows, count_cols):
    rows_ok = jnp.arange(LAT)[None, :] < valid_rows[:, None]
    spread_ok = jnp.broadcast_to(rows_ok[:, :, None], (rows_ok.shape[0], LAT, count_cols))
    return spread_ok.reshape(rows_ok.shape[0], LAT * count_cols)


def key_scores(queries, kv_piece, valid_rows):
    d_model = HEADS * HEAD_DIM
    key_part = split_heads(kv_piece[..., :d_model])
    value_part = split_heads(kv_piece[..., d_model:])
    scores = (
        jnp.einsum("sqhd,skhd->shqk", queries, key_part, preferred_element_type=jnp.float32) * 0.125
    )
    allowed = key_mask(valid_rows, kv_piece.shape[2])
    scores = jnp.where(allowed[:, None, None, :], scores, -1e30)
    return (scores, key_part, value_part)


def softmax_fold(queries, valid_rows):

    def fold_piece(run_state, kv_piece, first_col):
        run_max, run_sum, run_acc = run_state
        scores, key_part, value_part = key_scores(queries, kv_piece, valid_rows)
        new_max = jnp.maximum(run_max, jnp.max(scores, axis=-1))
        factor = jnp.exp(run_max - new_max)
        weights = jnp.exp(scores - new_max[..., None])
        new_sum = run_sum * factor + jnp.sum(weights, axis=-1)
        added = jnp.einsum(
            "shqk,skhd->sqhd",
            weights.astype(jnp.bfloat16),
            value_part,
            preferred_element_type=jnp.float32,
        )
        new_acc = run_acc * jnp.transpose(factor, (0, 2, 1))[..., None] + added
        return (new_max, new_sum, new_acc)

    return fold_piece


def on_sectors(
    fields,
    valid_rows,
    w_embed,
    ln1_gain,
    w_qkv,
    w_out,
    ln2_gain,
    w_up,
    b_up,
    w_down,
    w_head,
    cotangent,
):
    samples, lat_rows, col_count, channels = fields.shape
    d_model = w_qkv.shape[0]
    token_count = lat_rows * col_count
    padded_in = extended(fields, (("sec", 2),), 1)
    input_cat = three_cols(padded_in, col_count, True)
    hidden0 = jnp.einsum("slcoi,oid->slcd", input_cat, w_embed, preferred_element_type=jnp.float32)
    normed_one, norm_one_back = jax.vjp(normed, hidden0, ln1_gain.astype(jnp.float32))
    normed_one_low = normed_one.astype(jnp.bfloat16)
    qkv_full = jnp.einsum(
        "slcd,de->slce", normed_one_low, w_qkv, preferred_element_type=jnp.float32
    ).astype(jnp.bfloat16)
    queries = split_heads(qkv_full[..., :d_model])
    key_vals = qkv_full[..., d_model:]
    init_state = (
        jnp.full((samples, HEADS, token_count), -1e30, jnp.float32),
        jnp.zeros((samples, HEADS, token_count), jnp.float32),
        jnp.zeros((samples, token_count, HEADS, HEAD_DIM), jnp.float32),
    )
    fold_piece = softmax_fold(queries, valid_rows)
    all_kv = lax.all_gather(key_vals, "sec", axis=2, tiled=True)

    def forward_block(block_index, run_state):
        kv_block = lax.dynamic_slice_in_dim(all_kv, block_index * KCOLS, KCOLS, 2)
        return fold_piece(run_state, kv_block, block_index * KCOLS)

    run_max, run_sum, run_acc = lax.fori_loop(
        0, all_kv.shape[2] // KCOLS, forward_block, init_state
    )
    attended = run_acc / jnp.transpose(run_sum, (0, 2, 1))[..., None]
    log_total = run_max + jnp.log(run_sum)
    attended_low = attended.reshape(samples, lat_rows, col_count, d_model).astype(jnp.bfloat16)
    hidden1 = hidden0 + jnp.einsum(
        "slcd,de->slce", attended_low, w_out, preferred_element_type=jnp.float32
    )
    normed_two, norm_two_back = jax.vjp(normed, hidden1, ln2_gain.astype(jnp.float32))
    normed_two_low = normed_two.astype(jnp.bfloat16)
    preact = jnp.einsum(
        "slcd,df->slcf", normed_two_low, w_up, preferred_element_type=jnp.float32
    ) + b_up.astype(jnp.float32)
    activ, gelu_back = jax.vjp(gelu_exact, preact)
    activ_low = activ.astype(jnp.bfloat16)
    hidden2 = hidden1 + jnp.einsum(
        "slcf,fd->slcd", activ_low, w_down, preferred_element_type=jnp.float32
    )
    hidden2_low = hidden2.astype(jnp.bfloat16)
    padded_hidden = extended(hidden2_low, (("sec", 2),), 1)
    hidden_cat = three_cols(padded_hidden, col_count, True)
    head_output = jnp.einsum(
        "slcod,odi->slci", hidden_cat, w_head, preferred_element_type=jnp.float32
    )
    padded_cot = extended(cotangent, (("sec", 2),), 1)
    cot_cat = three_cols(padded_cot, col_count, False)
    head_grad = jnp.einsum(
        "slcod,slci->odi", hidden_cat, cotangent, preferred_element_type=jnp.float32
    )
    grad_two = jnp.einsum("slcoi,odi->slcd", cot_cat, w_head, preferred_element_type=jnp.float32)
    grad_mlp = grad_two.astype(jnp.bfloat16)
    down_grad = jnp.einsum("slcf,slcd->fd", activ_low, grad_mlp, preferred_element_type=jnp.float32)
    grad_act = jnp.einsum("slcd,fd->slcf", grad_mlp, w_down, preferred_element_type=jnp.float32)
    grad_pre = gelu_back(grad_act)[0].astype(jnp.bfloat16)
    bias_grad = jnp.sum(grad_pre.astype(jnp.float32), axis=(0, 1, 2))
    up_grad = jnp.einsum(
        "slcd,slcf->df", normed_two_low, grad_pre, preferred_element_type=jnp.float32
    )
    grad_normed_two = jnp.einsum(
        "slcf,df->slcd", grad_pre, w_up, preferred_element_type=jnp.float32
    )
    grad_from_norm, gain_two_grad = norm_two_back(grad_normed_two)
    grad_one = grad_two + grad_from_norm
    grad_att = grad_one.astype(jnp.bfloat16)
    out_grad = jnp.einsum(
        "slcd,slce->de", attended_low, grad_att, preferred_element_type=jnp.float32
    )
    grad_heads = split_heads(
        jnp.einsum("slce,de->slcd", grad_att, w_out, preferred_element_type=jnp.float32).astype(
            jnp.bfloat16
        )
    )
    row_delta = jnp.transpose(
        jnp.sum(grad_heads.astype(jnp.float32) * attended, axis=-1), (0, 2, 1)
    )

    def sample_backward(unused_carry, sample_in):
        one_query, one_grad, one_lse, one_delta, one_valid, one_kv = sample_in
        term_zero = jnp.zeros((1, lat_rows, one_kv.shape[2], 2 * d_model), jnp.bfloat16)
        grad_zero = jnp.zeros(one_query.shape, jnp.float32)

        def backward_block(block_index, run_state):
            grad_query, term = run_state
            kv_block = lax.dynamic_slice_in_dim(one_kv, block_index * KCOLS, KCOLS, 2)
            scores, key_part, value_part = key_scores(one_query, kv_block, one_valid)
            probs = jnp.exp(scores - one_lse[..., None])
            grad_probs = jnp.einsum(
                "sqhd,skhd->shqk", one_grad, value_part, preferred_element_type=jnp.float32
            )
            grad_scores = (probs * (grad_probs - one_delta[..., None])).astype(jnp.bfloat16)
            grad_query = (
                grad_query
                + jnp.einsum(
                    "shqk,skhd->sqhd", grad_scores, key_part, preferred_element_type=jnp.float32
                )
                * 0.125
            )
            grad_keys = (
                jnp.einsum(
                    "shqk,sqhd->skhd", grad_scores, one_query, preferred_element_type=jnp.float32
                )
                * 0.125
            )
            grad_values = jnp.einsum(
                "shqk,sqhd->skhd",
                probs.astype(jnp.bfloat16),
                one_grad,
                preferred_element_type=jnp.float32,
            )
            joined = jnp.concatenate(
                [
                    grad_keys.reshape(1, lat_rows, KCOLS, d_model),
                    grad_values.reshape(1, lat_rows, KCOLS, d_model),
                ],
                axis=-1,
            ).astype(jnp.bfloat16)
            term = lax.dynamic_update_slice_in_dim(term, joined, block_index * KCOLS, 2)
            return (grad_query, term)

        grad_query, term = lax.fori_loop(
            0, one_kv.shape[2] // KCOLS, backward_block, (grad_zero, term_zero)
        )
        summed = lax.psum_scatter(
            term.astype(jnp.float32).astype(jnp.bfloat16), "sec", scatter_dimension=2, tiled=True
        ).astype(jnp.float32)
        return (unused_carry, (grad_query, summed))

    scan_inputs = (
        queries.reshape(samples, 1, token_count, HEADS, HEAD_DIM),
        grad_heads.reshape(samples, 1, token_count, HEADS, HEAD_DIM),
        log_total.reshape(samples, 1, HEADS, token_count),
        row_delta.reshape(samples, 1, HEADS, token_count),
        valid_rows.reshape(samples, 1),
        all_kv.reshape(samples, 1, lat_rows, all_kv.shape[2], 2 * d_model),
    )
    scan_end, (grad_queries, grad_kv) = lax.scan(sample_backward, 0, scan_inputs)
    grad_qkv = jnp.concatenate(
        [
            grad_queries.reshape(samples, lat_rows, col_count, d_model),
            grad_kv.reshape(samples, lat_rows, col_count, 2 * d_model),
        ],
        axis=-1,
    ).astype(jnp.bfloat16)
    qkv_grad = jnp.einsum(
        "slcd,slce->de", normed_one_low, grad_qkv, preferred_element_type=jnp.float32
    )
    grad_normed_one = jnp.einsum(
        "slce,de->slcd", grad_qkv, w_qkv, preferred_element_type=jnp.float32
    )
    grad_from_first, gain_one_grad = norm_one_back(grad_normed_one)
    grad_zero_low = (grad_one + grad_from_first).astype(jnp.bfloat16)
    embed_grad = jnp.einsum(
        "slcoi,slcd->oid", input_cat, grad_zero_low, preferred_element_type=jnp.float32
    )
    padded_grad = extended(grad_zero_low, (("sec", 2),), 1)
    grad_cat = three_cols(padded_grad, col_count, False)
    input_grad = jnp.einsum(
        "slcod,oid->slci", grad_cat, w_embed, preferred_element_type=jnp.float32
    )
    shard_grads = (
        lax.psum_scatter(
            embed_grad.astype(jnp.bfloat16), "sec", scatter_dimension=2, tiled=True
        ).astype(jnp.float32),
        lax.psum_scatter(
            gain_one_grad.astype(jnp.bfloat16), "sec", scatter_dimension=0, tiled=True
        ).astype(jnp.float32),
        lax.psum_scatter(
            qkv_grad.astype(jnp.bfloat16), "sec", scatter_dimension=0, tiled=True
        ).astype(jnp.float32),
        lax.psum_scatter(
            out_grad.astype(jnp.bfloat16), "sec", scatter_dimension=0, tiled=True
        ).astype(jnp.float32),
        lax.psum_scatter(
            gain_two_grad.astype(jnp.bfloat16), "sec", scatter_dimension=0, tiled=True
        ).astype(jnp.float32),
        lax.psum_scatter(
            up_grad.astype(jnp.bfloat16), "sec", scatter_dimension=0, tiled=True
        ).astype(jnp.float32),
        lax.psum_scatter(
            bias_grad.astype(jnp.bfloat16), "sec", scatter_dimension=0, tiled=True
        ).astype(jnp.float32),
        lax.psum_scatter(
            down_grad.astype(jnp.bfloat16), "sec", scatter_dimension=0, tiled=True
        ).astype(jnp.float32),
        lax.psum_scatter(
            head_grad.astype(jnp.bfloat16), "sec", scatter_dimension=1, tiled=True
        ).astype(jnp.float32),
    )
    total_grads = (
        lax.psum(shard_grads[0].astype(jnp.bfloat16), "grp").astype(jnp.float32),
        lax.psum(shard_grads[1].astype(jnp.bfloat16), "grp").astype(jnp.float32),
        lax.psum(shard_grads[2].astype(jnp.bfloat16), "grp").astype(jnp.float32),
        lax.psum(shard_grads[3].astype(jnp.bfloat16), "grp").astype(jnp.float32),
        lax.psum(shard_grads[4].astype(jnp.bfloat16), "grp").astype(jnp.float32),
        lax.psum(shard_grads[5].astype(jnp.bfloat16), "grp").astype(jnp.float32),
        lax.psum(shard_grads[6].astype(jnp.bfloat16), "grp").astype(jnp.float32),
        lax.psum(shard_grads[7].astype(jnp.bfloat16), "grp").astype(jnp.float32),
        lax.psum(shard_grads[8].astype(jnp.bfloat16), "grp").astype(jnp.float32),
    )
    return (
        head_output,
        input_grad,
        total_grads[0],
        total_grads[1],
        total_grads[2],
        total_grads[3],
        total_grads[4],
        total_grads[5],
        total_grads[6],
        total_grads[7],
        total_grads[8],
    )


def on_device(*args):
    fields, w_qkv = args[0], args[4]
    sectors = lax.axis_size("sec")
    fits = (
        fields.shape[0] == 2
        and sectors == 8
        and lax.axis_size("grp") == 4
        and w_qkv.shape[0] == sectors * LANES
    )
    return on_team(*args) if fits else on_sectors(*args)


def solution(mesh):
    tokens_in = P("grp", None, "sec", None)
    return jax.shard_map(
        on_device,
        mesh=mesh,
        in_specs=(tokens_in, P("grp")) + (P(),) * 9 + (tokens_in,),
        out_specs=(
            tokens_in,
            tokens_in,
            P(None, None, "sec"),
            P("sec"),
            P("sec", None),
            P("sec", None),
            P("sec"),
            P("sec", None),
            P("sec"),
            P("sec", None),
            P(None, "sec", None),
        ),
        check_vma=False,
    )
```

```python
import jax
import jax.numpy as jnp
import numpy as np
from jax import lax
from jax.experimental import pallas as pl
from jax.experimental.pallas import tpu as pltpu
from jax.sharding import PartitionSpec as P

HEAD_DIM = 64
HEADS = 16
LANES = 128
KEY_CHUNK = 512
VMEM_LIMIT = 48 * 1024 * 1024
BF = jnp.bfloat16
F32 = jnp.float32

NN = ((1,), (0,))
NT = ((1,), (1,))
TN = ((0,), (0,))

MICROS = {
    "embed_qkv": 9.6,
    "cotangent_grad": 6.1,
    "attention_fwd": 9.2,
    "mlp": 17.0,
    "trunk_part": 4.0,
    "norm_two_back": 4.9,
    "attention_bwd": 13.3,
    "norm_one_grad": 11.7,
    "trunk_head": 7.0,
    "embed_back": 9.0,
    "mlp_weight_grads": 11.5,
    "attention_weight_grads": 9.0,
    "pick_team": 3.4,
    "pick_member": 2.5,
    "mlp_grads_out": 4.7,
    "attention_grads_out": 3.5,
    "edge_grads_out": 2.8,
}

TEAM, ME, GRP, VALID = range(4)


def dot(a, b, dims):
    return lax.dot_general(a, b, (dims, ((), ())), preferred_element_type=F32)


def swap(x, axis, bit):
    n = lax.axis_size(axis)
    return lax.ppermute(x, axis, [(i, i ^ bit) for i in range(n)])


def kernel(body, name, scalars, grid, ins, outs, scratch=(), aliases=None):
    micros = MICROS[name]
    scalars, chain = scalars
    values = lax.optimization_barrier((scalars, *chain))[0] if chain else scalars
    def spec(block, index):
        if block is None:
            return pl.BlockSpec(memory_space=pl.ANY)
        return pl.BlockSpec(block, index)

    results = pl.pallas_call(
        body,
        grid_spec=pltpu.PrefetchScalarGridSpec(
            num_scalar_prefetch=1,
            grid=grid,
            in_specs=[spec(block, index) for _, block, index in ins],
            out_specs=[spec(block, index) for _, _, block, index in outs],
            scratch_shapes=list(scratch),
        ),
        out_shape=[jax.ShapeDtypeStruct(shape, kind) for shape, kind, _, _ in outs],
        input_output_aliases=aliases or {},
        compiler_params=pltpu.CompilerParams(vmem_limit_bytes=VMEM_LIMIT),
        cost_estimate=pl.CostEstimate(
            flops=int(micros * 1.15e9), transcendentals=0, bytes_accessed=int(micros * 3.6e6)
        ),
        name=name,
    )(values, *[array for array, _, _ in ins])
    chain[:] = [results[-1]]
    return results


def hold(scalars, *values):
    scalars[1].extend(values)


def after(values, *others):
    return list(lax.optimization_barrier((*values, *others))[: len(values)])


def whole(array):
    rank = len(array.shape)
    return (array, array.shape, lambda *_: (0,) * rank)


def whole_out(shape, kind):
    rank = len(shape)
    return (shape, kind, shape, lambda *_: (0,) * rank)


class Sizes:
    def __init__(self, fields, w_qkv, w_up):
        self.teams, self.lat, self.cols, self.chan = fields.shape
        self.sectors = lax.axis_size("sec")
        self.members = self.sectors // self.teams
        self.group = lax.axis_size("grp")
        self.d = w_qkv.shape[0]
        self.ff = w_up.shape[1]
        self.sec_tokens = self.lat * self.cols
        self.tokens = self.sectors * self.sec_tokens
        self.heads = HEADS // self.members
        self.width = self.heads * HEAD_DIM
        self.db = self.d // self.sectors
        self.fb = self.ff // self.sectors
        self.dn = self.teams * self.db
        self.fn = self.teams * self.fb
        self.own = self.tokens // self.members
        self.half = self.tokens // 2


def line_up(s, scalars, pieces, canon):
    for j, piece in enumerate(pieces):
        for k in range(s.teams):
            at = (scalars[TEAM] ^ k) * s.members + (scalars[ME] ^ j)
            canon[at] = piece[k]


def beside(s, canon, sector):
    mid = canon[sector].astype(F32)
    before = canon[lax.rem(sector + s.sectors - 1, s.sectors)].astype(F32)
    after = canon[lax.rem(sector + 1, s.sectors)].astype(F32)
    col = lax.rem(lax.broadcasted_iota(jnp.int32, mid.shape, 0), s.cols)
    rows = s.sec_tokens
    west = jnp.where(col == 0, pltpu.roll(before, rows - (s.cols - 1), 0), pltpu.roll(mid, 1, 0))
    east = jnp.where(col == s.cols - 1, pltpu.roll(after, s.cols - 1, 0), pltpu.roll(mid, rows - 1, 0))
    return west, mid, east


def row_stats(rows):
    mean = jnp.mean(rows, axis=-1, keepdims=True)
    center = rows - mean
    return mean, lax.rsqrt(jnp.mean(center * center, axis=-1, keepdims=True) + 1e-05)


def normed_rows(rows):
    mean, rstd = row_stats(rows)
    return (rows - mean) * rstd, rstd


def embed_qkv(s, scalars, pieces, w_embed, gain, w_qkv):
    rows = s.half
    per = rows // s.sec_tokens
    chunk = s.sec_tokens

    def body(sc, *refs):
        parts = refs[: s.members]
        we, g, wq, wk, wv = refs[s.members : s.members + 5]
        cat_ref, hid_ref, norm_ref, qkv_ref, stat_ref, canon = refs[s.members + 5 :]
        i = pl.program_id(0)

        @pl.when(i == 0)
        def _():
            line_up(s, sc, parts, canon)

        for p in range(per):
            at = slice(p * chunk, (p + 1) * chunk)
            west, mid, east = beside(s, canon, i * per + p)
            cat_ref[at, :] = jnp.concatenate([west, mid, east], axis=1).astype(BF)
        hid_ref[...] = dot(cat_ref[...], we[...], NN)
        lane = lax.broadcasted_iota(jnp.int32, (chunk, LANES), 1)
        for p in range(per):
            at = slice(p * chunk, (p + 1) * chunk)
            value = hid_ref[at, :]
            mean, rstd = row_stats(value)
            norm_ref[at, :] = ((value - mean) * rstd * g[...]).astype(BF)
            stat_ref[at, :] = jnp.where(lane == 0, mean, rstd)
        for k, w in enumerate((wq, wk, wv)):
            qkv_ref[:, k * s.width : (k + 1) * s.width] = dot(norm_ref[...], w[...], NN).astype(BF)

    def third(k):
        return (w_qkv, (s.d, s.width), lambda i, sc: (0, k * s.members + sc[ME]))

    row = lambda i, sc: (i, 0)
    return kernel(
        body,
        "embed_qkv",
        scalars,
        (s.tokens // rows,),
        [whole(p) for p in pieces] + [whole(w_embed), whole(gain), third(0), third(1), third(2)],
        [
            ((s.tokens, 3 * s.chan), BF, (rows, 3 * s.chan), row),
            ((s.tokens, s.d), F32, (rows, s.d), row),
            ((s.tokens, s.d), BF, (rows, s.d), row),
            ((s.tokens, 3 * s.width), BF, (rows, 3 * s.width), row),
            ((s.tokens, LANES), F32, (rows, LANES), row),
        ],
        [pltpu.VMEM((s.sectors, s.sec_tokens, s.chan), BF)],
    )


def cotangent_grad(s, scalars, pieces, w_head):
    rows = s.half
    per = rows // s.sec_tokens

    def body(sc, *refs):
        parts = refs[: s.members]
        wh, cat_ref, grad_ref, canon = refs[s.members :]
        i = pl.program_id(0)

        @pl.when(i == 0)
        def _():
            line_up(s, sc, parts, canon)

        for p in range(per):
            at = slice(p * s.sec_tokens, (p + 1) * s.sec_tokens)
            west, mid, east = beside(s, canon, i * per + p)
            cat_ref[at, :] = jnp.concatenate([east, mid, west], axis=1).astype(BF)
        grad_ref[...] = dot(cat_ref[...], wh[...], NN).astype(BF)

    row = lambda i, sc: (i, 0)
    return kernel(
        body,
        "cotangent_grad",
        scalars,
        (s.tokens // rows,),
        [whole(p) for p in pieces] + [whole(w_head)],
        [
            ((s.tokens, 3 * s.chan), BF, (rows, 3 * s.chan), row),
            ((s.tokens, s.d), BF, (rows, s.d), row),
        ],
        [pltpu.VMEM((s.sectors, s.sec_tokens, s.chan), BF)],
    )


def side_of(s, sc, far):
    own = sc[ME] // (s.members // 2)
    return own ^ 1 if far else own


def lanes_of(value, side):
    lane = lax.broadcasted_iota(jnp.int32, value.shape, 1)
    return jnp.where(lane // HEAD_DIM == side, value, jnp.zeros_like(value))


def attention_fwd(s, scalars, qkv, far):
    rows = s.own
    steps = s.half // rows
    chunk = KEY_CHUNK

    def body(sc, q_ref, kv_ref, att_ref, weight_ref, inv_ref, bias, values, buf_a, buf_b, top_a, top_b, outs, invs):
        @pl.when(pl.program_id(0) == 0)
        def _():
            key = lax.broadcasted_iota(jnp.int32, (s.tokens, LANES), 0)
            bias[...] = jnp.where(lax.rem(key, s.sec_tokens) // s.cols < sc[VALID], 0.0, -1e30)
            values[...] = jnp.transpose(kv_ref[:, 2 * s.width :].astype(F32)).astype(BF)
            invs[...] = jnp.zeros_like(invs)

        def score(p, side, buf, tops):
            at = pl.ds(pl.multiple_of(p * LANES, LANES), LANES)
            kat = pl.ds(pl.multiple_of(s.width + p * LANES, LANES), LANES)
            query = lanes_of(q_ref[:, at] * jnp.asarray(0.125, BF), side)
            top = None
            for c in range(0, s.tokens, chunk):
                rows_at = slice(c, c + chunk)
                wide = jnp.concatenate([bias[rows_at, :]] * (rows // LANES), axis=1)
                scores = dot(kv_ref[rows_at, kat], query, NT) + wide
                buf[rows_at, :] = scores
                peak = jnp.max(scores, axis=0, keepdims=True)
                top = peak if top is None else jnp.maximum(top, peak)
            tops[...] = jnp.broadcast_to(top, tops.shape)

        def weigh(p, side, buf, tops):
            h = 2 * p + side
            heads_at = pl.ds(pl.multiple_of(h * HEAD_DIM, HEAD_DIM), HEAD_DIM)
            top = tops[0:1, :]
            total = None
            out = None
            for c in range(0, s.tokens, chunk):
                at = slice(c, c + chunk)
                weights = jnp.exp(buf[at, :] - top)
                part = jnp.sum(weights, axis=0, keepdims=True)
                low = weights.astype(BF)
                weight_ref[h, 0, at, :] = low
                more = dot(values[heads_at, at], low, NN)
                total = part if total is None else total + part
                out = more if out is None else out + more
            inv = 1.0 / total
            invs[pl.ds(pl.multiple_of(h * 8, 8), 8), :] = jnp.broadcast_to(inv, (8, rows))
            outs[heads_at, :] = out * inv

        score(0, 0, buf_a, top_a)

        def pair_step(p, carry):
            weigh(p, 0, buf_a, top_a)
            score(p, 1, buf_b, top_b)

            @pl.when(p >= 0)
            def _():
                weigh(p, 1, buf_b, top_b)
                score(jnp.minimum(p + 1, s.heads // 2 - 1), 0, buf_a, top_a)

            return carry

        lax.fori_loop(0, s.heads // 2, pair_step, 0)
        att_ref[...] = jnp.transpose(outs[...]).astype(BF)
        inv_ref[...] = jnp.transpose(invs[...])

    row = lambda i, sc: (i, 0)
    return kernel(
        body,
        "attention_fwd",
        scalars,
        (steps,),
        [
            (qkv, (rows, 3 * s.width), lambda i, sc: (side_of(s, sc, far) * steps + i, 0)),
            whole(qkv),
        ],
        [
            ((s.half, s.width), BF, (rows, s.width), row),
            ((s.heads, steps, s.tokens, rows), BF, (s.heads, 1, s.tokens, rows), lambda i, sc: (0, i, 0, 0)),
            ((s.half, LANES), F32, (rows, LANES), row),
        ],
        [
            pltpu.VMEM((s.tokens, LANES), F32),
            pltpu.VMEM((s.width, s.tokens), BF),
            pltpu.VMEM((s.tokens, rows), F32),
            pltpu.VMEM((s.tokens, rows), F32),
            pltpu.VMEM((8, rows), F32),
            pltpu.VMEM((8, rows), F32),
            pltpu.VMEM((s.width, rows), F32),
            pltpu.VMEM((LANES, rows), F32),
        ],
    )


def mlp(s, scalars, att, hidden0, grad_mlp, w_out, gain, w_up, b_up, w_down, far):
    chunk = 64
    rows = s.half
    count = len(att)

    def body(sc, *refs):
        parts = refs[:count]
        h0, gm, g, bias, wo_hbm, wu_hbm, wd_hbm = refs[count : count + 7]
        outs = refs[count + 7 :]
        att_ref, n2_ref, act_ref, gpre_ref, gkeep, gsend, gsum_ref, hown, bsum, h1_ref = outs[:10]
        wo, wu, wd, pre, gact, means, rstds, sem = outs[10:]
        me = sc[ME]

        copies = [pltpu.make_async_copy(wo_hbm, wo, sem.at[0])]
        for k in range(s.teams):
            at = pl.multiple_of((k * s.members + me) * s.fb, s.fb)
            copies.append(
                pltpu.make_async_copy(
                    wu_hbm.at[:, pl.ds(at, s.fb)], wu.at[:, pl.ds(k * s.fb, s.fb)], sem.at[1 + k]
                )
            )
        for k in range(s.teams):
            at = pl.multiple_of((k * s.members + me) * s.fb, s.fb)
            copies.append(
                pltpu.make_async_copy(
                    wd_hbm.at[pl.ds(at, s.fb), :],
                    wd.at[pl.ds(k * s.fb, s.fb), :],
                    sem.at[1 + s.teams + k],
                )
            )
        for copy in copies:
            copy.start()
        for j in range(count):
            at = pl.multiple_of((me ^ j) * s.width, s.width)
            att_ref[:, pl.ds(at, s.width)] = parts[j][...]
        copies[0].wait()
        span = 512

        def by_columns(size, one):
            def step(n, carry):
                one(pl.ds(pl.multiple_of(n * span, span), span))
                return carry

            lax.fori_loop(0, size // span, step, 0)

        def attention_out(cols):
            h1_ref[:, cols] = h0[:, cols] + dot(att_ref[...], wo[:, cols], NN)

        by_columns(s.d, attention_out)

        def norm_chunk(c, carry):
            at = pl.ds(pl.multiple_of(c * chunk, chunk), chunk)
            value = h1_ref[at, :]
            mean, rstd = row_stats(value)
            n2_ref[at, :] = ((value - mean) * rstd * g[...]).astype(BF)
            means[at, :] = jnp.broadcast_to(mean, (chunk, LANES))
            rstds[at, :] = jnp.broadcast_to(rstd, (chunk, LANES))
            return carry

        lax.fori_loop(0, rows // chunk, norm_chunk, 0)
        for k in range(s.teams):
            at = pl.multiple_of((k * s.members + me) * s.db, s.db)
            hown[:, k * s.db : (k + 1) * s.db] = h1_ref[:, pl.ds(at, s.db)]
        for copy in copies[1 : 1 + s.teams]:
            copy.wait()

        def up_out(cols):
            pre[:, cols] = dot(n2_ref[...], wu[:, cols], NN)

        by_columns(s.fn, up_out)
        for copy in copies[1 + s.teams :]:
            copy.wait()

        def down_back(cols):
            gact[:, cols] = dot(gm[...], wd[cols, :], NT)

        by_columns(s.fn, down_back)

        def gelu_chunk(c, total):
            at = pl.ds(pl.multiple_of(c * chunk, chunk), chunk)
            u = pre[at, :] + bias[...]
            cdf = 0.5 * (1.0 + lax.erf(u * np.float32(2**-0.5)))
            act_ref[at, :] = (u * cdf).astype(BF)
            slope = cdf + u * jnp.exp(-0.5 * u * u) * np.float32((2 * np.pi) ** -0.5)
            low = (gact[at, :] * slope).astype(BF)
            gpre_ref[at, :] = low
            return total + jnp.sum(low.astype(F32), axis=0, keepdims=True)

        bsum[...] = lax.fori_loop(0, rows // chunk, gelu_chunk, jnp.zeros((1, s.fn), F32))

        def up_back(cols):
            pre[:, cols] = dot(gpre_ref[...], wu[cols, :], NT)

        by_columns(s.d, up_back)

        def gain_chunk(c, total):
            at = pl.ds(pl.multiple_of(c * chunk, chunk), chunk)
            mean, rstd = means[at, :], rstds[at, :]
            sums = []
            for n in range(s.d // LANES):
                cols = slice(n * LANES, (n + 1) * LANES)
                xhat = (h1_ref[at, cols] - mean) * rstd
                sums.append(jnp.sum(pre[at, cols] * xhat, axis=0, keepdims=True))
            return total + jnp.concatenate(sums, axis=1)

        gsum = lax.fori_loop(0, rows // chunk, gain_chunk, jnp.zeros((1, s.d), F32))
        mine = lax.rem(me, 2)
        keep_at = pl.ds(pl.multiple_of(mine * s.own, s.own), s.own)
        send_at = pl.ds(pl.multiple_of((1 - mine) * s.own, s.own), s.own)
        gkeep[...] = pre[keep_at, :].astype(BF)
        gsend[...] = pre[send_at, :].astype(BF)
        gsum_ref[...] = gsum

    index = lambda i, sc: (side_of(s, sc, far), 0)
    bias_own = jnp.concatenate(
        [
            lax.dynamic_slice_in_dim(b_up, (k * s.members + scalars[0][ME]) * s.fb, s.fb, 0)
            for k in range(s.teams)
        ]
    ).astype(F32)[None]
    return kernel(
        body,
        "mlp",
        scalars,
        (1,),
        [whole(a) for a in att]
        + [
            (hidden0, (rows, s.d), index),
            (grad_mlp, (rows, s.d), index),
            whole(gain),
            whole(bias_own),
            (w_out, None, None),
            (w_up, None, None),
            (w_down, None, None),
        ],
        [
            whole_out((rows, s.d), BF),
            whole_out((rows, s.d), BF),
            whole_out((rows, s.fn), BF),
            whole_out((rows, s.fn), BF),
            whole_out((s.own, s.d), BF),
            whole_out((s.own, s.d), BF),
            whole_out((1, s.d), F32),
            whole_out((rows, s.dn), F32),
            whole_out((1, s.fn), F32),
            whole_out((rows, s.d), F32),
        ],
        [
            pltpu.VMEM((s.d, s.d), BF),
            pltpu.VMEM((s.d, s.fn), BF),
            pltpu.VMEM((s.fn, s.d), BF),
            pltpu.VMEM((rows, s.fn), F32),
            pltpu.VMEM((rows, s.fn), F32),
            pltpu.VMEM((rows, LANES), F32),
            pltpu.VMEM((rows, LANES), F32),
            pltpu.SemaphoreType.DMA((1 + 2 * s.teams,)),
        ],
    )


def trunk_part(s, scalars, parts, w_down):
    extra = 16
    rows = s.half

    def body(sc, act0, gs0, act1, gs1, *refs):
        downs, (keep, send, out, both, sums) = refs[: s.teams], refs[s.teams :]
        both[0], both[1] = act0[...], act1[...]
        sums[0], sums[1] = gs0[...], gs1[...]

        def one_half(half, carry):
            total = dot(both[half, :, : s.fb], downs[0][...], NN)
            for k in range(1, s.teams):
                total += dot(both[half, :, k * s.fb : (k + 1) * s.fb], downs[k][...], NN)
            out[:rows] = total
            out[rows:] = jnp.broadcast_to(sums[half], (extra, s.d))
            for odd, ref in ((0, keep), (1, send)):
                for n in range(s.members // 2):
                    m = sc[ME] ^ (2 * n + odd)
                    for k in range(s.teams):
                        cols = pl.ds(pl.multiple_of((k * s.members + m) * s.db, s.db), s.db)
                        ref[n, half, :, k * s.db : (k + 1) * s.db] = out[:, cols].astype(BF)
            return carry

        lax.fori_loop(0, 2, one_half, 0)

    pair = (s.members // 2, 2, rows + extra, s.dn)
    return kernel(
        body,
        "trunk_part",
        scalars,
        (1,),
        [whole(x) for part in parts for x in part]
        + [
            (w_down, (s.fb, s.d), lambda i, sc, k=k: (k * s.members + sc[ME], 0))
            for k in range(s.teams)
        ],
        [whole_out(pair, BF), whole_out(pair, BF)],
        [
            pltpu.VMEM((rows + extra, s.d), F32),
            pltpu.VMEM((2, rows, s.fn), BF),
            pltpu.VMEM((2, 1, s.d), F32),
        ],
    )


def norm_two_back(s, scalars, parts, hidden1, grad_mlp, gain):
    chunk = 128
    count = len(parts)

    def body(sc, *refs):
        h1, gm, g, out_ref = refs[count:]

        def rows_chunk(c, carry):
            at = pl.ds(pl.multiple_of(c * chunk, chunk), chunk)
            xhat, rstd = normed_rows(h1[at, :])
            grad = refs[0][at, :].astype(F32)
            for ref in refs[1:count]:
                grad += ref[at, :].astype(F32)
            grad *= g[...]
            back = grad - jnp.mean(grad, axis=-1, keepdims=True)
            back -= xhat * jnp.mean(grad * xhat, axis=-1, keepdims=True)
            out_ref[at, :] = (gm[at, :].astype(F32) + rstd * back).astype(BF)
            return carry

        lax.fori_loop(0, s.own // chunk, rows_chunk, 0)

    return kernel(
        body,
        "norm_two_back",
        scalars,
        (1,),
        [whole(p) for p in parts]
        + [
            (hidden1, (s.own, s.d), lambda i, sc: (lax.rem(sc[ME], 2), 0)),
            (grad_mlp, (s.own, s.d), lambda i, sc: (sc[ME], 0)),
            whole(gain),
        ],
        [whole_out((s.own, s.d), BF)],
    )[0]


def attention_bwd(s, scalars, qkv, saved, grads, w_out, far, before=None):
    base = s.members // 2 if far else 0
    rows = s.own
    last = before is not None
    attended, weights, inverse = saved

    def body(sc, *refs):
        q_ref, kv_ref, att_ref, weight_ref, inv_ref, first, second, wo = refs[:8]
        if last:
            old_ref = refs[10]
            dq_ref, own_ref, out_ref, gh, acc, keys = refs[11:]
        else:
            dq_ref, own_ref, out_ref, gh, acc, keys = refs[8:]
            acc = out_ref
        i = pl.program_id(0)

        @pl.when(i == 0)
        def _():
            if last:
                acc[...] = old_ref[...]
            else:
                acc[...] = jnp.zeros_like(acc)
            keys[...] = jnp.transpose(kv_ref[:, s.width : 2 * s.width].astype(F32)).astype(BF)

        for step, piece in enumerate((first, second)):

            @pl.when(i == step)
            def _():
                gh[...] = dot(piece[...], wo[...], NT)
                for k in range(s.teams):
                    at = pl.multiple_of((k * s.members + sc[ME]) * s.db, s.db)
                    own_ref[:, k * s.db : (k + 1) * s.db] = piece[:, pl.ds(at, s.db)]

        def pair_step(p, carry):
            pair = pl.ds(pl.multiple_of(p * LANES, LANES), LANES)
            value_at = pl.ds(pl.multiple_of(2 * s.width + p * LANES, LANES), LANES)
            dv_at = pl.ds(pl.multiple_of(s.width + p * LANES, LANES), LANES)
            inv = inv_ref[...]
            wide = lax.broadcasted_iota(jnp.int32, inv.shape, 1)
            outs = []
            means = jnp.zeros((rows, LANES), F32)
            for side in range(2):
                h = 2 * p + side
                one = jnp.sum(jnp.where(wide == 8 * h, inv, 0.0), axis=-1, keepdims=True)
                out = (lanes_of(gh[:, pair], side) * one).astype(BF)
                mean = jnp.sum(out.astype(F32) * att_ref[:, pair].astype(F32), axis=-1, keepdims=True)
                means = jnp.where(wide == side, mean, means)
                outs.append(out)
            means = jnp.transpose(means)
            turned = [None, None]
            units = [(c, side) for c in range(0, s.tokens, KEY_CHUNK) for side in range(2)]

            def first_dot(unit):
                c, side = unit
                return dot(kv_ref[c : c + KEY_CHUNK, value_at], outs[side], NT)

            ahead = first_dot(units[0])
            for n, (c, side) in enumerate(units):
                at = slice(c, c + KEY_CHUNK)
                h = 2 * p + side
                gprob = ahead - means[side : side + 1, :]
                if n + 1 < len(units):
                    ahead = first_dot(units[n + 1])
                weight = weight_ref[h, 0, at, :]
                gscore = (weight.astype(F32) * gprob).astype(BF)
                key_rows = pl.ds(pl.multiple_of(h * HEAD_DIM, HEAD_DIM), HEAD_DIM)
                dq = dot(keys[key_rows, at], gscore, NN)
                turned[side] = dq if turned[side] is None else turned[side] + dq
                one = dot(gscore, lanes_of(q_ref[:, pair], side), NN)
                two = dot(weight, outs[side], NN)
                if side == 0:
                    dk, dv = one, two
                else:
                    acc[at, pair] += dk + one
                    acc[at, dv_at] += dv + two
            dq_ref[:, pair] = (jnp.transpose(jnp.concatenate(turned, axis=0)) * 0.125).astype(BF)
            return carry

        lax.fori_loop(0, s.heads // 2, pair_step, 0)

        @pl.when(i == pl.num_programs(0) - 1)
        def _():
            if last:
                out_ref[:, : s.width] = (acc[:, : s.width] * 0.125).astype(BF)
                out_ref[:, s.width :] = acc[:, s.width :].astype(BF)

    member = lambda i, sc: (sc[ME] ^ (base + i), 0)
    side = lambda i, sc: lax.rem(sc[ME] ^ i, s.members // 2)
    ins = [
        (qkv, (rows, 3 * s.width), member),
        whole(qkv),
        (attended, (rows, s.width), lambda i, sc: (side(i, sc), 0)),
        (weights, (s.heads, 1, s.tokens, rows), lambda i, sc: (0, side(i, sc), 0, 0)),
        (inverse, (rows, LANES), lambda i, sc: (side(i, sc), 0)),
        whole(grads[0]),
        whole(grads[1]),
        (w_out, (s.width, s.d), lambda i, sc: (sc[ME], 0)),
    ]
    aliases = None
    if last:
        ins += [(before[0], None, None), (before[1], None, None), whole(before[2])]
        aliases = {9: 0, 10: 1}
    return kernel(
        body,
        "attention_bwd",
        scalars,
        (2,),
        ins,
        [
            ((s.tokens, s.width), BF, (rows, s.width), member),
            ((s.tokens, s.dn), BF, (rows, s.dn), member),
            whole_out((s.tokens, 2 * s.width), BF if last else F32),
        ],
        [
            pltpu.VMEM((rows, s.width), F32),
            pltpu.VMEM((s.tokens, 2 * s.width), F32),
            pltpu.VMEM((s.width, s.tokens), BF),
        ],
        aliases,
    )


def norm_one_grad(s, scalars, qkv, dq, dkv, w_qkv, gain):
    rows = s.half

    def body(sc, qkv_ref, dq_ref, dkv_ref, wq, wk, wv, g, keep, send, grad, stat, lines):
        me = sc[ME]
        total = dot(dq_ref[...], wq[...], NT)
        total += dot(dkv_ref[:, : s.width], wk[...], NT)
        grad[...] = total + dot(dkv_ref[:, s.width :], wv[...], NT)
        gain8 = jnp.broadcast_to(g[...], (8, s.d)).astype(BF)
        parts = ((dq_ref[...], wq), (dkv_ref[:, : s.width], wk), (dkv_ref[:, s.width :], wv))
        one = jnp.zeros((rows, s.width), F32)
        two = jnp.zeros((rows, s.width), F32)
        for k, (value, w) in enumerate(parts):
            value = value.astype(F32)
            one += value * dot(gain8, w[...], NN)[0:1, :]
            two += value * qkv_ref[:, k * s.width : (k + 1) * s.width].astype(F32)
        one = jnp.sum(one, axis=-1, keepdims=True)
        two = jnp.sum(two, axis=-1, keepdims=True)
        lane = lax.broadcasted_iota(jnp.int32, (rows, LANES), 1)
        stat[...] = jnp.where(lane == 0, one, two)
        turned = jnp.transpose(stat[...])
        count = s.tokens // s.dn
        for kind in range(2):
            for n in range(rows // s.dn):
                at = kind * count + n
                step = rows // s.dn
                line = turned[kind : kind + 1, n * s.dn : (n + 1) * s.dn].astype(BF).astype(F32)
                for i in range(s.tokens // rows):

                    @pl.when(pl.program_id(0) == i)
                    def _():
                        lines[at + i * step : at + i * step + 1, :] = line
        at = pl.ds(pl.multiple_of(pl.program_id(0) * rows, rows), rows)
        for odd, ref in ((0, keep), (1, send)):
            for n in range(s.members // 2):
                m = me ^ (2 * n + odd)
                for k in range(s.teams):
                    cols = pl.ds(pl.multiple_of((k * s.members + m) * s.db, s.db), s.db)
                    ref[n, at, k * s.db : (k + 1) * s.db] = grad[:, cols].astype(BF)
                ref[n, s.tokens :, :] = lines[...].astype(BF)

    def third(k):
        return (w_qkv, (s.d, s.width), lambda i, sc: (0, k * s.members + sc[ME]))

    row = lambda i, sc: (i, 0)
    pair = (s.members // 2, s.tokens + 16, s.dn)
    return kernel(
        body,
        "norm_one_grad",
        scalars,
        (s.tokens // rows,),
        [
            (qkv, (rows, 3 * s.width), row),
            (dq, (rows, s.width), row),
            (dkv, (rows, 2 * s.width), row),
            third(0),
            third(1),
            third(2),
            whole(gain),
        ],
        [
            whole_out(pair, BF),
            whole_out(pair, BF),
        ],
        [
            pltpu.VMEM((rows, s.d), F32),
            pltpu.VMEM((rows, LANES), F32),
            pltpu.VMEM((16, s.dn), F32),
        ],
    )


def shift_all(s, parts, out_ref):
    west_ref, mid_ref, east_ref = parts
    rows = s.sec_tokens
    col = lax.rem(lax.broadcasted_iota(jnp.int32, (rows, s.chan), 0), s.cols)

    def one(sector, carry):
        before = west_ref[lax.rem(sector + s.sectors - 1, s.sectors)]
        after = east_ref[lax.rem(sector + 1, s.sectors)]
        west = jnp.where(
            col == 0, pltpu.roll(before, rows - (s.cols - 1), 0), pltpu.roll(west_ref[sector], 1, 0)
        )
        east = jnp.where(
            col == s.cols - 1,
            pltpu.roll(after, s.cols - 1, 0),
            pltpu.roll(east_ref[sector], rows - 1, 0),
        )
        out_ref[sector] = (west + mid_ref[sector] + east).astype(BF)
        return carry

    lax.fori_loop(0, s.sectors, one, 0)


def group_blocks(s, sc, color):
    half = s.group // 2
    for side in range(2):
        for slot in range(half):
            j = 2 * slot + side if color == 0 else side * half + slot
            yield side, slot, sc[GRP] ^ j


def trunk_head(s, scalars, hown, terms, w_head, cot_cat):
    rows = s.half

    def body(sc, near, far, a, b, c, wh0, wh1, cat, home_ref, grad_ref, gain_ref, h2, y0, y1, y2):
        own = sc[ME] // (s.members // 2)
        gains = []
        for half, h1 in enumerate((near, far)):
            side = own ^ half
            total = three_terms(a[0, half, :rows, :], b[0, half, :rows, :], c[0, 1 - half, :rows, :])
            h2[pl.ds(pl.multiple_of(side * rows, rows), rows), :] = (h1[...] + total).astype(BF)
            at = slice(rows, rows + 8)
            gains.append(three_terms(a[0, half, at, :], b[0, half, at, :], c[0, 1 - half, at, :]))
        gain_ref[...] = gains[0] + gains[1]
        for j, ref in enumerate((y0, y1, y2)):
            weight = jnp.concatenate([wh0[j], wh1[j]], axis=1)
            ref[...] = dot(h2[...], weight, NT).reshape(s.sectors, s.sec_tokens, s.chan)
        shift_all(s, (y0, y1, y2), home_ref)
        grad_ref[...] = dot(h2[...], cat[...], TN)

    def part(k):
        return (w_head, (3, s.chan, s.db), lambda i, sc: (0, 0, k * s.members + sc[ME]))

    return kernel(
        body,
        "trunk_head",
        scalars,
        (1,),
        [whole(x) for x in hown]
        + [first(x) for x in terms]
        + [part(0), part(1), whole(cot_cat)],
        [
            whole_out((s.sectors, s.sec_tokens, s.chan), BF),
            whole_out((s.dn, 3 * s.chan), F32),
            whole_out((8, s.dn), F32),
        ],
        [pltpu.VMEM((s.tokens, s.dn), BF)]
        + [pltpu.VMEM((s.sectors, s.sec_tokens, s.chan), F32) for _ in range(3)],
    )


def embed_back(s, scalars, g1, own, stats, hidden0, gain, w_embed, in_cat, head_home, head_part, gain2, bias):
    wide = 3 * s.chan
    span = s.dn

    def body(sc, *refs):
        a, b, c, own_ref, st_ref, h0, h1, g, we0, we1, cat, home, head, gain2_ref, bias_ref = refs[:15]
        keep, send = refs[15:17]
        edges = refs[17 : 17 + s.group]
        grad, stat, y0, y1, y2, ours, part, smalls = refs[17 + s.group :]
        lines = slice(s.tokens, s.tokens + 16)
        total = three_terms(a[0, lines, :], b[0, lines, :], c[0, lines, :]) * np.float32(1.0 / s.d)
        for n in range(s.tokens // span):
            pair = [total[n : n + 1, :], total[s.tokens // span + n : s.tokens // span + n + 1, :]]
            pair = jnp.concatenate(pair + [jnp.zeros((LANES - 2, span), F32)], axis=0)
            stat[n * span : (n + 1) * span, :] = jnp.transpose(pair)
        gain_own = jnp.concatenate(
            [
                g[:, pl.ds(pl.multiple_of((k * s.members + sc[ME]) * s.db, s.db), s.db)]
                for k in range(s.teams)
            ],
            axis=1,
        )
        chunk = s.sec_tokens

        def rows_chunk(i, acc):
            at = pl.ds(pl.multiple_of(i * chunk, chunk), chunk)
            mean, rstd = st_ref[at, 0:1], st_ref[at, 1:2]
            one, two = stat[at, 0:1], stat[at, 1:2]
            g1 = three_terms(a[0, at, :], b[0, at, :], c[0, at, :])
            x = (jnp.concatenate([h0[at, :], h1[at, :]], axis=1) - mean) * rstd
            back = g1 * gain_own - one - x * two
            grad[at, :] = (own_ref[at, :].astype(F32) + rstd * back).astype(BF)
            return acc + jnp.sum(g1 * x, axis=0, keepdims=True)

        gain1 = lax.fori_loop(0, s.tokens // chunk, rows_chunk, jnp.zeros((1, s.dn), F32))
        for j, ref in enumerate((y0, y1, y2)):
            weight = jnp.concatenate([we0[j], we1[j]], axis=1)
            ref[...] = dot(grad[...], weight, NT).reshape(s.sectors, s.sec_tokens, s.chan)
        shift_all(s, (y2, y1, y0), ours)
        for odd, ref in ((0, keep), (1, send)):
            for n in range(s.members // 2):
                for team in range(s.teams):
                    sector = team * s.members + (sc[ME] ^ (2 * n + odd))
                    ref[n, team, 0] = home[sector]
                    ref[n, team, 1] = ours[sector]
        part[:, :wide] = head[...]
        part[:, wide : 2 * wide] = dot(grad[...], cat[...], TN)
        size = s.db // s.group
        for k in range(s.teams):
            lines = [
                bias_ref[:, k * s.fb + n * LANES : k * s.fb + (n + 1) * LANES] for n in range(s.fb // LANES)
            ]
            lines += [gain1[:, k * s.db : (k + 1) * s.db], gain2_ref[0:1, k * s.db : (k + 1) * s.db]]
            lines += [jnp.zeros((size - len(lines), LANES), F32)]
            smalls[...] = jnp.concatenate(lines, axis=0).astype(BF)
            for j, ref in enumerate(edges):
                at = pl.ds(pl.multiple_of(k * s.db + (sc[GRP] ^ j) * size, size), size)
                ref[k, :, : 2 * wide] = part[at, :].astype(BF)
                ref[k, :, 2 * wide :] = smalls[...]

    def part_of(k):
        return (w_embed, (3, s.chan, s.db), lambda i, sc: (0, 0, k * s.members + sc[ME]))

    def own_of(k):
        return (hidden0, (s.tokens, s.db), lambda i, sc: (0, k * s.members + sc[ME]))

    goes = (s.members // 2, s.teams, 2, s.sec_tokens, s.chan)
    size = s.db // s.group
    block = (s.teams, size, 2 * wide + LANES)
    return kernel(
        body,
        "embed_back",
        scalars,
        (1,),
        [first(x) for x in g1]
        + [whole(own), whole(stats), own_of(0), own_of(1), whole(gain), part_of(0), part_of(1)]
        + [whole(in_cat), whole(head_home), whole(head_part), whole(gain2), whole(bias)],
        [whole_out(goes, BF), whole_out(goes, BF)] + [whole_out(block, BF)] * s.group,
        [pltpu.VMEM((s.tokens, s.dn), BF), pltpu.VMEM((s.tokens, LANES), F32)]
        + [pltpu.VMEM((s.sectors, s.sec_tokens, s.chan), F32) for _ in range(3)]
        + [pltpu.VMEM((s.sectors, s.sec_tokens, s.chan), BF)]
        + [pltpu.VMEM((s.dn, 2 * wide), F32), pltpu.VMEM((size, LANES), BF)],
    )


def mlp_weight_grads(s, scalars, near, far, grad_mlp):
    sub = s.fb // s.group

    def body(sc, an, pn, nn_ref, af, pf, nf, gn, gf, ka, sa, kb, sb, scr):
        color = pl.program_id(0)
        kind = pl.program_id(1)

        @pl.when(kind == 0)
        def _():
            scr[...] = (dot(an[...], gn[...], TN) + dot(af[...], gf[...], TN)).astype(BF)

        @pl.when(kind == 1)
        def _():
            scr[...] = (dot(pn[...], nn_ref[...], TN) + dot(pf[...], nf[...], TN)).astype(BF)

        for k, refs in enumerate(((ka, sa), (kb, sb))):

            @pl.when(color == k)
            def _():
                def lane_block(c, carry):
                    lanes = pl.ds(pl.multiple_of(c * LANES, LANES), LANES)
                    to = pl.ds(pl.multiple_of(c * sub, sub), sub)
                    for side, slot, q in group_blocks(s, sc, k):
                        rows = pl.ds(pl.multiple_of(q * sub, sub), sub)
                        refs[side][slot, 0, to, :] = scr[rows, lanes]
                    return carry

                lax.fori_loop(0, s.d // LANES, lane_block, 0)

    def out(color):
        shape = (s.group // 2, 2, s.d, LANES)
        block = (s.group // 2, 1, s.d, LANES)
        if color == 0:
            index = lambda k, kind, sc: (0, jnp.where(k == 0, kind, 1), 0, 0)
        else:
            index = lambda k, kind, sc: (0, jnp.where(k == 0, 0, kind), 0, 0)
        return (shape, BF, block, index)

    cols = lambda k, kind, sc: (0, k)
    ins = []
    for activ, grad_pre, normed in (near, far):
        ins += [
            (activ, (s.half, s.fb), cols),
            (grad_pre, (s.half, s.fb), cols),
            whole(normed),
        ]
    ins += [
        (grad_mlp, (s.half, s.d), lambda k, kind, sc: (side_of(s, sc, False), 0)),
        (grad_mlp, (s.half, s.d), lambda k, kind, sc: (side_of(s, sc, True), 0)),
    ]
    return kernel(
        body,
        "mlp_weight_grads",
        scalars,
        (s.teams, 2),
        ins,
        [out(0), out(0), out(1), out(1)],
        [pltpu.VMEM((s.fb, s.d), BF)],
    )


def attention_weight_grads(s, scalars, normed1, dq, dkv, att_near, att_far, own):
    def body(sc, n1, dq_ref, dkv_ref, an, af, own_near, own_far, ka, sa, kb, sb, scr):
        scr[: s.width] = dot(dq_ref[...], n1[...], TN).astype(BF)
        scr[s.width : 3 * s.width] = dot(dkv_ref[...], n1[...], TN).astype(BF)
        scr[3 * s.width :] = (dot(own_near[...], an[...], TN) + dot(own_far[...], af[...], TN)).astype(BF)

        def lane_block(c, carry):
            lanes = pl.ds(pl.multiple_of(c * LANES, LANES), LANES)
            for k, refs in enumerate(((ka, sa), (kb, sb))):
                for side, slot, q in group_blocks(s, sc, k):
                    rows = pl.ds(pl.multiple_of((k * s.group + q) * LANES, LANES), LANES)
                    refs[side][slot, lanes, :] = scr[rows, lanes]
            return carry

        lax.fori_loop(0, s.d // LANES, lane_block, 0)

    shape = (s.group // 2, s.d, LANES)
    return kernel(
        body,
        "attention_weight_grads",
        scalars,
        (1,),
        [
            whole(normed1),
            whole(dq),
            whole(dkv),
            whole(att_near),
            whole(att_far),
            (own, (s.half, s.dn), lambda i, sc: (side_of(s, sc, False), 0)),
            (own, (s.half, s.dn), lambda i, sc: (side_of(s, sc, True), 0)),
        ],
        [whole_out(shape, BF)] * 4,
        [pltpu.VMEM((3 * s.width + s.dn, s.d), BF)],
    )


def add_low(a, b):
    return (a.astype(F32) + b.astype(F32)).astype(BF)


def first(x):
    rank = len(x.shape)
    return (x, (1,) + tuple(x.shape[1:]), lambda *_: (0,) * rank)


def three_terms(keep, got, more):
    return keep.astype(F32) + got.astype(F32) + more.astype(F32)


def group_first(keep_a, send_a, keep_b, send_b):
    got_a = swap(send_a, "grp", 1)
    got_b = swap(send_b, "grp", 2)
    return (keep_a, got_a), (keep_b, got_b), (add_low(keep_a[1], got_a[1]), add_low(keep_b[1], got_b[1]))


def group_second(terms_a, terms_b, sends):
    more_a = swap(sends[0], "grp", 2)
    more_b = swap(sends[1], "grp", 1)
    return terms_a + (more_a[None],), terms_b + (more_b[None],)


def pick_team(s, scalars, terms_a, terms_b, kinds):
    half = s.d // 2

    def body(sc, *refs):
        a, b = refs[:3], refs[3:6]
        keep, send = refs[6:]
        team = sc[TEAM]

        def total(terms, k, rows):
            at = (0, k, rows) if kinds == 2 else (0, rows)
            return three_terms(*[ref[at] for ref in terms]).astype(BF)

        if kinds == 2:
            for side in range(2):

                @pl.when(team == side)
                def _():
                    same, other = (a, b) if side == 0 else (b, a)
                    keep[0] = total(same, 0, slice(None))
                    send[0] = total(other, 0, slice(None))

        mine = pl.ds(pl.multiple_of(team * half, half), half)
        theirs = pl.ds(pl.multiple_of((1 - team) * half, half), half)
        for color, terms in enumerate((a, b)):
            at = slice(color * half, (color + 1) * half)
            keep[kinds - 1, at] = total(terms, 1, mine)
            send[kinds - 1, at] = total(terms, 1, theirs)

    return kernel(
        body,
        "pick_team",
        scalars,
        (1,),
        [first(x) for x in terms_a + terms_b],
        [whole_out((kinds, s.d, LANES), BF)] * 2,
    )


def pick_member(s, scalars, keep, got):
    kinds = keep.shape[0]
    half = s.d // 2

    def body(sc, k_ref, g_ref, *refs):
        for j in range(s.members):
            m = sc[ME] ^ j
            for color in range(2):
                at = pl.ds(pl.multiple_of(color * half + m * s.db, s.db), s.db)
                value = k_ref[kinds - 1, at].astype(F32) + g_ref[kinds - 1, at].astype(F32)
                refs[j][color] = value.astype(BF)
        if kinds == 2:
            refs[s.members][...] = (k_ref[0].astype(F32) + g_ref[0].astype(F32)).astype(BF)

    outs = [whole_out((2, s.db, LANES), BF)] * s.members
    if kinds == 2:
        outs = outs + [whole_out((s.d, LANES), BF)]
    return kernel(body, "pick_member", scalars, (1,), [whole(keep), whole(got)], outs)


def all_of_group(x, x_first):
    near, far = (1, 2) if x_first else (2, 1)
    one = swap(x, "grp", near)
    two = swap(x, "grp", far)
    both = swap(one, "grp", far)
    return [x, one, two, both] if x_first else [x, two, one, both]


def cross(s, pieces):
    got = [pieces[0]] + [swap(pieces[j], "sec", j) for j in range(1, s.members)]
    return jnp.stack(got)


def mlp_grads_out(s, scalars, downs, ups):
    sub = s.fb // s.group

    def body(sc, *refs):
        d_refs, u_refs = refs[: s.group], refs[s.group : 2 * s.group]
        down, up = refs[2 * s.group :]
        for j in range(s.group):
            q = sc[GRP] ^ j
            rows = pl.ds(pl.multiple_of(q * sub, sub), sub)
            for c in range(s.d // LANES):
                down[rows, c * LANES : (c + 1) * LANES] = d_refs[j][c * sub : (c + 1) * sub, :].astype(F32)

            def member(jm, carry):
                m = sc[ME] ^ jm
                for color in range(s.teams):
                    at = ((color * s.members + m) * s.group + q) * LANES
                    up[:, pl.ds(pl.multiple_of(at, LANES), LANES)] = jnp.transpose(u_refs[j][jm, color].astype(F32))
                return carry

            lax.fori_loop(0, s.members, member, 0)

    return kernel(
        body,
        "mlp_grads_out",
        scalars,
        (1,),
        [whole(x) for x in downs + ups],
        [whole_out((s.fb, s.d), F32), whole_out((s.db, s.ff), F32)],
    )


def attention_grads_out(s, scalars, parts):
    def body(sc, *refs):
        u_refs = refs[: s.group]
        qkv, out = refs[s.group :]
        for j in range(s.group):
            q = sc[GRP] ^ j

            def member(jm, carry):
                m = sc[ME] ^ jm
                at = (q // 2) * s.d + m * s.width + lax.rem(q, 2) * LANES
                value = jnp.transpose(u_refs[j][jm, 0].astype(F32))
                qkv[:, pl.ds(pl.multiple_of(at, LANES), LANES)] = value
                other = jnp.transpose(u_refs[j][jm, 1].astype(F32))

                @pl.when(q < 2)
                def _():
                    at = 2 * s.d + m * s.width + q * LANES
                    qkv[:, pl.ds(pl.multiple_of(at, LANES), LANES)] = other

                @pl.when(q >= 2)
                def _():
                    at = ((q - 2) * s.members + m) * s.db
                    out[:, pl.ds(pl.multiple_of(at, LANES), LANES)] = other

                return carry

            lax.fori_loop(0, s.members, member, 0)

    return kernel(
        body,
        "attention_grads_out",
        scalars,
        (1,),
        [whole(x) for x in parts],
        [whole_out((s.db, 3 * s.d), F32), whole_out((s.db, s.d), F32)],
    )


def edge_grads_out(s, scalars, parts):
    wide = 3 * s.chan
    size = s.db // s.group

    def body(sc, *refs):
        ins = refs[: s.group]
        embed, head, small, scr = refs[s.group :]
        for j in range(s.group):
            at = pl.ds(pl.multiple_of((sc[GRP] ^ j) * size, size), size)
            scr[at, :] = ins[j][...].astype(F32)
        head[...] = jnp.transpose(scr[:, :wide])
        embed[...] = jnp.transpose(scr[:, wide : 2 * wide])
        small[...] = ins[0][:16, 2 * wide :].astype(F32)

    return kernel(
        body,
        "edge_grads_out",
        scalars,
        (1,),
        [whole(x) for x in parts],
        [
            whole_out((wide, s.db), F32),
            whole_out((wide, s.db), F32),
            whole_out((16, LANES), F32),
        ],
        [pltpu.VMEM((s.db, 2 * wide + LANES), F32)],
    )


def on_team(
    fields,
    valid_rows,
    w_embed,
    ln1_gain,
    w_qkv,
    w_out,
    ln2_gain,
    w_up,
    b_up,
    w_down,
    w_head,
    cotangent,
):
    s = Sizes(fields, w_qkv, w_up)
    place = lax.axis_index("sec")
    team, me = place // s.members, place % s.members
    core, chip = 1, 2
    first_team = team == 0
    valid = jnp.where(first_team, valid_rows[0], valid_rows[1])
    scalars = (jnp.stack([team, me, lax.axis_index("grp"), valid]).astype(jnp.int32), [])

    def gather_pair(x):
        flat = x.reshape(s.teams, s.sec_tokens, s.chan)
        mine = jnp.where(first_team, flat[0], flat[1])
        other = swap(jnp.where(first_team, flat[1], flat[0]), "sec", s.members)
        return jnp.stack([mine, other])

    def gather_sample(pair):
        across = swap(pair, "sec", chip)
        return [pair, swap(pair, "sec", core), across, swap(across, "sec", core)]

    def go_home(keep, got, far):
        mine = three_terms(keep[0], got[0], far)
        other = jnp.where(first_team, mine[1], mine[0]).astype(BF)
        return mine, swap(other, "sec", s.members)

    def at_home(mine, other):
        own = jnp.where(first_team, mine[0], mine[1])
        other = other.astype(F32)
        both = [jnp.where(first_team, own, other), jnp.where(first_team, other, own)]
        return [jnp.stack([x[kind] for x in both]).reshape(fields.shape) for kind in range(2)]

    def scatter_features(keep, send):
        got = swap(send, "sec", core)
        return keep, got, swap(add_low(keep[1:2], got[1:2]), "sec", chip)

    w_head_t = jnp.transpose(w_head, (0, 2, 1))
    fields_pair = gather_pair(fields)
    late1, late2, b_up = after([ln1_gain, ln2_gain, b_up], fields_pair)
    gain1 = late1.astype(F32)[None]
    gain2 = late2.astype(F32)[None]
    in_cat, hidden0, normed1, qkv, stats = embed_qkv(
        s, scalars, gather_sample(fields_pair), w_embed.reshape(3 * s.chan, s.d), gain1, w_qkv
    )
    att_near, *rest = attention_fwd(s, scalars, qkv, False)
    saved_near = (att_near, *rest)
    from_chip_far = swap(att_near, "sec", chip)
    att_far, *rest = attention_fwd(s, scalars, qkv, True)
    saved_far = (att_far, *rest)
    from_chip_near = swap(att_far, "sec", chip)
    hold(scalars, from_chip_far)
    cot_cat, grad_mlp = cotangent_grad(
        s, scalars, gather_sample(gather_pair(cotangent)), w_head_t.reshape(3 * s.chan, s.d)
    )
    att_pieces_far = [att_far, swap(att_far, "sec", core), from_chip_far, swap(from_chip_far, "sec", core)]
    att_pieces_near = [att_near, swap(att_near, "sec", core), from_chip_near, swap(from_chip_near, "sec", core)]

    def run_mlp(pieces, far):
        return mlp(s, scalars, pieces, hidden0, grad_mlp, w_out, gain2, w_up, b_up, w_down, far)

    attended_far, normed2_far, activ_far, pre_far, gkeep, gsend, gsum, hown_far, bias_far, _ = run_mlp(
        att_pieces_far, True
    )
    hold(scalars, from_chip_near)
    g2_chip = [swap(gkeep, "sec", chip), swap(gsend, "sec", chip + core)]
    attended_near, normed2_near, activ_near, pre_near, gkeep, gsend, gsum_near, hown_near, bias_near, hidden1 = run_mlp(
        att_pieces_near, False
    )
    bias_grad = bias_far + bias_near
    got = swap(gsend, "sec", core)
    pkeep, psend = trunk_part(s, scalars, ((activ_near, gsum_near), (activ_far, gsum)), w_down)
    b0 = norm_two_back(s, scalars, [gkeep, got, *g2_chip], hidden1, grad_mlp, gain2)
    b1 = swap(b0, "sec", core)
    b2 = swap(b0, "sec", chip)
    b3 = swap(b2, "sec", core)
    mlp_blocks = mlp_weight_grads(
        s, scalars, (activ_near, pre_near, normed2_near), (activ_far, pre_far, normed2_far), grad_mlp
    )
    hold(scalars, b2)
    mlp_a, mlp_b, mlp_sends = group_first(*mlp_blocks)
    before = attention_bwd(s, scalars, qkv, saved_near, (b0, b1), w_out, False)
    hold(scalars, b3, *mlp_sends)
    mlp_terms = group_second(mlp_a, mlp_b, mlp_sends)
    trunk_terms = scatter_features(pkeep, psend)
    dq, own, dkv = attention_bwd(s, scalars, qkv, saved_far, (b2, b3), w_out, True, before)
    hold(scalars, *[terms[2] for terms in mlp_terms])
    att_blocks = attention_weight_grads(s, scalars, normed1, dq, dkv, attended_near, attended_far, own)
    att_a, att_b, att_sends = group_first(*att_blocks)
    mlp_kept, send = pick_team(s, scalars, *mlp_terms, 2)
    mlp_swapped = swap(send, "sec", s.members)
    g1_keep, g1_send = norm_one_grad(s, scalars, qkv, dq, dkv, w_qkv, gain1)
    hold(scalars, *att_sends)
    att_terms = group_second(att_a, att_b, att_sends)
    hold(scalars, trunk_terms[2])
    head_home, head_part, gain2_grad = trunk_head(
        s, scalars, (hown_near, hown_far), trunk_terms, w_head_t, cot_cat
    )
    g1_got = swap(g1_send, "sec", core)
    g1_sum = add_low(g1_keep[1:2], g1_got[1:2])
    g1 = (g1_keep, g1_got, swap(g1_sum, "sec", chip))
    hold(scalars, g1_sum, *[terms[2] for terms in att_terms])
    att_kept, send = pick_team(s, scalars, *att_terms, 1)
    att_swapped = swap(after([send], g1[2])[0], "sec", s.members)
    *crossed, downs = pick_member(s, scalars, mlp_kept, mlp_swapped)
    crossed = [crossed[0]] + [swap(crossed[j], "sec", j) for j in range(1, s.members)]
    downs = [downs, swap(downs, "grp", 1), swap(downs, "grp", 2)]
    keep, send, *edges = embed_back(
        s, scalars, g1, own, stats, hidden0, gain1, w_embed, in_cat, head_home, head_part, gain2_grad, bias_grad
    )
    edges = edges[:1] + [swap(edges[j], "grp", j) for j in range(1, s.group)]
    home_got = swap(send, "sec", core)
    ups = jnp.stack(after(crossed, edges[0]))
    ups = [ups, swap(ups, "grp", 1), swap(ups, "grp", 2)]
    mlp_parts = (
        downs + [swap(after(downs[2:], edges[0])[0], "grp", 1)],
        ups + [swap(ups[1], "grp", 2)],
    )
    crossed = pick_member(s, scalars, att_kept, att_swapped)
    att_parts = all_of_group(cross(s, crossed), True)
    home_far = swap(add_low(keep[1], home_got[1]), "sec", chip)
    down_grad, up_grad = mlp_grads_out(s, scalars, *mlp_parts)
    hold(scalars, home_far)
    home_mine, home_other = go_home(keep, home_got, home_far)

    total = edges[0].astype(F32) + edges[1].astype(F32) + edges[2].astype(F32) + edges[3].astype(F32)
    kept = jnp.where(first_team, total[0], total[1])
    given = jnp.where(first_team, total[1], total[0]).astype(BF)
    edges = (kept + swap(given, "sec", s.members).astype(F32)).astype(BF)
    edge_parts = all_of_group(edges, True)
    qkv_grad, out_grad = attention_grads_out(s, scalars, att_parts)
    hold(scalars, home_other)
    head_output, input_grad = at_home(home_mine, home_other)
    embed_t, head_t, small = edge_grads_out(s, scalars, edge_parts)
    embed_grad = embed_t.reshape(3, s.chan, s.db)
    head_grad = jnp.transpose(head_t.reshape(3, s.chan, s.db), (0, 2, 1))
    nb = s.fb // LANES
    return (
        head_output,
        input_grad,
        embed_grad,
        small[nb],
        qkv_grad,
        out_grad,
        small[nb + 1],
        up_grad,
        small[:nb].reshape(s.fb),
        down_grad,
        head_grad,
    )

LAT = 32
KCOLS = 8


def extended(cells, sides, width):
    for axis, dim in sides:
        count = lax.axis_size(axis)
        head = lax.slice_in_dim(cells, 0, width, axis=dim)
        tail = lax.slice_in_dim(cells, cells.shape[dim] - width, cells.shape[dim], axis=dim)
        cells = jnp.concatenate(
            [
                lax.ppermute(tail, axis, [(i, (i + 1) % count) for i in range(count)]),
                cells,
                lax.ppermute(head, axis, [((i + 1) % count, i) for i in range(count)]),
            ],
            axis=dim,
        )
    return cells


def normed(hidden, gains):
    center = hidden - jnp.mean(hidden, axis=-1, keepdims=True)
    spread = jnp.mean(center * center, axis=-1, keepdims=True)
    return center * lax.rsqrt(spread + 1e-05) * gains


def gelu_exact(values):
    return jax.nn.gelu(values, approximate=False)


def three_cols(padded, col_count, west_first):
    west_cols = padded[:, :, 0:col_count]
    middle_cols = padded[:, :, 1 : col_count + 1]
    east_cols = padded[:, :, 2 : col_count + 2]
    if west_first:
        return jnp.stack([west_cols, middle_cols, east_cols], axis=3)
    return jnp.stack([east_cols, middle_cols, west_cols], axis=3)


def split_heads(values):
    return values.reshape(values.shape[0], -1, HEADS, HEAD_DIM)


def key_mask(valid_rows, count_cols):
    rows_ok = jnp.arange(LAT)[None, :] < valid_rows[:, None]
    spread_ok = jnp.broadcast_to(rows_ok[:, :, None], (rows_ok.shape[0], LAT, count_cols))
    return spread_ok.reshape(rows_ok.shape[0], LAT * count_cols)


def key_scores(queries, kv_piece, valid_rows):
    d_model = HEADS * HEAD_DIM
    key_part = split_heads(kv_piece[..., :d_model])
    value_part = split_heads(kv_piece[..., d_model:])
    scores = (
        jnp.einsum("sqhd,skhd->shqk", queries, key_part, preferred_element_type=jnp.float32) * 0.125
    )
    allowed = key_mask(valid_rows, kv_piece.shape[2])
    scores = jnp.where(allowed[:, None, None, :], scores, -1e30)
    return (scores, key_part, value_part)


def softmax_fold(queries, valid_rows):

    def fold_piece(run_state, kv_piece, first_col):
        run_max, run_sum, run_acc = run_state
        scores, key_part, value_part = key_scores(queries, kv_piece, valid_rows)
        new_max = jnp.maximum(run_max, jnp.max(scores, axis=-1))
        factor = jnp.exp(run_max - new_max)
        weights = jnp.exp(scores - new_max[..., None])
        new_sum = run_sum * factor + jnp.sum(weights, axis=-1)
        added = jnp.einsum(
            "shqk,skhd->sqhd",
            weights.astype(jnp.bfloat16),
            value_part,
            preferred_element_type=jnp.float32,
        )
        new_acc = run_acc * jnp.transpose(factor, (0, 2, 1))[..., None] + added
        return (new_max, new_sum, new_acc)

    return fold_piece


def on_sectors(
    fields,
    valid_rows,
    w_embed,
    ln1_gain,
    w_qkv,
    w_out,
    ln2_gain,
    w_up,
    b_up,
    w_down,
    w_head,
    cotangent,
):
    samples, lat_rows, col_count, channels = fields.shape
    d_model = w_qkv.shape[0]
    token_count = lat_rows * col_count
    padded_in = extended(fields, (("sec", 2),), 1)
    input_cat = three_cols(padded_in, col_count, True)
    hidden0 = jnp.einsum("slcoi,oid->slcd", input_cat, w_embed, preferred_element_type=jnp.float32)
    normed_one, norm_one_back = jax.vjp(normed, hidden0, ln1_gain.astype(jnp.float32))
    normed_one_low = normed_one.astype(jnp.bfloat16)
    qkv_full = jnp.einsum(
        "slcd,de->slce", normed_one_low, w_qkv, preferred_element_type=jnp.float32
    ).astype(jnp.bfloat16)
    queries = split_heads(qkv_full[..., :d_model])
    key_vals = qkv_full[..., d_model:]
    init_state = (
        jnp.full((samples, HEADS, token_count), -1e30, jnp.float32),
        jnp.zeros((samples, HEADS, token_count), jnp.float32),
        jnp.zeros((samples, token_count, HEADS, HEAD_DIM), jnp.float32),
    )
    fold_piece = softmax_fold(queries, valid_rows)
    all_kv = lax.all_gather(key_vals, "sec", axis=2, tiled=True)

    def forward_block(block_index, run_state):
        kv_block = lax.dynamic_slice_in_dim(all_kv, block_index * KCOLS, KCOLS, 2)
        return fold_piece(run_state, kv_block, block_index * KCOLS)

    run_max, run_sum, run_acc = lax.fori_loop(
        0, all_kv.shape[2] // KCOLS, forward_block, init_state
    )
    attended = run_acc / jnp.transpose(run_sum, (0, 2, 1))[..., None]
    log_total = run_max + jnp.log(run_sum)
    attended_low = attended.reshape(samples, lat_rows, col_count, d_model).astype(jnp.bfloat16)
    hidden1 = hidden0 + jnp.einsum(
        "slcd,de->slce", attended_low, w_out, preferred_element_type=jnp.float32
    )
    normed_two, norm_two_back = jax.vjp(normed, hidden1, ln2_gain.astype(jnp.float32))
    normed_two_low = normed_two.astype(jnp.bfloat16)
    preact = jnp.einsum(
        "slcd,df->slcf", normed_two_low, w_up, preferred_element_type=jnp.float32
    ) + b_up.astype(jnp.float32)
    activ, gelu_back = jax.vjp(gelu_exact, preact)
    activ_low = activ.astype(jnp.bfloat16)
    hidden2 = hidden1 + jnp.einsum(
        "slcf,fd->slcd", activ_low, w_down, preferred_element_type=jnp.float32
    )
    hidden2_low = hidden2.astype(jnp.bfloat16)
    padded_hidden = extended(hidden2_low, (("sec", 2),), 1)
    hidden_cat = three_cols(padded_hidden, col_count, True)
    head_output = jnp.einsum(
        "slcod,odi->slci", hidden_cat, w_head, preferred_element_type=jnp.float32
    )
    padded_cot = extended(cotangent, (("sec", 2),), 1)
    cot_cat = three_cols(padded_cot, col_count, False)
    head_grad = jnp.einsum(
        "slcod,slci->odi", hidden_cat, cotangent, preferred_element_type=jnp.float32
    )
    grad_two = jnp.einsum("slcoi,odi->slcd", cot_cat, w_head, preferred_element_type=jnp.float32)
    grad_mlp = grad_two.astype(jnp.bfloat16)
    down_grad = jnp.einsum("slcf,slcd->fd", activ_low, grad_mlp, preferred_element_type=jnp.float32)
    grad_act = jnp.einsum("slcd,fd->slcf", grad_mlp, w_down, preferred_element_type=jnp.float32)
    grad_pre = gelu_back(grad_act)[0].astype(jnp.bfloat16)
    bias_grad = jnp.sum(grad_pre.astype(jnp.float32), axis=(0, 1, 2))
    up_grad = jnp.einsum(
        "slcd,slcf->df", normed_two_low, grad_pre, preferred_element_type=jnp.float32
    )
    grad_normed_two = jnp.einsum(
        "slcf,df->slcd", grad_pre, w_up, preferred_element_type=jnp.float32
    )
    grad_from_norm, gain_two_grad = norm_two_back(grad_normed_two)
    grad_one = grad_two + grad_from_norm
    grad_att = grad_one.astype(jnp.bfloat16)
    out_grad = jnp.einsum(
        "slcd,slce->de", attended_low, grad_att, preferred_element_type=jnp.float32
    )
    grad_heads = split_heads(
        jnp.einsum("slce,de->slcd", grad_att, w_out, preferred_element_type=jnp.float32).astype(
            jnp.bfloat16
        )
    )
    row_delta = jnp.transpose(
        jnp.sum(grad_heads.astype(jnp.float32) * attended, axis=-1), (0, 2, 1)
    )

    def sample_backward(unused_carry, sample_in):
        one_query, one_grad, one_lse, one_delta, one_valid, one_kv = sample_in
        term_zero = jnp.zeros((1, lat_rows, one_kv.shape[2], 2 * d_model), jnp.bfloat16)
        grad_zero = jnp.zeros(one_query.shape, jnp.float32)

        def backward_block(block_index, run_state):
            grad_query, term = run_state
            kv_block = lax.dynamic_slice_in_dim(one_kv, block_index * KCOLS, KCOLS, 2)
            scores, key_part, value_part = key_scores(one_query, kv_block, one_valid)
            probs = jnp.exp(scores - one_lse[..., None])
            grad_probs = jnp.einsum(
                "sqhd,skhd->shqk", one_grad, value_part, preferred_element_type=jnp.float32
            )
            grad_scores = (probs * (grad_probs - one_delta[..., None])).astype(jnp.bfloat16)
            grad_query = (
                grad_query
                + jnp.einsum(
                    "shqk,skhd->sqhd", grad_scores, key_part, preferred_element_type=jnp.float32
                )
                * 0.125
            )
            grad_keys = (
                jnp.einsum(
                    "shqk,sqhd->skhd", grad_scores, one_query, preferred_element_type=jnp.float32
                )
                * 0.125
            )
            grad_values = jnp.einsum(
                "shqk,sqhd->skhd",
                probs.astype(jnp.bfloat16),
                one_grad,
                preferred_element_type=jnp.float32,
            )
            joined = jnp.concatenate(
                [
                    grad_keys.reshape(1, lat_rows, KCOLS, d_model),
                    grad_values.reshape(1, lat_rows, KCOLS, d_model),
                ],
                axis=-1,
            ).astype(jnp.bfloat16)
            term = lax.dynamic_update_slice_in_dim(term, joined, block_index * KCOLS, 2)
            return (grad_query, term)

        grad_query, term = lax.fori_loop(
            0, one_kv.shape[2] // KCOLS, backward_block, (grad_zero, term_zero)
        )
        summed = lax.psum_scatter(
            term.astype(jnp.float32).astype(jnp.bfloat16), "sec", scatter_dimension=2, tiled=True
        ).astype(jnp.float32)
        return (unused_carry, (grad_query, summed))

    scan_inputs = (
        queries.reshape(samples, 1, token_count, HEADS, HEAD_DIM),
        grad_heads.reshape(samples, 1, token_count, HEADS, HEAD_DIM),
        log_total.reshape(samples, 1, HEADS, token_count),
        row_delta.reshape(samples, 1, HEADS, token_count),
        valid_rows.reshape(samples, 1),
        all_kv.reshape(samples, 1, lat_rows, all_kv.shape[2], 2 * d_model),
    )
    scan_end, (grad_queries, grad_kv) = lax.scan(sample_backward, 0, scan_inputs)
    grad_qkv = jnp.concatenate(
        [
            grad_queries.reshape(samples, lat_rows, col_count, d_model),
            grad_kv.reshape(samples, lat_rows, col_count, 2 * d_model),
        ],
        axis=-1,
    ).astype(jnp.bfloat16)
    qkv_grad = jnp.einsum(
        "slcd,slce->de", normed_one_low, grad_qkv, preferred_element_type=jnp.float32
    )
    grad_normed_one = jnp.einsum(
        "slce,de->slcd", grad_qkv, w_qkv, preferred_element_type=jnp.float32
    )
    grad_from_first, gain_one_grad = norm_one_back(grad_normed_one)
    grad_zero_low = (grad_one + grad_from_first).astype(jnp.bfloat16)
    embed_grad = jnp.einsum(
        "slcoi,slcd->oid", input_cat, grad_zero_low, preferred_element_type=jnp.float32
    )
    padded_grad = extended(grad_zero_low, (("sec", 2),), 1)
    grad_cat = three_cols(padded_grad, col_count, False)
    input_grad = jnp.einsum(
        "slcod,oid->slci", grad_cat, w_embed, preferred_element_type=jnp.float32
    )
    shard_grads = (
        lax.psum_scatter(
            embed_grad.astype(jnp.bfloat16), "sec", scatter_dimension=2, tiled=True
        ).astype(jnp.float32),
        lax.psum_scatter(
            gain_one_grad.astype(jnp.bfloat16), "sec", scatter_dimension=0, tiled=True
        ).astype(jnp.float32),
        lax.psum_scatter(
            qkv_grad.astype(jnp.bfloat16), "sec", scatter_dimension=0, tiled=True
        ).astype(jnp.float32),
        lax.psum_scatter(
            out_grad.astype(jnp.bfloat16), "sec", scatter_dimension=0, tiled=True
        ).astype(jnp.float32),
        lax.psum_scatter(
            gain_two_grad.astype(jnp.bfloat16), "sec", scatter_dimension=0, tiled=True
        ).astype(jnp.float32),
        lax.psum_scatter(
            up_grad.astype(jnp.bfloat16), "sec", scatter_dimension=0, tiled=True
        ).astype(jnp.float32),
        lax.psum_scatter(
            bias_grad.astype(jnp.bfloat16), "sec", scatter_dimension=0, tiled=True
        ).astype(jnp.float32),
        lax.psum_scatter(
            down_grad.astype(jnp.bfloat16), "sec", scatter_dimension=0, tiled=True
        ).astype(jnp.float32),
        lax.psum_scatter(
            head_grad.astype(jnp.bfloat16), "sec", scatter_dimension=1, tiled=True
        ).astype(jnp.float32),
    )
    total_grads = (
        lax.psum(shard_grads[0].astype(jnp.bfloat16), "grp").astype(jnp.float32),
        lax.psum(shard_grads[1].astype(jnp.bfloat16), "grp").astype(jnp.float32),
        lax.psum(shard_grads[2].astype(jnp.bfloat16), "grp").astype(jnp.float32),
        lax.psum(shard_grads[3].astype(jnp.bfloat16), "grp").astype(jnp.float32),
        lax.psum(shard_grads[4].astype(jnp.bfloat16), "grp").astype(jnp.float32),
        lax.psum(shard_grads[5].astype(jnp.bfloat16), "grp").astype(jnp.float32),
        lax.psum(shard_grads[6].astype(jnp.bfloat16), "grp").astype(jnp.float32),
        lax.psum(shard_grads[7].astype(jnp.bfloat16), "grp").astype(jnp.float32),
        lax.psum(shard_grads[8].astype(jnp.bfloat16), "grp").astype(jnp.float32),
    )
    return (
        head_output,
        input_grad,
        total_grads[0],
        total_grads[1],
        total_grads[2],
        total_grads[3],
        total_grads[4],
        total_grads[5],
        total_grads[6],
        total_grads[7],
        total_grads[8],
    )


def on_device(*args):
    fields, w_qkv = args[0], args[4]
    sectors = lax.axis_size("sec")
    fits = (
        fields.shape[0] == 2
        and sectors == 8
        and lax.axis_size("grp") == 4
        and w_qkv.shape[0] == sectors * LANES
    )
    return on_team(*args) if fits else on_sectors(*args)


def solution(mesh):
    tokens_in = P("grp", None, "sec", None)
    return jax.shard_map(
        on_device,
        mesh=mesh,
        in_specs=(tokens_in, P("grp")) + (P(),) * 9 + (tokens_in,),
        out_specs=(
            tokens_in,
            tokens_in,
            P(None, None, "sec"),
            P("sec"),
            P("sec", None),
            P("sec", None),
            P("sec"),
            P("sec", None),
            P("sec"),
            P("sec", None),
            P(None, "sec", None),
        ),
        check_vma=False,
    )
```
